32 devices in a mesh: dp: 8 (over y, x, core), ctx: 4 (over z).
Axes of the slice: x: 2, y: 2, z: 4, core: 2. Of those that a mesh axis runs over, the one named last changes fastest.
Arguments:
- tokens: bfloat16 [16, 256, 1024], P('dp', 'ctx'), may hold values from -6 to 6
- out_grad: bfloat16 [16, 256, 1024], P('dp', 'ctx'), may hold values from -6 to 6
- lengths: int32 [16], P('dp'), may hold values from 64 to 256, as said below
- w_qkv: bfloat16 [1024, 3072], replicated, may hold values from -0.1875 to 0.1875
- w_out: bfloat16 [1024, 1024], replicated, may hold values from -3 to 3
- w_in: bfloat16 [1024, 4096], replicated, may hold values from -0.1875 to 0.1875
- w_fc2: bfloat16 [4096, 1024], replicated, may hold values from -0.09375 to 0.09375
- vectors: float32 [12, 1024], replicated, may hold values from -0.15 to 1.3
- moment_one: float32 [32, 393600], P(('dp', 'ctx')), may hold values from -6 to 6
- moment_two: float32 [32, 393600], P(('dp', 'ctx')), may hold values from 1 to 100
Outputs:
- out: bfloat16 [16, 256, 1024], P('dp', 'ctx')
- tokens_grad: bfloat16 [16, 256, 1024], P('dp', 'ctx')
- grad_rows: float32 [32, 393600], P(('dp', 'ctx'))
- new_params: float32 [32, 393600], P(('dp', 'ctx'))
- new_one: float32 [32, 393600], P(('dp', 'ctx'))
- new_two: float32 [32, 393600], P(('dp', 'ctx'))
The draws below stay inside these ranges and needn't reach their ends.
Inputs may be any that keep to these rules, and one draw needn't show every extreme that they name: `lengths`: each slot holds one sequence starting at its first position; in every draw one slot is full and one holds 64 positions.
All inputs are finite; a program needn't handle non-finite values.
Results may differ from the reference program's by a relative error of at most 0.015.
Values may be sent and summed in bfloat16 or wider, within the bound.
A program may use at most 320 MiB of HBM per device.

```python
import math
import jax
import jax.numpy as jnp
from jax import lax

D = 1024
H = 16
HD = 64
FF = 4096
SLOTS = 16
SEQ = 256
VROWS = 12
SHARDS = 32
PER_DEV = 393600


def draw_lengths(key, part):
    first, second = jax.random.split(key)
    drawn = jax.random.randint(first, (SLOTS,), SEQ // 4, SEQ + 1, dtype=jnp.int32)
    order = jax.random.permutation(second, SLOTS)
    drawn = drawn.at[order[0]].set(SEQ)
    drawn = drawn.at[order[1]].set(SEQ // 4)
    return drawn


def draw_vectors(key, part):
    ratio = FF // D
    rows = jnp.arange(VROWS)[:, None]
    is_gain = (rows == 4 + ratio) | (rows == 6 + ratio)
    unit = jax.random.uniform(key, (VROWS, D), jnp.float32, -1.0, 1.0)
    bias_part = 0.15 * unit
    gain_part = 1.0 + 0.3 * unit
    return jnp.where(is_gain, gain_part, bias_part)


def block_levels(own_key, extent, shards, low, top_value):
    level = 1.0
    for position, parts in shards:
        steps = jax.random.uniform(jax.random.fold_in(jax.random.fold_in(own_key, 6), position), (parts,), jnp.float32, low / len(shards), top_value / len(shards))
        level = level * jnp.repeat(jnp.exp(steps), extent[position] // parts).reshape((-1,) + (1,) * (len(extent) - 1 - position))
    return level


def normal_values(stream_key, dims, scale, limit, cuts=(), kind=jnp.bfloat16):
    values = scale * jax.random.normal(stream_key, dims, jnp.float32)
    if cuts:
        values = values * block_levels(stream_key, dims, cuts, -0.22, 0.18)
    return jnp.clip(values, -limit, limit).astype(kind)


def setup_inputs(seed: int = 0) -> dict:
    key_list = jax.random.split(jax.random.key(seed), 11)
    return {
        "tokens": normal_values(key_list[0], (SLOTS, SEQ, D), 1.0, 6.0, ((0, 8), (1, 4))),
        "out_grad": normal_values(key_list[1], (SLOTS, SEQ, D), 1.0, 6.0, ((0, 8), (1, 4))),
        "lengths": draw_lengths(jax.random.fold_in(key_list[10], 71), 0),
        "w_qkv": normal_values(key_list[3], (D, 3 * D), D ** -0.5, 0.1875),
        "w_out": normal_values(key_list[4], (D, D), (max(D // 256, 1)) ** -0.5, 3.0),
        "w_in": normal_values(key_list[5], (D, FF), D ** -0.5, 0.1875),
        "w_fc2": normal_values(key_list[6], (FF, D), FF ** -0.5, 0.09375),
        "vectors": draw_vectors(jax.random.fold_in(key_list[10], 71), 0),
        "moment_one": normal_values(key_list[8], (SHARDS, PER_DEV), 1.0, 6.0, ((0, 32),), jnp.float32),
        "moment_two": jnp.clip(jnp.exp(math.log(100.0) - 4.6051702 * jax.random.uniform(key_list[9], (SHARDS, PER_DEV), jnp.float32) ** block_levels(key_list[9], (SHARDS, PER_DEV), ((0, 32),), -0.2, 0.2)), 1.0, 100.0),
    }


@jax.custom_vjp
def low(v):
    return lax.optimization_barrier(v.astype(jnp.bfloat16)).astype(jnp.float32)

@jax.custom_vjp
def low_back(v):
    return v

def low_keep(v):
    return (low(v), None)

def low_pass(kept, grad):
    return (grad,)

def back_keep(v):
    return (v, None)

def back_low(kept, grad):
    return (low(grad),)
low.defvjp(low_keep, low_pass)
low_back.defvjp(back_keep, back_low)
EPSILON = 1e-05
learn_rate = 0.01
beta_one = 0.9
beta_two = 0.999
adam_eps = 1e-08
decay_rate = 0.01
step_count = 10.0

def layer_norm(values, gain, shift):
    center = values - lax.optimization_barrier(jnp.mean(values, axis=-1, keepdims=True))
    spread = lax.optimization_barrier(jnp.mean(center * center, axis=-1, keepdims=True))
    return center * lax.rsqrt(spread + EPSILON) * gain + shift

def split_vectors(vectors):
    ratio = FF // D
    return (vectors[0], vectors[1], vectors[2], vectors[3:3 + ratio].reshape(FF), vectors[3 + ratio], vectors[4 + ratio], vectors[5 + ratio], vectors[6 + ratio], vectors[7 + ratio])

def forward(tokens, w_qkv, w_out, w_in, w_fc2, vectors, valid):
    highest = lax.Precision.HIGHEST
    bias_q, bias_v, bias_o, bias_in, bias_fc2, gain_one, shift_one, gain_two, shift_two = split_vectors(vectors)
    joined = jnp.dot(tokens, w_qkv, precision=highest)
    queries = low(low_back((joined[:, :D] + bias_q) * 0.125)).reshape(SEQ, H, HD)
    keys = low(low_back(joined[:, D:2 * D])).reshape(SEQ, H, HD)
    values = low(low_back(joined[:, 2 * D:] + bias_v)).reshape(SEQ, H, HD)
    key_live = valid > 0.5

    def attend_block(block):
        scores = low_back(jnp.einsum('qhd,khd->hqk', block, keys, precision=highest))
        scores = jnp.where(key_live[None, None, :], scores, -1e+30)
        maximum = lax.optimization_barrier(jnp.max(scores, axis=-1, keepdims=True))
        expo = jnp.exp(scores - maximum)
        probs = low(expo / lax.optimization_barrier(jnp.sum(expo, axis=-1, keepdims=True)))
        return jnp.einsum('hqk,khd->qhd', probs, values, precision=highest)
    block_rows = min(512, SEQ)
    mixed = lax.map(jax.checkpoint(attend_block), queries.reshape(SEQ // block_rows, block_rows, H, HD))
    mixed = low(low_back(mixed.reshape(SEQ, D)))
    branch = low_back(jnp.dot(mixed, w_out, precision=highest) + bias_o)
    normed = layer_norm(tokens + branch, gain_one, shift_one)
    hidden_pre = low_back(jnp.dot(low(normed), w_in, precision=highest) + bias_in)
    hidden = low(jax.nn.gelu(hidden_pre, approximate=False))
    second = low_back(jnp.dot(hidden, w_fc2, precision=highest) + bias_fc2)
    result = layer_norm(normed + second, gain_two, shift_two)
    return result * valid[:, None]

def reference(tokens, out_grad, lengths, w_qkv, w_out, w_in, w_fc2, vectors, moment_one, moment_two):
    weights = (w_qkv.astype(jnp.float32), w_out.astype(jnp.float32), w_in.astype(jnp.float32), w_fc2.astype(jnp.float32), vectors.astype(jnp.float32))
    positions = jnp.arange(SEQ, dtype=jnp.int32)

    def one_slot(totals, slot):
        slot_tokens, slot_grad, length = slot
        valid = (positions < length).astype(jnp.float32)

        def layer(inputs, *params):
            return forward(inputs, *params, valid)
        result, pullback = jax.vjp(layer, slot_tokens.astype(jnp.float32), *weights)
        grads = pullback(slot_grad.astype(jnp.float32))
        new_totals = tuple((total + grad for total, grad in zip(totals, grads[1:])))
        return (new_totals, (result.astype(jnp.bfloat16), grads[0].astype(jnp.bfloat16)))
    start = tuple((jnp.zeros_like(weight) for weight in weights))
    totals, (out, tokens_grad) = lax.scan(one_slot, start, (tokens, out_grad, lengths))
    grad_rows = jnp.concatenate([grad.reshape(SHARDS, -1) for grad in totals], axis=1)
    params = jnp.concatenate([weight.reshape(SHARDS, -1) for weight in weights], axis=1)
    new_one = beta_one * moment_one + (1.0 - beta_one) * grad_rows
    new_two = beta_two * moment_two + (1.0 - beta_two) * grad_rows * grad_rows
    fix_one = 1.0 - beta_one ** step_count
    fix_two = 1.0 - beta_two ** step_count
    update = new_one / fix_one / (jnp.sqrt(new_two / fix_two) + adam_eps)
    new_params = params - learn_rate * (update + decay_rate * params)
    return (out, tokens_grad, grad_rows, new_params, new_one, new_two)
```

```python
from functools import partial

import jax
import jax.numpy as jnp
from jax import lax
from jax.experimental import pallas as pl
from jax.experimental.pallas import tpu as pltpu
from jax.sharding import PartitionSpec as P

D = 1024
H = 16
HD = 64
FF = 4096


EPSILON = 1e-05
learn_rate = 0.01
beta_one = 0.9
beta_two = 0.999
adam_eps = 1e-08
decay_rate = 0.01
step_count = 10.0


def layer_norm(values, gain, shift):
    center = values - jnp.mean(values, axis=-1, keepdims=True)
    spread = jnp.mean(center * center, axis=-1, keepdims=True)
    return center * lax.rsqrt(spread + EPSILON) * gain + shift


def split_vectors(vectors):
    ratio = FF // D
    return (
        vectors[0],
        vectors[1],
        vectors[2],
        vectors[3 : 3 + ratio].reshape(FF),
        vectors[3 + ratio],
        vectors[4 + ratio],
        vectors[5 + ratio],
        vectors[6 + ratio],
        vectors[7 + ratio],
    )


def inner(left, right):
    return lax.dot_general(
        left, right, (((0,), (0,)), ((), ())), preferred_element_type=jnp.float32
    )


def through(left, weight):
    return lax.dot_general(
        left, weight, (((1,), (1,)), ((), ())), preferred_element_type=jnp.float32
    )


def run_slots(function, items):
    return lax.map(lambda item: function(*item), items)


def heads_block():
    return 4


def split_heads(matrix):
    count = matrix.shape[0]
    group = heads_block()
    return jnp.moveaxis(matrix.reshape(count, H // group, group, HD), 1, 0)


def join_heads(blocked):
    return jnp.moveaxis(blocked, 0, 1).reshape(blocked.shape[1], H * HD)


def split_stats(stats):
    group = heads_block()
    return stats.reshape(H // group, group, stats.shape[-1])


def shard_piece(left, right, number, shard_count):
    weight_rows = left.shape[1]
    columns = right.shape[1]
    per_shard = weight_rows * columns // shard_count
    block = inner(left, right).reshape(-1)
    return block.reshape(number, per_shard)


def project(flat_tokens, w_qkv, vectors):
    joined = jnp.dot(flat_tokens, w_qkv, preferred_element_type=jnp.float32)
    queries = ((joined[:, :D] + vectors[0]) * 0.125).astype(jnp.bfloat16)
    keys = joined[:, D : 2 * D].astype(jnp.bfloat16)
    values = (joined[:, 2 * D :] + vectors[1]).astype(jnp.bfloat16)
    return (queries, keys, values)


def attend_slot(queries, keys, values, live):
    rows = queries.shape[0]

    def attend_one_block(item):
        query_heads, key_heads, value_heads = item
        scores = jnp.einsum(
            "qhd,khd->hqk", query_heads, key_heads, preferred_element_type=jnp.float32
        )
        scores = jnp.where(live[None, None, :], scores, -1e30)
        maximum = jnp.max(scores, axis=-1, keepdims=True)
        expo = jnp.exp(scores - maximum)
        total = jnp.sum(expo, axis=-1, keepdims=True)
        probs_low = (expo / total).astype(jnp.bfloat16)
        mixed = jnp.einsum(
            "hqk,khd->qhd", probs_low, value_heads, preferred_element_type=jnp.float32
        )
        return (mixed, (maximum + jnp.log(total))[..., 0])

    mixed, log_total = lax.map(
        attend_one_block, (split_heads(queries), split_heads(keys), split_heads(values))
    )
    return (join_heads(mixed), log_total.reshape(H, rows))


def query_back(queries, keys, values, live, log_total, grad_mixed, with_keys):
    rows = queries.shape[0]

    def query_one_block(item):
        query_heads, key_heads, value_heads, grad_heads, block_log = item
        scores = jnp.einsum(
            "qhd,khd->hqk", query_heads, key_heads, preferred_element_type=jnp.float32
        )
        scores = jnp.where(live[None, None, :], scores, -1e30)
        probs = jnp.exp(scores - block_log[:, :, None])
        grad_probs = jnp.einsum(
            "qhd,khd->hqk", grad_heads, value_heads, preferred_element_type=jnp.float32
        )
        row_sums = jnp.sum(probs * grad_probs, axis=-1)
        grad_scores = (probs * (grad_probs - row_sums[:, :, None])).astype(jnp.bfloat16)
        grad_query = jnp.einsum(
            "hqk,khd->qhd", grad_scores, key_heads, preferred_element_type=jnp.float32
        )
        grad_key = jnp.einsum(
            "hqk,qhd->khd", grad_scores, query_heads, preferred_element_type=jnp.float32
        )
        grad_value = jnp.einsum(
            "hqk,qhd->khd",
            probs.astype(jnp.bfloat16),
            grad_heads,
            preferred_element_type=jnp.float32,
        )
        return (grad_query, row_sums, grad_key, grad_value)

    items = (
        split_heads(queries),
        split_heads(keys),
        split_heads(values),
        split_heads(grad_mixed),
        split_stats(log_total),
    )
    results = lax.map(query_one_block, items)
    grad_query, row_sums, grad_key, grad_value = results
    return (
        join_heads(grad_query),
        row_sums.reshape(H, rows),
        join_heads(grad_key),
        join_heads(grad_value),
    )


def tail(flat_tokens, mixed, w_out, w_in, w_fc2, vectors):
    bias_q, bias_v, bias_o, bias_in, bias_fc2, gain_one, shift_one, gain_two, shift_two = (
        split_vectors(vectors)
    )
    mixed_low = mixed.astype(jnp.bfloat16)
    summed_one = (
        flat_tokens.astype(jnp.float32)
        + jnp.dot(mixed_low, w_out, preferred_element_type=jnp.float32)
        + bias_o
    )
    normed = layer_norm(summed_one, gain_one, shift_one)
    normed_low = normed.astype(jnp.bfloat16)
    hidden_pre = jnp.dot(normed_low, w_in, preferred_element_type=jnp.float32) + bias_in
    hidden_low = jax.nn.gelu(hidden_pre, approximate=False).astype(jnp.bfloat16)
    summed_two = normed + jnp.dot(hidden_low, w_fc2, preferred_element_type=jnp.float32) + bias_fc2
    result = layer_norm(summed_two, gain_two, shift_two)
    return (mixed_low, summed_one, normed_low, hidden_pre, hidden_low, summed_two, result)


def body(tokens, out_grad, lengths, w_qkv, w_out, w_in, w_fc2, vectors, moment_one, moment_two):
    slots, piece, width = tokens.shape
    length = piece * lax.axis_size("ctx")
    local_pos = lax.axis_index("ctx") * piece + jnp.arange(piece, dtype=jnp.int32)
    own_live = local_pos[None, :] < lengths[:, None]
    valid = own_live.astype(jnp.float32)
    key_live = jnp.arange(length, dtype=jnp.int32)[None, :] < lengths[:, None]
    bias_q, bias_v, bias_o, bias_in, bias_fc2, gain_one, shift_one, gain_two, shift_two = (
        split_vectors(vectors)
    )
    flat_tokens = tokens.reshape(slots * piece, width)
    queries, keys, values = project(flat_tokens, w_qkv, vectors)
    keys_all, values_all = (
        lax.all_gather(keys.reshape(slots, piece, width), "ctx", axis=1, tiled=True),
        lax.all_gather(values.reshape(slots, piece, width), "ctx", axis=1, tiled=True),
    )
    mixed, log_total = run_slots(
        attend_slot, (queries.reshape(slots, piece, width), keys_all, values_all, key_live)
    )
    saved = tail(flat_tokens, mixed.reshape(slots * piece, width), w_out, w_in, w_fc2, vectors)
    out = (saved[6].reshape(slots, piece, width) * valid[..., None]).astype(jnp.bfloat16)
    again = lax.optimization_barrier(flat_tokens)
    queries, keys, values = project(again, w_qkv, vectors)
    keys_all, values_all = (
        lax.all_gather(keys.reshape(slots, piece, width), "ctx", axis=1, tiled=True),
        lax.all_gather(values.reshape(slots, piece, width), "ctx", axis=1, tiled=True),
    )
    mixed, log_total = run_slots(
        attend_slot, (queries.reshape(slots, piece, width), keys_all, values_all, key_live)
    )
    saved = tail(again, mixed.reshape(slots * piece, width), w_out, w_in, w_fc2, vectors)
    mixed_low, summed_one, normed_low, hidden_pre, hidden_low, summed_two, result = saved
    cotangent = (out_grad.astype(jnp.float32) * valid[..., None]).reshape(slots * piece, width)
    unused_two, norm_two_back = jax.vjp(layer_norm, summed_two, gain_two, shift_two)
    grad_two, grad_gain_two, grad_shift_two = norm_two_back(cotangent)
    grad_fc2_low = grad_two.astype(jnp.bfloat16)
    bias_fc2_grad = jnp.sum(grad_fc2_low.astype(jnp.float32), axis=0)
    grad_hidden = through(grad_fc2_low, w_fc2)
    unused_gelu, gelu_back = jax.vjp(partial(jax.nn.gelu, approximate=False), hidden_pre)
    grad_pre_low = gelu_back(grad_hidden)[0].astype(jnp.bfloat16)
    bias_in_grad = jnp.sum(grad_pre_low.astype(jnp.float32), axis=0)
    grad_normed = grad_two + through(grad_pre_low, w_in)
    unused_one, norm_one_back = jax.vjp(layer_norm, summed_one, gain_one, shift_one)
    grad_one, grad_gain_one, grad_shift_one = norm_one_back(grad_normed)
    grad_branch_low = grad_one.astype(jnp.bfloat16)
    bias_out_grad = jnp.sum(grad_branch_low.astype(jnp.float32), axis=0)
    grad_mixed_low = (
        through(grad_branch_low, w_out).astype(jnp.bfloat16).reshape(slots, piece, width)
    )
    queries_slots = queries.reshape(slots, piece, width)
    grad_query, row_sums, grad_key, grad_value = run_slots(
        partial(query_back, with_keys=True),
        (queries_slots, keys_all, values_all, key_live, log_total, grad_mixed_low),
    )
    grad_key, grad_value = (
        lax.psum_scatter(
            grad_key.astype(jnp.bfloat16), "ctx", scatter_dimension=1, tiled=True
        ).astype(jnp.float32),
        lax.psum_scatter(
            grad_value.astype(jnp.bfloat16), "ctx", scatter_dimension=1, tiled=True
        ).astype(jnp.float32),
    )
    rows = slots * piece
    grad_query_low = grad_query.reshape(rows, width).astype(jnp.bfloat16) * jnp.bfloat16(0.125)
    grad_key_low = grad_key.reshape(rows, width).astype(jnp.bfloat16)
    grad_value_low = grad_value.reshape(rows, width).astype(jnp.bfloat16)
    grad_joined = jnp.concatenate([grad_query_low, grad_key_low, grad_value_low], axis=1)
    bias_q_grad = jnp.sum(grad_query_low.astype(jnp.float32), axis=0)
    bias_v_grad = jnp.sum(grad_value_low.astype(jnp.float32), axis=0)
    tokens_grad = (
        (grad_one + through(grad_joined, w_qkv)).reshape(slots, piece, width).astype(jnp.bfloat16)
    )
    vector_grad = jnp.concatenate(
        [
            bias_q_grad[None],
            bias_v_grad[None],
            bias_out_grad[None],
            bias_in_grad.reshape(FF // D, D),
            bias_fc2_grad[None],
            grad_gain_one[None],
            grad_shift_one[None],
            grad_gain_two[None],
            grad_shift_two[None],
        ],
        axis=0,
    )
    count = lax.axis_size(("dp", "ctx"))
    vector_rows = vector_grad.reshape(count, -1)
    pairs = (
        (flat_tokens, grad_joined),
        (mixed_low, grad_branch_low),
        (normed_low, grad_pre_low),
        (hidden_low, grad_fc2_low),
    )
    blocks = [
        shard_piece(left, right, 1 * lax.axis_size(("dp", "ctx")), count) for left, right in pairs
    ]
    blocks.append(vector_rows)
    grad_rows = lax.psum_scatter(
        jnp.concatenate(blocks, axis=1), ("dp", "ctx"), scatter_dimension=0, tiled=True
    )
    index = lax.axis_index(("dp", "ctx"))
    params = jnp.concatenate(
        [
            lax.dynamic_slice_in_dim(weight.reshape(count, -1), index, 1, 0).astype(jnp.float32)
            for weight in (w_qkv, w_out, w_in, w_fc2, vectors)
        ],
        axis=1,
    )
    new_one = beta_one * moment_one + (1.0 - beta_one) * grad_rows
    new_two = beta_two * moment_two + (1.0 - beta_two) * grad_rows * grad_rows
    fix_one = 1.0 - beta_one**step_count
    fix_two = 1.0 - beta_two**step_count
    update = new_one / fix_one / (jnp.sqrt(new_two / fix_two) + adam_eps)
    new_params = params - learn_rate * (update + decay_rate * params)
    return (out, tokens_grad, grad_rows, new_params, new_one, new_two)


BF16 = jnp.bfloat16
F32 = jnp.float32


def layer_norm_stats(values):
    center = values - jnp.mean(values, axis=-1, keepdims=True)
    spread = jnp.mean(center * center, axis=-1, keepdims=True)
    return center, lax.rsqrt(spread + EPSILON)


def layer_norm_back(center, scale, gain, cotangent):
    scaled = cotangent * gain
    mean_scaled = jnp.mean(scaled, axis=-1, keepdims=True)
    mean_cross = jnp.mean(scaled * center, axis=-1, keepdims=True)
    return scale * (scaled - mean_scaled - center * (scale * scale) * mean_cross)


def normal_cdf(values):
    return 0.5 * (1.0 + lax.erf(values * 0.7071067811865476))


def dot(left, right):
    return jnp.dot(left, right, preferred_element_type=F32)


def positions(axis, shape, slot, piece):
    place = lax.broadcasted_iota(jnp.int32, shape, axis)
    block = lax.div(place, piece)
    half = lax.div(block, 2)
    step = lax.rem(block, 2)
    return (2 * half + lax.rem(slot + step, 2)) * piece + lax.rem(place, piece)


def head_probs(queries, keys, live):
    scores = through(queries, keys)
    scores = jnp.where(live, scores, -1e30)
    expo = jnp.exp(scores - jnp.max(scores, axis=-1, keepdims=True))
    return expo / jnp.sum(expo, axis=-1, keepdims=True)


def full(shape):
    return pl.BlockSpec(shape, lambda i, *s: (0,) * len(shape))


def call(kernel, scalars, grid, ins, outs, scratch=(), flops=0, moved=0, name=None):
    arrays, in_specs = zip(*ins)
    shapes, out_specs = zip(*outs)
    return pl.pallas_call(
        kernel,
        out_shape=shapes,
        grid_spec=pltpu.PrefetchScalarGridSpec(
            num_scalar_prefetch=1,
            grid=(grid,),
            in_specs=list(in_specs),
            out_specs=list(out_specs),
            scratch_shapes=list(scratch),
        ),
        compiler_params=pltpu.CompilerParams(
            dimension_semantics=("arbitrary",), vmem_limit_bytes=60 * 1024 * 1024
        ),
        cost_estimate=pl.CostEstimate(flops=flops, bytes_accessed=moved, transcendentals=0),
        name=name,
    )(scalars, *arrays)


def attention_kernel(piece, sc, own, other, wq, wk, wv, wo, vec, rows_out, saved_out, part_out):
    core, slot, length = sc[0], sc[1], sc[2]
    half = own.shape[0]

    @pl.when(pl.program_id(0) == 0)
    def _():
        rows_out[pl.ds(pl.multiple_of(core * half, half), half), :] = own[...]
        rows_out[pl.ds(pl.multiple_of((1 - core) * half, half), half), :] = other[...]
        part_out[...] = jnp.zeros_like(part_out)

    rows = rows_out[...]
    queries = ((dot(rows, wq[...]) + vec[0:1, :]) * 0.125).astype(BF16)
    keys = dot(rows, wk[...]).astype(BF16)
    values = (dot(rows, wv[...]) + vec[1:2, :]).astype(BF16)
    width = queries.shape[1]
    live = positions(1, (1, 2 * half), slot, piece) < length
    lane = lax.broadcasted_iota(jnp.int32, (1, width), 1)
    mixed = jnp.zeros(queries.shape, F32)
    for head in range(width // HD):
        mine = lax.div(lane, HD) == head
        probs = head_probs(jnp.where(mine, queries, jnp.zeros_like(queries)), keys, live)
        mixed = jnp.where(mine, dot(probs.astype(BF16), values), mixed)
    mixed_low = mixed.astype(BF16)
    saved_out[0, :, 0:width] = queries
    saved_out[0, :, width : 2 * width] = keys
    saved_out[0, :, 2 * width : 3 * width] = values
    saved_out[0, :, 3 * width : 4 * width] = mixed_low
    part_out[...] += dot(mixed_low, wo[...])


def feed_kernel(sc, rows, part, peer, vec, bias, w_up, w_down, sum_out, low_out, own_out, pre_out, part_out):
    core = sc[0]
    length, half = rows.shape[0], own_out.shape[0]

    @pl.when(pl.program_id(0) == 0)
    def _():
        @pl.loop(0, length // 32)
        def _(chunk):
            at = pl.ds(pl.multiple_of(chunk * 32, 32), 32)
            summed = rows[at, :].astype(F32) + (part[at, :] + peer[at, :]) + vec[2:3, :]
            center, scale = layer_norm_stats(summed)
            sum_out[at, :] = summed
            low_out[at, :] = (center * scale * vec[8:9, :] + vec[9:10, :]).astype(BF16)

        own_out[...] = low_out[pl.ds(pl.multiple_of(core * half, half), half), :]
        part_out[...] = jnp.zeros_like(part_out)

    pre = dot(low_out[...], w_up[...]) + bias[...]
    pre_out[...] = pre
    part_out[...] += dot((pre * normal_cdf(pre)).astype(BF16), w_down[...])


def feed_back_kernel(
    piece, sc, summed, part, peer, grad_own, grad_other, vec, pre, w_up, w_down,
    result_out, low_out, own_out, grad_out, vec_out, part_out, cot,
):
    core, slot, length = sc[0], sc[1], sc[2]
    rows, half = summed.shape[0], grad_own.shape[0]

    @pl.when(pl.program_id(0) == 0)
    def _():
        cot[pl.ds(pl.multiple_of(core * half, half), half), :] = grad_own[...]
        cot[pl.ds(pl.multiple_of((1 - core) * half, half), half), :] = grad_other[...]
        vec_out[...] = jnp.zeros_like(vec_out)

        @pl.loop(0, rows // 32)
        def _(chunk):
            start = pl.multiple_of(chunk * 32, 32)
            at = pl.ds(start, 32)
            center, scale = layer_norm_stats(summed[at, :])
            normed = center * scale * vec[8:9, :] + vec[9:10, :]
            center, scale = layer_norm_stats(normed + (part[at, :] + peer[at, :]) + vec[7:8, :])
            place = start + lax.broadcasted_iota(jnp.int32, (32, 1), 0)
            block = lax.div(place, piece)
            spot = 2 * lax.div(block, 2) + lax.rem(slot + lax.rem(block, 2), 2)
            valid = (spot * piece + lax.rem(place, piece) < length).astype(F32)
            unit = center * scale
            low_out[at, :] = (valid * (unit * vec[10:11, :] + vec[11:12, :])).astype(BF16)
            error = cot[at, :].astype(F32) * valid
            grad = layer_norm_back(center, scale, vec[10:11, :], error)
            grad_out[at, :] = grad
            grad_low = grad.astype(BF16).astype(F32)
            vec_out[0:1, :] += jnp.sum(grad_low, axis=0, keepdims=True)
            vec_out[1:2, :] += jnp.sum(error * unit, axis=0, keepdims=True)
            vec_out[2:3, :] += jnp.sum(error, axis=0, keepdims=True)

        result_out[...] = low_out[pl.ds(pl.multiple_of(core * half, half), half), :]
        low_out[...] = grad_out[...].astype(BF16)
        own_out[...] = low_out[pl.ds(pl.multiple_of(core * half, half), half), :]
        part_out[...] = jnp.zeros_like(part_out)

    value = pre[...]
    slope = normal_cdf(value) + value * (jnp.exp(-0.5 * value * value) * 0.3989422804014327)
    grad_pre = (through(low_out[...], w_down[...]) * slope).astype(BF16)
    part_out[...] += through(grad_pre, w_up[...])


def attention_back_kernel(
    piece, parts, sc, summed, grad_two, part, peer, vec, wo, saved, wq, wk, wv, *rest
):
    outs, (low_out, own_out, vec_out, side_out, keep_out, send_out, acc) = (
        rest[:parts],
        rest[parts:],
    )
    core, slot, length = sc[0], sc[1], sc[2]
    step = pl.program_id(0)
    rows, half = summed.shape[0], own_out.shape[0]
    mine_at = pl.ds(pl.multiple_of(core * half, half), half)
    other_at = pl.ds(pl.multiple_of((1 - core) * half, half), half)

    @pl.when(step == 0)
    def _():
        vec_out[...] = jnp.zeros_like(vec_out)

        @pl.loop(0, rows // 32)
        def _(chunk):
            at = pl.ds(pl.multiple_of(chunk * 32, 32), 32)
            center, scale = layer_norm_stats(summed[at, :])
            error = grad_two[at, :] + (part[at, :] + peer[at, :])
            grad = layer_norm_back(center, scale, vec[8:9, :], error)
            acc[at, :] = grad
            low = grad.astype(BF16)
            low_out[at, :] = low
            vec_out[0:1, :] += jnp.sum(low.astype(F32), axis=0, keepdims=True)
            vec_out[1:2, :] += jnp.sum(error * (center * scale), axis=0, keepdims=True)
            vec_out[2:3, :] += jnp.sum(error, axis=0, keepdims=True)

        own_out[...] = low_out[mine_at, :]
        acc[other_at, :] = jnp.zeros((half, acc.shape[1]), F32)

    width = wo.shape[0]
    grad_mixed = through(low_out[...], wo[...]).astype(BF16)
    queries = saved[0, :, 0:width]
    keys = saved[0, :, width : 2 * width]
    values = saved[0, :, 2 * width : 3 * width]
    live = positions(1, (1, rows), slot, piece) < length
    lane = lax.broadcasted_iota(jnp.int32, (1, width), 1)
    grad_q = jnp.zeros((rows, width), F32)
    grad_k = grad_q
    grad_v = grad_q
    for head in range(width // HD):
        mine = lax.div(lane, HD) == head
        probs = head_probs(jnp.where(mine, queries, jnp.zeros_like(queries)), keys, live)
        grad_probs = through(jnp.where(mine, grad_mixed, jnp.zeros_like(grad_mixed)), values)
        dsum = jnp.sum(probs * grad_probs, axis=-1, keepdims=True)
        grad_scores = (probs * (grad_probs - dsum)).astype(BF16)
        grad_q = jnp.where(mine, dot(grad_scores, keys), grad_q)
        grad_k = jnp.where(mine, inner(grad_scores, queries), grad_k)
        grad_v = jnp.where(mine, inner(probs.astype(BF16), grad_mixed), grad_v)
    grad_q = grad_q.astype(BF16) * jnp.bfloat16(0.125)
    grad_k = grad_k.astype(BF16)
    grad_v = grad_v.astype(BF16)
    side_out[0, 0:1, :] = jnp.sum(grad_q.astype(F32), axis=0, keepdims=True)
    side_out[0, 1:2, :] = jnp.sum(grad_v.astype(F32), axis=0, keepdims=True)
    for number in range(parts):

        @pl.when(step == number)
        def _(out=outs[number]):
            out[:, 0:width] = grad_q
            out[:, width : 2 * width] = grad_k
            out[:, 2 * width : 3 * width] = grad_v
            out[:, 3 * width : 4 * width] = saved[0, :, 3 * width : 4 * width]

    acc[...] += through(grad_q, wq[...]) + through(grad_k, wk[...]) + through(grad_v, wv[...])

    @pl.when(step == parts - 1)
    def _():
        keep_out[...] = acc[mine_at, :]
        send_out[...] = acc[other_at, :]


def gather_rows(sc, dest, own, mine, theirs):
    core = sc[0]
    length = own.shape[0]
    half = length // 2
    dest[0:length, :] = own[...]
    for number, (one, two) in enumerate(zip(mine, theirs)):
        base = (number + 1) * length
        dest[pl.ds(pl.multiple_of(base + core * half, half), half), :] = one[...]
        dest[pl.ds(pl.multiple_of(base + (1 - core) * half, half), half), :] = two[...]


def feed_grad_kernel(others, lines, sc, *refs):
    size = 1 + 2 * others
    left = refs[:size]
    right = refs[size : 2 * size]
    w_up, w_down, bias, out, bias_out, lefts, rights, hidden, grads = refs[2 * size :]
    gather_rows(sc, lefts, left[0], left[1 : 1 + others], left[1 + others :])
    gather_rows(sc, rights, right[0], right[1 : 1 + others], right[1 + others :])
    total = lefts.shape[0]
    bias_out[...] = jnp.zeros_like(bias_out)

    @pl.loop(0, total // 256)
    def _(chunk):
        at = pl.ds(pl.multiple_of(chunk * 256, 256), 256)
        pre = dot(lefts[at, :], w_up[...]) + bias[...]
        cdf = normal_cdf(pre)
        slope = cdf + pre * (jnp.exp(-0.5 * pre * pre) * 0.3989422804014327)
        hidden[at, :] = (pre * cdf).astype(BF16)
        low = (through(rights[at, :], w_down[...]) * slope).astype(BF16)
        grads[at, :] = low
        bias_out[...] += jnp.sum(low.astype(F32), axis=0, keepdims=True)

    count = out.shape[0]
    chunk_down = out.shape[1] // 2
    down = inner(hidden[...], rights[...]).astype(BF16)
    for number in range(count):
        out[number, 0:chunk_down, :] = down[number * chunk_down : (number + 1) * chunk_down, :]
    columns = grads.shape[1]
    packs = out.shape[2] // columns
    groups = lefts.shape[1] // (lines * count)
    per_pack = groups // packs
    for group in range(groups):
        start = group * lines * count
        up = inner(lefts[:, start : start + lines * count], grads[...]).astype(BF16)
        row = chunk_down + (group % per_pack) * lines
        col = (group // per_pack) * columns
        for number in range(count):
            out[number, row : row + lines, col : col + columns] = up[
                number * lines : (number + 1) * lines, :
            ]


def input_grad_kernel(others, lines, sc, *refs):
    size = 1 + 2 * others
    left = refs[:size]
    right = refs[size : 2 * size]
    joined = refs[2 * size : 2 * size + 1 + others]
    out, lefts, rights, joint = refs[2 * size + 1 + others :]
    gather_rows(sc, lefts, left[0], left[1 : 1 + others], left[1 + others :])
    gather_rows(sc, rights, right[0], right[1 : 1 + others], right[1 + others :])
    length = joined[0].shape[0]
    for number, block in enumerate(joined):
        joint[number * length : (number + 1) * length, :] = block[...]
    columns = joint.shape[1] // 4
    count = out.shape[0]
    groups = lefts.shape[1] // (lines * count)
    across = inner(joint[:, 3 * columns : 4 * columns], rights[...]).astype(BF16)
    for group in range(groups):
        start = group * lines * count
        block = inner(lefts[:, start : start + lines * count], joint[:, 0 : 3 * columns])
        block = block.astype(BF16)
        row = group * lines
        for number in range(count):
            at = slice(number * lines, (number + 1) * lines)
            out[number, row : row + lines, 0 : 3 * columns] = block[at, :]
            out[number, row : row + lines, 3 * columns : 4 * columns] = across[
                at, group * columns : (group + 1) * columns
            ]


def swap(value, mask):
    size = lax.axis_size("dp")
    return lax.ppermute(value, "dp", [(i, i ^ mask) for i in range(size)])


def spread_rows(pieces):
    devices, depth = lax.axis_size("dp"), lax.axis_size("ctx")
    place = lax.axis_index("ctx")
    got = []
    for step in range(2):
        pairs = []
        for dp in range(devices):
            for z in range(depth):
                target = (dp - dp % 2 + z // 2) * depth + 2 * (dp % 2) + (z + step) % 2
                pairs.append((dp * depth + z, target))
        picked = jnp.where((place + step) % 2 == 0, pieces[0], pieces[1])
        got.append(lax.ppermute(picked, ("dp", "ctx"), pairs))
    return got


def return_rows(half):
    devices, depth = lax.axis_size("dp"), lax.axis_size("ctx")
    place = lax.axis_index("ctx")
    piece = half.shape[0] // 2
    got = []
    for step in range(2):
        pairs = []
        for dp in range(devices):
            for z in range(depth):
                target = (dp - dp % 2 + z // 2) * depth + 2 * (dp % 2) + (z + step) % 2
                pairs.append((target, dp * depth + z))
        got.append(
            lax.ppermute(half[step * piece : (step + 1) * piece], ("dp", "ctx"), pairs)
        )
    even = place % 2 == 0
    return jnp.stack([jnp.where(even, got[0], got[1]), jnp.where(even, got[1], got[0])])


def gather_plane(own):
    chips = lax.axis_size("dp") // 2
    mine = [swap(own, 2 * mask) for mask in range(1, chips)]
    return mine + [swap(value, 1) for value in mine]


def scatter_line(chunks):
    depth = chunks.shape[0]
    place = lax.axis_index("ctx")

    def take(number):
        number = jnp.clip(number, 0, depth - 1)
        return lax.dynamic_index_in_dim(chunks, number, 0, keepdims=False)

    right, left = None, None
    for step in range(1, depth):
        out_right = take(depth - step + place)
        out_left = take(place - (depth - step))
        if right is not None:
            out_right = (out_right.astype(F32) + right.astype(F32)).astype(BF16)
            out_left = (out_left.astype(F32) + left.astype(F32)).astype(BF16)
        right = lax.ppermute(out_right, "ctx", [(z, z + 1) for z in range(step)])
        left = lax.ppermute(
            out_left, "ctx", [(z, z - 1) for z in range(depth - 1, depth - 1 - step, -1)]
        )
    return take(place).astype(F32) + right.astype(F32) + left.astype(F32)


def trade_columns(blocks):
    size = blocks.shape[0]
    rows = blocks.shape[1]
    me = lax.axis_index("dp")
    held = blocks
    bit = 1
    while bit < size:
        pair = held.reshape(held.shape[0] // 2, 2, rows, held.shape[2])
        mine = (me // bit) % 2
        keep = lax.dynamic_index_in_dim(pair, mine, 1, keepdims=False)
        send = lax.dynamic_index_in_dim(pair, 1 - mine, 1, keepdims=False)
        got = swap(send.astype(BF16), bit).astype(F32)
        low = mine == 0
        held = jnp.concatenate([jnp.where(low, keep, got), jnp.where(low, got, keep)], axis=2)
        bit *= 2
    return held[0]


def total_over_devices(value):
    bit = 1
    while bit < lax.axis_size("dp"):
        value = value + swap(value, bit)
        bit *= 2
    depth = lax.axis_size("ctx")
    bit = 1
    while bit < depth:
        value = value + lax.ppermute(value, "ctx", [(z, z ^ bit) for z in range(depth)])
        bit *= 2
    return value


def slot_body(tokens, out_grad, lengths, w_qkv, w_out, w_in, w_fc2, vectors, moment_one, moment_two):
    slots, piece, width = tokens.shape
    devices, depth = lax.axis_size("dp"), lax.axis_size("ctx")
    chips = devices // 2
    count = devices * depth
    me, slot = lax.axis_index("dp"), lax.axis_index("ctx")
    core, chip = me % 2, me // 2
    half = 2 * piece
    rows = 2 * half
    block = D // devices
    features = w_in.shape[1]
    lines = D // count

    first = spread_rows(tokens)
    own = jnp.concatenate(first, axis=0)
    other = swap(own, 1)
    peer_lengths = swap(lengths, 1)
    owner = slot // 2
    length = jnp.where(owner == core, lengths, peer_lengths)
    length = jnp.where(slot % 2 == 0, length[0], length[1])
    scalars = jnp.stack([core, slot, length, chip, me]).astype(jnp.int32)
    grad_pieces = spread_rows(out_grad)
    grad_own = jnp.concatenate(grad_pieces, axis=0)
    grad_other = swap(grad_own, 1)
    ratio = features // D
    bias_in = vectors[3 : 3 + ratio].reshape(1, features)

    def head_block(i, s):
        return 2 * jnp.bitwise_xor(i, s[3]) + s[0]

    token_rows, saved, part = call(
        partial(attention_kernel, piece),
        scalars,
        chips,
        [
            (own, full((half, D))),
            (other, full((half, D))),
            (w_qkv, pl.BlockSpec((D, block), lambda i, s: (0, head_block(i, s)))),
            (w_qkv, pl.BlockSpec((D, block), lambda i, s: (0, devices + head_block(i, s)))),
            (w_qkv, pl.BlockSpec((D, block), lambda i, s: (0, 2 * devices + head_block(i, s)))),
            (w_out, pl.BlockSpec((block, D), lambda i, s: (head_block(i, s), 0))),
            (vectors, pl.BlockSpec((vectors.shape[0], block), lambda i, s: (0, head_block(i, s)))),
        ],
        [
            (jax.ShapeDtypeStruct((rows, D), BF16), full((rows, D))),
            (
                jax.ShapeDtypeStruct((chips, rows, 4 * block), BF16),
                pl.BlockSpec((1, rows, 4 * block), lambda i, s: (i, 0, 0)),
            ),
            (jax.ShapeDtypeStruct((rows, D), F32), full((rows, D))),
        ],
        flops=2 * rows * D * 4 * D // 2,
        moved=6 * 1024 * 1024,
        name="attention",
    )
    peer = swap(part, 1)
    token_plane = gather_plane(own)

    wide = 512
    steps = features // 2 // wide
    vec_spec = full(vectors.shape)
    up_spec = pl.BlockSpec((D, wide), lambda i, s: (0, s[0] * steps + i))
    down_spec = pl.BlockSpec((wide, D), lambda i, s: (s[0] * steps + i, 0))
    row_f32 = (jax.ShapeDtypeStruct((rows, D), F32), full((rows, D)))
    row_low = (jax.ShapeDtypeStruct((rows, D), BF16), full((rows, D)))
    half_low = (jax.ShapeDtypeStruct((half, D), BF16), full((half, D)))
    half_f32 = (jax.ShapeDtypeStruct((half, D), F32), full((half, D)))
    summed, normed_low, normed_own, hidden_pre, part = call(
        feed_kernel,
        scalars,
        steps,
        [
            (token_rows, full((rows, D))),
            (part, full((rows, D))),
            (peer, full((rows, D))),
            (vectors, vec_spec),
            (bias_in, pl.BlockSpec((1, wide), lambda i, s: (0, s[0] * steps + i))),
            (w_in, up_spec),
            (w_fc2, down_spec),
        ],
        [
            row_f32,
            row_low,
            half_low,
            (
                jax.ShapeDtypeStruct((rows, features // 2), F32),
                pl.BlockSpec((rows, wide), lambda i, s: (0, i)),
            ),
            row_f32,
        ],
        flops=2 * rows * D * features,
        moved=14 * 1024 * 1024,
        name="feed",
    )
    peer = swap(part, 1)
    normed_plane = gather_plane(normed_own)

    result, grad_low, grad_low_own, grad_two, vec_two, part = call(
        partial(feed_back_kernel, piece),
        scalars,
        steps,
        [
            (summed, full((rows, D))),
            (part, full((rows, D))),
            (peer, full((rows, D))),
            (grad_own, full((half, D))),
            (grad_other, full((half, D))),
            (vectors, vec_spec),
            (hidden_pre, pl.BlockSpec((rows, wide), lambda i, s: (0, i))),
            (w_in, up_spec),
            (w_fc2, down_spec),
        ],
        [
            half_low,
            row_low,
            half_low,
            row_f32,
            (jax.ShapeDtypeStruct((8, D), F32), full((8, D))),
            row_f32,
        ],
        scratch=[pltpu.VMEM((rows, D), BF16)],
        flops=2 * rows * D * features,
        moved=16 * 1024 * 1024,
        name="feed_back",
    )
    peer = swap(part, 1)
    grad_plane = gather_plane(grad_low_own)
    out = return_rows(result)

    *joined, branch_low, branch_own, vec_one, side, keep, send = call(
        partial(attention_back_kernel, piece, chips),
        scalars,
        chips,
        [
            (summed, full((rows, D))),
            (grad_two, full((rows, D))),
            (part, full((rows, D))),
            (peer, full((rows, D))),
            (vectors, vec_spec),
            (w_out, pl.BlockSpec((block, D), lambda i, s: (head_block(i, s), 0))),
            (saved, pl.BlockSpec((1, rows, 4 * block), lambda i, s: (i, 0, 0))),
            (w_qkv, pl.BlockSpec((D, block), lambda i, s: (0, head_block(i, s)))),
            (w_qkv, pl.BlockSpec((D, block), lambda i, s: (0, devices + head_block(i, s)))),
            (w_qkv, pl.BlockSpec((D, block), lambda i, s: (0, 2 * devices + head_block(i, s)))),
        ],
        [(jax.ShapeDtypeStruct((rows, 4 * block), BF16), full((rows, 4 * block)))] * chips
        + [
            row_low,
            half_low,
            (jax.ShapeDtypeStruct((8, D), F32), full((8, D))),
            (
                jax.ShapeDtypeStruct((chips, 8, block), F32),
                pl.BlockSpec((1, 8, block), lambda i, s: (jnp.bitwise_xor(i, s[3]), 0, 0)),
            ),
            half_f32,
            half_f32,
        ],
        scratch=[pltpu.VMEM((rows, D), F32)],
        flops=2 * rows * D * 4 * D // 2 * 2,
        moved=8 * 1024 * 1024,
        name="attention_back",
    )
    tokens_half = (keep + swap(send, 1)).astype(BF16)
    tokens_grad = return_rows(tokens_half)
    branch_plane = gather_plane(branch_own)
    joined_plane = [joined[0]] + [swap(joined[mask], 2 * mask) for mask in range(1, chips)]

    others = chips - 1
    total = rows * chips
    part_f = features // devices
    half_spec = full((half, D))
    plane_specs = [full((rows, D))] + [half_spec] * (2 * others)
    packed, bias_rows = call(
        partial(feed_grad_kernel, others, lines),
        scalars,
        1,
        list(zip([normed_low] + normed_plane, plane_specs))
        + list(zip([grad_low] + grad_plane, plane_specs))
        + [
            (w_in, pl.BlockSpec((D, part_f), lambda i, s: (0, s[4]))),
            (w_fc2, pl.BlockSpec((part_f, D), lambda i, s: (s[4], 0))),
            (bias_in, pl.BlockSpec((1, part_f), lambda i, s: (0, s[4]))),
        ],
        [
            (
                jax.ShapeDtypeStruct((depth, 2 * part_f // depth, D), BF16),
                full((depth, 2 * part_f // depth, D)),
            ),
            (jax.ShapeDtypeStruct((1, part_f), F32), full((1, part_f))),
        ],
        scratch=[
            pltpu.VMEM((total, D), BF16),
            pltpu.VMEM((total, D), BF16),
            pltpu.VMEM((total, part_f), BF16),
            pltpu.VMEM((total, part_f), BF16),
        ],
        flops=2 * total * D * part_f * 4,
        moved=10 * 1024 * 1024,
        name="feed_grad",
    )
    feed_sum = scatter_line(packed)
    (packed_two,) = call(
        partial(input_grad_kernel, others, lines),
        scalars,
        1,
        list(zip([token_rows] + token_plane, plane_specs))
        + list(zip([branch_low] + branch_plane, plane_specs))
        + [(value, full((rows, 4 * block))) for value in joined_plane],
        [
            (
                jax.ShapeDtypeStruct((depth, devices * lines, 4 * block), BF16),
                full((depth, devices * lines, 4 * block)),
            ),
        ],
        scratch=[
            pltpu.VMEM((total, D), BF16),
            pltpu.VMEM((total, D), BF16),
            pltpu.VMEM((total, 4 * block), BF16),
        ],
        flops=2 * total * D * 4 * block,
        moved=8 * 1024 * 1024,
        name="input_grad",
    )
    input_sum = scatter_line(packed_two)

    down_rows = part_f // depth
    grad_fc2 = feed_sum[:down_rows]
    packs = D // part_f
    in_blocks = (
        feed_sum[down_rows:]
        .reshape(devices // packs, lines, packs, part_f)
        .transpose(2, 0, 1, 3)
        .reshape(devices, lines, part_f)
    )
    grad_in = trade_columns(in_blocks)
    by_owner = input_sum.reshape(devices, lines, 4 * block)
    grad_joint = trade_columns(by_owner[:, :, : 3 * block])
    grad_qkv = (
        grad_joint.reshape(lines, devices, 3, block).transpose(0, 2, 1, 3).reshape(lines, 3 * D)
    )
    grad_out_w = by_owner[:, :, 3 * block :].transpose(1, 0, 2).reshape(lines, D)

    once = (core == 0).astype(F32)
    side_rows = side[:, :2].transpose(1, 0, 2)
    spot = jnp.arange(2, dtype=jnp.int32)[None, None, :, None] == core
    side_rows = jnp.where(spot, side_rows[:, :, None, :], 0.0).reshape(2, D)
    bias_grad = lax.dynamic_update_slice_in_dim(
        jnp.zeros((1, features), F32), bias_rows, me * part_f, 1
    ).reshape(ratio, D)
    vector_grad = jnp.concatenate(
        [
            side_rows,
            vec_one[0:1] * once,
            bias_grad,
            vec_two[0:1] * once,
            vec_one[1:3] * once,
            vec_two[1:3] * once,
        ],
        axis=0,
    )
    vector_grad = total_over_devices(vector_grad).reshape(count, -1)
    index = me * depth + slot
    own_vectors = lax.dynamic_slice_in_dim(vector_grad, index, 1, 0)
    grad_rows = jnp.concatenate(
        [value.reshape(1, -1) for value in (grad_qkv, grad_out_w, grad_in, grad_fc2, own_vectors)],
        axis=1,
    )
    return (out, tokens_grad) + update(
        grad_rows, index, count, (w_qkv, w_out, w_in, w_fc2, vectors), moment_one, moment_two
    )


def update(grad_rows, index, count, weights, moment_one, moment_two):
    pieces = []
    for weight in weights:
        if weight.shape[0] % count == 0:
            lines = weight.shape[0] // count
            piece = lax.dynamic_slice_in_dim(weight, index * lines, lines, 0)
        else:
            piece = lax.dynamic_slice_in_dim(weight.reshape(count, -1), index, 1, 0)
        pieces.append(piece.reshape(1, -1).astype(F32))
    params = jnp.concatenate(pieces, axis=1)
    new_one = beta_one * moment_one + (1.0 - beta_one) * grad_rows
    new_two = beta_two * moment_two + (1.0 - beta_two) * grad_rows * grad_rows
    fix_one = 1.0 - beta_one**step_count
    fix_two = 1.0 - beta_two**step_count
    change = new_one / fix_one / (jnp.sqrt(new_two / fix_two) + adam_eps)
    new_params = params - learn_rate * (change + decay_rate * params)
    return (grad_rows, new_params, new_one, new_two)


def layer(tokens, *rest):
    slots, piece, width = tokens.shape
    devices, depth = lax.axis_size("dp"), lax.axis_size("ctx")
    fits = slots == 2 and depth == 2 * slots and devices % 2 == 0
    if fits and (H * HD // devices) % 128 == 0 and (FF // devices) % 128 == 0:
        return slot_body(tokens, *rest)
    return body(tokens, *rest)


def solution(mesh):
    placed = (
        P("dp", "ctx", None),
        P("dp", "ctx", None),
        P("dp"),
        P(),
        P(),
        P(),
        P(),
        P(),
        P(("dp", "ctx"), None),
        P(("dp", "ctx"), None),
    )
    return jax.shard_map(
        layer,
        mesh=mesh,
        in_specs=placed,
        out_specs=(
            P("dp", "ctx", None),
            P("dp", "ctx", None),
            P(("dp", "ctx"), None),
            P(("dp", "ctx"), None),
            P(("dp", "ctx"), None),
            P(("dp", "ctx"), None),
        ),
        check_vma=False,
    )
```

```python
from functools import partial

import jax
import jax.numpy as jnp
from jax import lax
from jax.experimental import pallas as pl
from jax.experimental.pallas import tpu as pltpu
from jax.sharding import PartitionSpec as P

D = 1024
H = 16
HD = 64
FF = 4096


EPSILON = 1e-05
learn_rate = 0.01
beta_one = 0.9
beta_two = 0.999
adam_eps = 1e-08
decay_rate = 0.01
step_count = 10.0


def layer_norm(values, gain, shift):
    center = values - jnp.mean(values, axis=-1, keepdims=True)
    spread = jnp.mean(center * center, axis=-1, keepdims=True)
    return center * lax.rsqrt(spread + EPSILON) * gain + shift


def split_vectors(vectors):
    ratio = FF // D
    return (
        vectors[0],
        vectors[1],
        vectors[2],
        vectors[3 : 3 + ratio].reshape(FF),
        vectors[3 + ratio],
        vectors[4 + ratio],
        vectors[5 + ratio],
        vectors[6 + ratio],
        vectors[7 + ratio],
    )


def inner(left, right):
    return lax.dot_general(
        left, right, (((0,), (0,)), ((), ())), preferred_element_type=jnp.float32
    )


def through(left, weight):
    return lax.dot_general(
        left, weight, (((1,), (1,)), ((), ())), preferred_element_type=jnp.float32
    )


def run_slots(function, items):
    return lax.map(lambda item: function(*item), items)


def heads_block():
    return 4


def split_heads(matrix):
    count = matrix.shape[0]
    group = heads_block()
    return jnp.moveaxis(matrix.reshape(count, H // group, group, HD), 1, 0)


def join_heads(blocked):
    return jnp.moveaxis(blocked, 0, 1).reshape(blocked.shape[1], H * HD)


def split_stats(stats):
    group = heads_block()
    return stats.reshape(H // group, group, stats.shape[-1])


def shard_piece(left, right, number, shard_count):
    weight_rows = left.shape[1]
    columns = right.shape[1]
    per_shard = weight_rows * columns // shard_count
    block = inner(left, right).reshape(-1)
    return block.reshape(number, per_shard)


def project(flat_tokens, w_qkv, vectors):
    joined = jnp.dot(flat_tokens, w_qkv, preferred_element_type=jnp.float32)
    queries = ((joined[:, :D] + vectors[0]) * 0.125).astype(jnp.bfloat16)
    keys = joined[:, D : 2 * D].astype(jnp.bfloat16)
    values = (joined[:, 2 * D :] + vectors[1]).astype(jnp.bfloat16)
    return (queries, keys, values)


def attend_slot(queries, keys, values, live):
    rows = queries.shape[0]

    def attend_one_block(item):
        query_heads, key_heads, value_heads = item
        scores = jnp.einsum(
            "qhd,khd->hqk", query_heads, key_heads, preferred_element_type=jnp.float32
        )
        scores = jnp.where(live[None, None, :], scores, -1e30)
        maximum = jnp.max(scores, axis=-1, keepdims=True)
        expo = jnp.exp(scores - maximum)
        total = jnp.sum(expo, axis=-1, keepdims=True)
        probs_low = (expo / total).astype(jnp.bfloat16)
        mixed = jnp.einsum(
            "hqk,khd->qhd", probs_low, value_heads, preferred_element_type=jnp.float32
        )
        return (mixed, (maximum + jnp.log(total))[..., 0])

    mixed, log_total = lax.map(
        attend_one_block, (split_heads(queries), split_heads(keys), split_heads(values))
    )
    return (join_heads(mixed), log_total.reshape(H, rows))


def query_back(queries, keys, values, live, log_total, grad_mixed, with_keys):
    rows = queries.shape[0]

    def query_one_block(item):
        query_heads, key_heads, value_heads, grad_heads, block_log = item
        scores = jnp.einsum(
            "qhd,khd->hqk", query_heads, key_heads, preferred_element_type=jnp.float32
        )
        scores = jnp.where(live[None, None, :], scores, -1e30)
        probs = jnp.exp(scores - block_log[:, :, None])
        grad_probs = jnp.einsum(
            "qhd,khd->hqk", grad_heads, value_heads, preferred_element_type=jnp.float32
        )
        row_sums = jnp.sum(probs * grad_probs, axis=-1)
        grad_scores = (probs * (grad_probs - row_sums[:, :, None])).astype(jnp.bfloat16)
        grad_query = jnp.einsum(
            "hqk,khd->qhd", grad_scores, key_heads, preferred_element_type=jnp.float32
        )
        grad_key = jnp.einsum(
            "hqk,qhd->khd", grad_scores, query_heads, preferred_element_type=jnp.float32
        )
        grad_value = jnp.einsum(
            "hqk,qhd->khd",
            probs.astype(jnp.bfloat16),
            grad_heads,
            preferred_element_type=jnp.float32,
        )
        return (grad_query, row_sums, grad_key, grad_value)

    items = (
        split_heads(queries),
        split_heads(keys),
        split_heads(values),
        split_heads(grad_mixed),
        split_stats(log_total),
    )
    results = lax.map(query_one_block, items)
    grad_query, row_sums, grad_key, grad_value = results
    return (
        join_heads(grad_query),
        row_sums.reshape(H, rows),
        join_heads(grad_key),
        join_heads(grad_value),
    )


def tail(flat_tokens, mixed, w_out, w_in, w_fc2, vectors):
    bias_q, bias_v, bias_o, bias_in, bias_fc2, gain_one, shift_one, gain_two, shift_two = (
        split_vectors(vectors)
    )
    mixed_low = mixed.astype(jnp.bfloat16)
    summed_one = (
        flat_tokens.astype(jnp.float32)
        + jnp.dot(mixed_low, w_out, preferred_element_type=jnp.float32)
        + bias_o
    )
    normed = layer_norm(summed_one, gain_one, shift_one)
    normed_low = normed.astype(jnp.bfloat16)
    hidden_pre = jnp.dot(normed_low, w_in, preferred_element_type=jnp.float32) + bias_in
    hidden_low = jax.nn.gelu(hidden_pre, approximate=False).astype(jnp.bfloat16)
    summed_two = normed + jnp.dot(hidden_low, w_fc2, preferred_element_type=jnp.float32) + bias_fc2
    result = layer_norm(summed_two, gain_two, shift_two)
    return (mixed_low, summed_one, normed_low, hidden_pre, hidden_low, summed_two, result)


def body(tokens, out_grad, lengths, w_qkv, w_out, w_in, w_fc2, vectors, moment_one, moment_two):
    slots, piece, width = tokens.shape
    length = piece * lax.axis_size("ctx")
    local_pos = lax.axis_index("ctx") * piece + jnp.arange(piece, dtype=jnp.int32)
    own_live = local_pos[None, :] < lengths[:, None]
    valid = own_live.astype(jnp.float32)
    key_live = jnp.arange(length, dtype=jnp.int32)[None, :] < lengths[:, None]
    bias_q, bias_v, bias_o, bias_in, bias_fc2, gain_one, shift_one, gain_two, shift_two = (
        split_vectors(vectors)
    )
    flat_tokens = tokens.reshape(slots * piece, width)
    queries, keys, values = project(flat_tokens, w_qkv, vectors)
    keys_all, values_all = (
        lax.all_gather(keys.reshape(slots, piece, width), "ctx", axis=1, tiled=True),
        lax.all_gather(values.reshape(slots, piece, width), "ctx", axis=1, tiled=True),
    )
    mixed, log_total = run_slots(
        attend_slot, (queries.reshape(slots, piece, width), keys_all, values_all, key_live)
    )
    saved = tail(flat_tokens, mixed.reshape(slots * piece, width), w_out, w_in, w_fc2, vectors)
    out = (saved[6].reshape(slots, piece, width) * valid[..., None]).astype(jnp.bfloat16)
    again = lax.optimization_barrier(flat_tokens)
    queries, keys, values = project(again, w_qkv, vectors)
    keys_all, values_all = (
        lax.all_gather(keys.reshape(slots, piece, width), "ctx", axis=1, tiled=True),
        lax.all_gather(values.reshape(slots, piece, width), "ctx", axis=1, tiled=True),
    )
    mixed, log_total = run_slots(
        attend_slot, (queries.reshape(slots, piece, width), keys_all, values_all, key_live)
    )
    saved = tail(again, mixed.reshape(slots * piece, width), w_out, w_in, w_fc2, vectors)
    mixed_low, summed_one, normed_low, hidden_pre, hidden_low, summed_two, result = saved
    cotangent = (out_grad.astype(jnp.float32) * valid[..., None]).reshape(slots * piece, width)
    unused_two, norm_two_back = jax.vjp(layer_norm, summed_two, gain_two, shift_two)
    grad_two, grad_gain_two, grad_shift_two = norm_two_back(cotangent)
    grad_fc2_low = grad_two.astype(jnp.bfloat16)
    bias_fc2_grad = jnp.sum(grad_fc2_low.astype(jnp.float32), axis=0)
    grad_hidden = through(grad_fc2_low, w_fc2)
    unused_gelu, gelu_back = jax.vjp(partial(jax.nn.gelu, approximate=False), hidden_pre)
    grad_pre_low = gelu_back(grad_hidden)[0].astype(jnp.bfloat16)
    bias_in_grad = jnp.sum(grad_pre_low.astype(jnp.float32), axis=0)
    grad_normed = grad_two + through(grad_pre_low, w_in)
    unused_one, norm_one_back = jax.vjp(layer_norm, summed_one, gain_one, shift_one)
    grad_one, grad_gain_one, grad_shift_one = norm_one_back(grad_normed)
    grad_branch_low = grad_one.astype(jnp.bfloat16)
    bias_out_grad = jnp.sum(grad_branch_low.astype(jnp.float32), axis=0)
    grad_mixed_low = (
        through(grad_branch_low, w_out).astype(jnp.bfloat16).reshape(slots, piece, width)
    )
    queries_slots = queries.reshape(slots, piece, width)
    grad_query, row_sums, grad_key, grad_value = run_slots(
        partial(query_back, with_keys=True),
        (queries_slots, keys_all, values_all, key_live, log_total, grad_mixed_low),
    )
    grad_key, grad_value = (
        lax.psum_scatter(
            grad_key.astype(jnp.bfloat16), "ctx", scatter_dimension=1, tiled=True
        ).astype(jnp.float32),
        lax.psum_scatter(
            grad_value.astype(jnp.bfloat16), "ctx", scatter_dimension=1, tiled=True
        ).astype(jnp.float32),
    )
    rows = slots * piece
    grad_query_low = grad_query.reshape(rows, width).astype(jnp.bfloat16) * jnp.bfloat16(0.125)
    grad_key_low = grad_key.reshape(rows, width).astype(jnp.bfloat16)
    grad_value_low = grad_value.reshape(rows, width).astype(jnp.bfloat16)
    grad_joined = jnp.concatenate([grad_query_low, grad_key_low, grad_value_low], axis=1)
    bias_q_grad = jnp.sum(grad_query_low.astype(jnp.float32), axis=0)
    bias_v_grad = jnp.sum(grad_value_low.astype(jnp.float32), axis=0)
    tokens_grad = (
        (grad_one + through(grad_joined, w_qkv)).reshape(slots, piece, width).astype(jnp.bfloat16)
    )
    vector_grad = jnp.concatenate(
        [
            bias_q_grad[None],
            bias_v_grad[None],
            bias_out_grad[None],
            bias_in_grad.reshape(FF // D, D),
            bias_fc2_grad[None],
            grad_gain_one[None],
            grad_shift_one[None],
            grad_gain_two[None],
            grad_shift_two[None],
        ],
        axis=0,
    )
    count = lax.axis_size(("dp", "ctx"))
    vector_rows = vector_grad.reshape(count, -1)
    pairs = (
        (flat_tokens, grad_joined),
        (mixed_low, grad_branch_low),
        (normed_low, grad_pre_low),
        (hidden_low, grad_fc2_low),
    )
    blocks = [
        shard_piece(left, right, 1 * lax.axis_size(("dp", "ctx")), count) for left, right in pairs
    ]
    blocks.append(vector_rows)
    grad_rows = lax.psum_scatter(
        jnp.concatenate(blocks, axis=1), ("dp", "ctx"), scatter_dimension=0, tiled=True
    )
    index = lax.axis_index(("dp", "ctx"))
    params = jnp.concatenate(
        [
            lax.dynamic_slice_in_dim(weight.reshape(count, -1), index, 1, 0).astype(jnp.float32)
            for weight in (w_qkv, w_out, w_in, w_fc2, vectors)
        ],
        axis=1,
    )
    new_one = beta_one * moment_one + (1.0 - beta_one) * grad_rows
    new_two = beta_two * moment_two + (1.0 - beta_two) * grad_rows * grad_rows
    fix_one = 1.0 - beta_one**step_count
    fix_two = 1.0 - beta_two**step_count
    update = new_one / fix_one / (jnp.sqrt(new_two / fix_two) + adam_eps)
    new_params = params - learn_rate * (update + decay_rate * params)
    return (out, tokens_grad, grad_rows, new_params, new_one, new_two)


BF16 = jnp.bfloat16
F32 = jnp.float32


def layer_norm_stats(values):
    center = values - jnp.mean(values, axis=-1, keepdims=True)
    spread = jnp.mean(center * center, axis=-1, keepdims=True)
    return center, lax.rsqrt(spread + EPSILON)


def layer_norm_back(center, scale, gain, cotangent):
    scaled = cotangent * gain
    mean_scaled = jnp.mean(scaled, axis=-1, keepdims=True)
    mean_cross = jnp.mean(scaled * center, axis=-1, keepdims=True)
    return scale * (scaled - mean_scaled - center * (scale * scale) * mean_cross)


def normal_cdf(values):
    return 0.5 * (1.0 + lax.erf(values * 0.7071067811865476))


def dot(left, right):
    return jnp.dot(left, right, preferred_element_type=F32)


def positions(axis, shape, slot, piece):
    place = lax.broadcasted_iota(jnp.int32, shape, axis)
    block = lax.div(place, piece)
    half = lax.div(block, 2)
    step = lax.rem(block, 2)
    return (2 * half + lax.rem(slot + step, 2)) * piece + lax.rem(place, piece)


def head_probs(queries, keys, live):
    scores = through(queries, keys)
    scores = jnp.where(live, scores, -1e30)
    expo = jnp.exp(scores - jnp.max(scores, axis=-1, keepdims=True))
    return expo / jnp.sum(expo, axis=-1, keepdims=True)


MESH = pl.DeviceIdType.MESH


class Links:
    def __init__(self, sends, recvs):
        self.sends, self.recvs = sends, recvs
        self.used = 0
        self.open = []

    def copy(self, source, target, device):
        self.used += 1
        return self.again(source, target, device)

    def again(self, source, target, device):
        number = self.used - 1
        return pltpu.make_async_remote_copy(
            src_ref=source,
            dst_ref=target,
            send_sem=self.sends.at[number],
            recv_sem=self.recvs.at[number],
            device_id=device,
            device_id_type=MESH,
        )

    def send(self, source, target, device):
        made = self.copy(source, target, device)
        made.start()
        self.open.append((made, None))
        return made

    def send_if(self, condition, source, target, device):
        made = self.copy(source, target, device)
        pl.when(condition)(made.start)
        self.open.append((made, condition))
        return made

    def send_or_keep(self, here, source, target, device):
        number = self.used
        made = self.copy(source, target, device)
        local = pltpu.make_async_copy(source, target, self.recvs.at[number])
        pl.when(here)(local.start)
        away = jnp.logical_not(here)
        pl.when(away)(made.start)
        self.open.append((made, away))

        def wait():
            pl.when(here)(local.wait)
            pl.when(away)(made.wait_recv)

        return wait

    def close(self):
        for made, condition in self.open:
            if condition is None:
                made.wait_send()
            else:
                pl.when(condition)(made.wait_send)


def flip(value, mask):
    result = value
    bit = 1
    while bit <= mask:
        if mask & bit:
            result = result + bit * (1 - 2 * lax.rem(lax.div(value, bit), 2))
        bit *= 2
    return result


def flip_traced(value, mask, size):
    result = value
    bit = 1
    while bit < size:
        set_bit = lax.rem(lax.div(mask, bit), 2)
        result = result + bit * set_bit * (1 - 2 * lax.rem(lax.div(value, bit), 2))
        bit *= 2
    return result


def at_rows(start, size):
    return pl.ds(pl.multiple_of(start, 64), size)


def slot_kernel(devices, depth, features, *refs):
    (
        tokens, out_grad, lens, vec, w_qkv, w_out, w_in, w_fc2,
        out_ref, tgrad_ref, g_qkv, g_out, g_in, g_fc2, g_vec,
        wqkv, wo, w_up, w_down,
        x_all, n_all, g_all, b_all, j_all, j_send, g_rows, lens_peer,
        qkv, mixed, part, part_a, part_b, part_c, part_d, summed, grad_two, grad_one,
        pre_s, hid, hid_all, gp_all, packed, right, left, packed_two, right_two, left_two,
        trade_in, got_in, trade_qkv, got_qkv, vec_s, vec_got, dqkv, out_half, out_got, tg_half, tg_got,
        local_sems, sends, recvs,
    ) = refs
    chips = devices // 2
    me, slot = lax.axis_index("dp"), lax.axis_index("ctx")
    core, chip = lax.rem(me, 2), lax.div(me, 2)
    base = me - core
    peer = (base + 1 - core, slot)
    piece = tokens.shape[1]
    half = 2 * piece
    rows = 2 * half
    block = D // devices
    wide = features // devices
    lines = D // (devices * depth)
    net = Links(sends, recvs)
    mine_at = at_rows(core * half, half)
    other_at = at_rows((1 - core) * half, half)
    chunk = 32

    loads = []

    def load(source, target):
        made = pltpu.make_async_copy(source, target, local_sems.at[len(loads)])
        made.start()
        loads.append(made)

    where = [2 * flip(chip, mask) + core for mask in range(chips)]
    for mask in range(chips):
        for kind in range(3):
            start = pl.multiple_of(kind * D + where[mask] * block, block)
            load(
                w_qkv.at[:, pl.ds(start, block)],
                wqkv.at[:, (3 * mask + kind) * block : (3 * mask + kind + 1) * block],
            )
    n_qkv = len(loads)
    for mask in range(chips):
        start = pl.multiple_of(where[mask] * block, block)
        load(w_out.at[pl.ds(start, block), :], wo.at[mask * block : (mask + 1) * block, :])
    n_out = len(loads)
    for mask in range(chips):
        start = pl.multiple_of(where[mask] * wide, wide)
        load(w_in.at[:, pl.ds(start, wide)], w_up.at[:, mask * wide : (mask + 1) * wide])
    n_up = len(loads)
    for mask in range(chips):
        start = pl.multiple_of(where[mask] * wide, wide)
        load(w_fc2.at[pl.ds(start, wide), :], w_down.at[mask * wide : (mask + 1) * wide, :])

    barrier = pltpu.get_barrier_semaphore()
    friends = [(flip(me, mask), slot) for mask in range(1, devices)]
    for shift in range(1, depth):
        far = lax.rem(slot + shift, depth)
        friends += [(me, far), (flip(me, 1), far)]
    for friend in friends:
        pl.semaphore_signal(barrier, inc=1, device_id=friend, device_id_type=MESH)
    pl.semaphore_wait(barrier, len(friends))

    def spread(source, target):
        waits = []
        for step in range(2):
            pick = lax.rem(slot + step, 2)
            upper = lax.div(slot, 2)
            place = 2 * core + pick
            here = jnp.logical_and(upper == core, place == slot)
            waits.append(
                net.send_or_keep(
                    here,
                    source.at[pick],
                    target.at[at_rows((2 * upper + step) * piece, piece)],
                    (base + upper, place),
                )
            )
        return waits

    def pass_on(waits, target):
        made = []
        for step, wait in enumerate(waits):
            wait()
            spot = target.at[at_rows((2 * core + step) * piece, piece)]
            made.append(net.send(spot, spot, peer))
        return made

    token_waits = spread(tokens, x_all)
    grad_waits = spread(out_grad, g_rows)
    lens_copy = net.send(lens, lens_peer, peer)
    vec_s[...] = jnp.zeros_like(vec_s)
    token_passes = pass_on(token_waits, x_all)

    def plane_start(target):
        source = target.at[mine_at]
        return [
            net.send(
                source, target.at[at_rows(mask * rows + core * half, half)], (flip(me, 2 * mask), slot)
            )
            for mask in range(1, chips)
        ]

    def plane_pass(copies, target):
        made = []
        for mask, copy in enumerate(copies, 1):
            copy.wait_recv()
            spot = target.at[at_rows(mask * rows + core * half, half)]
            made.append(net.send(spot, spot, peer))
        return made

    x_plane = plane_start(x_all)
    for made in loads[:n_qkv]:
        made.wait()
    lens_copy.wait_recv()
    for made in token_passes:
        made.wait_recv()
    owned = jnp.where(lax.div(slot, 2) == core, lens[...], lens_peer[...])
    length = jnp.where(lax.rem(slot, 2) == 0, owned[0:1, 0:1], owned[1:2, 0:1])
    live = positions(1, (1, rows), slot, piece) < length
    lane = lax.broadcasted_iota(jnp.int32, (1, block), 1)

    @pl.loop(0, chips)
    def _(mask):
        spot = 2 * flip_traced(chip, mask, chips) + core
        lanes = pl.ds(pl.multiple_of(spot * block, block), block)
        joined = dot(x_all[0:rows, :], wqkv[:, pl.ds(pl.multiple_of(mask * 3 * block, block), 3 * block)])
        queries = ((joined[:, 0:block] + vec[0:1, lanes]) * 0.125).astype(BF16)
        keys = joined[:, block : 2 * block].astype(BF16)
        values = (joined[:, 2 * block :] + vec[1:2, lanes]).astype(BF16)
        total = jnp.zeros((rows, block), F32)
        for head in range(block // HD):
            mine = lax.div(lane, HD) == head
            probs = head_probs(jnp.where(mine, queries, jnp.zeros_like(queries)), keys, live)
            total = jnp.where(mine, dot(probs.astype(BF16), values), total)
        start = pl.multiple_of(mask * 3 * block, block)
        qkv[:, pl.ds(start, block)] = queries
        qkv[:, pl.ds(pl.multiple_of(start + block, block), block)] = keys
        qkv[:, pl.ds(pl.multiple_of(start + 2 * block, block), block)] = values
        mixed[:, pl.ds(pl.multiple_of(mask * block, block), block)] = total.astype(BF16)

    for made in loads[n_qkv:n_out]:
        made.wait()

    def exchange(compute, target, before):
        made = []
        for number, at in enumerate((other_at, mine_at)):
            if before is not None:
                before[number].wait_send()
            part[at, :] = compute(at)
            made.append(net.copy(part.at[at], target.at[at], peer))
            made[-1].start()
        return made

    first = exchange(lambda at: dot(mixed[at, :], wo[...]), part_a, None)
    grad_passes = pass_on(grad_waits, g_rows)

    def norm_one(start):
        @pl.loop(0, half // chunk)
        def _(step):
            at = pl.ds(pl.multiple_of(start + step * chunk, chunk), chunk)
            total = x_all[at, :].astype(F32) + (part[at, :] + part_a[at, :]) + vec[2:3, :]
            center, scale = layer_norm_stats(total)
            summed[at, :] = total
            n_all[at, :] = (center * scale * vec[8:9, :] + vec[9:10, :]).astype(BF16)

    first[0].wait_recv()
    norm_one(core * half)
    n_plane = plane_start(n_all)
    first[1].wait_recv()
    norm_one((1 - core) * half)
    for made in loads[n_out:]:
        made.wait()

    def bias_of(mask):
        spot = flip_traced(chip, mask, chips)
        lanes = pl.ds(pl.multiple_of(core * wide, wide), wide)
        result = vec[3:4, lanes]
        for row in range(1, chips):
            result = jnp.where(spot == row, vec[3 + row : 4 + row, lanes], result)
        return result

    @pl.loop(0, chips)
    def _(mask):
        at = pl.ds(pl.multiple_of(mask * wide, wide), wide)
        value = dot(n_all[0:rows, :], w_up[:, at]) + bias_of(mask)
        pre_s[:, at] = value
        hid[:, at] = (value * normal_cdf(value)).astype(BF16)

    second = exchange(lambda at: dot(hid[at, :], w_down[...]), part_b, first)
    for made in grad_passes:
        made.wait_recv()

    def norm_two(start, own):
        @pl.loop(0, half // chunk)
        def _(step):
            begin = pl.multiple_of(start + step * chunk, chunk)
            at = pl.ds(begin, chunk)
            center, scale = layer_norm_stats(summed[at, :])
            normed = center * scale * vec[8:9, :] + vec[9:10, :]
            center, scale = layer_norm_stats(normed + (part[at, :] + part_b[at, :]) + vec[7:8, :])
            place = begin + lax.broadcasted_iota(jnp.int32, (chunk, 1), 0)
            piece_of = lax.div(place, piece)
            spot = 2 * lax.div(piece_of, 2) + lax.rem(slot + lax.rem(piece_of, 2), 2)
            valid = (spot * piece + lax.rem(place, piece) < length).astype(F32)
            unit = center * scale
            error = g_rows[at, :].astype(F32) * valid
            grad = layer_norm_back(center, scale, vec[10:11, :], error)
            grad_two[at, :] = grad
            low = grad.astype(BF16)
            g_all[at, :] = low
            if own:
                out_half[pl.ds(pl.multiple_of(step * chunk, chunk), chunk), :] = (
                    valid * (unit * vec[10:11, :] + vec[11:12, :])
                ).astype(BF16)
                vec_s[7:8, :] += jnp.sum(low.astype(F32), axis=0, keepdims=True)
                vec_s[10:11, :] += jnp.sum(error * unit, axis=0, keepdims=True)
                vec_s[11:12, :] += jnp.sum(error, axis=0, keepdims=True)

    def go_back(source, target):
        waits = []
        for step in range(2):
            place = 2 * core + lax.rem(slot + step, 2)
            upper = lax.div(slot, 2)
            here = jnp.logical_and(upper == core, place == slot)
            waits.append(
                net.send_or_keep(
                    here,
                    source.at[step * piece : (step + 1) * piece],
                    target.at[lax.rem(slot, 2)],
                    (base + upper, place),
                )
            )
        return waits

    second[0].wait_recv()
    norm_two(core * half, True)
    g_plane = plane_start(g_all)
    second[1].wait_recv()
    norm_two((1 - core) * half, False)
    out_waits = go_back(out_half, out_got)
    n_pass = plane_pass(n_plane, n_all)
    x_pass = plane_pass(x_plane, x_all)

    def slope_of(value, cdf):
        return cdf + value * (jnp.exp(-0.5 * value * value) * 0.3989422804014327)

    @pl.loop(0, chips)
    def _(mask):
        at = pl.ds(pl.multiple_of(mask * wide, wide), wide)
        value = pre_s[:, at]
        grad = through(g_all[0:rows, :], w_down[at, :])
        hid[:, at] = (grad * slope_of(value, normal_cdf(value))).astype(BF16)

    third = exchange(lambda at: through(hid[at, :], w_up[...]), part_c, second)

    def norm_one_back(start, own):
        @pl.loop(0, half // chunk)
        def _(step):
            at = pl.ds(pl.multiple_of(start + step * chunk, chunk), chunk)
            center, scale = layer_norm_stats(summed[at, :])
            error = grad_two[at, :] + (part[at, :] + part_c[at, :])
            grad = layer_norm_back(center, scale, vec[8:9, :], error)
            low = grad.astype(BF16)
            b_all[at, :] = low
            grad_one[at, :] = grad
            if own:
                vec_s[2:3, :] += jnp.sum(low.astype(F32), axis=0, keepdims=True)
                vec_s[8:9, :] += jnp.sum(error * (center * scale), axis=0, keepdims=True)
                vec_s[9:10, :] += jnp.sum(error, axis=0, keepdims=True)

    third[0].wait_recv()
    norm_one_back(core * half, True)
    b_plane = plane_start(b_all)
    third[1].wait_recv()
    norm_one_back((1 - core) * half, False)
    g_pass = plane_pass(g_plane, g_all)

    bias_mine = bias_of(0)

    def feed_rows(mask):
        at = slice(mask * rows, (mask + 1) * rows)
        value = dot(n_all[at, :], w_up[:, 0:wide]) + bias_mine
        cdf = normal_cdf(value)
        hid_all[at, :] = (value * cdf).astype(BF16)
        low = (through(g_all[at, :], w_down[0:wide, :]) * slope_of(value, cdf)).astype(BF16)
        gp_all[at, :] = low
        return jnp.sum(low.astype(F32), axis=0, keepdims=True)

    bias_sum = feed_rows(0)
    for mask in range(1, chips):
        n_pass[mask - 1].wait_recv()
        g_pass[mask - 1].wait_recv()
        bias_sum = bias_sum + feed_rows(mask)
    lanes = pl.ds(pl.multiple_of(core * wide, wide), wide)
    for row in range(chips):
        vec_s[3 + row : 4 + row, lanes] = jnp.where(chip == row, bias_sum, jnp.zeros_like(bias_sum))
    down_rows = wide // depth
    packs = D // wide
    per_pack = devices // packs
    span = lines * depth
    down = inner(hid_all[...], g_all[...]).astype(BF16)
    for number in range(depth):
        packed[number, 0:down_rows, :] = down[number * down_rows : (number + 1) * down_rows, :]
    for group in range(devices):
        up = inner(n_all[:, group * span : (group + 1) * span], gp_all[...]).astype(BF16)
        row = down_rows + (group % per_pack) * lines
        col = (group // per_pack) * wide
        for number in range(depth):
            packed[number, row : row + lines, col : col + wide] = up[
                number * lines : (number + 1) * lines, :
            ]

    class Line:
        def __init__(self, chunks, from_left, from_right):
            self.chunks, self.from_left, self.from_right = chunks, from_left, from_right
            self.up, self.down, self.first_up, self.first_down = [], [], [], []
            after = (me, lax.rem(slot + 1, depth))
            before = (me, lax.rem(slot + depth - 1, depth))
            for order in range(depth - 1):
                top, low = depth - 1 - order, order
                spot = from_left.at[order]
                self.up.append(net.copy(spot, spot, after))
                self.first_up.append(net.again(chunks.at[top], spot, after))
                net.open.append((self.up[-1], slot < top))
                spot = from_right.at[order]
                self.down.append(net.copy(spot, spot, before))
                self.first_down.append(net.again(chunks.at[low], spot, before))
                net.open.append((self.down[-1], slot > low))

        def first(self):
            for order in range(depth - 1):
                pl.when(slot == 0)(self.first_up[order].start)
                pl.when(slot == depth - 1)(self.first_down[order].start)

        def stage(self, order):
            top, low = depth - 1 - order, order

            @pl.when(jnp.logical_and(slot >= 1, slot <= top))
            def _():
                self.up[order].wait_recv()

            @pl.when(jnp.logical_and(slot >= 1, slot < top))
            def _():
                self.from_left[order] = (
                    self.from_left[order].astype(F32) + self.chunks[top].astype(F32)
                ).astype(BF16)
                self.up[order].start()

            @pl.when(jnp.logical_and(slot <= depth - 2, slot >= low))
            def _():
                self.down[order].wait_recv()

            @pl.when(jnp.logical_and(slot <= depth - 2, slot > low))
            def _():
                self.from_right[order] = (
                    self.from_right[order].astype(F32) + self.chunks[low].astype(F32)
                ).astype(BF16)
                self.down[order].start()

    feed_line = Line(packed, right, left)
    feed_line.first()

    grad_parts = range(1, chips)

    def attention_back(mask):
        start = mask * 3 * block
        queries = qkv[:, start : start + block]
        keys = qkv[:, start + block : start + 2 * block]
        values = qkv[:, start + 2 * block : start + 3 * block]
        grad_mixed = through(b_all[0:rows, :], wo[mask * block : (mask + 1) * block, :]).astype(BF16)
        grad_q = jnp.zeros((rows, block), F32)
        grad_k = grad_q
        grad_v = grad_q
        for head in range(block // HD):
            mine = lax.div(lane, HD) == head
            probs = head_probs(jnp.where(mine, queries, jnp.zeros_like(queries)), keys, live)
            grad_probs = through(jnp.where(mine, grad_mixed, jnp.zeros_like(grad_mixed)), values)
            dsum = jnp.sum(probs * grad_probs, axis=-1, keepdims=True)
            grad_scores = (probs * (grad_probs - dsum)).astype(BF16)
            grad_q = jnp.where(mine, dot(grad_scores, keys), grad_q)
            grad_k = jnp.where(mine, inner(grad_scores, queries), grad_k)
            grad_v = jnp.where(mine, inner(probs.astype(BF16), grad_mixed), grad_v)
        grad_q = grad_q.astype(BF16) * jnp.bfloat16(0.125)
        grad_k = grad_k.astype(BF16)
        grad_v = grad_v.astype(BF16)
        spot = pl.ds(pl.multiple_of(where[mask] * block, block), block)
        vec_s[0:1, spot] = jnp.sum(grad_q.astype(F32), axis=0, keepdims=True)
        vec_s[1:2, spot] = jnp.sum(grad_v.astype(F32), axis=0, keepdims=True)
        dqkv[:, start : start + block] = grad_q
        dqkv[:, start + block : start + 2 * block] = grad_k
        dqkv[:, start + 2 * block : start + 3 * block] = grad_v
        if mask:
            joint = j_send.at[mask - 1]
        else:
            joint = j_all.at[0:rows]
        joint[:, 0:block] = grad_q
        joint[:, block : 2 * block] = grad_k
        joint[:, 2 * block : 3 * block] = grad_v
        joint[:, 3 * block : 4 * block] = mixed[:, mask * block : (mask + 1) * block]
        if mask:
            return net.send(
                joint, j_all.at[mask * rows : (mask + 1) * rows], (flip(me, 2 * mask), slot)
            )
        return None

    j_copies = [attention_back(mask) for mask in grad_parts]
    attention_back(0)
    feed_line.stage(0)
    b_pass = plane_pass(b_plane, b_all)
    for made in third:
        made.wait_send()
    part[0:half, :] = through(dqkv[other_at, :], wqkv[...])
    tg_copy = net.copy(part.at[0:half], part_d, peer)
    tg_copy.start()
    part[half:rows, :] = grad_one[mine_at, :] + through(dqkv[mine_at, :], wqkv[...])
    tg_copy.wait_recv()
    tg_half[...] = (part[half:rows, :] + part_d[...]).astype(BF16)
    tg_waits = go_back(tg_half, tg_got)

    for made in b_pass + x_pass + j_copies:
        made.wait_recv()
    across = inner(j_all[:, 3 * block : 4 * block], b_all[...]).astype(BF16)
    for group in range(devices):
        both = inner(x_all[:, group * span : (group + 1) * span], j_all[:, 0 : 3 * block]).astype(BF16)
        row = group * lines
        for number in range(depth):
            at = slice(number * lines, (number + 1) * lines)
            packed_two[number, row : row + lines, 0 : 3 * block] = both[at, :]
            packed_two[number, row : row + lines, 3 * block : 4 * block] = across[
                at, group * block : (group + 1) * block
            ]
    input_line = Line(packed_two, right_two, left_two)
    input_line.first()

    hops = []
    bit = 1
    while bit < devices:
        hops.append((flip(me, bit), slot))
        bit *= 2
    bit = 1
    while bit < depth:
        hops.append((me, flip(slot, bit)))
        bit *= 2

    def vector_hop(number):
        made = net.copy(vec_s, vec_got.at[number], hops[number])
        made.start()
        made.wait()
        vec_s[...] += vec_got[number]

    def finish(line, target, rows_at):
        target[...] = line.chunks[slot, rows_at, :].astype(F32)

        @pl.when(slot >= 1)
        def _():
            target[...] += line.from_left[depth - 1 - slot, rows_at, :].astype(F32)

        @pl.when(slot <= depth - 2)
        def _():
            target[...] += line.from_right[slot, rows_at, :].astype(F32)

    vector_hop(0)
    feed_line.stage(1)
    vector_hop(1)
    vector_hop(2)
    feed_line.stage(2)
    finish(feed_line, g_fc2, slice(0, down_rows))
    low_part = part_d.at[0:down_rows]
    finish(feed_line, low_part, slice(down_rows, 2 * down_rows))
    for group in range(devices):
        row = (group % per_pack) * lines
        col = (group // per_pack) * wide
        trade_in[group] = low_part[row : row + lines, col : col + wide].astype(BF16)

    def trade(source, target):
        return [
            net.send(source.at[flip(me, mask)], target.at[me], (flip(me, mask), slot))
            for mask in range(1, devices)
        ]

    in_copies = trade(trade_in, got_in)
    input_line.stage(0)
    vector_hop(3)
    input_line.stage(1)
    vector_hop(4)
    for made in in_copies:
        made.wait_recv()
    got_in[me] = trade_in[me]
    for group in range(devices):
        g_in[:, group * wide : (group + 1) * wide] = got_in[group].astype(F32)
    g_vec[...] = vec_s[0 : g_vec.shape[0], :]
    for wait in out_waits + tg_waits:
        wait()
    out_ref[...] = out_got[...]
    tgrad_ref[...] = tg_got[...]
    input_line.stage(2)
    tg_copy.wait_send()
    total = part.at[0 : 2 * half, 0 : 4 * block]
    finish(input_line, total, slice(0, rows))
    for group in range(devices):
        trade_qkv[group] = total[group * lines : (group + 1) * lines, 0 : 3 * block].astype(BF16)
        g_out[:, group * block : (group + 1) * block] = total[
            group * lines : (group + 1) * lines, 3 * block : 4 * block
        ]
    for made in trade(trade_qkv, got_qkv):
        made.wait_recv()
    got_qkv[me] = trade_qkv[me]
    for group in range(devices):
        for kind in range(3):
            g_qkv[:, kind * D + group * block : kind * D + (group + 1) * block] = got_qkv[
                group, :, kind * block : (kind + 1) * block
            ].astype(F32)
    net.close()


def slot_body(tokens, out_grad, lengths, w_qkv, w_out, w_in, w_fc2, vectors, moment_one, moment_two):
    slots, piece, width = tokens.shape
    devices, depth = lax.axis_size("dp"), lax.axis_size("ctx")
    chips = devices // 2
    count = devices * depth
    features = w_in.shape[1]
    half = 2 * piece
    rows = 2 * half
    block = D // devices
    wide = features // devices
    lines = D // count
    total = rows * chips
    hops = (devices.bit_length() - 1) + (depth.bit_length() - 1)
    lens = jnp.broadcast_to(lengths[:, None], (slots, 128))
    low = lambda *shape: pltpu.VMEM(shape, BF16)
    wide_f32 = lambda *shape: pltpu.VMEM(shape, F32)
    anywhere = pl.BlockSpec(memory_space=pl.ANY)
    inside = pl.BlockSpec(memory_space=pltpu.VMEM)
    copies = 96
    out, tokens_grad, grad_qkv, grad_out_w, grad_in, grad_fc2, vector_grad = pl.pallas_call(
        partial(slot_kernel, devices, depth, features),
        out_shape=(
            jax.ShapeDtypeStruct(tokens.shape, BF16),
            jax.ShapeDtypeStruct(tokens.shape, BF16),
            jax.ShapeDtypeStruct((lines, 3 * D), F32),
            jax.ShapeDtypeStruct((lines, D), F32),
            jax.ShapeDtypeStruct((lines, features), F32),
            jax.ShapeDtypeStruct((features // count, D), F32),
            jax.ShapeDtypeStruct(vectors.shape, F32),
        ),
        in_specs=[anywhere, anywhere, inside, inside] + [anywhere] * 4,
        out_specs=(inside,) * 7,
        scratch_shapes=[
            low(D, 3 * D // 2),
            low(D // 2, D),
            low(D, features // 2),
            low(features // 2, D),
            low(total, D),
            low(total, D),
            low(total, D),
            low(total, D),
            low(total, 4 * block),
            low(chips - 1, rows, 4 * block),
            low(rows, D),
            pltpu.VMEM((slots, 128), jnp.int32),
            low(rows, 3 * D // 2),
            low(rows, D // 2),
            wide_f32(rows, D),
            wide_f32(rows, D),
            wide_f32(rows, D),
            wide_f32(rows, D),
            wide_f32(half, D),
            wide_f32(rows, D),
            wide_f32(rows, D),
            wide_f32(rows, D),
            wide_f32(rows, features // 2),
            low(rows, features // 2),
            low(total, wide),
            low(total, wide),
            low(depth, 2 * wide // depth, D),
            low(depth - 1, 2 * wide // depth, D),
            low(depth - 1, 2 * wide // depth, D),
            low(depth, devices * lines, 4 * block),
            low(depth - 1, devices * lines, 4 * block),
            low(depth - 1, devices * lines, 4 * block),
            low(devices, lines, wide),
            low(devices, lines, wide),
            low(devices, lines, 3 * block),
            low(devices, lines, 3 * block),
            wide_f32(16, D),
            wide_f32(hops, 16, D),
            low(rows, 3 * D // 2),
            low(half, D),
            low(*tokens.shape),
            low(half, D),
            low(*tokens.shape),
            pltpu.SemaphoreType.DMA((6 * chips,)),
            pltpu.SemaphoreType.DMA((copies,)),
            pltpu.SemaphoreType.DMA((copies,)),
        ],
        compiler_params=pltpu.CompilerParams(
            collective_id=0, has_side_effects=True, vmem_limit_bytes=64 * 1024 * 1024 - 64 * 1024
        ),
        name="slot",
    )(tokens, out_grad, lens, vectors, w_qkv, w_out, w_in, w_fc2)
    index = lax.axis_index("dp") * depth + lax.axis_index("ctx")
    own_vectors = lax.dynamic_slice_in_dim(vector_grad.reshape(count, -1), index, 1, 0)
    grad_rows = jnp.concatenate(
        [value.reshape(1, -1) for value in (grad_qkv, grad_out_w, grad_in, grad_fc2, own_vectors)],
        axis=1,
    )
    return (out, tokens_grad) + update(
        grad_rows, index, count, (w_qkv, w_out, w_in, w_fc2, vectors), moment_one, moment_two
    )


def update(grad_rows, index, count, weights, moment_one, moment_two):
    pieces = []
    for weight in weights:
        if weight.shape[0] % count == 0:
            lines = weight.shape[0] // count
            piece = lax.dynamic_slice_in_dim(weight, index * lines, lines, 0)
        else:
            piece = lax.dynamic_slice_in_dim(weight.reshape(count, -1), index, 1, 0)
        pieces.append(piece.reshape(1, -1).astype(F32))
    params = jnp.concatenate(pieces, axis=1)
    new_one = beta_one * moment_one + (1.0 - beta_one) * grad_rows
    new_two = beta_two * moment_two + (1.0 - beta_two) * grad_rows * grad_rows
    fix_one = 1.0 - beta_one**step_count
    fix_two = 1.0 - beta_two**step_count
    change = new_one / fix_one / (jnp.sqrt(new_two / fix_two) + adam_eps)
    new_params = params - learn_rate * (change + decay_rate * params)
    return (grad_rows, new_params, new_one, new_two)


def layer(tokens, *rest):
    slots, piece, width = tokens.shape
    devices, depth = lax.axis_size("dp"), lax.axis_size("ctx")
    fits = slots == 2 and depth == 2 * slots and devices % 2 == 0
    if fits and (H * HD // devices) % 128 == 0 and (FF // devices) % 128 == 0:
        return slot_body(tokens, *rest)
    return body(tokens, *rest)


def solution(mesh):
    placed = (
        P("dp", "ctx", None),
        P("dp", "ctx", None),
        P("dp"),
        P(),
        P(),
        P(),
        P(),
        P(),
        P(("dp", "ctx"), None),
        P(("dp", "ctx"), None),
    )
    return jax.shard_map(
        layer,
        mesh=mesh,
        in_specs=placed,
        out_specs=(
            P("dp", "ctx", None),
            P("dp", "ctx", None),
            P(("dp", "ctx"), None),
            P(("dp", "ctx"), None),
            P(("dp", "ctx"), None),
            P(("dp", "ctx"), None),
        ),
        check_vma=False,
    )
```

```python
from functools import partial

import jax
import jax.numpy as jnp
from jax import lax
from jax.experimental import pallas as pl
from jax.experimental.pallas import tpu as pltpu
from jax.sharding import PartitionSpec as P

D = 1024
H = 16
HD = 64
FF = 4096


EPSILON = 1e-05
learn_rate = 0.01
beta_one = 0.9
beta_two = 0.999
adam_eps = 1e-08
decay_rate = 0.01
step_count = 10.0


def layer_norm(values, gain, shift):
    center = values - jnp.mean(values, axis=-1, keepdims=True)
    spread = jnp.mean(center * center, axis=-1, keepdims=True)
    return center * lax.rsqrt(spread + EPSILON) * gain + shift


def split_vectors(vectors):
    ratio = FF // D
    return (
        vectors[0],
        vectors[1],
        vectors[2],
        vectors[3 : 3 + ratio].reshape(FF),
        vectors[3 + ratio],
        vectors[4 + ratio],
        vectors[5 + ratio],
        vectors[6 + ratio],
        vectors[7 + ratio],
    )


def inner(left, right):
    return lax.dot_general(
        left, right, (((0,), (0,)), ((), ())), preferred_element_type=jnp.float32
    )


def through(left, weight):
    return lax.dot_general(
        left, weight, (((1,), (1,)), ((), ())), preferred_element_type=jnp.float32
    )


def run_slots(function, items):
    return lax.map(lambda item: function(*item), items)


def heads_block():
    return 4


def split_heads(matrix):
    count = matrix.shape[0]
    group = heads_block()
    return jnp.moveaxis(matrix.reshape(count, H // group, group, HD), 1, 0)


def join_heads(blocked):
    return jnp.moveaxis(blocked, 0, 1).reshape(blocked.shape[1], H * HD)


def split_stats(stats):
    group = heads_block()
    return stats.reshape(H // group, group, stats.shape[-1])


def shard_piece(left, right, number, shard_count):
    weight_rows = left.shape[1]
    columns = right.shape[1]
    per_shard = weight_rows * columns // shard_count
    block = inner(left, right).reshape(-1)
    return block.reshape(number, per_shard)


def project(flat_tokens, w_qkv, vectors):
    joined = jnp.dot(flat_tokens, w_qkv, preferred_element_type=jnp.float32)
    queries = ((joined[:, :D] + vectors[0]) * 0.125).astype(jnp.bfloat16)
    keys = joined[:, D : 2 * D].astype(jnp.bfloat16)
    values = (joined[:, 2 * D :] + vectors[1]).astype(jnp.bfloat16)
    return (queries, keys, values)


def attend_slot(queries, keys, values, live):
    rows = queries.shape[0]

    def attend_one_block(item):
        query_heads, key_heads, value_heads = item
        scores = jnp.einsum(
            "qhd,khd->hqk", query_heads, key_heads, preferred_element_type=jnp.float32
        )
        scores = jnp.where(live[None, None, :], scores, -1e30)
        maximum = jnp.max(scores, axis=-1, keepdims=True)
        expo = jnp.exp(scores - maximum)
        total = jnp.sum(expo, axis=-1, keepdims=True)
        probs_low = (expo / total).astype(jnp.bfloat16)
        mixed = jnp.einsum(
            "hqk,khd->qhd", probs_low, value_heads, preferred_element_type=jnp.float32
        )
        return (mixed, (maximum + jnp.log(total))[..., 0])

    mixed, log_total = lax.map(
        attend_one_block, (split_heads(queries), split_heads(keys), split_heads(values))
    )
    return (join_heads(mixed), log_total.reshape(H, rows))


def query_back(queries, keys, values, live, log_total, grad_mixed, with_keys):
    rows = queries.shape[0]

    def query_one_block(item):
        query_heads, key_heads, value_heads, grad_heads, block_log = item
        scores = jnp.einsum(
            "qhd,khd->hqk", query_heads, key_heads, preferred_element_type=jnp.float32
        )
        scores = jnp.where(live[None, None, :], scores, -1e30)
        probs = jnp.exp(scores - block_log[:, :, None])
        grad_probs = jnp.einsum(
            "qhd,khd->hqk", grad_heads, value_heads, preferred_element_type=jnp.float32
        )
        row_sums = jnp.sum(probs * grad_probs, axis=-1)
        grad_scores = (probs * (grad_probs - row_sums[:, :, None])).astype(jnp.bfloat16)
        grad_query = jnp.einsum(
            "hqk,khd->qhd", grad_scores, key_heads, preferred_element_type=jnp.float32
        )
        grad_key = jnp.einsum(
            "hqk,qhd->khd", grad_scores, query_heads, preferred_element_type=jnp.float32
        )
        grad_value = jnp.einsum(
            "hqk,qhd->khd",
            probs.astype(jnp.bfloat16),
            grad_heads,
            preferred_element_type=jnp.float32,
        )
        return (grad_query, row_sums, grad_key, grad_value)

    items = (
        split_heads(queries),
        split_heads(keys),
        split_heads(values),
        split_heads(grad_mixed),
        split_stats(log_total),
    )
    results = lax.map(query_one_block, items)
    grad_query, row_sums, grad_key, grad_value = results
    return (
        join_heads(grad_query),
        row_sums.reshape(H, rows),
        join_heads(grad_key),
        join_heads(grad_value),
    )


def tail(flat_tokens, mixed, w_out, w_in, w_fc2, vectors):
    bias_q, bias_v, bias_o, bias_in, bias_fc2, gain_one, shift_one, gain_two, shift_two = (
        split_vectors(vectors)
    )
    mixed_low = mixed.astype(jnp.bfloat16)
    summed_one = (
        flat_tokens.astype(jnp.float32)
        + jnp.dot(mixed_low, w_out, preferred_element_type=jnp.float32)
        + bias_o
    )
    normed = layer_norm(summed_one, gain_one, shift_one)
    normed_low = normed.astype(jnp.bfloat16)
    hidden_pre = jnp.dot(normed_low, w_in, preferred_element_type=jnp.float32) + bias_in
    hidden_low = jax.nn.gelu(hidden_pre, approximate=False).astype(jnp.bfloat16)
    summed_two = normed + jnp.dot(hidden_low, w_fc2, preferred_element_type=jnp.float32) + bias_fc2
    result = layer_norm(summed_two, gain_two, shift_two)
    return (mixed_low, summed_one, normed_low, hidden_pre, hidden_low, summed_two, result)


def body(tokens, out_grad, lengths, w_qkv, w_out, w_in, w_fc2, vectors, moment_one, moment_two):
    slots, piece, width = tokens.shape
    length = piece * lax.axis_size("ctx")
    local_pos = lax.axis_index("ctx") * piece + jnp.arange(piece, dtype=jnp.int32)
    own_live = local_pos[None, :] < lengths[:, None]
    valid = own_live.astype(jnp.float32)
    key_live = jnp.arange(length, dtype=jnp.int32)[None, :] < lengths[:, None]
    bias_q, bias_v, bias_o, bias_in, bias_fc2, gain_one, shift_one, gain_two, shift_two = (
        split_vectors(vectors)
    )
    flat_tokens = tokens.reshape(slots * piece, width)
    queries, keys, values = project(flat_tokens, w_qkv, vectors)
    keys_all, values_all = (
        lax.all_gather(keys.reshape(slots, piece, width), "ctx", axis=1, tiled=True),
        lax.all_gather(values.reshape(slots, piece, width), "ctx", axis=1, tiled=True),
    )
    mixed, log_total = run_slots(
        attend_slot, (queries.reshape(slots, piece, width), keys_all, values_all, key_live)
    )
    saved = tail(flat_tokens, mixed.reshape(slots * piece, width), w_out, w_in, w_fc2, vectors)
    out = (saved[6].reshape(slots, piece, width) * valid[..., None]).astype(jnp.bfloat16)
    again = lax.optimization_barrier(flat_tokens)
    queries, keys, values = project(again, w_qkv, vectors)
    keys_all, values_all = (
        lax.all_gather(keys.reshape(slots, piece, width), "ctx", axis=1, tiled=True),
        lax.all_gather(values.reshape(slots, piece, width), "ctx", axis=1, tiled=True),
    )
    mixed, log_total = run_slots(
        attend_slot, (queries.reshape(slots, piece, width), keys_all, values_all, key_live)
    )
    saved = tail(again, mixed.reshape(slots * piece, width), w_out, w_in, w_fc2, vectors)
    mixed_low, summed_one, normed_low, hidden_pre, hidden_low, summed_two, result = saved
    cotangent = (out_grad.astype(jnp.float32) * valid[..., None]).reshape(slots * piece, width)
    unused_two, norm_two_back = jax.vjp(layer_norm, summed_two, gain_two, shift_two)
    grad_two, grad_gain_two, grad_shift_two = norm_two_back(cotangent)
    grad_fc2_low = grad_two.astype(jnp.bfloat16)
    bias_fc2_grad = jnp.sum(grad_fc2_low.astype(jnp.float32), axis=0)
    grad_hidden = through(grad_fc2_low, w_fc2)
    unused_gelu, gelu_back = jax.vjp(partial(jax.nn.gelu, approximate=False), hidden_pre)
    grad_pre_low = gelu_back(grad_hidden)[0].astype(jnp.bfloat16)
    bias_in_grad = jnp.sum(grad_pre_low.astype(jnp.float32), axis=0)
    grad_normed = grad_two + through(grad_pre_low, w_in)
    unused_one, norm_one_back = jax.vjp(layer_norm, summed_one, gain_one, shift_one)
    grad_one, grad_gain_one, grad_shift_one = norm_one_back(grad_normed)
    grad_branch_low = grad_one.astype(jnp.bfloat16)
    bias_out_grad = jnp.sum(grad_branch_low.astype(jnp.float32), axis=0)
    grad_mixed_low = (
        through(grad_branch_low, w_out).astype(jnp.bfloat16).reshape(slots, piece, width)
    )
    queries_slots = queries.reshape(slots, piece, width)
    grad_query, row_sums, grad_key, grad_value = run_slots(
        partial(query_back, with_keys=True),
        (queries_slots, keys_all, values_all, key_live, log_total, grad_mixed_low),
    )
    grad_key, grad_value = (
        lax.psum_scatter(
            grad_key.astype(jnp.bfloat16), "ctx", scatter_dimension=1, tiled=True
        ).astype(jnp.float32),
        lax.psum_scatter(
            grad_value.astype(jnp.bfloat16), "ctx", scatter_dimension=1, tiled=True
        ).astype(jnp.float32),
    )
    rows = slots * piece
    grad_query_low = grad_query.reshape(rows, width).astype(jnp.bfloat16) * jnp.bfloat16(0.125)
    grad_key_low = grad_key.reshape(rows, width).astype(jnp.bfloat16)
    grad_value_low = grad_value.reshape(rows, width).astype(jnp.bfloat16)
    grad_joined = jnp.concatenate([grad_query_low, grad_key_low, grad_value_low], axis=1)
    bias_q_grad = jnp.sum(grad_query_low.astype(jnp.float32), axis=0)
    bias_v_grad = jnp.sum(grad_value_low.astype(jnp.float32), axis=0)
    tokens_grad = (
        (grad_one + through(grad_joined, w_qkv)).reshape(slots, piece, width).astype(jnp.bfloat16)
    )
    vector_grad = jnp.concatenate(
        [
            bias_q_grad[None],
            bias_v_grad[None],
            bias_out_grad[None],
            bias_in_grad.reshape(FF // D, D),
            bias_fc2_grad[None],
            grad_gain_one[None],
            grad_shift_one[None],
            grad_gain_two[None],
            grad_shift_two[None],
        ],
        axis=0,
    )
    count = lax.axis_size(("dp", "ctx"))
    vector_rows = vector_grad.reshape(count, -1)
    pairs = (
        (flat_tokens, grad_joined),
        (mixed_low, grad_branch_low),
        (normed_low, grad_pre_low),
        (hidden_low, grad_fc2_low),
    )
    blocks = [
        shard_piece(left, right, 1 * lax.axis_size(("dp", "ctx")), count) for left, right in pairs
    ]
    blocks.append(vector_rows)
    grad_rows = lax.psum_scatter(
        jnp.concatenate(blocks, axis=1), ("dp", "ctx"), scatter_dimension=0, tiled=True
    )
    index = lax.axis_index(("dp", "ctx"))
    params = jnp.concatenate(
        [
            lax.dynamic_slice_in_dim(weight.reshape(count, -1), index, 1, 0).astype(jnp.float32)
            for weight in (w_qkv, w_out, w_in, w_fc2, vectors)
        ],
        axis=1,
    )
    new_one = beta_one * moment_one + (1.0 - beta_one) * grad_rows
    new_two = beta_two * moment_two + (1.0 - beta_two) * grad_rows * grad_rows
    fix_one = 1.0 - beta_one**step_count
    fix_two = 1.0 - beta_two**step_count
    update = new_one / fix_one / (jnp.sqrt(new_two / fix_two) + adam_eps)
    new_params = params - learn_rate * (update + decay_rate * params)
    return (out, tokens_grad, grad_rows, new_params, new_one, new_two)


BF16 = jnp.bfloat16
F32 = jnp.float32


def layer_norm_stats(values):
    center = values - jnp.mean(values, axis=-1, keepdims=True)
    spread = jnp.mean(center * center, axis=-1, keepdims=True)
    return center, lax.rsqrt(spread + EPSILON)


def layer_norm_back(center, scale, gain, cotangent):
    scaled = cotangent * gain
    mean_scaled = jnp.mean(scaled, axis=-1, keepdims=True)
    mean_cross = jnp.mean(scaled * center, axis=-1, keepdims=True)
    return scale * (scaled - mean_scaled - center * (scale * scale) * mean_cross)


def normal_cdf(values):
    return 0.5 * (1.0 + lax.erf(values * 0.7071067811865476))


def dot(left, right):
    return jnp.dot(left, right, preferred_element_type=F32)


def positions(axis, shape, slot, piece):
    place = lax.broadcasted_iota(jnp.int32, shape, axis)
    block = lax.div(place, piece)
    half = lax.div(block, 2)
    step = lax.rem(block, 2)
    return (2 * half + lax.rem(slot + step, 2)) * piece + lax.rem(place, piece)


def head_probs(queries, keys, live):
    scores = through(queries, keys)
    scores = jnp.where(live, scores, -1e30)
    expo = jnp.exp(scores - jnp.max(scores, axis=-1, keepdims=True))
    return expo / jnp.sum(expo, axis=-1, keepdims=True)


MESH = pl.DeviceIdType.MESH


class Links:
    def __init__(self, sends, recvs):
        self.sends, self.recvs = sends, recvs
        self.used = 0
        self.open = []

    def copy(self, source, target, device):
        self.used += 1
        return self.again(source, target, device)

    def again(self, source, target, device):
        number = self.used - 1
        return pltpu.make_async_remote_copy(
            src_ref=source,
            dst_ref=target,
            send_sem=self.sends.at[number],
            recv_sem=self.recvs.at[number],
            device_id=device,
            device_id_type=MESH,
        )

    def send(self, source, target, device):
        made = self.copy(source, target, device)
        made.start()
        self.open.append((made, None))
        return made

    def send_if(self, condition, source, target, device):
        made = self.copy(source, target, device)
        pl.when(condition)(made.start)
        self.open.append((made, condition))
        return made

    def send_or_keep(self, here, source, target, device):
        number = self.used
        made = self.copy(source, target, device)
        local = pltpu.make_async_copy(source, target, self.recvs.at[number])
        pl.when(here)(local.start)
        away = jnp.logical_not(here)
        pl.when(away)(made.start)
        self.open.append((made, away))

        def wait():
            pl.when(here)(local.wait)
            pl.when(away)(made.wait_recv)

        return wait

    def close(self):
        for made, condition in self.open:
            if condition is None:
                made.wait_send()
            else:
                pl.when(condition)(made.wait_send)


def flip(value, mask):
    result = value
    bit = 1
    while bit <= mask:
        if mask & bit:
            result = result + bit * (1 - 2 * lax.rem(lax.div(value, bit), 2))
        bit *= 2
    return result


def flip_traced(value, mask, size):
    result = value
    bit = 1
    while bit < size:
        set_bit = lax.rem(lax.div(mask, bit), 2)
        result = result + bit * set_bit * (1 - 2 * lax.rem(lax.div(value, bit), 2))
        bit *= 2
    return result


def at_rows(start, size):
    return pl.ds(pl.multiple_of(start, 64), size)


def slot_kernel(devices, depth, features, *refs):
    (
        tokens, out_grad, lengths, vec, w_qkv, w_out, w_in, w_fc2,
        out_ref, tgrad_ref, g_qkv, g_out, g_in, g_fc2, g_vec,
        wqkv, wo, w_up, w_down,
        x_all, n_all, g_all, b_all, j_all, j_send, g_rows, lens_peer,
        qkv, mixed, part, part_a, part_b, part_c, part_d, summed, grad_two, grad_one,
        pre_s, hid, hid_all, gp_all, packed, right, left, packed_two, right_two, left_two,
        trade_in, got_in, trade_qkv, got_qkv, vec_s, vec_by, sums, dqkv, out_half, out_got, tg_half, tg_got, lens,
        local_sems, sends, recvs,
    ) = refs
    chips = devices // 2
    me, slot = lax.axis_index("dp"), lax.axis_index("ctx")
    core, chip = lax.rem(me, 2), lax.div(me, 2)
    base = me - core
    peer = (base + 1 - core, slot)
    piece = tokens.shape[1]
    half = 2 * piece
    rows = 2 * half
    block = D // devices
    wide = features // devices
    lines = D // (devices * depth)
    net = Links(sends, recvs)
    mine_at = at_rows(core * half, half)
    other_at = at_rows((1 - core) * half, half)
    chunk = 32

    row_of = lax.broadcasted_iota(jnp.int32, lens.shape, 0)
    lens[...] = jnp.where(row_of == 0, lengths[0], lengths[1])
    vec_s[...] = jnp.zeros_like(vec_s)
    loads = []

    def load(source, target):
        made = pltpu.make_async_copy(source, target, local_sems.at[len(loads)])
        made.start()
        loads.append(made)

    where = [2 * flip(chip, mask) + core for mask in range(chips)]
    for mask in range(chips):
        for kind in range(3):
            start = pl.multiple_of(kind * D + where[mask] * block, block)
            load(
                w_qkv.at[:, pl.ds(start, block)],
                wqkv.at[:, (3 * mask + kind) * block : (3 * mask + kind + 1) * block],
            )
    n_qkv = len(loads)
    for mask in range(chips):
        start = pl.multiple_of(where[mask] * block, block)
        load(w_out.at[pl.ds(start, block), :], wo.at[mask * block : (mask + 1) * block, :])
    n_out = len(loads)
    for mask in range(chips):
        start = pl.multiple_of(where[mask] * wide, wide)
        load(w_in.at[:, pl.ds(start, wide)], w_up.at[:, mask * wide : (mask + 1) * wide])
    n_up = len(loads)
    for mask in range(chips):
        start = pl.multiple_of(where[mask] * wide, wide)
        load(w_fc2.at[pl.ds(start, wide), :], w_down.at[mask * wide : (mask + 1) * wide, :])

    barrier = pltpu.get_barrier_semaphore()
    friends = [(flip(me, mask), slot) for mask in range(1, devices)]
    for shift in range(1, depth):
        far = lax.rem(slot + shift, depth)
        friends += [(me, far), (flip(me, 1), far)]
    for friend in friends:
        pl.semaphore_signal(barrier, inc=1, device_id=friend, device_id_type=MESH)
    pl.semaphore_wait(barrier, len(friends))

    def spread(source, target):
        waits = []
        for step in range(2):
            pick = lax.rem(slot + step, 2)
            upper = lax.div(slot, 2)
            place = 2 * core + pick
            here = jnp.logical_and(upper == core, place == slot)
            waits.append(
                net.send_or_keep(
                    here,
                    source.at[pick],
                    target.at[at_rows((2 * upper + step) * piece, piece)],
                    (base + upper, place),
                )
            )
        return waits

    def pass_on(waits, target):
        made = []
        for step, wait in enumerate(waits):
            wait()
            spot = target.at[at_rows((2 * core + step) * piece, piece)]
            made.append(net.send(spot, spot, peer))
        return made

    token_waits = spread(tokens, x_all)
    grad_waits = spread(out_grad, g_rows)
    lens_copy = net.send(lens, lens_peer, peer)
    token_passes = pass_on(token_waits, x_all)

    def plane_start(target):
        source = target.at[mine_at]
        return [
            net.send(
                source, target.at[at_rows(mask * rows + core * half, half)], (flip(me, 2 * mask), slot)
            )
            for mask in range(1, chips)
        ]

    def plane_pass(copies, target):
        made = []
        for mask, copy in enumerate(copies, 1):
            copy.wait_recv()
            spot = target.at[at_rows(mask * rows + core * half, half)]
            made.append(net.send(spot, spot, peer))
        return made

    x_plane = plane_start(x_all)
    for made in loads[:n_qkv]:
        made.wait()
    lens_copy.wait_recv()
    for made in token_passes:
        made.wait_recv()
    owned = jnp.where(lax.div(slot, 2) == core, lens[...], lens_peer[...])
    length = jnp.where(lax.rem(slot, 2) == 0, owned[0:1, 0:1], owned[1:2, 0:1])
    live = positions(1, (1, rows), slot, piece) < length
    lane = lax.broadcasted_iota(jnp.int32, (1, block), 1)

    @pl.loop(0, chips)
    def _(mask):
        spot = 2 * flip_traced(chip, mask, chips) + core
        lanes = pl.ds(pl.multiple_of(spot * block, block), block)
        joined = dot(x_all[0:rows, :], wqkv[:, pl.ds(pl.multiple_of(mask * 3 * block, block), 3 * block)])
        queries = ((joined[:, 0:block] + vec[0:1, lanes]) * 0.125).astype(BF16)
        keys = joined[:, block : 2 * block].astype(BF16)
        values = (joined[:, 2 * block :] + vec[1:2, lanes]).astype(BF16)
        total = jnp.zeros((rows, block), F32)
        for head in range(block // HD):
            mine = lax.div(lane, HD) == head
            probs = head_probs(jnp.where(mine, queries, jnp.zeros_like(queries)), keys, live)
            total = jnp.where(mine, dot(probs.astype(BF16), values), total)
        start = pl.multiple_of(mask * 3 * block, block)
        qkv[:, pl.ds(start, block)] = queries
        qkv[:, pl.ds(pl.multiple_of(start + block, block), block)] = keys
        qkv[:, pl.ds(pl.multiple_of(start + 2 * block, block), block)] = values
        mixed[:, pl.ds(pl.multiple_of(mask * block, block), block)] = total.astype(BF16)

    for made in loads[n_qkv:n_out]:
        made.wait()

    def exchange(compute, target, before):
        made = []
        for number, at in enumerate((other_at, mine_at)):
            if before is not None:
                before[number].wait_send()
            part[at, :] = compute(at)
            made.append(net.copy(part.at[at], target.at[at], peer))
            made[-1].start()
        return made

    first = exchange(lambda at: dot(mixed[at, :], wo[...]), part_a, None)
    grad_passes = pass_on(grad_waits, g_rows)

    def norm_one(start):
        @pl.loop(0, half // chunk)
        def _(step):
            at = pl.ds(pl.multiple_of(start + step * chunk, chunk), chunk)
            total = x_all[at, :].astype(F32) + (part[at, :] + part_a[at, :]) + vec[2:3, :]
            center, scale = layer_norm_stats(total)
            summed[at, :] = total
            n_all[at, :] = (center * scale * vec[8:9, :] + vec[9:10, :]).astype(BF16)

    first[0].wait_recv()
    norm_one(core * half)
    n_plane = plane_start(n_all)
    first[1].wait_recv()
    norm_one((1 - core) * half)
    for made in loads[n_out:]:
        made.wait()

    def bias_of(mask):
        spot = flip_traced(chip, mask, chips)
        lanes = pl.ds(pl.multiple_of(core * wide, wide), wide)
        result = vec[3:4, lanes]
        for row in range(1, chips):
            result = jnp.where(spot == row, vec[3 + row : 4 + row, lanes], result)
        return result

    @pl.loop(0, chips)
    def _(mask):
        at = pl.ds(pl.multiple_of(mask * wide, wide), wide)
        value = dot(n_all[0:rows, :], w_up[:, at]) + bias_of(mask)
        pre_s[:, at] = value
        hid[:, at] = (value * normal_cdf(value)).astype(BF16)

    second = exchange(lambda at: dot(hid[at, :], w_down[...]), part_b, first)
    for made in grad_passes:
        made.wait_recv()

    def norm_two(start, own):
        @pl.loop(0, half // chunk)
        def _(step):
            begin = pl.multiple_of(start + step * chunk, chunk)
            at = pl.ds(begin, chunk)
            center, scale = layer_norm_stats(summed[at, :])
            normed = center * scale * vec[8:9, :] + vec[9:10, :]
            center, scale = layer_norm_stats(normed + (part[at, :] + part_b[at, :]) + vec[7:8, :])
            place = begin + lax.broadcasted_iota(jnp.int32, (chunk, 1), 0)
            piece_of = lax.div(place, piece)
            spot = 2 * lax.div(piece_of, 2) + lax.rem(slot + lax.rem(piece_of, 2), 2)
            valid = (spot * piece + lax.rem(place, piece) < length).astype(F32)
            unit = center * scale
            error = g_rows[at, :].astype(F32) * valid
            grad = layer_norm_back(center, scale, vec[10:11, :], error)
            grad_two[at, :] = grad
            low = grad.astype(BF16)
            g_all[at, :] = low
            if own:
                out_half[pl.ds(pl.multiple_of(step * chunk, chunk), chunk), :] = (
                    valid * (unit * vec[10:11, :] + vec[11:12, :])
                ).astype(BF16)
                vec_s[7:8, :] += jnp.sum(low.astype(F32), axis=0, keepdims=True)
                vec_s[10:11, :] += jnp.sum(error * unit, axis=0, keepdims=True)
                vec_s[11:12, :] += jnp.sum(error, axis=0, keepdims=True)

    def go_back(source, target):
        waits = []
        for step in range(2):
            place = 2 * core + lax.rem(slot + step, 2)
            upper = lax.div(slot, 2)
            here = jnp.logical_and(upper == core, place == slot)
            waits.append(
                net.send_or_keep(
                    here,
                    source.at[step * piece : (step + 1) * piece],
                    target.at[lax.rem(slot, 2)],
                    (base + upper, place),
                )
            )
        return waits

    second[0].wait_recv()
    norm_two(core * half, True)
    g_plane = plane_start(g_all)
    second[1].wait_recv()
    norm_two((1 - core) * half, False)
    out_waits = go_back(out_half, out_got)
    n_pass = plane_pass(n_plane, n_all)
    x_pass = plane_pass(x_plane, x_all)

    def slope_of(value, cdf):
        return cdf + value * (jnp.exp(-0.5 * value * value) * 0.3989422804014327)

    @pl.loop(0, chips)
    def _(mask):
        at = pl.ds(pl.multiple_of(mask * wide, wide), wide)
        value = pre_s[:, at]
        grad = through(g_all[0:rows, :], w_down[at, :])
        hid[:, at] = (grad * slope_of(value, normal_cdf(value))).astype(BF16)

    third = exchange(lambda at: through(hid[at, :], w_up[...]), part_c, second)

    def norm_one_back(start, own):
        @pl.loop(0, half // chunk)
        def _(step):
            at = pl.ds(pl.multiple_of(start + step * chunk, chunk), chunk)
            center, scale = layer_norm_stats(summed[at, :])
            error = grad_two[at, :] + (part[at, :] + part_c[at, :])
            grad = layer_norm_back(center, scale, vec[8:9, :], error)
            low = grad.astype(BF16)
            b_all[at, :] = low
            grad_one[at, :] = grad
            if own:
                vec_s[2:3, :] += jnp.sum(low.astype(F32), axis=0, keepdims=True)
                vec_s[8:9, :] += jnp.sum(error * (center * scale), axis=0, keepdims=True)
                vec_s[9:10, :] += jnp.sum(error, axis=0, keepdims=True)

    third[0].wait_recv()
    norm_one_back(core * half, True)
    b_plane = plane_start(b_all)
    third[1].wait_recv()
    norm_one_back((1 - core) * half, False)
    g_pass = plane_pass(g_plane, g_all)

    bias_mine = bias_of(0)

    def feed_rows(mask):
        at = slice(mask * rows, (mask + 1) * rows)
        value = dot(n_all[at, :], w_up[:, 0:wide]) + bias_mine
        cdf = normal_cdf(value)
        hid_all[at, :] = (value * cdf).astype(BF16)
        low = (through(g_all[at, :], w_down[0:wide, :]) * slope_of(value, cdf)).astype(BF16)
        gp_all[at, :] = low
        return jnp.sum(low.astype(F32), axis=0, keepdims=True)

    bias_sum = feed_rows(0)
    for mask in range(1, chips):
        n_pass[mask - 1].wait_recv()
        g_pass[mask - 1].wait_recv()
        bias_sum = bias_sum + feed_rows(mask)
    lanes = pl.ds(pl.multiple_of(core * wide, wide), wide)
    for row in range(chips):
        vec_s[3 + row : 4 + row, lanes] = jnp.where(chip == row, bias_sum, jnp.zeros_like(bias_sum))
    down_rows = wide // depth
    packs = D // wide
    per_pack = devices // packs
    span = lines * depth
    down = inner(hid_all[...], g_all[...]).astype(BF16)
    for number in range(depth):
        packed[number, 0:down_rows, :] = down[number * down_rows : (number + 1) * down_rows, :]
    for group in range(devices):
        up = inner(n_all[:, group * span : (group + 1) * span], gp_all[...]).astype(BF16)
        row = down_rows + (group % per_pack) * lines
        col = (group // per_pack) * wide
        for number in range(depth):
            packed[number, row : row + lines, col : col + wide] = up[
                number * lines : (number + 1) * lines, :
            ]

    class Line:
        def __init__(self, chunks, from_left, from_right):
            self.chunks, self.from_left, self.from_right = chunks, from_left, from_right
            self.up, self.down, self.first_up, self.first_down = [], [], [], []
            after = (me, lax.rem(slot + 1, depth))
            before = (me, lax.rem(slot + depth - 1, depth))
            for order in range(depth - 1):
                top, low = depth - 1 - order, order
                spot = from_left.at[order]
                self.up.append(net.copy(spot, spot, after))
                self.first_up.append(net.again(chunks.at[top], spot, after))
                net.open.append((self.up[-1], slot < top))
                spot = from_right.at[order]
                self.down.append(net.copy(spot, spot, before))
                self.first_down.append(net.again(chunks.at[low], spot, before))
                net.open.append((self.down[-1], slot > low))

        def first(self):
            for order in range(depth - 1):
                pl.when(slot == 0)(self.first_up[order].start)
                pl.when(slot == depth - 1)(self.first_down[order].start)

        def stage(self, time):
            for order in range(time):
                top, low = depth - 1 - order, order

                @pl.when(slot == time - order)
                def _(order=order, top=top):
                    self.up[order].wait_recv()
                    if time < depth - 1:
                        self.from_left[order] = (
                            self.from_left[order].astype(F32) + self.chunks[top].astype(F32)
                        ).astype(BF16)
                        self.up[order].start()

                @pl.when(depth - 1 - slot == time - order)
                def _(order=order, low=low):
                    self.down[order].wait_recv()
                    if time < depth - 1:
                        self.from_right[order] = (
                            self.from_right[order].astype(F32) + self.chunks[low].astype(F32)
                        ).astype(BF16)
                        self.down[order].start()

    feed_line = Line(packed, right, left)
    feed_line.first()

    grad_parts = range(1, chips)

    def attention_back(mask):
        start = mask * 3 * block
        queries = qkv[:, start : start + block]
        keys = qkv[:, start + block : start + 2 * block]
        values = qkv[:, start + 2 * block : start + 3 * block]
        grad_mixed = through(b_all[0:rows, :], wo[mask * block : (mask + 1) * block, :]).astype(BF16)
        grad_q = jnp.zeros((rows, block), F32)
        grad_k = grad_q
        grad_v = grad_q
        for head in range(block // HD):
            mine = lax.div(lane, HD) == head
            probs = head_probs(jnp.where(mine, queries, jnp.zeros_like(queries)), keys, live)
            grad_probs = through(jnp.where(mine, grad_mixed, jnp.zeros_like(grad_mixed)), values)
            dsum = jnp.sum(probs * grad_probs, axis=-1, keepdims=True)
            grad_scores = (probs * (grad_probs - dsum)).astype(BF16)
            grad_q = jnp.where(mine, dot(grad_scores, keys), grad_q)
            grad_k = jnp.where(mine, inner(grad_scores, queries), grad_k)
            grad_v = jnp.where(mine, inner(probs.astype(BF16), grad_mixed), grad_v)
        grad_q = grad_q.astype(BF16) * jnp.bfloat16(0.125)
        grad_k = grad_k.astype(BF16)
        grad_v = grad_v.astype(BF16)
        spot = pl.ds(pl.multiple_of(where[mask] * block, block), block)
        vec_s[0:1, spot] = jnp.sum(grad_q.astype(F32), axis=0, keepdims=True)
        vec_s[1:2, spot] = jnp.sum(grad_v.astype(F32), axis=0, keepdims=True)
        dqkv[:, start : start + block] = grad_q
        dqkv[:, start + block : start + 2 * block] = grad_k
        dqkv[:, start + 2 * block : start + 3 * block] = grad_v
        if mask:
            joint = j_send.at[mask - 1]
        else:
            joint = j_all.at[0:rows]
        joint[:, 0:block] = grad_q
        joint[:, block : 2 * block] = grad_k
        joint[:, 2 * block : 3 * block] = grad_v
        joint[:, 3 * block : 4 * block] = mixed[:, mask * block : (mask + 1) * block]
        if mask:
            return net.send(
                joint, j_all.at[mask * rows : (mask + 1) * rows], (flip(me, 2 * mask), slot)
            )
        return None

    j_copies = [attention_back(mask) for mask in grad_parts]
    attention_back(0)
    b_pass = plane_pass(b_plane, b_all)
    for made in third:
        made.wait_send()
    part[0:half, :] = through(dqkv[other_at, :], wqkv[...])
    tg_copy = net.copy(part.at[0:half], part_d, peer)
    tg_copy.start()
    part[half:rows, :] = grad_one[mine_at, :] + through(dqkv[mine_at, :], wqkv[...])
    tg_copy.wait_recv()
    tg_half[...] = (part[half:rows, :] + part_d[...]).astype(BF16)
    feed_line.stage(1)
    tg_waits = go_back(tg_half, tg_got)

    tiles = vec.shape[0] * D // 128
    share = tiles // (devices * depth)
    vec_by[...] = jnp.zeros_like(vec_by)
    for tile in range(tiles):
        owner, lane_group = tile // share, tile % share
        row, col = tile // (D // 128), (tile % (D // 128)) * 128
        spot = (owner % depth) * 16 + owner // depth
        vec_by[spot : spot + 1, lane_group * 128 : (lane_group + 1) * 128] = vec_s[
            row : row + 1, col : col + 128
        ]
    for number in range(depth):
        packed_two[number, rows : rows + 16, :] = vec_by[number * 16 : (number + 1) * 16, :].astype(BF16)

    for made in b_pass + x_pass + j_copies:
        made.wait_recv()
    across = inner(j_all[:, 3 * block : 4 * block], b_all[...]).astype(BF16)
    for group in range(devices):
        both = inner(x_all[:, group * span : (group + 1) * span], j_all[:, 0 : 3 * block]).astype(BF16)
        row = group * lines
        for number in range(depth):
            at = slice(number * lines, (number + 1) * lines)
            packed_two[number, row : row + lines, 0 : 3 * block] = both[at, :]
            packed_two[number, row : row + lines, 3 * block : 4 * block] = across[
                at, group * block : (group + 1) * block
            ]
    input_line = Line(packed_two, right_two, left_two)
    input_line.first()

    def finish(line, target, rows_at):
        target[...] = line.chunks[slot, rows_at, :].astype(F32)

        @pl.when(slot >= 1)
        def _():
            target[...] += line.from_left[depth - 1 - slot, rows_at, :].astype(F32)

        @pl.when(slot <= depth - 2)
        def _():
            target[...] += line.from_right[slot, rows_at, :].astype(F32)

    for time in range(2, depth):
        feed_line.stage(time)
    finish(feed_line, g_fc2, slice(0, down_rows))
    low_part = part_d.at[0:down_rows]
    finish(feed_line, low_part, slice(down_rows, 2 * down_rows))
    for group in range(devices):
        row = (group % per_pack) * lines
        col = (group // per_pack) * wide
        trade_in[group] = low_part[row : row + lines, col : col + wide].astype(BF16)

    def trade(source, target):
        return [
            net.send(source.at[flip(me, mask)], target.at[me], (flip(me, mask), slot))
            for mask in range(1, devices)
        ]

    in_copies = trade(trade_in, got_in)
    input_line.stage(1)
    for made in in_copies:
        made.wait_recv()
    got_in[me] = trade_in[me]
    for group in range(devices):
        g_in[:, group * wide : (group + 1) * wide] = got_in[group].astype(F32)
    for time in range(2, depth):
        input_line.stage(time)
    tg_copy.wait_send()
    finish(input_line, sums, slice(0, rows + 16))
    first_row = lax.broadcasted_iota(jnp.int32, (16, 3 * block), 0) == 0
    for group in range(devices):
        trade_qkv[group, 0:lines, :] = sums[group * lines : (group + 1) * lines, 0 : 3 * block].astype(BF16)
        trade_qkv[group, lines : lines + 16, :] = jnp.where(
            first_row, sums[rows + group : rows + group + 1, 0 : 3 * block], 0.0
        ).astype(BF16)
        g_out[:, group * block : (group + 1) * block] = sums[
            group * lines : (group + 1) * lines, 3 * block : 4 * block
        ]
    qkv_copies = trade(trade_qkv, got_qkv)
    for wait in out_waits + tg_waits:
        wait()
    out_ref[...] = out_got[...]
    tgrad_ref[...] = tg_got[...]
    for made in qkv_copies:
        made.wait_recv()
    got_qkv[me] = trade_qkv[me]
    vec_sum = jnp.zeros((16, 3 * block), F32)
    for group in range(devices):
        vec_sum = vec_sum + got_qkv[group, lines : lines + 16, :].astype(F32)
        for kind in range(3):
            g_qkv[:, kind * D + group * block : kind * D + (group + 1) * block] = got_qkv[
                group, 0:lines, kind * block : (kind + 1) * block
            ].astype(F32)
    g_vec[...] = vec_sum[0:8, :]
    net.close()


def adam_kernel(count, *refs):
    (
        g_qkv, g_out, g_in, g_fc2, g_vec, vec, out_in, tgrad_in, w_qkv, w_out, w_in, w_fc2, m_one, m_two,
        out_ref, tgrad_ref, rows_out, params_out, one_out, two_out,
        grads, params, one, two, b_qkv, b_out, b_in, b_fc2, vec_flat, in_sems, w_sems, out_sems,
    ) = refs
    index = lax.axis_index("dp") * lax.axis_size("ctx") + lax.axis_index("ctx")
    size = m_one.shape[1] // 128
    parts = in_sems.shape[1]
    step = grads.shape[0] // parts
    spans = [(number * step, min((number + 1) * step, size) - number * step) for number in range(parts)]
    loads = []
    for number, (start, length) in enumerate(spans):
        pair = []
        for kind, (source, target) in enumerate(((m_one, one), (m_two, two))):
            pair.append(
                pltpu.make_async_copy(
                    source.reshape(size, 128).at[start : start + length],
                    target.at[start : start + length],
                    in_sems.at[kind, number],
                )
            )
            pair[-1].start()
        loads.append(pair)
    weights = []
    for number, (source, target) in enumerate(
        ((w_qkv, b_qkv), (w_out, b_out), (w_in, b_in), (w_fc2, b_fc2))
    ):
        lines = target.shape[0]
        start = pl.multiple_of(index * lines, lines)
        weights.append(
            pltpu.make_async_copy(source.at[pl.ds(start, lines), :], target, w_sems.at[number])
        )
        weights[-1].start()
    out_ref[...] = out_in[...]
    tgrad_ref[...] = tgrad_in[...]

    def flatten(source, target, base):
        lines, groups = source.shape[0], source.shape[1] // 128
        for col in range(groups):
            value = source[:, col * 128 : (col + 1) * 128].astype(F32)
            for row in range(0, lines, 8):
                target[pl.ds(base + row * groups + col, 8, stride=groups), :] = value[row : row + 8, :]

    base = 0
    for grad in (g_qkv, g_out, g_in, g_fc2):
        flatten(grad, grads, base)
        base += grad.shape[0] * grad.shape[1] // 128
    share = g_vec.shape[1] // 128
    groups = vec.shape[1] // 128
    for col in range(groups):
        lanes = slice(col * 128, (col + 1) * 128)
        vec_flat[pl.ds(col, 8, stride=groups), :] = vec[0:8, lanes]
        for row in range(8, vec.shape[0]):
            vec_flat[row * groups + col : row * groups + col + 1, :] = vec[row : row + 1, lanes]
    place = lax.broadcasted_iota(jnp.int32, vec_flat.shape, 0)
    for number in range(share):
        grads[base + number : base + number + 1, :] = g_vec[0:1, number * 128 : (number + 1) * 128]
        params[base + number : base + number + 1, :] = jnp.sum(
            jnp.where(place == index * share + number, vec_flat[...], 0.0), axis=0, keepdims=True
        )
    base = 0
    for made, weight in zip(weights, (b_qkv, b_out, b_in, b_fc2)):
        made.wait()
        flatten(weight, params, base)
        base += weight.shape[0] * weight.shape[1] // 128
    fix_one = 1.0 / (1.0 - beta_one**step_count)
    fix_two = 1.0 / (1.0 - beta_two**step_count)
    copies = []
    for number, (start, length) in enumerate(spans):
        for made in loads[number]:
            made.wait()

        @pl.loop(0, step // 56)
        def _(chunk, start=start):
            at = pl.ds(pl.multiple_of(start + chunk * 56, 8), 56)
            grad, param = grads[at, :], params[at, :]
            new_one = beta_one * one[at, :] + (1.0 - beta_one) * grad
            new_two = beta_two * two[at, :] + (1.0 - beta_two) * grad * grad
            one[at, :] = new_one
            two[at, :] = new_two
            change = new_one * fix_one / (jnp.sqrt(new_two * fix_two) + adam_eps)
            params[at, :] = param - learn_rate * (change + decay_rate * param)

        for kind, (source, target) in enumerate(
            ((grads, rows_out), (params, params_out), (one, one_out), (two, two_out))
        ):
            copies.append(
                pltpu.make_async_copy(
                    source.at[start : start + length],
                    target.reshape(size, 128).at[start : start + length],
                    out_sems.at[kind, number],
                )
            )
            copies[-1].start()
    for made in copies:
        made.wait()


def slot_body(tokens, out_grad, lengths, w_qkv, w_out, w_in, w_fc2, vectors, moment_one, moment_two):
    slots, piece, width = tokens.shape
    devices, depth = lax.axis_size("dp"), lax.axis_size("ctx")
    chips = devices // 2
    count = devices * depth
    features = w_in.shape[1]
    half = 2 * piece
    rows = 2 * half
    block = D // devices
    wide = features // devices
    lines = D // count
    total = rows * chips
    low = lambda *shape: pltpu.VMEM(shape, BF16)
    wide_f32 = lambda *shape: pltpu.VMEM(shape, F32)
    anywhere = pl.BlockSpec(memory_space=pl.ANY)
    inside = pl.BlockSpec(memory_space=pltpu.VMEM)
    copies = 96
    out, tokens_grad, grad_qkv, grad_out_w, grad_in, grad_fc2, vector_grad = pl.pallas_call(
        partial(slot_kernel, devices, depth, features),
        out_shape=(
            jax.ShapeDtypeStruct(tokens.shape, BF16),
            jax.ShapeDtypeStruct(tokens.shape, BF16),
            jax.ShapeDtypeStruct((lines, 3 * D), F32),
            jax.ShapeDtypeStruct((lines, D), F32),
            jax.ShapeDtypeStruct((lines, features), F32),
            jax.ShapeDtypeStruct((features // count, D), F32),
            jax.ShapeDtypeStruct((8, 3 * block), F32),
        ),
        in_specs=[anywhere, anywhere, pl.BlockSpec(memory_space=pltpu.SMEM), inside] + [anywhere] * 4,
        out_specs=(inside,) * 7,
        scratch_shapes=[
            low(D, 3 * D // 2),
            low(D // 2, D),
            low(D, features // 2),
            low(features // 2, D),
            low(total, D),
            low(total, D),
            low(total, D),
            low(total, D),
            low(total, 4 * block),
            low(chips - 1, rows, 4 * block),
            low(rows, D),
            pltpu.VMEM((slots, 128), jnp.int32),
            low(rows, 3 * D // 2),
            low(rows, D // 2),
            wide_f32(rows, D),
            wide_f32(rows, D),
            wide_f32(rows, D),
            wide_f32(rows, D),
            wide_f32(half, D),
            wide_f32(rows, D),
            wide_f32(rows, D),
            wide_f32(rows, D),
            wide_f32(rows, features // 2),
            low(rows, features // 2),
            low(total, wide),
            low(total, wide),
            low(depth, 2 * wide // depth, D),
            low(depth - 1, 2 * wide // depth, D),
            low(depth - 1, 2 * wide // depth, D),
            low(depth, devices * lines + 16, 4 * block),
            low(depth - 1, devices * lines + 16, 4 * block),
            low(depth - 1, devices * lines + 16, 4 * block),
            low(devices, lines, wide),
            low(devices, lines, wide),
            low(devices, lines + 16, 3 * block),
            low(devices, lines + 16, 3 * block),
            wide_f32(16, D),
            wide_f32(16 * depth, 4 * block),
            wide_f32(rows + 16, 4 * block),
            low(rows, 3 * D // 2),
            low(half, D),
            low(*tokens.shape),
            low(half, D),
            low(*tokens.shape),
            pltpu.VMEM((slots, 128), jnp.int32),
            pltpu.SemaphoreType.DMA((6 * chips,)),
            pltpu.SemaphoreType.DMA((copies,)),
            pltpu.SemaphoreType.DMA((copies,)),
        ],
        compiler_params=pltpu.CompilerParams(
            collective_id=0, has_side_effects=True, vmem_limit_bytes=64 * 1024 * 1024 - 64 * 1024
        ),
        name="slot",
    )(tokens, out_grad, lengths, vectors, w_qkv, w_out, w_in, w_fc2)
    size = moment_one.shape[1] // 128
    padded = (size + 279) // 280 * 280
    flat = jax.ShapeDtypeStruct(moment_one.shape, F32)
    return pl.pallas_call(
        partial(adam_kernel, count),
        out_shape=(
            jax.ShapeDtypeStruct(tokens.shape, BF16),
            jax.ShapeDtypeStruct(tokens.shape, BF16),
            flat,
            flat,
            flat,
            flat,
        ),
        in_specs=[inside] * 8 + [anywhere] * 6,
        out_specs=(inside, inside) + (anywhere,) * 4,
        scratch_shapes=[wide_f32(padded, 128)] * 4
        + [
            low(lines, 3 * D),
            low(lines, D),
            low(lines, features),
            low(features // count, D),
            wide_f32(vectors.shape[0] * D // 128, 128),
            pltpu.SemaphoreType.DMA((2, 5)),
            pltpu.SemaphoreType.DMA((4,)),
            pltpu.SemaphoreType.DMA((4, 5)),
        ],
        compiler_params=pltpu.CompilerParams(vmem_limit_bytes=32 * 1024 * 1024),
        name="adam",
    )(
        grad_qkv, grad_out_w, grad_in, grad_fc2, vector_grad, vectors, out, tokens_grad,
        w_qkv, w_out, w_in, w_fc2, moment_one, moment_two,
    )


def layer(tokens, *rest):
    slots, piece, width = tokens.shape
    devices, depth = lax.axis_size("dp"), lax.axis_size("ctx")
    fits = slots == 2 and depth == 2 * slots and devices % 2 == 0
    if fits and (H * HD // devices) % 128 == 0 and (FF // devices) % 128 == 0:
        return slot_body(tokens, *rest)
    return body(tokens, *rest)


def solution(mesh):
    placed = (
        P("dp", "ctx", None),
        P("dp", "ctx", None),
        P("dp"),
        P(),
        P(),
        P(),
        P(),
        P(),
        P(("dp", "ctx"), None),
        P(("dp", "ctx"), None),
    )
    return jax.shard_map(
        layer,
        mesh=mesh,
        in_specs=placed,
        out_specs=(
            P("dp", "ctx", None),
            P("dp", "ctx", None),
            P(("dp", "ctx"), None),
            P(("dp", "ctx"), None),
            P(("dp", "ctx"), None),
            P(("dp", "ctx"), None),
        ),
        check_vma=False,
    )
```

```python
from functools import partial

import jax
import jax.numpy as jnp
from jax import lax
from jax.experimental import pallas as pl
from jax.experimental.pallas import tpu as pltpu
from jax.sharding import PartitionSpec as P

D = 1024
H = 16
HD = 64
FF = 4096


EPSILON = 1e-05
learn_rate = 0.01
beta_one = 0.9
beta_two = 0.999
adam_eps = 1e-08
decay_rate = 0.01
step_count = 10.0


def layer_norm(values, gain, shift):
    center = values - jnp.mean(values, axis=-1, keepdims=True)
    spread = jnp.mean(center * center, axis=-1, keepdims=True)
    return center * lax.rsqrt(spread + EPSILON) * gain + shift


def split_vectors(vectors):
    ratio = FF // D
    return (
        vectors[0],
        vectors[1],
        vectors[2],
        vectors[3 : 3 + ratio].reshape(FF),
        vectors[3 + ratio],
        vectors[4 + ratio],
        vectors[5 + ratio],
        vectors[6 + ratio],
        vectors[7 + ratio],
    )


def inner(left, right):
    return lax.dot_general(
        left, right, (((0,), (0,)), ((), ())), preferred_element_type=jnp.float32
    )


def through(left, weight):
    return lax.dot_general(
        left, weight, (((1,), (1,)), ((), ())), preferred_element_type=jnp.float32
    )


def run_slots(function, items):
    return lax.map(lambda item: function(*item), items)


def heads_block():
    return 4


def split_heads(matrix):
    count = matrix.shape[0]
    group = heads_block()
    return jnp.moveaxis(matrix.reshape(count, H // group, group, HD), 1, 0)


def join_heads(blocked):
    return jnp.moveaxis(blocked, 0, 1).reshape(blocked.shape[1], H * HD)


def split_stats(stats):
    group = heads_block()
    return stats.reshape(H // group, group, stats.shape[-1])


def shard_piece(left, right, number, shard_count):
    weight_rows = left.shape[1]
    columns = right.shape[1]
    per_shard = weight_rows * columns // shard_count
    block = inner(left, right).reshape(-1)
    return block.reshape(number, per_shard)


def project(flat_tokens, w_qkv, vectors):
    joined = jnp.dot(flat_tokens, w_qkv, preferred_element_type=jnp.float32)
    queries = ((joined[:, :D] + vectors[0]) * 0.125).astype(jnp.bfloat16)
    keys = joined[:, D : 2 * D].astype(jnp.bfloat16)
    values = (joined[:, 2 * D :] + vectors[1]).astype(jnp.bfloat16)
    return (queries, keys, values)


def attend_slot(queries, keys, values, live):
    rows = queries.shape[0]

    def attend_one_block(item):
        query_heads, key_heads, value_heads = item
        scores = jnp.einsum(
            "qhd,khd->hqk", query_heads, key_heads, preferred_element_type=jnp.float32
        )
        scores = jnp.where(live[None, None, :], scores, -1e30)
        maximum = jnp.max(scores, axis=-1, keepdims=True)
        expo = jnp.exp(scores - maximum)
        total = jnp.sum(expo, axis=-1, keepdims=True)
        probs_low = (expo / total).astype(jnp.bfloat16)
        mixed = jnp.einsum(
            "hqk,khd->qhd", probs_low, value_heads, preferred_element_type=jnp.float32
        )
        return (mixed, (maximum + jnp.log(total))[..., 0])

    mixed, log_total = lax.map(
        attend_one_block, (split_heads(queries), split_heads(keys), split_heads(values))
    )
    return (join_heads(mixed), log_total.reshape(H, rows))


def query_back(queries, keys, values, live, log_total, grad_mixed, with_keys):
    rows = queries.shape[0]

    def query_one_block(item):
        query_heads, key_heads, value_heads, grad_heads, block_log = item
        scores = jnp.einsum(
            "qhd,khd->hqk", query_heads, key_heads, preferred_element_type=jnp.float32
        )
        scores = jnp.where(live[None, None, :], scores, -1e30)
        probs = jnp.exp(scores - block_log[:, :, None])
        grad_probs = jnp.einsum(
            "qhd,khd->hqk", grad_heads, value_heads, preferred_element_type=jnp.float32
        )
        row_sums = jnp.sum(probs * grad_probs, axis=-1)
        grad_scores = (probs * (grad_probs - row_sums[:, :, None])).astype(jnp.bfloat16)
        grad_query = jnp.einsum(
            "hqk,khd->qhd", grad_scores, key_heads, preferred_element_type=jnp.float32
        )
        grad_key = jnp.einsum(
            "hqk,qhd->khd", grad_scores, query_heads, preferred_element_type=jnp.float32
        )
        grad_value = jnp.einsum(
            "hqk,qhd->khd",
            probs.astype(jnp.bfloat16),
            grad_heads,
            preferred_element_type=jnp.float32,
        )
        return (grad_query, row_sums, grad_key, grad_value)

    items = (
        split_heads(queries),
        split_heads(keys),
        split_heads(values),
        split_heads(grad_mixed),
        split_stats(log_total),
    )
    results = lax.map(query_one_block, items)
    grad_query, row_sums, grad_key, grad_value = results
    return (
        join_heads(grad_query),
        row_sums.reshape(H, rows),
        join_heads(grad_key),
        join_heads(grad_value),
    )


def tail(flat_tokens, mixed, w_out, w_in, w_fc2, vectors):
    bias_q, bias_v, bias_o, bias_in, bias_fc2, gain_one, shift_one, gain_two, shift_two = (
        split_vectors(vectors)
    )
    mixed_low = mixed.astype(jnp.bfloat16)
    summed_one = (
        flat_tokens.astype(jnp.float32)
        + jnp.dot(mixed_low, w_out, preferred_element_type=jnp.float32)
        + bias_o
    )
    normed = layer_norm(summed_one, gain_one, shift_one)
    normed_low = normed.astype(jnp.bfloat16)
    hidden_pre = jnp.dot(normed_low, w_in, preferred_element_type=jnp.float32) + bias_in
    hidden_low = jax.nn.gelu(hidden_pre, approximate=False).astype(jnp.bfloat16)
    summed_two = normed + jnp.dot(hidden_low, w_fc2, preferred_element_type=jnp.float32) + bias_fc2
    result = layer_norm(summed_two, gain_two, shift_two)
    return (mixed_low, summed_one, normed_low, hidden_pre, hidden_low, summed_two, result)


def body(tokens, out_grad, lengths, w_qkv, w_out, w_in, w_fc2, vectors, moment_one, moment_two):
    slots, piece, width = tokens.shape
    length = piece * lax.axis_size("ctx")
    local_pos = lax.axis_index("ctx") * piece + jnp.arange(piece, dtype=jnp.int32)
    own_live = local_pos[None, :] < lengths[:, None]
    valid = own_live.astype(jnp.float32)
    key_live = jnp.arange(length, dtype=jnp.int32)[None, :] < lengths[:, None]
    bias_q, bias_v, bias_o, bias_in, bias_fc2, gain_one, shift_one, gain_two, shift_two = (
        split_vectors(vectors)
    )
    flat_tokens = tokens.reshape(slots * piece, width)
    queries, keys, values = project(flat_tokens, w_qkv, vectors)
    keys_all, values_all = (
        lax.all_gather(keys.reshape(slots, piece, width), "ctx", axis=1, tiled=True),
        lax.all_gather(values.reshape(slots, piece, width), "ctx", axis=1, tiled=True),
    )
    mixed, log_total = run_slots(
        attend_slot, (queries.reshape(slots, piece, width), keys_all, values_all, key_live)
    )
    saved = tail(flat_tokens, mixed.reshape(slots * piece, width), w_out, w_in, w_fc2, vectors)
    out = (saved[6].reshape(slots, piece, width) * valid[..., None]).astype(jnp.bfloat16)
    again = lax.optimization_barrier(flat_tokens)
    queries, keys, values = project(again, w_qkv, vectors)
    keys_all, values_all = (
        lax.all_gather(keys.reshape(slots, piece, width), "ctx", axis=1, tiled=True),
        lax.all_gather(values.reshape(slots, piece, width), "ctx", axis=1, tiled=True),
    )
    mixed, log_total = run_slots(
        attend_slot, (queries.reshape(slots, piece, width), keys_all, values_all, key_live)
    )
    saved = tail(again, mixed.reshape(slots * piece, width), w_out, w_in, w_fc2, vectors)
    mixed_low, summed_one, normed_low, hidden_pre, hidden_low, summed_two, result = saved
    cotangent = (out_grad.astype(jnp.float32) * valid[..., None]).reshape(slots * piece, width)
    unused_two, norm_two_back = jax.vjp(layer_norm, summed_two, gain_two, shift_two)
    grad_two, grad_gain_two, grad_shift_two = norm_two_back(cotangent)
    grad_fc2_low = grad_two.astype(jnp.bfloat16)
    bias_fc2_grad = jnp.sum(grad_fc2_low.astype(jnp.float32), axis=0)
    grad_hidden = through(grad_fc2_low, w_fc2)
    unused_gelu, gelu_back = jax.vjp(partial(jax.nn.gelu, approximate=False), hidden_pre)
    grad_pre_low = gelu_back(grad_hidden)[0].astype(jnp.bfloat16)
    bias_in_grad = jnp.sum(grad_pre_low.astype(jnp.float32), axis=0)
    grad_normed = grad_two + through(grad_pre_low, w_in)
    unused_one, norm_one_back = jax.vjp(layer_norm, summed_one, gain_one, shift_one)
    grad_one, grad_gain_one, grad_shift_one = norm_one_back(grad_normed)
    grad_branch_low = grad_one.astype(jnp.bfloat16)
    bias_out_grad = jnp.sum(grad_branch_low.astype(jnp.float32), axis=0)
    grad_mixed_low = (
        through(grad_branch_low, w_out).astype(jnp.bfloat16).reshape(slots, piece, width)
    )
    queries_slots = queries.reshape(slots, piece, width)
    grad_query, row_sums, grad_key, grad_value = run_slots(
        partial(query_back, with_keys=True),
        (queries_slots, keys_all, values_all, key_live, log_total, grad_mixed_low),
    )
    grad_key, grad_value = (
        lax.psum_scatter(
            grad_key.astype(jnp.bfloat16), "ctx", scatter_dimension=1, tiled=True
        ).astype(jnp.float32),
        lax.psum_scatter(
            grad_value.astype(jnp.bfloat16), "ctx", scatter_dimension=1, tiled=True
        ).astype(jnp.float32),
    )
    rows = slots * piece
    grad_query_low = grad_query.reshape(rows, width).astype(jnp.bfloat16) * jnp.bfloat16(0.125)
    grad_key_low = grad_key.reshape(rows, width).astype(jnp.bfloat16)
    grad_value_low = grad_value.reshape(rows, width).astype(jnp.bfloat16)
    grad_joined = jnp.concatenate([grad_query_low, grad_key_low, grad_value_low], axis=1)
    bias_q_grad = jnp.sum(grad_query_low.astype(jnp.float32), axis=0)
    bias_v_grad = jnp.sum(grad_value_low.astype(jnp.float32), axis=0)
    tokens_grad = (
        (grad_one + through(grad_joined, w_qkv)).reshape(slots, piece, width).astype(jnp.bfloat16)
    )
    vector_grad = jnp.concatenate(
        [
            bias_q_grad[None],
            bias_v_grad[None],
            bias_out_grad[None],
            bias_in_grad.reshape(FF // D, D),
            bias_fc2_grad[None],
            grad_gain_one[None],
            grad_shift_one[None],
            grad_gain_two[None],
            grad_shift_two[None],
        ],
        axis=0,
    )
    count = lax.axis_size(("dp", "ctx"))
    vector_rows = vector_grad.reshape(count, -1)
    pairs = (
        (flat_tokens, grad_joined),
        (mixed_low, grad_branch_low),
        (normed_low, grad_pre_low),
        (hidden_low, grad_fc2_low),
    )
    blocks = [
        shard_piece(left, right, 1 * lax.axis_size(("dp", "ctx")), count) for left, right in pairs
    ]
    blocks.append(vector_rows)
    grad_rows = lax.psum_scatter(
        jnp.concatenate(blocks, axis=1), ("dp", "ctx"), scatter_dimension=0, tiled=True
    )
    index = lax.axis_index(("dp", "ctx"))
    params = jnp.concatenate(
        [
            lax.dynamic_slice_in_dim(weight.reshape(count, -1), index, 1, 0).astype(jnp.float32)
            for weight in (w_qkv, w_out, w_in, w_fc2, vectors)
        ],
        axis=1,
    )
    new_one = beta_one * moment_one + (1.0 - beta_one) * grad_rows
    new_two = beta_two * moment_two + (1.0 - beta_two) * grad_rows * grad_rows
    fix_one = 1.0 - beta_one**step_count
    fix_two = 1.0 - beta_two**step_count
    update = new_one / fix_one / (jnp.sqrt(new_two / fix_two) + adam_eps)
    new_params = params - learn_rate * (update + decay_rate * params)
    return (out, tokens_grad, grad_rows, new_params, new_one, new_two)


BF16 = jnp.bfloat16
F32 = jnp.float32


def layer_norm_stats(values):
    center = values - jnp.mean(values, axis=-1, keepdims=True)
    spread = jnp.mean(center * center, axis=-1, keepdims=True)
    return center, lax.rsqrt(spread + EPSILON)


def layer_norm_back(center, scale, gain, cotangent):
    scaled = cotangent * gain
    mean_scaled = jnp.mean(scaled, axis=-1, keepdims=True)
    mean_cross = jnp.mean(scaled * center, axis=-1, keepdims=True)
    return scale * (scaled - mean_scaled - center * (scale * scale) * mean_cross)


def normal_cdf(values):
    return 0.5 * (1.0 + lax.erf(values * 0.7071067811865476))


def dot(left, right):
    return jnp.dot(left, right, preferred_element_type=F32)


def positions(axis, shape, slot, piece):
    place = lax.broadcasted_iota(jnp.int32, shape, axis)
    block = lax.div(place, piece)
    half = lax.div(block, 2)
    step = lax.rem(block, 2)
    return (2 * half + lax.rem(slot + step, 2)) * piece + lax.rem(place, piece)


def head_probs(queries, keys, live):
    scores = through(queries, keys)
    scores = jnp.where(live, scores, -1e30)
    expo = jnp.exp(scores - jnp.max(scores, axis=-1, keepdims=True))
    return expo / jnp.sum(expo, axis=-1, keepdims=True)


MESH = pl.DeviceIdType.MESH


class Links:
    def __init__(self, sends, recvs):
        self.sends, self.recvs = sends, recvs
        self.used = 0
        self.open = []

    def copy(self, source, target, device):
        self.used += 1
        return self.again(source, target, device)

    def again(self, source, target, device):
        number = self.used - 1
        return pltpu.make_async_remote_copy(
            src_ref=source,
            dst_ref=target,
            send_sem=self.sends.at[number],
            recv_sem=self.recvs.at[number],
            device_id=device,
            device_id_type=MESH,
        )

    def send(self, source, target, device):
        made = self.copy(source, target, device)
        made.start()
        self.open.append((made, None))
        return made

    def send_if(self, condition, source, target, device):
        made = self.copy(source, target, device)
        pl.when(condition)(made.start)
        self.open.append((made, condition))
        return made

    def send_or_keep(self, here, source, target, device):
        number = self.used
        made = self.copy(source, target, device)
        local = pltpu.make_async_copy(source, target, self.recvs.at[number])
        pl.when(here)(local.start)
        away = jnp.logical_not(here)
        pl.when(away)(made.start)
        self.open.append((made, away))

        def wait():
            pl.when(here)(local.wait)
            pl.when(away)(made.wait_recv)

        return wait

    def close(self):
        for made, condition in self.open:
            if condition is None:
                made.wait_send()
            else:
                pl.when(condition)(made.wait_send)


def flip(value, mask):
    result = value
    bit = 1
    while bit <= mask:
        if mask & bit:
            result = result + bit * (1 - 2 * lax.rem(lax.div(value, bit), 2))
        bit *= 2
    return result


def flip_traced(value, mask, size):
    result = value
    bit = 1
    while bit < size:
        set_bit = lax.rem(lax.div(mask, bit), 2)
        result = result + bit * set_bit * (1 - 2 * lax.rem(lax.div(value, bit), 2))
        bit *= 2
    return result


def at_rows(start, size):
    return pl.ds(pl.multiple_of(start, 64), size)


def slot_kernel(devices, depth, features, *refs):
    (
        tokens, out_grad, lengths, vec, w_qkv, w_out, w_in, w_fc2,
        out_ref, tgrad_ref, g_qkv, g_out, g_in, g_fc2, g_vec,
        wqkv, wo, w_up, w_down,
        x_all, n_all, g_all, b_all, j_all, j_send, g_rows, lens_peer,
        qkv, mixed, part, part_a, part_b, part_c, part_d, summed, grad_two, grad_one,
        pre_s, hid, hid_all, gp_all, packed, right, left, packed_two, right_two, left_two,
        trade_in, got_in, trade_qkv, got_qkv, vec_s, vec_by, sums, dqkv, out_half, out_got, tg_half, tg_got, lens,
        local_sems, sends, recvs,
    ) = refs
    chips = devices // 2
    me, slot = lax.axis_index("dp"), lax.axis_index("ctx")
    core, chip = lax.rem(me, 2), lax.div(me, 2)
    base = me - core
    peer = (base + 1 - core, slot)
    piece = tokens.shape[1]
    half = 2 * piece
    rows = 2 * half
    block = D // devices
    wide = features // devices
    lines = D // (devices * depth)
    net = Links(sends, recvs)
    mine_at = at_rows(core * half, half)
    other_at = at_rows((1 - core) * half, half)
    chunk = 32

    row_of = lax.broadcasted_iota(jnp.int32, lens.shape, 0)
    lens[...] = jnp.where(row_of == 0, lengths[0], lengths[1])
    vec_s[...] = jnp.zeros_like(vec_s)
    loads = []

    def load(source, target):
        made = pltpu.make_async_copy(source, target, local_sems.at[len(loads)])
        made.start()
        loads.append(made)

    where = [2 * flip(chip, mask) + core for mask in range(chips)]
    for mask in range(chips):
        for kind in range(3):
            start = pl.multiple_of(kind * D + where[mask] * block, block)
            load(
                w_qkv.at[:, pl.ds(start, block)],
                wqkv.at[:, (3 * mask + kind) * block : (3 * mask + kind + 1) * block],
            )
    n_qkv = len(loads)
    for mask in range(chips):
        start = pl.multiple_of(where[mask] * block, block)
        load(w_out.at[pl.ds(start, block), :], wo.at[mask * block : (mask + 1) * block, :])
    n_out = len(loads)
    for mask in range(chips):
        start = pl.multiple_of(where[mask] * wide, wide)
        load(w_in.at[:, pl.ds(start, wide)], w_up.at[:, mask * wide : (mask + 1) * wide])
    n_up = len(loads)
    for mask in range(chips):
        start = pl.multiple_of(where[mask] * wide, wide)
        load(w_fc2.at[pl.ds(start, wide), :], w_down.at[mask * wide : (mask + 1) * wide, :])

    barrier = pltpu.get_barrier_semaphore()
    friends = [(flip(me, mask), slot) for mask in range(1, devices)]
    for shift in range(1, depth):
        far = lax.rem(slot + shift, depth)
        friends += [(me, far), (flip(me, 1), far)]
    for friend in friends:
        pl.semaphore_signal(barrier, inc=1, device_id=friend, device_id_type=MESH)
    pl.semaphore_wait(barrier, len(friends))

    def spread(source, target):
        waits = []
        for step in range(2):
            pick = lax.rem(slot + step, 2)
            upper = lax.div(slot, 2)
            place = 2 * core + pick
            here = jnp.logical_and(upper == core, place == slot)
            waits.append(
                net.send_or_keep(
                    here,
                    source.at[pick],
                    target.at[at_rows((2 * upper + step) * piece, piece)],
                    (base + upper, place),
                )
            )
        return waits

    def pass_on(waits, target):
        made = []
        for step, wait in enumerate(waits):
            wait()
            spot = target.at[at_rows((2 * core + step) * piece, piece)]
            made.append(net.send(spot, spot, peer))
        return made

    token_waits = spread(tokens, x_all)
    grad_waits = spread(out_grad, g_rows)
    lens_copy = net.send(lens, lens_peer, peer)
    token_passes = pass_on(token_waits, x_all)

    def plane_start(target):
        source = target.at[mine_at]
        return [
            net.send(
                source, target.at[at_rows(mask * rows + core * half, half)], (flip(me, 2 * mask), slot)
            )
            for mask in range(1, chips)
        ]

    def plane_pass(copies, target):
        made = []
        for mask, copy in enumerate(copies, 1):
            copy.wait_recv()
            spot = target.at[at_rows(mask * rows + core * half, half)]
            made.append(net.send(spot, spot, peer))
        return made

    x_plane = plane_start(x_all)
    for made in loads[:n_qkv]:
        made.wait()
    lens_copy.wait_recv()
    for made in token_passes:
        made.wait_recv()
    owned = jnp.where(lax.div(slot, 2) == core, lens[...], lens_peer[...])
    length = jnp.where(lax.rem(slot, 2) == 0, owned[0:1, 0:1], owned[1:2, 0:1])
    live = positions(1, (1, rows), slot, piece) < length
    lane = lax.broadcasted_iota(jnp.int32, (1, block), 1)

    @pl.loop(0, chips)
    def _(mask):
        spot = 2 * flip_traced(chip, mask, chips) + core
        lanes = pl.ds(pl.multiple_of(spot * block, block), block)
        joined = dot(x_all[0:rows, :], wqkv[:, pl.ds(pl.multiple_of(mask * 3 * block, block), 3 * block)])
        queries = ((joined[:, 0:block] + vec[0:1, lanes]) * 0.125).astype(BF16)
        keys = joined[:, block : 2 * block].astype(BF16)
        values = (joined[:, 2 * block :] + vec[1:2, lanes]).astype(BF16)
        total = jnp.zeros((rows, block), F32)
        for head in range(block // HD):
            mine = lax.div(lane, HD) == head
            probs = head_probs(jnp.where(mine, queries, jnp.zeros_like(queries)), keys, live)
            total = jnp.where(mine, dot(probs.astype(BF16), values), total)
        start = pl.multiple_of(mask * 3 * block, block)
        qkv[:, pl.ds(start, block)] = queries
        qkv[:, pl.ds(pl.multiple_of(start + block, block), block)] = keys
        qkv[:, pl.ds(pl.multiple_of(start + 2 * block, block), block)] = values
        mixed[:, pl.ds(pl.multiple_of(mask * block, block), block)] = total.astype(BF16)

    for made in loads[n_qkv:n_out]:
        made.wait()

    def exchange(compute, target, before):
        made = []
        for number, at in enumerate((other_at, mine_at)):
            if before is not None:
                before[number].wait_send()
            part[at, :] = compute(at)
            made.append(net.copy(part.at[at], target.at[at], peer))
            made[-1].start()
        return made

    first = exchange(lambda at: dot(mixed[at, :], wo[...]), part_a, None)
    grad_passes = pass_on(grad_waits, g_rows)

    def norm_one(start):
        @pl.loop(0, half // chunk)
        def _(step):
            at = pl.ds(pl.multiple_of(start + step * chunk, chunk), chunk)
            total = x_all[at, :].astype(F32) + (part[at, :] + part_a[at, :]) + vec[2:3, :]
            center, scale = layer_norm_stats(total)
            summed[at, :] = total
            n_all[at, :] = (center * scale * vec[8:9, :] + vec[9:10, :]).astype(BF16)

    first[0].wait_recv()
    norm_one(core * half)
    n_plane = plane_start(n_all)
    first[1].wait_recv()
    norm_one((1 - core) * half)
    for made in loads[n_out:]:
        made.wait()

    def bias_of(mask):
        spot = flip_traced(chip, mask, chips)
        lanes = pl.ds(pl.multiple_of(core * wide, wide), wide)
        result = vec[3:4, lanes]
        for row in range(1, chips):
            result = jnp.where(spot == row, vec[3 + row : 4 + row, lanes], result)
        return result

    @pl.loop(0, chips)
    def _(mask):
        at = pl.ds(pl.multiple_of(mask * wide, wide), wide)
        value = dot(n_all[0:rows, :], w_up[:, at]) + bias_of(mask)
        pre_s[:, at] = value
        hid[:, at] = (value * normal_cdf(value)).astype(BF16)

    second = exchange(lambda at: dot(hid[at, :], w_down[...]), part_b, first)
    for made in grad_passes:
        made.wait_recv()

    def norm_two(start, own):
        @pl.loop(0, half // chunk)
        def _(step):
            begin = pl.multiple_of(start + step * chunk, chunk)
            at = pl.ds(begin, chunk)
            center, scale = layer_norm_stats(summed[at, :])
            normed = center * scale * vec[8:9, :] + vec[9:10, :]
            center, scale = layer_norm_stats(normed + (part[at, :] + part_b[at, :]) + vec[7:8, :])
            place = begin + lax.broadcasted_iota(jnp.int32, (chunk, 1), 0)
            piece_of = lax.div(place, piece)
            spot = 2 * lax.div(piece_of, 2) + lax.rem(slot + lax.rem(piece_of, 2), 2)
            valid = (spot * piece + lax.rem(place, piece) < length).astype(F32)
            unit = center * scale
            error = g_rows[at, :].astype(F32) * valid
            grad = layer_norm_back(center, scale, vec[10:11, :], error)
            grad_two[at, :] = grad
            low = grad.astype(BF16)
            g_all[at, :] = low
            if own:
                out_half[pl.ds(pl.multiple_of(step * chunk, chunk), chunk), :] = (
                    valid * (unit * vec[10:11, :] + vec[11:12, :])
                ).astype(BF16)
                vec_s[7:8, :] += jnp.sum(low.astype(F32), axis=0, keepdims=True)
                vec_s[10:11, :] += jnp.sum(error * unit, axis=0, keepdims=True)
                vec_s[11:12, :] += jnp.sum(error, axis=0, keepdims=True)

    def go_back(source, target):
        waits = []
        for step in range(2):
            place = 2 * core + lax.rem(slot + step, 2)
            upper = lax.div(slot, 2)
            here = jnp.logical_and(upper == core, place == slot)
            waits.append(
                net.send_or_keep(
                    here,
                    source.at[step * piece : (step + 1) * piece],
                    target.at[lax.rem(slot, 2)],
                    (base + upper, place),
                )
            )
        return waits

    second[0].wait_recv()
    norm_two(core * half, True)
    g_plane = plane_start(g_all)
    second[1].wait_recv()
    norm_two((1 - core) * half, False)
    out_waits = go_back(out_half, out_got)
    n_pass = plane_pass(n_plane, n_all)
    x_pass = plane_pass(x_plane, x_all)

    def slope_of(value, cdf):
        return cdf + value * (jnp.exp(-0.5 * value * value) * 0.3989422804014327)

    @pl.loop(0, chips)
    def _(mask):
        at = pl.ds(pl.multiple_of(mask * wide, wide), wide)
        value = pre_s[:, at]
        grad = through(g_all[0:rows, :], w_down[at, :])
        hid[:, at] = (grad * slope_of(value, normal_cdf(value))).astype(BF16)

    third = exchange(lambda at: through(hid[at, :], w_up[...]), part_c, second)

    def norm_one_back(start, own):
        @pl.loop(0, half // chunk)
        def _(step):
            at = pl.ds(pl.multiple_of(start + step * chunk, chunk), chunk)
            center, scale = layer_norm_stats(summed[at, :])
            error = grad_two[at, :] + (part[at, :] + part_c[at, :])
            grad = layer_norm_back(center, scale, vec[8:9, :], error)
            low = grad.astype(BF16)
            b_all[at, :] = low
            grad_one[at, :] = grad
            if own:
                vec_s[2:3, :] += jnp.sum(low.astype(F32), axis=0, keepdims=True)
                vec_s[8:9, :] += jnp.sum(error * (center * scale), axis=0, keepdims=True)
                vec_s[9:10, :] += jnp.sum(error, axis=0, keepdims=True)

    third[0].wait_recv()
    norm_one_back(core * half, True)
    b_plane = plane_start(b_all)
    third[1].wait_recv()
    norm_one_back((1 - core) * half, False)
    g_pass = plane_pass(g_plane, g_all)

    bias_mine = bias_of(0)

    def feed_rows(mask):
        at = slice(mask * rows, (mask + 1) * rows)
        value = dot(n_all[at, :], w_up[:, 0:wide]) + bias_mine
        cdf = normal_cdf(value)
        hid_all[at, :] = (value * cdf).astype(BF16)
        low = (through(g_all[at, :], w_down[0:wide, :]) * slope_of(value, cdf)).astype(BF16)
        gp_all[at, :] = low
        return jnp.sum(low.astype(F32), axis=0, keepdims=True)

    bias_sum = feed_rows(0)
    for mask in range(1, chips):
        n_pass[mask - 1].wait_recv()
        g_pass[mask - 1].wait_recv()
        bias_sum = bias_sum + feed_rows(mask)
    lanes = pl.ds(pl.multiple_of(core * wide, wide), wide)
    for row in range(chips):
        vec_s[3 + row : 4 + row, lanes] = jnp.where(chip == row, bias_sum, jnp.zeros_like(bias_sum))
    down_rows = wide // depth
    packs = D // wide
    per_pack = devices // packs
    span = lines * depth
    down = inner(hid_all[...], g_all[...]).astype(BF16)
    for number in range(depth):
        packed[number, 0:down_rows, :] = down[number * down_rows : (number + 1) * down_rows, :]
    for group in range(devices):
        up = inner(n_all[:, group * span : (group + 1) * span], gp_all[...]).astype(BF16)
        row = down_rows + (group % per_pack) * lines
        col = (group // per_pack) * wide
        for number in range(depth):
            packed[number, row : row + lines, col : col + wide] = up[
                number * lines : (number + 1) * lines, :
            ]

    class Line:
        def __init__(self, chunks, from_left, from_right):
            self.chunks, self.from_left, self.from_right = chunks, from_left, from_right
            self.up, self.down, self.first_up, self.first_down = [], [], [], []
            after = (me, lax.rem(slot + 1, depth))
            before = (me, lax.rem(slot + depth - 1, depth))
            for order in range(depth - 1):
                top, low = depth - 1 - order, order
                spot = from_left.at[order]
                self.up.append(net.copy(spot, spot, after))
                self.first_up.append(net.again(chunks.at[top], spot, after))
                net.open.append((self.up[-1], slot < top))
                spot = from_right.at[order]
                self.down.append(net.copy(spot, spot, before))
                self.first_down.append(net.again(chunks.at[low], spot, before))
                net.open.append((self.down[-1], slot > low))

        def first(self):
            for order in range(depth - 1):
                pl.when(slot == 0)(self.first_up[order].start)
                pl.when(slot == depth - 1)(self.first_down[order].start)

        def stage(self, time):
            for order in range(time):
                top, low = depth - 1 - order, order

                @pl.when(slot == time - order)
                def _(order=order, top=top):
                    self.up[order].wait_recv()
                    if time < depth - 1:
                        self.from_left[order] = (
                            self.from_left[order].astype(F32) + self.chunks[top].astype(F32)
                        ).astype(BF16)
                        self.up[order].start()

                @pl.when(depth - 1 - slot == time - order)
                def _(order=order, low=low):
                    self.down[order].wait_recv()
                    if time < depth - 1:
                        self.from_right[order] = (
                            self.from_right[order].astype(F32) + self.chunks[low].astype(F32)
                        ).astype(BF16)
                        self.down[order].start()

    feed_line = Line(packed, right, left)
    feed_line.first()

    grad_parts = range(1, chips)

    def attention_back(mask):
        start = mask * 3 * block
        queries = qkv[:, start : start + block]
        keys = qkv[:, start + block : start + 2 * block]
        values = qkv[:, start + 2 * block : start + 3 * block]
        grad_mixed = through(b_all[0:rows, :], wo[mask * block : (mask + 1) * block, :]).astype(BF16)
        grad_q = jnp.zeros((rows, block), F32)
        grad_k = grad_q
        grad_v = grad_q
        for head in range(block // HD):
            mine = lax.div(lane, HD) == head
            probs = head_probs(jnp.where(mine, queries, jnp.zeros_like(queries)), keys, live)
            grad_probs = through(jnp.where(mine, grad_mixed, jnp.zeros_like(grad_mixed)), values)
            dsum = jnp.sum(probs * grad_probs, axis=-1, keepdims=True)
            grad_scores = (probs * (grad_probs - dsum)).astype(BF16)
            grad_q = jnp.where(mine, dot(grad_scores, keys), grad_q)
            grad_k = jnp.where(mine, inner(grad_scores, queries), grad_k)
            grad_v = jnp.where(mine, inner(probs.astype(BF16), grad_mixed), grad_v)
        grad_q = grad_q.astype(BF16) * jnp.bfloat16(0.125)
        grad_k = grad_k.astype(BF16)
        grad_v = grad_v.astype(BF16)
        spot = pl.ds(pl.multiple_of(where[mask] * block, block), block)
        vec_s[0:1, spot] = jnp.sum(grad_q.astype(F32), axis=0, keepdims=True)
        vec_s[1:2, spot] = jnp.sum(grad_v.astype(F32), axis=0, keepdims=True)
        dqkv[:, start : start + block] = grad_q
        dqkv[:, start + block : start + 2 * block] = grad_k
        dqkv[:, start + 2 * block : start + 3 * block] = grad_v
        if mask:
            joint = j_send.at[mask - 1]
        else:
            joint = j_all.at[0:rows]
        joint[:, 0:block] = grad_q
        joint[:, block : 2 * block] = grad_k
        joint[:, 2 * block : 3 * block] = grad_v
        joint[:, 3 * block : 4 * block] = mixed[:, mask * block : (mask + 1) * block]
        if mask:
            return net.send(
                joint, j_all.at[mask * rows : (mask + 1) * rows], (flip(me, 2 * mask), slot)
            )
        return None

    j_copies = [attention_back(mask) for mask in grad_parts]
    attention_back(0)
    b_pass = plane_pass(b_plane, b_all)
    for made in third:
        made.wait_send()
    part[0:half, :] = through(dqkv[other_at, :], wqkv[...])
    tg_copy = net.copy(part.at[0:half], part_d, peer)
    tg_copy.start()
    part[half:rows, :] = grad_one[mine_at, :] + through(dqkv[mine_at, :], wqkv[...])
    tg_copy.wait_recv()
    tg_half[...] = (part[half:rows, :] + part_d[...]).astype(BF16)
    feed_line.stage(1)
    tg_waits = go_back(tg_half, tg_got)

    tiles = vec.shape[0] * D // 128
    share = tiles // (devices * depth)
    vec_by[...] = jnp.zeros_like(vec_by)
    for tile in range(tiles):
        owner, lane_group = tile // share, tile % share
        row, col = tile // (D // 128), (tile % (D // 128)) * 128
        spot = (owner % depth) * 16 + owner // depth
        vec_by[spot : spot + 1, lane_group * 128 : (lane_group + 1) * 128] = vec_s[
            row : row + 1, col : col + 128
        ]
    for number in range(depth):
        packed_two[number, rows : rows + 16, :] = vec_by[number * 16 : (number + 1) * 16, :].astype(BF16)

    for made in b_pass + x_pass + j_copies:
        made.wait_recv()
    across = inner(j_all[:, 3 * block : 4 * block], b_all[...]).astype(BF16)
    for group in range(devices):
        both = inner(x_all[:, group * span : (group + 1) * span], j_all[:, 0 : 3 * block]).astype(BF16)
        row = group * lines
        for number in range(depth):
            at = slice(number * lines, (number + 1) * lines)
            packed_two[number, row : row + lines, 0 : 3 * block] = both[at, :]
            packed_two[number, row : row + lines, 3 * block : 4 * block] = across[
                at, group * block : (group + 1) * block
            ]
    input_line = Line(packed_two, right_two, left_two)
    input_line.first()

    def finish(line, target, rows_at):
        target[...] = line.chunks[slot, rows_at, :].astype(F32)

        @pl.when(slot >= 1)
        def _():
            target[...] += line.from_left[depth - 1 - slot, rows_at, :].astype(F32)

        @pl.when(slot <= depth - 2)
        def _():
            target[...] += line.from_right[slot, rows_at, :].astype(F32)

    for time in range(2, depth):
        feed_line.stage(time)
    finish(feed_line, g_fc2, slice(0, down_rows))
    low_part = part_d.at[0:down_rows]
    finish(feed_line, low_part, slice(down_rows, 2 * down_rows))
    for group in range(devices):
        row = (group % per_pack) * lines
        col = (group // per_pack) * wide
        trade_in[group] = low_part[row : row + lines, col : col + wide].astype(BF16)

    def trade(source, target):
        return [
            net.send(source.at[flip(me, mask)], target.at[me], (flip(me, mask), slot))
            for mask in range(1, devices)
        ]

    in_copies = trade(trade_in, got_in)
    input_line.stage(1)
    for made in in_copies:
        made.wait_recv()
    got_in[me] = trade_in[me]
    for group in range(devices):
        g_in[:, group * wide : (group + 1) * wide] = got_in[group].astype(F32)
    for time in range(2, depth):
        input_line.stage(time)
    tg_copy.wait_send()
    finish(input_line, sums, slice(0, rows + 16))
    first_row = lax.broadcasted_iota(jnp.int32, (16, 3 * block), 0) == 0
    for group in range(devices):
        trade_qkv[group, 0:lines, :] = sums[group * lines : (group + 1) * lines, 0 : 3 * block].astype(BF16)
        trade_qkv[group, lines : lines + 16, :] = jnp.where(
            first_row, sums[rows + group : rows + group + 1, 0 : 3 * block], 0.0
        ).astype(BF16)
        g_out[:, group * block : (group + 1) * block] = sums[
            group * lines : (group + 1) * lines, 3 * block : 4 * block
        ]
    qkv_copies = trade(trade_qkv, got_qkv)
    for wait in out_waits + tg_waits:
        wait()
    out_ref[...] = out_got[...]
    tgrad_ref[...] = tg_got[...]
    for made in qkv_copies:
        made.wait_recv()
    got_qkv[me] = trade_qkv[me]
    vec_sum = jnp.zeros((16, 3 * block), F32)
    for group in range(devices):
        vec_sum = vec_sum + got_qkv[group, lines : lines + 16, :].astype(F32)
        for kind in range(3):
            g_qkv[:, kind * D + group * block : kind * D + (group + 1) * block] = got_qkv[
                group, 0:lines, kind * block : (kind + 1) * block
            ].astype(F32)
    g_vec[...] = vec_sum[0:8, :]
    net.close()


def adam_kernel(count, *refs):
    (
        g_qkv, g_out, g_in, g_fc2, g_vec, vec, out_in, tgrad_in, w_qkv, w_out, w_in, w_fc2, m_one, m_two,
        out_ref, tgrad_ref, rows_out, params_out, one_out, two_out,
        grads, params, one, two, b_qkv, b_out, b_in, b_fc2, vec_flat, in_sems, w_sems, out_sems,
    ) = refs
    index = lax.axis_index("dp") * lax.axis_size("ctx") + lax.axis_index("ctx")
    size = m_one.shape[1] // 128
    parts = in_sems.shape[1]
    step = grads.shape[0] // parts
    spans = [(number * step, min((number + 1) * step, size) - number * step) for number in range(parts)]
    loads = []
    for number, (start, length) in enumerate(spans):
        pair = []
        for kind, (source, target) in enumerate(((m_one, one), (m_two, two))):
            pair.append(
                pltpu.make_async_copy(
                    source.reshape(size, 128).at[start : start + length],
                    target.at[start : start + length],
                    in_sems.at[kind, number],
                )
            )
            pair[-1].start()
        loads.append(pair)
    weights = []
    for number, (source, target) in enumerate(
        ((w_qkv, b_qkv), (w_out, b_out), (w_in, b_in), (w_fc2, b_fc2))
    ):
        lines = target.shape[0]
        start = pl.multiple_of(index * lines, lines)
        weights.append(
            pltpu.make_async_copy(source.at[pl.ds(start, lines), :], target, w_sems.at[number])
        )
        weights[-1].start()
    out_ref[...] = out_in[...]
    tgrad_ref[...] = tgrad_in[...]

    def flatten(source, target, base):
        lines, groups = source.shape[0], source.shape[1] // 128
        for col in range(groups):
            value = source[:, col * 128 : (col + 1) * 128].astype(F32)
            for row in range(0, lines, 8):
                target[pl.ds(base + row * groups + col, 8, stride=groups), :] = value[row : row + 8, :]

    base = 0
    for grad in (g_qkv, g_out, g_in, g_fc2):
        flatten(grad, grads, base)
        base += grad.shape[0] * grad.shape[1] // 128
    share = g_vec.shape[1] // 128
    groups = vec.shape[1] // 128
    for col in range(groups):
        lanes = slice(col * 128, (col + 1) * 128)
        vec_flat[pl.ds(col, 8, stride=groups), :] = vec[0:8, lanes]
        for row in range(8, vec.shape[0]):
            vec_flat[row * groups + col : row * groups + col + 1, :] = vec[row : row + 1, lanes]
    place = lax.broadcasted_iota(jnp.int32, vec_flat.shape, 0)
    for number in range(share):
        grads[base + number : base + number + 1, :] = g_vec[0:1, number * 128 : (number + 1) * 128]
        params[base + number : base + number + 1, :] = jnp.sum(
            jnp.where(place == index * share + number, vec_flat[...], 0.0), axis=0, keepdims=True
        )
    base = 0
    for made, weight in zip(weights, (b_qkv, b_out, b_in, b_fc2)):
        made.wait()
        flatten(weight, params, base)
        base += weight.shape[0] * weight.shape[1] // 128
    fix_one = 1.0 / (1.0 - beta_one**step_count)
    fix_two = 1.0 / (1.0 - beta_two**step_count)
    copies = []
    for number, (start, length) in enumerate(spans):
        for made in loads[number]:
            made.wait()

        @pl.loop(0, step // 56)
        def _(chunk, start=start):
            at = pl.ds(pl.multiple_of(start + chunk * 56, 8), 56)
            grad, param = grads[at, :], params[at, :]
            new_one = beta_one * one[at, :] + (1.0 - beta_one) * grad
            new_two = beta_two * two[at, :] + (1.0 - beta_two) * grad * grad
            one[at, :] = new_one
            two[at, :] = new_two
            change = new_one * fix_one / (jnp.sqrt(new_two * fix_two) + adam_eps)
            params[at, :] = param - learn_rate * (change + decay_rate * param)

        for kind, (source, target) in enumerate(
            ((grads, rows_out), (params, params_out), (one, one_out), (two, two_out))
        ):
            copies.append(
                pltpu.make_async_copy(
                    source.at[start : start + length],
                    target.reshape(size, 128).at[start : start + length],
                    out_sems.at[kind, number],
                )
            )
            copies[-1].start()
    for made in copies:
        made.wait()


def slot_body(tokens, out_grad, lengths, w_qkv, w_out, w_in, w_fc2, vectors, moment_one, moment_two):
    slots, piece, width = tokens.shape
    devices, depth = lax.axis_size("dp"), lax.axis_size("ctx")
    chips = devices // 2
    count = devices * depth
    features = w_in.shape[1]
    half = 2 * piece
    rows = 2 * half
    block = D // devices
    wide = features // devices
    lines = D // count
    total = rows * chips
    low = lambda *shape: pltpu.VMEM(shape, BF16)
    wide_f32 = lambda *shape: pltpu.VMEM(shape, F32)
    anywhere = pl.BlockSpec(memory_space=pl.ANY)
    inside = pl.BlockSpec(memory_space=pltpu.VMEM)
    copies = 96
    out, tokens_grad, grad_qkv, grad_out_w, grad_in, grad_fc2, vector_grad = pl.pallas_call(
        partial(slot_kernel, devices, depth, features),
        out_shape=(
            jax.ShapeDtypeStruct(tokens.shape, BF16),
            jax.ShapeDtypeStruct(tokens.shape, BF16),
            jax.ShapeDtypeStruct((lines, 3 * D), F32),
            jax.ShapeDtypeStruct((lines, D), F32),
            jax.ShapeDtypeStruct((lines, features), F32),
            jax.ShapeDtypeStruct((features // count, D), F32),
            jax.ShapeDtypeStruct((8, 3 * block), F32),
        ),
        in_specs=[anywhere, anywhere, pl.BlockSpec(memory_space=pltpu.SMEM), inside] + [anywhere] * 4,
        out_specs=(inside,) * 7,
        scratch_shapes=[
            low(D, 3 * D // 2),
            low(D // 2, D),
            low(D, features // 2),
            low(features // 2, D),
            low(total, D),
            low(total, D),
            low(total, D),
            low(total, D),
            low(total, 4 * block),
            low(chips - 1, rows, 4 * block),
            low(rows, D),
            pltpu.VMEM((slots, 128), jnp.int32),
            low(rows, 3 * D // 2),
            low(rows, D // 2),
            wide_f32(rows, D),
            wide_f32(rows, D),
            wide_f32(rows, D),
            wide_f32(rows, D),
            wide_f32(half, D),
            wide_f32(rows, D),
            wide_f32(rows, D),
            wide_f32(rows, D),
            wide_f32(rows, features // 2),
            low(rows, features // 2),
            low(total, wide),
            low(total, wide),
            low(depth, 2 * wide // depth, D),
            low(depth - 1, 2 * wide // depth, D),
            low(depth - 1, 2 * wide // depth, D),
            low(depth, devices * lines + 16, 4 * block),
            low(depth - 1, devices * lines + 16, 4 * block),
            low(depth - 1, devices * lines + 16, 4 * block),
            low(devices, lines, wide),
            low(devices, lines, wide),
            low(devices, lines + 16, 3 * block),
            low(devices, lines + 16, 3 * block),
            wide_f32(16, D),
            wide_f32(16 * depth, 4 * block),
            wide_f32(rows + 16, 4 * block),
            low(rows, 3 * D // 2),
            low(half, D),
            low(*tokens.shape),
            low(half, D),
            low(*tokens.shape),
            pltpu.VMEM((slots, 128), jnp.int32),
            pltpu.SemaphoreType.DMA((6 * chips,)),
            pltpu.SemaphoreType.DMA((copies,)),
            pltpu.SemaphoreType.DMA((copies,)),
        ],
        compiler_params=pltpu.CompilerParams(
            collective_id=0, has_side_effects=True, vmem_limit_bytes=64 * 1024 * 1024 - 64 * 1024
        ),
        name="slot",
    )(tokens, out_grad, lengths, vectors, w_qkv, w_out, w_in, w_fc2)
    size = moment_one.shape[1] // 128
    padded = (size + 279) // 280 * 280
    flat = jax.ShapeDtypeStruct(moment_one.shape, F32)
    return pl.pallas_call(
        partial(adam_kernel, count),
        out_shape=(
            jax.ShapeDtypeStruct(tokens.shape, BF16),
            jax.ShapeDtypeStruct(tokens.shape, BF16),
            flat,
            flat,
            flat,
            flat,
        ),
        in_specs=[inside] * 8 + [anywhere] * 6,
        out_specs=(inside, inside) + (anywhere,) * 4,
        scratch_shapes=[wide_f32(padded, 128)] * 4
        + [
            low(lines, 3 * D),
            low(lines, D),
            low(lines, features),
            low(features // count, D),
            wide_f32(vectors.shape[0] * D // 128, 128),
            pltpu.SemaphoreType.DMA((2, 5)),
            pltpu.SemaphoreType.DMA((4,)),
            pltpu.SemaphoreType.DMA((4, 5)),
        ],
        compiler_params=pltpu.CompilerParams(vmem_limit_bytes=64 * 1024 * 1024 - 64 * 1024),
        name="adam",
    )(
        grad_qkv, grad_out_w, grad_in, grad_fc2, vector_grad, vectors, out, tokens_grad,
        w_qkv, w_out, w_in, w_fc2, moment_one, moment_two,
    )


def layer(tokens, *rest):
    slots, piece, width = tokens.shape
    devices, depth = lax.axis_size("dp"), lax.axis_size("ctx")
    fits = slots == 2 and depth == 2 * slots and devices % 2 == 0
    if fits and (H * HD // devices) % 128 == 0 and (FF // devices) % 128 == 0:
        return slot_body(tokens, *rest)
    return body(tokens, *rest)


def solution(mesh):
    placed = (
        P("dp", "ctx", None),
        P("dp", "ctx", None),
        P("dp"),
        P(),
        P(),
        P(),
        P(),
        P(),
        P(("dp", "ctx"), None),
        P(("dp", "ctx"), None),
    )
    return jax.shard_map(
        layer,
        mesh=mesh,
        in_specs=placed,
        out_specs=(
            P("dp", "ctx", None),
            P("dp", "ctx", None),
            P(("dp", "ctx"), None),
            P(("dp", "ctx"), None),
            P(("dp", "ctx"), None),
            P(("dp", "ctx"), None),
        ),
        check_vma=False,
    )
```

```python
from functools import partial

import jax
import jax.numpy as jnp
from jax import lax
from jax.experimental import pallas as pl
from jax.experimental.pallas import tpu as pltpu
from jax.sharding import PartitionSpec as P

D = 1024
H = 16
HD = 64
FF = 4096


EPSILON = 1e-05
learn_rate = 0.01
beta_one = 0.9
beta_two = 0.999
adam_eps = 1e-08
decay_rate = 0.01
step_count = 10.0


def layer_norm(values, gain, shift):
    center = values - jnp.mean(values, axis=-1, keepdims=True)
    spread = jnp.mean(center * center, axis=-1, keepdims=True)
    return center * lax.rsqrt(spread + EPSILON) * gain + shift


def split_vectors(vectors):
    ratio = FF // D
    return (
        vectors[0],
        vectors[1],
        vectors[2],
        vectors[3 : 3 + ratio].reshape(FF),
        vectors[3 + ratio],
        vectors[4 + ratio],
        vectors[5 + ratio],
        vectors[6 + ratio],
        vectors[7 + ratio],
    )


def inner(left, right):
    return lax.dot_general(
        left, right, (((0,), (0,)), ((), ())), preferred_element_type=jnp.float32
    )


def through(left, weight):
    return lax.dot_general(
        left, weight, (((1,), (1,)), ((), ())), preferred_element_type=jnp.float32
    )


def run_slots(function, items):
    return lax.map(lambda item: function(*item), items)


def heads_block():
    return 4


def split_heads(matrix):
    count = matrix.shape[0]
    group = heads_block()
    return jnp.moveaxis(matrix.reshape(count, H // group, group, HD), 1, 0)


def join_heads(blocked):
    return jnp.moveaxis(blocked, 0, 1).reshape(blocked.shape[1], H * HD)


def split_stats(stats):
    group = heads_block()
    return stats.reshape(H // group, group, stats.shape[-1])


def shard_piece(left, right, number, shard_count):
    weight_rows = left.shape[1]
    columns = right.shape[1]
    per_shard = weight_rows * columns // shard_count
    block = inner(left, right).reshape(-1)
    return block.reshape(number, per_shard)


def project(flat_tokens, w_qkv, vectors):
    joined = jnp.dot(flat_tokens, w_qkv, preferred_element_type=jnp.float32)
    queries = ((joined[:, :D] + vectors[0]) * 0.125).astype(jnp.bfloat16)
    keys = joined[:, D : 2 * D].astype(jnp.bfloat16)
    values = (joined[:, 2 * D :] + vectors[1]).astype(jnp.bfloat16)
    return (queries, keys, values)


def attend_slot(queries, keys, values, live):
    rows = queries.shape[0]

    def attend_one_block(item):
        query_heads, key_heads, value_heads = item
        scores = jnp.einsum(
            "qhd,khd->hqk", query_heads, key_heads, preferred_element_type=jnp.float32
        )
        scores = jnp.where(live[None, None, :], scores, -1e30)
        maximum = jnp.max(scores, axis=-1, keepdims=True)
        expo = jnp.exp(scores - maximum)
        total = jnp.sum(expo, axis=-1, keepdims=True)
        probs_low = (expo / total).astype(jnp.bfloat16)
        mixed = jnp.einsum(
            "hqk,khd->qhd", probs_low, value_heads, preferred_element_type=jnp.float32
        )
        return (mixed, (maximum + jnp.log(total))[..., 0])

    mixed, log_total = lax.map(
        attend_one_block, (split_heads(queries), split_heads(keys), split_heads(values))
    )
    return (join_heads(mixed), log_total.reshape(H, rows))


def query_back(queries, keys, values, live, log_total, grad_mixed, with_keys):
    rows = queries.shape[0]

    def query_one_block(item):
        query_heads, key_heads, value_heads, grad_heads, block_log = item
        scores = jnp.einsum(
            "qhd,khd->hqk", query_heads, key_heads, preferred_element_type=jnp.float32
        )
        scores = jnp.where(live[None, None, :], scores, -1e30)
        probs = jnp.exp(scores - block_log[:, :, None])
        grad_probs = jnp.einsum(
            "qhd,khd->hqk", grad_heads, value_heads, preferred_element_type=jnp.float32
        )
        row_sums = jnp.sum(probs * grad_probs, axis=-1)
        grad_scores = (probs * (grad_probs - row_sums[:, :, None])).astype(jnp.bfloat16)
        grad_query = jnp.einsum(
            "hqk,khd->qhd", grad_scores, key_heads, preferred_element_type=jnp.float32
        )
        grad_key = jnp.einsum(
            "hqk,qhd->khd", grad_scores, query_heads, preferred_element_type=jnp.float32
        )
        grad_value = jnp.einsum(
            "hqk,qhd->khd",
            probs.astype(jnp.bfloat16),
            grad_heads,
            preferred_element_type=jnp.float32,
        )
        return (grad_query, row_sums, grad_key, grad_value)

    items = (
        split_heads(queries),
        split_heads(keys),
        split_heads(values),
        split_heads(grad_mixed),
        split_stats(log_total),
    )
    results = lax.map(query_one_block, items)
    grad_query, row_sums, grad_key, grad_value = results
    return (
        join_heads(grad_query),
        row_sums.reshape(H, rows),
        join_heads(grad_key),
        join_heads(grad_value),
    )


def tail(flat_tokens, mixed, w_out, w_in, w_fc2, vectors):
    bias_q, bias_v, bias_o, bias_in, bias_fc2, gain_one, shift_one, gain_two, shift_two = (
        split_vectors(vectors)
    )
    mixed_low = mixed.astype(jnp.bfloat16)
    summed_one = (
        flat_tokens.astype(jnp.float32)
        + jnp.dot(mixed_low, w_out, preferred_element_type=jnp.float32)
        + bias_o
    )
    normed = layer_norm(summed_one, gain_one, shift_one)
    normed_low = normed.astype(jnp.bfloat16)
    hidden_pre = jnp.dot(normed_low, w_in, preferred_element_type=jnp.float32) + bias_in
    hidden_low = jax.nn.gelu(hidden_pre, approximate=False).astype(jnp.bfloat16)
    summed_two = normed + jnp.dot(hidden_low, w_fc2, preferred_element_type=jnp.float32) + bias_fc2
    result = layer_norm(summed_two, gain_two, shift_two)
    return (mixed_low, summed_one, normed_low, hidden_pre, hidden_low, summed_two, result)


def body(tokens, out_grad, lengths, w_qkv, w_out, w_in, w_fc2, vectors, moment_one, moment_two):
    slots, piece, width = tokens.shape
    length = piece * lax.axis_size("ctx")
    local_pos = lax.axis_index("ctx") * piece + jnp.arange(piece, dtype=jnp.int32)
    own_live = local_pos[None, :] < lengths[:, None]
    valid = own_live.astype(jnp.float32)
    key_live = jnp.arange(length, dtype=jnp.int32)[None, :] < lengths[:, None]
    bias_q, bias_v, bias_o, bias_in, bias_fc2, gain_one, shift_one, gain_two, shift_two = (
        split_vectors(vectors)
    )
    flat_tokens = tokens.reshape(slots * piece, width)
    queries, keys, values = project(flat_tokens, w_qkv, vectors)
    keys_all, values_all = (
        lax.all_gather(keys.reshape(slots, piece, width), "ctx", axis=1, tiled=True),
        lax.all_gather(values.reshape(slots, piece, width), "ctx", axis=1, tiled=True),
    )
    mixed, log_total = run_slots(
        attend_slot, (queries.reshape(slots, piece, width), keys_all, values_all, key_live)
    )
    saved = tail(flat_tokens, mixed.reshape(slots * piece, width), w_out, w_in, w_fc2, vectors)
    out = (saved[6].reshape(slots, piece, width) * valid[..., None]).astype(jnp.bfloat16)
    again = lax.optimization_barrier(flat_tokens)
    queries, keys, values = project(again, w_qkv, vectors)
    keys_all, values_all = (
        lax.all_gather(keys.reshape(slots, piece, width), "ctx", axis=1, tiled=True),
        lax.all_gather(values.reshape(slots, piece, width), "ctx", axis=1, tiled=True),
    )
    mixed, log_total = run_slots(
        attend_slot, (queries.reshape(slots, piece, width), keys_all, values_all, key_live)
    )
    saved = tail(again, mixed.reshape(slots * piece, width), w_out, w_in, w_fc2, vectors)
    mixed_low, summed_one, normed_low, hidden_pre, hidden_low, summed_two, result = saved
    cotangent = (out_grad.astype(jnp.float32) * valid[..., None]).reshape(slots * piece, width)
    unused_two, norm_two_back = jax.vjp(layer_norm, summed_two, gain_two, shift_two)
    grad_two, grad_gain_two, grad_shift_two = norm_two_back(cotangent)
    grad_fc2_low = grad_two.astype(jnp.bfloat16)
    bias_fc2_grad = jnp.sum(grad_fc2_low.astype(jnp.float32), axis=0)
    grad_hidden = through(grad_fc2_low, w_fc2)
    unused_gelu, gelu_back = jax.vjp(partial(jax.nn.gelu, approximate=False), hidden_pre)
    grad_pre_low = gelu_back(grad_hidden)[0].astype(jnp.bfloat16)
    bias_in_grad = jnp.sum(grad_pre_low.astype(jnp.float32), axis=0)
    grad_normed = grad_two + through(grad_pre_low, w_in)
    unused_one, norm_one_back = jax.vjp(layer_norm, summed_one, gain_one, shift_one)
    grad_one, grad_gain_one, grad_shift_one = norm_one_back(grad_normed)
    grad_branch_low = grad_one.astype(jnp.bfloat16)
    bias_out_grad = jnp.sum(grad_branch_low.astype(jnp.float32), axis=0)
    grad_mixed_low = (
        through(grad_branch_low, w_out).astype(jnp.bfloat16).reshape(slots, piece, width)
    )
    queries_slots = queries.reshape(slots, piece, width)
    grad_query, row_sums, grad_key, grad_value = run_slots(
        partial(query_back, with_keys=True),
        (queries_slots, keys_all, values_all, key_live, log_total, grad_mixed_low),
    )
    grad_key, grad_value = (
        lax.psum_scatter(
            grad_key.astype(jnp.bfloat16), "ctx", scatter_dimension=1, tiled=True
        ).astype(jnp.float32),
        lax.psum_scatter(
            grad_value.astype(jnp.bfloat16), "ctx", scatter_dimension=1, tiled=True
        ).astype(jnp.float32),
    )
    rows = slots * piece
    grad_query_low = grad_query.reshape(rows, width).astype(jnp.bfloat16) * jnp.bfloat16(0.125)
    grad_key_low = grad_key.reshape(rows, width).astype(jnp.bfloat16)
    grad_value_low = grad_value.reshape(rows, width).astype(jnp.bfloat16)
    grad_joined = jnp.concatenate([grad_query_low, grad_key_low, grad_value_low], axis=1)
    bias_q_grad = jnp.sum(grad_query_low.astype(jnp.float32), axis=0)
    bias_v_grad = jnp.sum(grad_value_low.astype(jnp.float32), axis=0)
    tokens_grad = (
        (grad_one + through(grad_joined, w_qkv)).reshape(slots, piece, width).astype(jnp.bfloat16)
    )
    vector_grad = jnp.concatenate(
        [
            bias_q_grad[None],
            bias_v_grad[None],
            bias_out_grad[None],
            bias_in_grad.reshape(FF // D, D),
            bias_fc2_grad[None],
            grad_gain_one[None],
            grad_shift_one[None],
            grad_gain_two[None],
            grad_shift_two[None],
        ],
        axis=0,
    )
    count = lax.axis_size(("dp", "ctx"))
    vector_rows = vector_grad.reshape(count, -1)
    pairs = (
        (flat_tokens, grad_joined),
        (mixed_low, grad_branch_low),
        (normed_low, grad_pre_low),
        (hidden_low, grad_fc2_low),
    )
    blocks = [
        shard_piece(left, right, 1 * lax.axis_size(("dp", "ctx")), count) for left, right in pairs
    ]
    blocks.append(vector_rows)
    grad_rows = lax.psum_scatter(
        jnp.concatenate(blocks, axis=1), ("dp", "ctx"), scatter_dimension=0, tiled=True
    )
    index = lax.axis_index(("dp", "ctx"))
    params = jnp.concatenate(
        [
            lax.dynamic_slice_in_dim(weight.reshape(count, -1), index, 1, 0).astype(jnp.float32)
            for weight in (w_qkv, w_out, w_in, w_fc2, vectors)
        ],
        axis=1,
    )
    new_one = beta_one * moment_one + (1.0 - beta_one) * grad_rows
    new_two = beta_two * moment_two + (1.0 - beta_two) * grad_rows * grad_rows
    fix_one = 1.0 - beta_one**step_count
    fix_two = 1.0 - beta_two**step_count
    update = new_one / fix_one / (jnp.sqrt(new_two / fix_two) + adam_eps)
    new_params = params - learn_rate * (update + decay_rate * params)
    return (out, tokens_grad, grad_rows, new_params, new_one, new_two)


BF16 = jnp.bfloat16
F32 = jnp.float32


def layer_norm_stats(values):
    center = values - jnp.mean(values, axis=-1, keepdims=True)
    spread = jnp.mean(center * center, axis=-1, keepdims=True)
    return center, lax.rsqrt(spread + EPSILON)


def layer_norm_back(center, scale, gain, cotangent):
    scaled = cotangent * gain
    mean_scaled = jnp.mean(scaled, axis=-1, keepdims=True)
    mean_cross = jnp.mean(scaled * center, axis=-1, keepdims=True)
    return scale * (scaled - mean_scaled - center * (scale * scale) * mean_cross)


def normal_cdf(values):
    return 0.5 * (1.0 + lax.erf(values * 0.7071067811865476))


def dot(left, right):
    return jnp.dot(left, right, preferred_element_type=F32)


def positions(axis, shape, slot, piece):
    place = lax.broadcasted_iota(jnp.int32, shape, axis)
    block = lax.div(place, piece)
    half = lax.div(block, 2)
    step = lax.rem(block, 2)
    return (2 * half + lax.rem(slot + step, 2)) * piece + lax.rem(place, piece)


def head_probs(queries, keys, live):
    scores = through(queries, keys)
    scores = jnp.where(live, scores, -1e30)
    expo = jnp.exp(scores - jnp.max(scores, axis=-1, keepdims=True))
    return expo / jnp.sum(expo, axis=-1, keepdims=True)


MESH = pl.DeviceIdType.MESH


class Links:
    def __init__(self, sends, recvs):
        self.sends, self.recvs = sends, recvs
        self.used = 0
        self.open = []

    def copy(self, source, target, device):
        self.used += 1
        return self.again(source, target, device)

    def again(self, source, target, device):
        number = self.used - 1
        return pltpu.make_async_remote_copy(
            src_ref=source,
            dst_ref=target,
            send_sem=self.sends.at[number],
            recv_sem=self.recvs.at[number],
            device_id=device,
            device_id_type=MESH,
        )

    def forward(self, source, target, device, earlier):
        self.used += 1
        return pltpu.make_async_remote_copy(
            src_ref=source,
            dst_ref=target,
            send_sem=self.sends.at[self.used - 1],
            recv_sem=self.recvs.at[earlier],
            device_id=device,
            device_id_type=MESH,
        )

    def send(self, source, target, device):
        made = self.copy(source, target, device)
        made.start()
        self.open.append((made, None))
        return made

    def send_if(self, condition, source, target, device):
        made = self.copy(source, target, device)
        pl.when(condition)(made.start)
        self.open.append((made, condition))
        return made

    def send_or_keep(self, here, source, target, device):
        number = self.used
        made = self.copy(source, target, device)
        local = pltpu.make_async_copy(source, target, self.recvs.at[number])
        pl.when(here)(local.start)
        away = jnp.logical_not(here)
        pl.when(away)(made.start)
        self.open.append((made, away))

        def wait():
            pl.when(here)(local.wait)
            pl.when(away)(made.wait_recv)

        return wait

    def close(self):
        for made, condition in self.open:
            if condition is None:
                made.wait_send()
            else:
                pl.when(condition)(made.wait_send)


def flip(value, mask):
    result = value
    bit = 1
    while bit <= mask:
        if mask & bit:
            result = result + bit * (1 - 2 * lax.rem(lax.div(value, bit), 2))
        bit *= 2
    return result


def flip_traced(value, mask, size):
    result = value
    bit = 1
    while bit < size:
        set_bit = lax.rem(lax.div(mask, bit), 2)
        result = result + bit * set_bit * (1 - 2 * lax.rem(lax.div(value, bit), 2))
        bit *= 2
    return result


def at_rows(start, size):
    return pl.ds(pl.multiple_of(start, 64), size)


def slot_kernel(devices, depth, features, *refs):
    (
        tokens, out_grad, lengths, vec, w_qkv, w_out, w_in, w_fc2,
        out_ref, tgrad_ref, g_qkv, g_out, g_in, g_fc2, g_vec,
        wqkv, wo, w_up, w_down,
        x_all, n_all, g_all, b_all, j_all, j_send, g_rows, lens_peer,
        qkv, mixed, part, part_a, part_b, part_c, part_d, summed, grad_two, grad_one,
        pre_s, hid, hid_all, gp_all, packed, plane_got, up_mine, down_mine, packed_two, right_two, left_two,
        trade_in, got_in, trade_qkv, got_qkv, vec_s, vec_by, sums, dqkv, out_half, out_got, tg_half, tg_got, lens,
        local_sems, sends, recvs,
    ) = refs
    chips = devices // 2
    me, slot = lax.axis_index("dp"), lax.axis_index("ctx")
    core, chip = lax.rem(me, 2), lax.div(me, 2)
    base = me - core
    peer = (base + 1 - core, slot)
    piece = tokens.shape[1]
    half = 2 * piece
    rows = 2 * half
    block = D // devices
    wide = features // devices
    lines = D // (devices * depth)
    net = Links(sends, recvs)
    mine_at = at_rows(core * half, half)
    other_at = at_rows((1 - core) * half, half)
    chunk = 32

    row_of = lax.broadcasted_iota(jnp.int32, lens.shape, 0)
    lens[...] = jnp.where(row_of == 0, lengths[0], lengths[1])
    vec_s[...] = jnp.zeros_like(vec_s)
    loads = []

    def load(source, target):
        made = pltpu.make_async_copy(source, target, local_sems.at[len(loads)])
        made.start()
        loads.append(made)

    where = [2 * flip(chip, mask) + core for mask in range(chips)]
    for mask in range(chips):
        for kind in range(3):
            start = pl.multiple_of(kind * D + where[mask] * block, block)
            load(
                w_qkv.at[:, pl.ds(start, block)],
                wqkv.at[:, (3 * mask + kind) * block : (3 * mask + kind + 1) * block],
            )
    n_qkv = len(loads)
    for mask in range(chips):
        start = pl.multiple_of(where[mask] * block, block)
        load(w_out.at[pl.ds(start, block), :], wo.at[mask * block : (mask + 1) * block, :])
    n_out = len(loads)
    for mask in range(chips):
        start = pl.multiple_of(where[mask] * wide, wide)
        load(w_in.at[:, pl.ds(start, wide)], w_up.at[:, mask * wide : (mask + 1) * wide])
    n_up = len(loads)
    for mask in range(chips):
        start = pl.multiple_of(where[mask] * wide, wide)
        load(w_fc2.at[pl.ds(start, wide), :], w_down.at[mask * wide : (mask + 1) * wide, :])

    barrier = pltpu.get_barrier_semaphore()
    friends = [(flip(me, mask), slot) for mask in range(1, devices)]
    for shift in range(1, depth):
        far = lax.rem(slot + shift, depth)
        friends += [(me, far), (flip(me, 1), far)]
    for friend in friends:
        pl.semaphore_signal(barrier, inc=1, device_id=friend, device_id_type=MESH)
    pl.semaphore_wait(barrier, len(friends))

    def spread(source, target):
        waits = []
        for step in range(2):
            pick = lax.rem(slot + step, 2)
            upper = lax.div(slot, 2)
            place = 2 * core + pick
            here = jnp.logical_and(upper == core, place == slot)
            waits.append(
                net.send_or_keep(
                    here,
                    source.at[pick],
                    target.at[at_rows((2 * upper + step) * piece, piece)],
                    (base + upper, place),
                )
            )
        return waits

    def pass_on(waits, target):
        made = []
        for step, wait in enumerate(waits):
            wait()
            spot = target.at[at_rows((2 * core + step) * piece, piece)]
            made.append(net.send(spot, spot, peer))
        return made

    token_waits = spread(tokens, x_all)
    grad_waits = spread(out_grad, g_rows)
    lens_copy = net.send(lens, lens_peer, peer)
    token_passes = pass_on(token_waits, x_all)

    def plane_start(target):
        source = target.at[mine_at]
        return [
            net.send(
                source, target.at[at_rows(mask * rows + core * half, half)], (flip(me, 2 * mask), slot)
            )
            for mask in range(1, chips)
        ]

    def plane_pass(copies, target):
        made = []
        for mask, copy in enumerate(copies, 1):
            copy.wait_recv()
            spot = target.at[at_rows(mask * rows + core * half, half)]
            made.append(net.send(spot, spot, peer))
        return made

    class Column:
        def __init__(self, target):
            self.target = target
            self.parts, self.numbers = {}, {}
            for place in (2, 1, 3):
                far = lax.rem(slot + depth - place, depth)
                made = net.copy(target.at[mine_at], self.spot(place), (me, far))
                self.parts[place], self.numbers[place] = made, net.used - 1
                goes = {1: slot != 0, 2: slot >= 0, 3: slot != depth - 1}[place]
                net.open.append((made, goes))
                pl.when(goes)(made.start)
            self.passes = {}

        def spot(self, place):
            return self.target.at[at_rows(place * rows + core * half, half)]

        def relay(self):
            self.parts[2].wait_recv()
            up = net.forward(self.spot(2), self.spot(1), (me, depth - 1), self.numbers[1])
            down = net.forward(self.spot(2), self.spot(3), (me, 0), self.numbers[3])
            for made, here in ((up, slot == 2), (down, slot == 1)):
                pl.when(here)(made.start)
                net.open.append((made, here))
            self.passes[2] = net.send(self.spot(2), self.spot(2), peer)

        def hand_over(self, place):
            self.parts[place].wait_recv()
            self.passes[place] = net.send(self.spot(place), self.spot(place), peer)

    x_plane = plane_start(x_all)
    for made in loads[:n_qkv]:
        made.wait()
    lens_copy.wait_recv()
    for made in token_passes:
        made.wait_recv()
    owned = jnp.where(lax.div(slot, 2) == core, lens[...], lens_peer[...])
    length = jnp.where(lax.rem(slot, 2) == 0, owned[0:1, 0:1], owned[1:2, 0:1])
    live = positions(1, (1, rows), slot, piece) < length
    lane = lax.broadcasted_iota(jnp.int32, (1, block), 1)

    @pl.loop(0, chips)
    def _(mask):
        spot = 2 * flip_traced(chip, mask, chips) + core
        lanes = pl.ds(pl.multiple_of(spot * block, block), block)
        joined = dot(x_all[0:rows, :], wqkv[:, pl.ds(pl.multiple_of(mask * 3 * block, block), 3 * block)])
        queries = ((joined[:, 0:block] + vec[0:1, lanes]) * 0.125).astype(BF16)
        keys = joined[:, block : 2 * block].astype(BF16)
        values = (joined[:, 2 * block :] + vec[1:2, lanes]).astype(BF16)
        total = jnp.zeros((rows, block), F32)
        for head in range(block // HD):
            mine = lax.div(lane, HD) == head
            probs = head_probs(jnp.where(mine, queries, jnp.zeros_like(queries)), keys, live)
            total = jnp.where(mine, dot(probs.astype(BF16), values), total)
        start = pl.multiple_of(mask * 3 * block, block)
        qkv[:, pl.ds(start, block)] = queries
        qkv[:, pl.ds(pl.multiple_of(start + block, block), block)] = keys
        qkv[:, pl.ds(pl.multiple_of(start + 2 * block, block), block)] = values
        mixed[:, pl.ds(pl.multiple_of(mask * block, block), block)] = total.astype(BF16)

    for made in loads[n_qkv:n_out]:
        made.wait()

    def exchange(compute, target, before):
        made = []
        for number, at in enumerate((other_at, mine_at)):
            if before is not None:
                before[number].wait_send()
            part[at, :] = compute(at)
            made.append(net.copy(part.at[at], target.at[at], peer))
            made[-1].start()
        return made

    first = exchange(lambda at: dot(mixed[at, :], wo[...]), part_a, None)
    grad_passes = pass_on(grad_waits, g_rows)

    def norm_one(start):
        @pl.loop(0, half // chunk)
        def _(step):
            at = pl.ds(pl.multiple_of(start + step * chunk, chunk), chunk)
            total = x_all[at, :].astype(F32) + (part[at, :] + part_a[at, :]) + vec[2:3, :]
            center, scale = layer_norm_stats(total)
            summed[at, :] = total
            n_all[at, :] = (center * scale * vec[8:9, :] + vec[9:10, :]).astype(BF16)

    first[0].wait_recv()
    norm_one(core * half)
    n_column = Column(n_all)
    first[1].wait_recv()
    norm_one((1 - core) * half)
    for made in loads[n_out:]:
        made.wait()

    for number in range(chips):
        fine_cols = wide // depth
        begin = flip_traced(chip, number, chips) * wide + slot * fine_cols
        at = pl.ds(pl.multiple_of(begin, fine_cols), fine_cols)
        up_mine[:, number * fine_cols : (number + 1) * fine_cols] = w_up[:, at]
        down_mine[number * fine_cols : (number + 1) * fine_cols, :] = w_down[at, :]

    def bias_of(mask):
        spot = flip_traced(chip, mask, chips)
        lanes = pl.ds(pl.multiple_of(core * wide, wide), wide)
        result = vec[3:4, lanes]
        for row in range(1, chips):
            result = jnp.where(spot == row, vec[3 + row : 4 + row, lanes], result)
        return result

    @pl.loop(0, chips)
    def _(mask):
        at = pl.ds(pl.multiple_of(mask * wide, wide), wide)
        value = dot(n_all[0:rows, :], w_up[:, at]) + bias_of(mask)
        pre_s[:, at] = value
        hid[:, at] = (value * normal_cdf(value)).astype(BF16)

    second = exchange(lambda at: dot(hid[at, :], w_down[...]), part_b, first)
    for made in grad_passes:
        made.wait_recv()

    def norm_two(start, own):
        @pl.loop(0, half // chunk)
        def _(step):
            begin = pl.multiple_of(start + step * chunk, chunk)
            at = pl.ds(begin, chunk)
            center, scale = layer_norm_stats(summed[at, :])
            normed = center * scale * vec[8:9, :] + vec[9:10, :]
            center, scale = layer_norm_stats(normed + (part[at, :] + part_b[at, :]) + vec[7:8, :])
            place = begin + lax.broadcasted_iota(jnp.int32, (chunk, 1), 0)
            piece_of = lax.div(place, piece)
            spot = 2 * lax.div(piece_of, 2) + lax.rem(slot + lax.rem(piece_of, 2), 2)
            valid = (spot * piece + lax.rem(place, piece) < length).astype(F32)
            unit = center * scale
            error = g_rows[at, :].astype(F32) * valid
            grad = layer_norm_back(center, scale, vec[10:11, :], error)
            grad_two[at, :] = grad
            low = grad.astype(BF16)
            g_all[at, :] = low
            if own:
                out_half[pl.ds(pl.multiple_of(step * chunk, chunk), chunk), :] = (
                    valid * (unit * vec[10:11, :] + vec[11:12, :])
                ).astype(BF16)
                vec_s[7:8, :] += jnp.sum(low.astype(F32), axis=0, keepdims=True)
                vec_s[10:11, :] += jnp.sum(error * unit, axis=0, keepdims=True)
                vec_s[11:12, :] += jnp.sum(error, axis=0, keepdims=True)

    def go_back(source, target):
        waits = []
        for step in range(2):
            place = 2 * core + lax.rem(slot + step, 2)
            upper = lax.div(slot, 2)
            here = jnp.logical_and(upper == core, place == slot)
            waits.append(
                net.send_or_keep(
                    here,
                    source.at[step * piece : (step + 1) * piece],
                    target.at[lax.rem(slot, 2)],
                    (base + upper, place),
                )
            )
        return waits

    second[0].wait_recv()
    norm_two(core * half, True)
    g_column = Column(g_all)
    second[1].wait_recv()
    norm_two((1 - core) * half, False)
    n_column.relay()
    x_pass = plane_pass(x_plane, x_all)

    def slope_of(value, cdf):
        return cdf + value * (jnp.exp(-0.5 * value * value) * 0.3989422804014327)

    @pl.loop(0, chips)
    def _(mask):
        at = pl.ds(pl.multiple_of(mask * wide, wide), wide)
        value = pre_s[:, at]
        grad = through(g_all[0:rows, :], w_down[at, :])
        hid[:, at] = (grad * slope_of(value, normal_cdf(value))).astype(BF16)

    third = exchange(lambda at: through(hid[at, :], w_up[...]), part_c, second)

    def norm_one_back(start, own):
        @pl.loop(0, half // chunk)
        def _(step):
            at = pl.ds(pl.multiple_of(start + step * chunk, chunk), chunk)
            center, scale = layer_norm_stats(summed[at, :])
            error = grad_two[at, :] + (part[at, :] + part_c[at, :])
            grad = layer_norm_back(center, scale, vec[8:9, :], error)
            low = grad.astype(BF16)
            b_all[at, :] = low
            grad_one[at, :] = grad
            if own:
                vec_s[2:3, :] += jnp.sum(low.astype(F32), axis=0, keepdims=True)
                vec_s[8:9, :] += jnp.sum(error * (center * scale), axis=0, keepdims=True)
                vec_s[9:10, :] += jnp.sum(error, axis=0, keepdims=True)

    third[0].wait_recv()
    norm_one_back(core * half, True)
    b_plane = plane_start(b_all)
    third[1].wait_recv()
    norm_one_back((1 - core) * half, False)
    n_column.hand_over(1)
    n_column.hand_over(3)

    class Line:
        def __init__(self, chunks, from_left, from_right):
            self.chunks, self.from_left, self.from_right = chunks, from_left, from_right
            self.up, self.down, self.first_up, self.first_down = [], [], [], []
            after = (me, lax.rem(slot + 1, depth))
            before = (me, lax.rem(slot + depth - 1, depth))
            for order in range(depth - 1):
                top, low = depth - 1 - order, order
                spot = from_left.at[order]
                self.up.append(net.copy(spot, spot, after))
                self.first_up.append(net.again(chunks.at[top], spot, after))
                net.open.append((self.up[-1], slot < top))
                spot = from_right.at[order]
                self.down.append(net.copy(spot, spot, before))
                self.first_down.append(net.again(chunks.at[low], spot, before))
                net.open.append((self.down[-1], slot > low))

        def first(self):
            for order in range(depth - 1):
                pl.when(slot == 0)(self.first_up[order].start)
                pl.when(slot == depth - 1)(self.first_down[order].start)

        def stage(self, time):
            for order in range(time):
                top, low = depth - 1 - order, order

                @pl.when(slot == time - order)
                def _(order=order, top=top):
                    self.up[order].wait_recv()
                    if time < depth - 1:
                        self.from_left[order] = (
                            self.from_left[order].astype(F32) + self.chunks[top].astype(F32)
                        ).astype(BF16)
                        self.up[order].start()

                @pl.when(depth - 1 - slot == time - order)
                def _(order=order, low=low):
                    self.down[order].wait_recv()
                    if time < depth - 1:
                        self.from_right[order] = (
                            self.from_right[order].astype(F32) + self.chunks[low].astype(F32)
                        ).astype(BF16)
                        self.down[order].start()

    grad_parts = range(1, chips)

    def attention_back(mask):
        start = mask * 3 * block
        queries = qkv[:, start : start + block]
        keys = qkv[:, start + block : start + 2 * block]
        values = qkv[:, start + 2 * block : start + 3 * block]
        grad_mixed = through(b_all[0:rows, :], wo[mask * block : (mask + 1) * block, :]).astype(BF16)
        grad_q = jnp.zeros((rows, block), F32)
        grad_k = grad_q
        grad_v = grad_q
        for head in range(block // HD):
            mine = lax.div(lane, HD) == head
            probs = head_probs(jnp.where(mine, queries, jnp.zeros_like(queries)), keys, live)
            grad_probs = through(jnp.where(mine, grad_mixed, jnp.zeros_like(grad_mixed)), values)
            dsum = jnp.sum(probs * grad_probs, axis=-1, keepdims=True)
            grad_scores = (probs * (grad_probs - dsum)).astype(BF16)
            grad_q = jnp.where(mine, dot(grad_scores, keys), grad_q)
            grad_k = jnp.where(mine, inner(grad_scores, queries), grad_k)
            grad_v = jnp.where(mine, inner(probs.astype(BF16), grad_mixed), grad_v)
        grad_q = grad_q.astype(BF16) * jnp.bfloat16(0.125)
        grad_k = grad_k.astype(BF16)
        grad_v = grad_v.astype(BF16)
        spot = pl.ds(pl.multiple_of(where[mask] * block, block), block)
        vec_s[0:1, spot] = jnp.sum(grad_q.astype(F32), axis=0, keepdims=True)
        vec_s[1:2, spot] = jnp.sum(grad_v.astype(F32), axis=0, keepdims=True)
        dqkv[:, start : start + block] = grad_q
        dqkv[:, start + block : start + 2 * block] = grad_k
        dqkv[:, start + 2 * block : start + 3 * block] = grad_v
        if mask:
            joint = j_send.at[mask - 1]
        else:
            joint = j_all.at[0:rows]
        joint[:, 0:block] = grad_q
        joint[:, block : 2 * block] = grad_k
        joint[:, 2 * block : 3 * block] = grad_v
        joint[:, 3 * block : 4 * block] = mixed[:, mask * block : (mask + 1) * block]
        if mask:
            return net.send(
                joint, j_all.at[mask * rows : (mask + 1) * rows], (flip(me, 2 * mask), slot)
            )
        return None

    j_copies = [attention_back(mask) for mask in grad_parts]
    attention_back(0)
    b_pass = plane_pass(b_plane, b_all)
    for made in third:
        made.wait_send()
    part[0:half, :] = through(dqkv[other_at, :], wqkv[...])
    tg_copy = net.copy(part.at[0:half], part_d, peer)
    tg_copy.start()
    part[half:rows, :] = grad_one[mine_at, :] + through(dqkv[mine_at, :], wqkv[...])
    tg_copy.wait_recv()
    tg_half[...] = (part[half:rows, :] + part_d[...]).astype(BF16)

    fine = wide // depth
    span = lines * depth
    features_at = pl.ds(pl.multiple_of((depth * core + slot) * fine, fine), fine)
    bias_mine = jnp.concatenate([vec[3 + number : 4 + number, features_at] for number in range(chips)], axis=1)

    def feed_rows(place):
        at = slice(place * rows, (place + 1) * rows)
        value = dot(n_all[at, :], up_mine[...]) + bias_mine
        cdf = normal_cdf(value)
        hid_all[at, :] = (value * cdf).astype(BF16)
        low = (through(g_all[at, :], down_mine[...]) * slope_of(value, cdf)).astype(BF16)
        gp_all[at, :] = low
        return jnp.sum(low.astype(F32), axis=0, keepdims=True)

    bias_sum = feed_rows(0)
    g_column.relay()
    g_column.hand_over(1)
    g_column.hand_over(3)
    out_waits = go_back(out_half, out_got)
    tg_waits = go_back(tg_half, tg_got)
    for place in (2, 1, 3):
        n_column.passes[place].wait_recv()
        g_column.passes[place].wait_recv()
        bias_sum = bias_sum + feed_rows(place)
    for number in range(chips):
        vec_s[3 + number : 4 + number, features_at] = bias_sum[:, number * fine : (number + 1) * fine]
    depth_rows = D // chips
    for number in range(chips):
        block_up = inner(n_all[:, number * depth_rows : (number + 1) * depth_rows], gp_all[...]).astype(BF16)
        packed[number, fine : 2 * fine, 0:wide] = block_up[0:fine, :]
        packed[number, fine : 2 * fine, wide : 2 * wide] = block_up[fine : 2 * fine, :]

    def scatter_plane(lines_at):
        return [
            net.send(
                packed.at[flip_traced(chip, mask, chips), lines_at],
                plane_got.at[mask - 1, lines_at],
                (flip(me, 2 * mask), slot),
            )
            for mask in range(1, chips)
        ]

    up_copies = scatter_plane(slice(fine, 2 * fine))
    packed[:, 0:fine, :] = inner(hid_all[...], g_all[...]).astype(BF16).reshape(chips, fine, D)
    down_copies = scatter_plane(slice(0, fine))

    tiles = vec.shape[0] * D // 128
    share = tiles // (devices * depth)
    vec_by[...] = jnp.zeros_like(vec_by)
    for tile in range(tiles):
        owner, lane_group = tile // share, tile % share
        row, col = tile // (D // 128), (tile % (D // 128)) * 128
        spot = (owner % depth) * 16 + owner // depth
        vec_by[spot : spot + 1, lane_group * 128 : (lane_group + 1) * 128] = vec_s[
            row : row + 1, col : col + 128
        ]
    for number in range(depth):
        packed_two[number, rows : rows + 16, :] = vec_by[number * 16 : (number + 1) * 16, :].astype(BF16)

    for made in b_pass + x_pass + j_copies:
        made.wait_recv()
    across = inner(j_all[:, 3 * block : 4 * block], b_all[...]).astype(BF16)
    for group in range(devices):
        both = inner(x_all[:, group * span : (group + 1) * span], j_all[:, 0 : 3 * block]).astype(BF16)
        row = group * lines
        for number in range(depth):
            at = slice(number * lines, (number + 1) * lines)
            packed_two[number, row : row + lines, 0 : 3 * block] = both[at, :]
            packed_two[number, row : row + lines, 3 * block : 4 * block] = across[
                at, group * block : (group + 1) * block
            ]
    input_line = Line(packed_two, right_two, left_two)
    input_line.first()

    def finish(line, target, rows_at):
        target[...] = line.chunks[slot, rows_at, :].astype(F32)

        @pl.when(slot >= 1)
        def _():
            target[...] += line.from_left[depth - 1 - slot, rows_at, :].astype(F32)

        @pl.when(slot <= depth - 2)
        def _():
            target[...] += line.from_right[slot, rows_at, :].astype(F32)

    def plane_sum(copies, lines_at):
        for made in copies:
            made.wait_recv()
        value = packed[chip, lines_at, :].astype(F32)
        for number in range(chips - 1):
            value = value + plane_got[number, lines_at, :].astype(F32)
        return value

    def trade(source, target):
        return [
            net.send(source.at[flip(me, mask)], target.at[me], (flip(me, mask), slot))
            for mask in range(1, devices)
        ]

    input_line.stage(1)
    low_sum = plane_sum(up_copies, slice(fine, 2 * fine)).astype(BF16)
    for upper in range(2):
        for number in range(depth):
            trade_in[upper * depth + number] = low_sum[
                number * lines : (number + 1) * lines, upper * wide : (upper + 1) * wide
            ]
    here = core * depth + slot
    in_copies = []
    for shift in range(1, 2 * depth):
        far = lax.rem(slot + shift % depth, depth)
        upper = core if shift < depth else 1 - core
        in_copies.append(net.send(trade_in.at[upper * depth + far], got_in.at[here], (base + upper, far)))
    for time in range(2, depth):
        input_line.stage(time)
    tg_copy.wait_send()
    finish(input_line, sums, slice(0, rows + 16))
    first_row = lax.broadcasted_iota(jnp.int32, (16, 3 * block), 0) == 0
    for group in range(devices):
        trade_qkv[group, 0:lines, :] = sums[group * lines : (group + 1) * lines, 0 : 3 * block].astype(BF16)
        trade_qkv[group, lines : lines + 16, :] = jnp.where(
            first_row, sums[rows + group : rows + group + 1, 0 : 3 * block], 0.0
        ).astype(BF16)
        g_out[:, group * block : (group + 1) * block] = sums[
            group * lines : (group + 1) * lines, 3 * block : 4 * block
        ]
    qkv_copies = trade(trade_qkv, got_qkv)
    for made in in_copies:
        made.wait_recv()
    got_in[here] = trade_in[here]
    for group in range(2 * depth):
        for number in range(chips):
            start = number * 2 * wide + group * fine
            g_in[:, start : start + fine] = got_in[group, :, number * fine : (number + 1) * fine].astype(F32)
    g_fc2[...] = plane_sum(down_copies, slice(0, fine))
    for wait in out_waits + tg_waits:
        wait()
    out_ref[...] = out_got[...]
    tgrad_ref[...] = tg_got[...]
    for made in qkv_copies:
        made.wait_recv()
    got_qkv[me] = trade_qkv[me]
    vec_sum = jnp.zeros((16, 3 * block), F32)
    for group in range(devices):
        vec_sum = vec_sum + got_qkv[group, lines : lines + 16, :].astype(F32)
        for kind in range(3):
            g_qkv[:, kind * D + group * block : kind * D + (group + 1) * block] = got_qkv[
                group, 0:lines, kind * block : (kind + 1) * block
            ].astype(F32)
    g_vec[...] = vec_sum[0:8, :]
    net.close()


def adam_kernel(count, *refs):
    (
        g_qkv, g_out, g_in, g_fc2, g_vec, vec, out_in, tgrad_in, w_qkv, w_out, w_in, w_fc2, m_one, m_two,
        out_ref, tgrad_ref, rows_out, params_out, one_out, two_out,
        grads, params, one, two, b_qkv, b_out, b_in, b_fc2, vec_flat, in_sems, w_sems, out_sems,
    ) = refs
    index = lax.axis_index("dp") * lax.axis_size("ctx") + lax.axis_index("ctx")
    size = m_one.shape[1] // 128
    parts = in_sems.shape[1]
    step = grads.shape[0] // parts
    spans = [(number * step, min((number + 1) * step, size) - number * step) for number in range(parts)]
    loads = []
    for number, (start, length) in enumerate(spans):
        pair = []
        for kind, (source, target) in enumerate(((m_one, one), (m_two, two))):
            pair.append(
                pltpu.make_async_copy(
                    source.reshape(size, 128).at[start : start + length],
                    target.at[start : start + length],
                    in_sems.at[kind, number],
                )
            )
            pair[-1].start()
        loads.append(pair)
    weights = []
    for number, (source, target) in enumerate(
        ((w_qkv, b_qkv), (w_out, b_out), (w_in, b_in), (w_fc2, b_fc2))
    ):
        lines = target.shape[0]
        start = pl.multiple_of(index * lines, lines)
        weights.append(
            pltpu.make_async_copy(source.at[pl.ds(start, lines), :], target, w_sems.at[number])
        )
        weights[-1].start()
    out_ref[...] = out_in[...]
    tgrad_ref[...] = tgrad_in[...]

    def flatten(source, target, base):
        lines, groups = source.shape[0], source.shape[1] // 128
        for col in range(groups):
            value = source[:, col * 128 : (col + 1) * 128].astype(F32)
            for row in range(0, lines, 8):
                target[pl.ds(base + row * groups + col, 8, stride=groups), :] = value[row : row + 8, :]

    base = 0
    for grad in (g_qkv, g_out, g_in, g_fc2):
        flatten(grad, grads, base)
        base += grad.shape[0] * grad.shape[1] // 128
    share = g_vec.shape[1] // 128
    groups = vec.shape[1] // 128
    for col in range(groups):
        lanes = slice(col * 128, (col + 1) * 128)
        vec_flat[pl.ds(col, 8, stride=groups), :] = vec[0:8, lanes]
        for row in range(8, vec.shape[0]):
            vec_flat[row * groups + col : row * groups + col + 1, :] = vec[row : row + 1, lanes]
    place = lax.broadcasted_iota(jnp.int32, vec_flat.shape, 0)
    for number in range(share):
        grads[base + number : base + number + 1, :] = g_vec[0:1, number * 128 : (number + 1) * 128]
        params[base + number : base + number + 1, :] = jnp.sum(
            jnp.where(place == index * share + number, vec_flat[...], 0.0), axis=0, keepdims=True
        )
    base = 0
    for made, weight in zip(weights, (b_qkv, b_out, b_in, b_fc2)):
        made.wait()
        flatten(weight, params, base)
        base += weight.shape[0] * weight.shape[1] // 128
    fix_one = 1.0 / (1.0 - beta_one**step_count)
    fix_two = 1.0 / (1.0 - beta_two**step_count)
    copies = []
    for number, (start, length) in enumerate(spans):
        for made in loads[number]:
            made.wait()

        @pl.loop(0, step // 56)
        def _(chunk, start=start):
            at = pl.ds(pl.multiple_of(start + chunk * 56, 8), 56)
            grad, param = grads[at, :], params[at, :]
            new_one = beta_one * one[at, :] + (1.0 - beta_one) * grad
            new_two = beta_two * two[at, :] + (1.0 - beta_two) * grad * grad
            one[at, :] = new_one
            two[at, :] = new_two
            change = new_one * fix_one / (jnp.sqrt(new_two * fix_two) + adam_eps)
            params[at, :] = param - learn_rate * (change + decay_rate * param)

        for kind, (source, target) in enumerate(
            ((grads, rows_out), (params, params_out), (one, one_out), (two, two_out))
        ):
            copies.append(
                pltpu.make_async_copy(
                    source.at[start : start + length],
                    target.reshape(size, 128).at[start : start + length],
                    out_sems.at[kind, number],
                )
            )
            copies[-1].start()
    for made in copies:
        made.wait()


def slot_body(tokens, out_grad, lengths, w_qkv, w_out, w_in, w_fc2, vectors, moment_one, moment_two):
    slots, piece, width = tokens.shape
    devices, depth = lax.axis_size("dp"), lax.axis_size("ctx")
    chips = devices // 2
    count = devices * depth
    features = w_in.shape[1]
    half = 2 * piece
    rows = 2 * half
    block = D // devices
    wide = features // devices
    lines = D // count
    total = rows * chips
    low = lambda *shape: pltpu.VMEM(shape, BF16)
    wide_f32 = lambda *shape: pltpu.VMEM(shape, F32)
    anywhere = pl.BlockSpec(memory_space=pl.ANY)
    inside = pl.BlockSpec(memory_space=pltpu.VMEM)
    copies = 96
    out, tokens_grad, grad_qkv, grad_out_w, grad_in, grad_fc2, vector_grad = pl.pallas_call(
        partial(slot_kernel, devices, depth, features),
        out_shape=(
            jax.ShapeDtypeStruct(tokens.shape, BF16),
            jax.ShapeDtypeStruct(tokens.shape, BF16),
            jax.ShapeDtypeStruct((lines, 3 * D), F32),
            jax.ShapeDtypeStruct((lines, D), F32),
            jax.ShapeDtypeStruct((lines, features), F32),
            jax.ShapeDtypeStruct((features // count, D), F32),
            jax.ShapeDtypeStruct((8, 3 * block), F32),
        ),
        in_specs=[anywhere, anywhere, pl.BlockSpec(memory_space=pltpu.SMEM), inside] + [anywhere] * 4,
        out_specs=(inside,) * 7,
        scratch_shapes=[
            low(D, 3 * D // 2),
            low(D // 2, D),
            low(D, features // 2),
            low(features // 2, D),
            low(total, D),
            low(total, D),
            low(total, D),
            low(total, D),
            low(total, 4 * block),
            low(chips - 1, rows, 4 * block),
            low(rows, D),
            pltpu.VMEM((slots, 128), jnp.int32),
            low(rows, 3 * D // 2),
            low(rows, D // 2),
            wide_f32(rows, D),
            wide_f32(rows, D),
            wide_f32(rows, D),
            wide_f32(rows, D),
            wide_f32(half, D),
            wide_f32(rows, D),
            wide_f32(rows, D),
            wide_f32(rows, D),
            wide_f32(rows, features // 2),
            low(rows, features // 2),
            low(total, wide),
            low(total, wide),
            low(chips, 2 * wide // depth, D),
            low(chips - 1, 2 * wide // depth, D),
            low(D, wide),
            low(wide, D),
            low(depth, devices * lines + 16, 4 * block),
            low(depth - 1, devices * lines + 16, 4 * block),
            low(depth - 1, devices * lines + 16, 4 * block),
            low(devices, lines, wide),
            low(devices, lines, wide),
            low(devices, lines + 16, 3 * block),
            low(devices, lines + 16, 3 * block),
            wide_f32(16, D),
            wide_f32(16 * depth, 4 * block),
            wide_f32(rows + 16, 4 * block),
            low(rows, 3 * D // 2),
            low(half, D),
            low(*tokens.shape),
            low(half, D),
            low(*tokens.shape),
            pltpu.VMEM((slots, 128), jnp.int32),
            pltpu.SemaphoreType.DMA((6 * chips,)),
            pltpu.SemaphoreType.DMA((copies,)),
            pltpu.SemaphoreType.DMA((copies,)),
        ],
        compiler_params=pltpu.CompilerParams(
            collective_id=0, has_side_effects=True, vmem_limit_bytes=64 * 1024 * 1024 - 64 * 1024
        ),
        name="slot",
    )(tokens, out_grad, lengths, vectors, w_qkv, w_out, w_in, w_fc2)
    size = moment_one.shape[1] // 128
    padded = (size + 279) // 280 * 280
    flat = jax.ShapeDtypeStruct(moment_one.shape, F32)
    return pl.pallas_call(
        partial(adam_kernel, count),
        out_shape=(
            jax.ShapeDtypeStruct(tokens.shape, BF16),
            jax.ShapeDtypeStruct(tokens.shape, BF16),
            flat,
            flat,
            flat,
            flat,
        ),
        in_specs=[inside] * 8 + [anywhere] * 6,
        out_specs=(inside, inside) + (anywhere,) * 4,
        scratch_shapes=[wide_f32(padded, 128)] * 4
        + [
            low(lines, 3 * D),
            low(lines, D),
            low(lines, features),
            low(features // count, D),
            wide_f32(vectors.shape[0] * D // 128, 128),
            pltpu.SemaphoreType.DMA((2, 5)),
            pltpu.SemaphoreType.DMA((4,)),
            pltpu.SemaphoreType.DMA((4, 5)),
        ],
        compiler_params=pltpu.CompilerParams(vmem_limit_bytes=64 * 1024 * 1024 - 64 * 1024),
        name="adam",
    )(
        grad_qkv, grad_out_w, grad_in, grad_fc2, vector_grad, vectors, out, tokens_grad,
        w_qkv, w_out, w_in, w_fc2, moment_one, moment_two,
    )


def layer(tokens, *rest):
    slots, piece, width = tokens.shape
    devices, depth = lax.axis_size("dp"), lax.axis_size("ctx")
    fits = slots == 2 and depth == 2 * slots and devices == 2 * depth and FF == (devices // 2) * D
    if fits and (H * HD // devices) % 128 == 0 and (FF // devices) % 128 == 0:
        return slot_body(tokens, *rest)
    return body(tokens, *rest)


def solution(mesh):
    placed = (
        P("dp", "ctx", None),
        P("dp", "ctx", None),
        P("dp"),
        P(),
        P(),
        P(),
        P(),
        P(),
        P(("dp", "ctx"), None),
        P(("dp", "ctx"), None),
    )
    return jax.shard_map(
        layer,
        mesh=mesh,
        in_specs=placed,
        out_specs=(
            P("dp", "ctx", None),
            P("dp", "ctx", None),
            P(("dp", "ctx"), None),
            P(("dp", "ctx"), None),
            P(("dp", "ctx"), None),
            P(("dp", "ctx"), None),
        ),
        check_vma=False,
    )
```

```python
from functools import partial

import jax
import jax.numpy as jnp
from jax import lax
from jax.experimental import pallas as pl
from jax.experimental.pallas import tpu as pltpu
from jax.sharding import PartitionSpec as P

D = 1024
H = 16
HD = 64
FF = 4096


EPSILON = 1e-05
learn_rate = 0.01
beta_one = 0.9
beta_two = 0.999
adam_eps = 1e-08
decay_rate = 0.01
step_count = 10.0


def layer_norm(values, gain, shift):
    center = values - jnp.mean(values, axis=-1, keepdims=True)
    spread = jnp.mean(center * center, axis=-1, keepdims=True)
    return center * lax.rsqrt(spread + EPSILON) * gain + shift


def split_vectors(vectors):
    ratio = FF // D
    return (
        vectors[0],
        vectors[1],
        vectors[2],
        vectors[3 : 3 + ratio].reshape(FF),
        vectors[3 + ratio],
        vectors[4 + ratio],
        vectors[5 + ratio],
        vectors[6 + ratio],
        vectors[7 + ratio],
    )


def inner(left, right):
    return lax.dot_general(
        left, right, (((0,), (0,)), ((), ())), preferred_element_type=jnp.float32
    )


def through(left, weight):
    return lax.dot_general(
        left, weight, (((1,), (1,)), ((), ())), preferred_element_type=jnp.float32
    )


def run_slots(function, items):
    return lax.map(lambda item: function(*item), items)


def heads_block():
    return 4


def split_heads(matrix):
    count = matrix.shape[0]
    group = heads_block()
    return jnp.moveaxis(matrix.reshape(count, H // group, group, HD), 1, 0)


def join_heads(blocked):
    return jnp.moveaxis(blocked, 0, 1).reshape(blocked.shape[1], H * HD)


def split_stats(stats):
    group = heads_block()
    return stats.reshape(H // group, group, stats.shape[-1])


def shard_piece(left, right, number, shard_count):
    weight_rows = left.shape[1]
    columns = right.shape[1]
    per_shard = weight_rows * columns // shard_count
    block = inner(left, right).reshape(-1)
    return block.reshape(number, per_shard)


def project(flat_tokens, w_qkv, vectors):
    joined = jnp.dot(flat_tokens, w_qkv, preferred_element_type=jnp.float32)
    queries = ((joined[:, :D] + vectors[0]) * 0.125).astype(jnp.bfloat16)
    keys = joined[:, D : 2 * D].astype(jnp.bfloat16)
    values = (joined[:, 2 * D :] + vectors[1]).astype(jnp.bfloat16)
    return (queries, keys, values)


def attend_slot(queries, keys, values, live):
    rows = queries.shape[0]

    def attend_one_block(item):
        query_heads, key_heads, value_heads = item
        scores = jnp.einsum(
            "qhd,khd->hqk", query_heads, key_heads, preferred_element_type=jnp.float32
        )
        scores = jnp.where(live[None, None, :], scores, -1e30)
        maximum = jnp.max(scores, axis=-1, keepdims=True)
        expo = jnp.exp(scores - maximum)
        total = jnp.sum(expo, axis=-1, keepdims=True)
        probs_low = (expo / total).astype(jnp.bfloat16)
        mixed = jnp.einsum(
            "hqk,khd->qhd", probs_low, value_heads, preferred_element_type=jnp.float32
        )
        return (mixed, (maximum + jnp.log(total))[..., 0])

    mixed, log_total = lax.map(
        attend_one_block, (split_heads(queries), split_heads(keys), split_heads(values))
    )
    return (join_heads(mixed), log_total.reshape(H, rows))


def query_back(queries, keys, values, live, log_total, grad_mixed, with_keys):
    rows = queries.shape[0]

    def query_one_block(item):
        query_heads, key_heads, value_heads, grad_heads, block_log = item
        scores = jnp.einsum(
            "qhd,khd->hqk", query_heads, key_heads, preferred_element_type=jnp.float32
        )
        scores = jnp.where(live[None, None, :], scores, -1e30)
        probs = jnp.exp(scores - block_log[:, :, None])
        grad_probs = jnp.einsum(
            "qhd,khd->hqk", grad_heads, value_heads, preferred_element_type=jnp.float32
        )
        row_sums = jnp.sum(probs * grad_probs, axis=-1)
        grad_scores = (probs * (grad_probs - row_sums[:, :, None])).astype(jnp.bfloat16)
        grad_query = jnp.einsum(
            "hqk,khd->qhd", grad_scores, key_heads, preferred_element_type=jnp.float32
        )
        grad_key = jnp.einsum(
            "hqk,qhd->khd", grad_scores, query_heads, preferred_element_type=jnp.float32
        )
        grad_value = jnp.einsum(
            "hqk,qhd->khd",
            probs.astype(jnp.bfloat16),
            grad_heads,
            preferred_element_type=jnp.float32,
        )
        return (grad_query, row_sums, grad_key, grad_value)

    items = (
        split_heads(queries),
        split_heads(keys),
        split_heads(values),
        split_heads(grad_mixed),
        split_stats(log_total),
    )
    results = lax.map(query_one_block, items)
    grad_query, row_sums, grad_key, grad_value = results
    return (
        join_heads(grad_query),
        row_sums.reshape(H, rows),
        join_heads(grad_key),
        join_heads(grad_value),
    )


def tail(flat_tokens, mixed, w_out, w_in, w_fc2, vectors):
    bias_q, bias_v, bias_o, bias_in, bias_fc2, gain_one, shift_one, gain_two, shift_two = (
        split_vectors(vectors)
    )
    mixed_low = mixed.astype(jnp.bfloat16)
    summed_one = (
        flat_tokens.astype(jnp.float32)
        + jnp.dot(mixed_low, w_out, preferred_element_type=jnp.float32)
        + bias_o
    )
    normed = layer_norm(summed_one, gain_one, shift_one)
    normed_low = normed.astype(jnp.bfloat16)
    hidden_pre = jnp.dot(normed_low, w_in, preferred_element_type=jnp.float32) + bias_in
    hidden_low = jax.nn.gelu(hidden_pre, approximate=False).astype(jnp.bfloat16)
    summed_two = normed + jnp.dot(hidden_low, w_fc2, preferred_element_type=jnp.float32) + bias_fc2
    result = layer_norm(summed_two, gain_two, shift_two)
    return (mixed_low, summed_one, normed_low, hidden_pre, hidden_low, summed_two, result)


def body(tokens, out_grad, lengths, w_qkv, w_out, w_in, w_fc2, vectors, moment_one, moment_two):
    slots, piece, width = tokens.shape
    length = piece * lax.axis_size("ctx")
    local_pos = lax.axis_index("ctx") * piece + jnp.arange(piece, dtype=jnp.int32)
    own_live = local_pos[None, :] < lengths[:, None]
    valid = own_live.astype(jnp.float32)
    key_live = jnp.arange(length, dtype=jnp.int32)[None, :] < lengths[:, None]
    bias_q, bias_v, bias_o, bias_in, bias_fc2, gain_one, shift_one, gain_two, shift_two = (
        split_vectors(vectors)
    )
    flat_tokens = tokens.reshape(slots * piece, width)
    queries, keys, values = project(flat_tokens, w_qkv, vectors)
    keys_all, values_all = (
        lax.all_gather(keys.reshape(slots, piece, width), "ctx", axis=1, tiled=True),
        lax.all_gather(values.reshape(slots, piece, width), "ctx", axis=1, tiled=True),
    )
    mixed, log_total = run_slots(
        attend_slot, (queries.reshape(slots, piece, width), keys_all, values_all, key_live)
    )
    saved = tail(flat_tokens, mixed.reshape(slots * piece, width), w_out, w_in, w_fc2, vectors)
    out = (saved[6].reshape(slots, piece, width) * valid[..., None]).astype(jnp.bfloat16)
    again = lax.optimization_barrier(flat_tokens)
    queries, keys, values = project(again, w_qkv, vectors)
    keys_all, values_all = (
        lax.all_gather(keys.reshape(slots, piece, width), "ctx", axis=1, tiled=True),
        lax.all_gather(values.reshape(slots, piece, width), "ctx", axis=1, tiled=True),
    )
    mixed, log_total = run_slots(
        attend_slot, (queries.reshape(slots, piece, width), keys_all, values_all, key_live)
    )
    saved = tail(again, mixed.reshape(slots * piece, width), w_out, w_in, w_fc2, vectors)
    mixed_low, summed_one, normed_low, hidden_pre, hidden_low, summed_two, result = saved
    cotangent = (out_grad.astype(jnp.float32) * valid[..., None]).reshape(slots * piece, width)
    unused_two, norm_two_back = jax.vjp(layer_norm, summed_two, gain_two, shift_two)
    grad_two, grad_gain_two, grad_shift_two = norm_two_back(cotangent)
    grad_fc2_low = grad_two.astype(jnp.bfloat16)
    bias_fc2_grad = jnp.sum(grad_fc2_low.astype(jnp.float32), axis=0)
    grad_hidden = through(grad_fc2_low, w_fc2)
    unused_gelu, gelu_back = jax.vjp(partial(jax.nn.gelu, approximate=False), hidden_pre)
    grad_pre_low = gelu_back(grad_hidden)[0].astype(jnp.bfloat16)
    bias_in_grad = jnp.sum(grad_pre_low.astype(jnp.float32), axis=0)
    grad_normed = grad_two + through(grad_pre_low, w_in)
    unused_one, norm_one_back = jax.vjp(layer_norm, summed_one, gain_one, shift_one)
    grad_one, grad_gain_one, grad_shift_one = norm_one_back(grad_normed)
    grad_branch_low = grad_one.astype(jnp.bfloat16)
    bias_out_grad = jnp.sum(grad_branch_low.astype(jnp.float32), axis=0)
    grad_mixed_low = (
        through(grad_branch_low, w_out).astype(jnp.bfloat16).reshape(slots, piece, width)
    )
    queries_slots = queries.reshape(slots, piece, width)
    grad_query, row_sums, grad_key, grad_value = run_slots(
        partial(query_back, with_keys=True),
        (queries_slots, keys_all, values_all, key_live, log_total, grad_mixed_low),
    )
    grad_key, grad_value = (
        lax.psum_scatter(
            grad_key.astype(jnp.bfloat16), "ctx", scatter_dimension=1, tiled=True
        ).astype(jnp.float32),
        lax.psum_scatter(
            grad_value.astype(jnp.bfloat16), "ctx", scatter_dimension=1, tiled=True
        ).astype(jnp.float32),
    )
    rows = slots * piece
    grad_query_low = grad_query.reshape(rows, width).astype(jnp.bfloat16) * jnp.bfloat16(0.125)
    grad_key_low = grad_key.reshape(rows, width).astype(jnp.bfloat16)
    grad_value_low = grad_value.reshape(rows, width).astype(jnp.bfloat16)
    grad_joined = jnp.concatenate([grad_query_low, grad_key_low, grad_value_low], axis=1)
    bias_q_grad = jnp.sum(grad_query_low.astype(jnp.float32), axis=0)
    bias_v_grad = jnp.sum(grad_value_low.astype(jnp.float32), axis=0)
    tokens_grad = (
        (grad_one + through(grad_joined, w_qkv)).reshape(slots, piece, width).astype(jnp.bfloat16)
    )
    vector_grad = jnp.concatenate(
        [
            bias_q_grad[None],
            bias_v_grad[None],
            bias_out_grad[None],
            bias_in_grad.reshape(FF // D, D),
            bias_fc2_grad[None],
            grad_gain_one[None],
            grad_shift_one[None],
            grad_gain_two[None],
            grad_shift_two[None],
        ],
        axis=0,
    )
    count = lax.axis_size(("dp", "ctx"))
    vector_rows = vector_grad.reshape(count, -1)
    pairs = (
        (flat_tokens, grad_joined),
        (mixed_low, grad_branch_low),
        (normed_low, grad_pre_low),
        (hidden_low, grad_fc2_low),
    )
    blocks = [
        shard_piece(left, right, 1 * lax.axis_size(("dp", "ctx")), count) for left, right in pairs
    ]
    blocks.append(vector_rows)
    grad_rows = lax.psum_scatter(
        jnp.concatenate(blocks, axis=1), ("dp", "ctx"), scatter_dimension=0, tiled=True
    )
    index = lax.axis_index(("dp", "ctx"))
    params = jnp.concatenate(
        [
            lax.dynamic_slice_in_dim(weight.reshape(count, -1), index, 1, 0).astype(jnp.float32)
            for weight in (w_qkv, w_out, w_in, w_fc2, vectors)
        ],
        axis=1,
    )
    new_one = beta_one * moment_one + (1.0 - beta_one) * grad_rows
    new_two = beta_two * moment_two + (1.0 - beta_two) * grad_rows * grad_rows
    fix_one = 1.0 - beta_one**step_count
    fix_two = 1.0 - beta_two**step_count
    update = new_one / fix_one / (jnp.sqrt(new_two / fix_two) + adam_eps)
    new_params = params - learn_rate * (update + decay_rate * params)
    return (out, tokens_grad, grad_rows, new_params, new_one, new_two)


BF16 = jnp.bfloat16
F32 = jnp.float32


def layer_norm_stats(values):
    center = values - jnp.mean(values, axis=-1, keepdims=True)
    spread = jnp.mean(center * center, axis=-1, keepdims=True)
    return center, lax.rsqrt(spread + EPSILON)


def layer_norm_back(center, scale, gain, cotangent):
    scaled = cotangent * gain
    mean_scaled = jnp.mean(scaled, axis=-1, keepdims=True)
    mean_cross = jnp.mean(scaled * center, axis=-1, keepdims=True)
    return scale * (scaled - mean_scaled - center * (scale * scale) * mean_cross)


def normal_cdf(values):
    return 0.5 * (1.0 + lax.erf(values * 0.7071067811865476))


def dot(left, right):
    return jnp.dot(left, right, preferred_element_type=F32)


def positions(axis, shape, slot, piece):
    place = lax.broadcasted_iota(jnp.int32, shape, axis)
    block = lax.div(place, piece)
    half = lax.div(block, 2)
    step = lax.rem(block, 2)
    return (2 * half + lax.rem(slot + step, 2)) * piece + lax.rem(place, piece)


def head_probs(queries, keys, live):
    scores = through(queries, keys)
    scores = jnp.where(live, scores, -1e30)
    expo = jnp.exp(scores - jnp.max(scores, axis=-1, keepdims=True))
    return expo / jnp.sum(expo, axis=-1, keepdims=True)


MESH = pl.DeviceIdType.MESH


class Links:
    def __init__(self, sends, recvs):
        self.sends, self.recvs = sends, recvs
        self.used = 0
        self.open = []

    def copy(self, source, target, device):
        self.used += 1
        return self.again(source, target, device)

    def again(self, source, target, device):
        number = self.used - 1
        return pltpu.make_async_remote_copy(
            src_ref=source,
            dst_ref=target,
            send_sem=self.sends.at[number],
            recv_sem=self.recvs.at[number],
            device_id=device,
            device_id_type=MESH,
        )

    def forward(self, source, target, device, earlier):
        self.used += 1
        return pltpu.make_async_remote_copy(
            src_ref=source,
            dst_ref=target,
            send_sem=self.sends.at[self.used - 1],
            recv_sem=self.recvs.at[earlier],
            device_id=device,
            device_id_type=MESH,
        )

    def send(self, source, target, device):
        made = self.copy(source, target, device)
        made.start()
        self.open.append((made, None))
        return made

    def send_if(self, condition, source, target, device):
        made = self.copy(source, target, device)
        pl.when(condition)(made.start)
        self.open.append((made, condition))
        return made

    def send_or_keep(self, here, source, target, device):
        number = self.used
        made = self.copy(source, target, device)
        local = pltpu.make_async_copy(source, target, self.recvs.at[number])
        pl.when(here)(local.start)
        away = jnp.logical_not(here)
        pl.when(away)(made.start)
        self.open.append((made, away))

        def wait():
            pl.when(here)(local.wait)
            pl.when(away)(made.wait_recv)

        return wait

    def close(self):
        for made, condition in self.open:
            if condition is None:
                made.wait_send()
            else:
                pl.when(condition)(made.wait_send)


def flip(value, mask):
    result = value
    bit = 1
    while bit <= mask:
        if mask & bit:
            result = result + bit * (1 - 2 * lax.rem(lax.div(value, bit), 2))
        bit *= 2
    return result


def flip_traced(value, mask, size):
    result = value
    bit = 1
    while bit < size:
        set_bit = lax.rem(lax.div(mask, bit), 2)
        result = result + bit * set_bit * (1 - 2 * lax.rem(lax.div(value, bit), 2))
        bit *= 2
    return result


def at_rows(start, size):
    return pl.ds(pl.multiple_of(start, 64), size)


def slot_kernel(devices, depth, features, *refs):
    (
        tokens, out_grad, lengths, vec, w_qkv, w_out, w_in, w_fc2,
        out_ref, tgrad_ref, g_qkv, g_out, g_in, g_fc2, g_vec,
        wqkv, wo, w_up, w_down,
        x_all, n_all, g_all, m_all, b_all, j_all, j_send, g_rows, lens_peer,
        qkv, part, part_a, part_b, part_c, part_d, summed, grad_two, grad_one,
        pre_s, hid, hid_all, gp_all, packed, plane_got, up_mine, down_mine, packed_two, right_two, left_two,
        trade_in, got_in, trade_qkv, got_qkv, vec_s, vec_by, vec_got, sums, dqkv, out_half, out_got, tg_half, tg_got, lens,
        local_sems, sends, recvs,
    ) = refs
    chips = devices // 2
    me, slot = lax.axis_index("dp"), lax.axis_index("ctx")
    core, chip = lax.rem(me, 2), lax.div(me, 2)
    base = me - core
    peer = (base + 1 - core, slot)
    piece = tokens.shape[1]
    half = 2 * piece
    rows = 2 * half
    block = D // devices
    wide = features // devices
    lines = D // (devices * depth)
    net = Links(sends, recvs)
    mine_at = at_rows(core * half, half)
    other_at = at_rows((1 - core) * half, half)
    chunk = 32

    row_of = lax.broadcasted_iota(jnp.int32, lens.shape, 0)
    lens[...] = jnp.where(row_of == 0, lengths[0], lengths[1])
    vec_s[...] = jnp.zeros_like(vec_s)
    loads = []

    def load(source, target):
        made = pltpu.make_async_copy(source, target, local_sems.at[len(loads)])
        made.start()
        loads.append(made)

    where = [2 * flip(chip, mask) + core for mask in range(chips)]
    for mask in range(chips):
        for kind in range(3):
            start = pl.multiple_of(kind * D + where[mask] * block, block)
            load(
                w_qkv.at[:, pl.ds(start, block)],
                wqkv.at[:, (3 * mask + kind) * block : (3 * mask + kind + 1) * block],
            )
    n_qkv = len(loads)
    for number in range(chips):
        start = pl.multiple_of((2 * number + core) * block, block)
        load(w_out.at[pl.ds(start, block), :], wo.at[number * block : (number + 1) * block, :])
    n_out = len(loads)
    for mask in range(chips):
        start = pl.multiple_of(where[mask] * wide, wide)
        load(w_in.at[:, pl.ds(start, wide)], w_up.at[:, mask * wide : (mask + 1) * wide])
    n_up = len(loads)
    for mask in range(chips):
        start = pl.multiple_of(where[mask] * wide, wide)
        load(w_fc2.at[pl.ds(start, wide), :], w_down.at[mask * wide : (mask + 1) * wide, :])

    barrier = pltpu.get_barrier_semaphore()
    friends = [(flip(me, mask), slot) for mask in range(1, devices)]
    for shift in range(1, depth):
        far = lax.rem(slot + shift, depth)
        friends += [(me, far), (flip(me, 1), far)]
    for friend in friends:
        pl.semaphore_signal(barrier, inc=1, device_id=friend, device_id_type=MESH)
    pl.semaphore_wait(barrier, len(friends))

    def spread(source, target):
        waits = []
        for step in range(2):
            pick = lax.rem(slot + step, 2)
            upper = lax.div(slot, 2)
            place = 2 * core + pick
            here = jnp.logical_and(upper == core, place == slot)
            waits.append(
                net.send_or_keep(
                    here,
                    source.at[pick],
                    target.at[at_rows((2 * upper + step) * piece, piece)],
                    (base + upper, place),
                )
            )
        return waits

    def pass_on(waits, target):
        made = []
        for step, wait in enumerate(waits):
            wait()
            spot = target.at[at_rows((2 * core + step) * piece, piece)]
            made.append(net.send(spot, spot, peer))
        return made

    token_waits = spread(tokens, x_all)
    grad_waits = spread(out_grad, g_rows)
    lens_copy = net.send(lens, lens_peer, peer)
    token_passes = pass_on(token_waits, x_all)

    def plane_start(target):
        source = target.at[mine_at]
        return [
            net.send(
                source, target.at[at_rows(mask * rows + core * half, half)], (flip(me, 2 * mask), slot)
            )
            for mask in range(1, chips)
        ]

    def plane_pass(copies, target):
        made = []
        for mask, copy in enumerate(copies, 1):
            copy.wait_recv()
            spot = target.at[at_rows(mask * rows + core * half, half)]
            made.append(net.send(spot, spot, peer))
        return made

    class Column:
        def __init__(self, target):
            self.target = target
            self.parts, self.numbers = {}, {}
            for place in (2, 1, 3):
                far = lax.rem(slot + depth - place, depth)
                made = net.copy(target.at[mine_at], self.spot(place), (me, far))
                self.parts[place], self.numbers[place] = made, net.used - 1
                goes = {1: slot != 0, 2: slot >= 0, 3: slot != depth - 1}[place]
                net.open.append((made, goes))
                pl.when(goes)(made.start)
            self.passes = {}

        def spot(self, place):
            return self.target.at[at_rows(place * rows + core * half, half)]

        def relay(self):
            self.parts[2].wait_recv()
            up = net.forward(self.spot(2), self.spot(1), (me, depth - 1), self.numbers[1])
            down = net.forward(self.spot(2), self.spot(3), (me, 0), self.numbers[3])
            for made, here in ((up, slot == 2), (down, slot == 1)):
                pl.when(here)(made.start)
                net.open.append((made, here))
            self.passes[2] = net.send(self.spot(2), self.spot(2), peer)

        def hand_over(self, place):
            self.parts[place].wait_recv()
            self.passes[place] = net.send(self.spot(place), self.spot(place), peer)

    x_plane = plane_start(x_all)
    for made in loads[:n_qkv]:
        made.wait()
    lens_copy.wait_recv()
    for made in token_passes:
        made.wait_recv()
    owned = jnp.where(lax.div(slot, 2) == core, lens[...], lens_peer[...])
    length = jnp.where(lax.rem(slot, 2) == 0, owned[0:1, 0:1], owned[1:2, 0:1])
    live = positions(1, (1, rows), slot, piece) < length
    lane = lax.broadcasted_iota(jnp.int32, (1, block), 1)

    @pl.loop(0, chips)
    def _(mask):
        spot = 2 * flip_traced(chip, mask, chips) + core
        lanes = pl.ds(pl.multiple_of(spot * block, block), block)
        joined = dot(x_all[0:rows, :], wqkv[:, pl.ds(pl.multiple_of(mask * 3 * block, block), 3 * block)])
        queries = ((joined[:, 0:block] + vec[0:1, lanes]) * 0.125).astype(BF16)
        keys = joined[:, block : 2 * block].astype(BF16)
        values = (joined[:, 2 * block :] + vec[1:2, lanes]).astype(BF16)
        total = jnp.zeros((rows, block), F32)
        for head in range(block // HD):
            mine = lax.div(lane, HD) == head
            probs = head_probs(jnp.where(mine, queries, jnp.zeros_like(queries)), keys, live)
            total = jnp.where(mine, dot(probs.astype(BF16), values), total)
        start = pl.multiple_of(mask * 3 * block, block)
        qkv[:, pl.ds(start, block)] = queries
        qkv[:, pl.ds(pl.multiple_of(start + block, block), block)] = keys
        qkv[:, pl.ds(pl.multiple_of(start + 2 * block, block), block)] = values
        lanes = pl.ds(pl.multiple_of(core * chips * block + lax.div(spot, 2) * block, block), block)
        m_all[0:rows, lanes] = total.astype(BF16)

    for made in loads[n_qkv:n_out]:
        made.wait()

    def exchange(compute, target, before):
        made = []
        for number, at in enumerate((other_at, mine_at)):
            if before is not None:
                before[number].wait_send()
            part[at, :] = compute(at)
            made.append(net.copy(part.at[at], target.at[at], peer))
            made[-1].start()
        return made

    my_lanes = pl.ds(pl.multiple_of(core * chips * block, chips * block), chips * block)
    first = exchange(lambda at: dot(m_all[at, my_lanes], wo[...]), part_a, None)
    own_mixed = m_all.at[0:rows, my_lanes]
    m_passes = [net.send(own_mixed, own_mixed, peer)]
    m_plane = [
        net.send(own_mixed, m_all.at[mask * rows : (mask + 1) * rows, my_lanes], (flip(me, 2 * mask), slot))
        for mask in range(1, chips)
    ]
    grad_passes = pass_on(grad_waits, g_rows)

    def norm_one(start):
        @pl.loop(0, half // chunk)
        def _(step):
            at = pl.ds(pl.multiple_of(start + step * chunk, chunk), chunk)
            total = x_all[at, :].astype(F32) + (part[at, :] + part_a[at, :]) + vec[2:3, :]
            center, scale = layer_norm_stats(total)
            summed[at, :] = total
            n_all[at, :] = (center * scale * vec[8:9, :] + vec[9:10, :]).astype(BF16)

    first[0].wait_recv()
    norm_one(core * half)
    n_column = Column(n_all)
    first[1].wait_recv()
    norm_one((1 - core) * half)
    for made in loads[n_out:]:
        made.wait()

    for number in range(chips):
        fine_cols = wide // depth
        begin = flip_traced(chip, number, chips) * wide + slot * fine_cols
        at = pl.ds(pl.multiple_of(begin, fine_cols), fine_cols)
        up_mine[:, number * fine_cols : (number + 1) * fine_cols] = w_up[:, at]
        down_mine[number * fine_cols : (number + 1) * fine_cols, :] = w_down[at, :]

    def bias_of(mask):
        spot = flip_traced(chip, mask, chips)
        lanes = pl.ds(pl.multiple_of(core * wide, wide), wide)
        result = vec[3:4, lanes]
        for row in range(1, chips):
            result = jnp.where(spot == row, vec[3 + row : 4 + row, lanes], result)
        return result

    @pl.loop(0, chips)
    def _(mask):
        at = pl.ds(pl.multiple_of(mask * wide, wide), wide)
        value = dot(n_all[0:rows, :], w_up[:, at]) + bias_of(mask)
        pre_s[:, at] = value
        hid[:, at] = (value * normal_cdf(value)).astype(BF16)

    second = exchange(lambda at: dot(hid[at, :], w_down[...]), part_b, first)
    for made in grad_passes:
        made.wait_recv()

    def norm_two(start, own):
        @pl.loop(0, half // chunk)
        def _(step):
            begin = pl.multiple_of(start + step * chunk, chunk)
            at = pl.ds(begin, chunk)
            center, scale = layer_norm_stats(summed[at, :])
            normed = center * scale * vec[8:9, :] + vec[9:10, :]
            center, scale = layer_norm_stats(normed + (part[at, :] + part_b[at, :]) + vec[7:8, :])
            place = begin + lax.broadcasted_iota(jnp.int32, (chunk, 1), 0)
            piece_of = lax.div(place, piece)
            spot = 2 * lax.div(piece_of, 2) + lax.rem(slot + lax.rem(piece_of, 2), 2)
            valid = (spot * piece + lax.rem(place, piece) < length).astype(F32)
            unit = center * scale
            error = g_rows[at, :].astype(F32) * valid
            grad = layer_norm_back(center, scale, vec[10:11, :], error)
            grad_two[at, :] = grad
            low = grad.astype(BF16)
            g_all[at, :] = low
            if own:
                out_half[pl.ds(pl.multiple_of(step * chunk, chunk), chunk), :] = (
                    valid * (unit * vec[10:11, :] + vec[11:12, :])
                ).astype(BF16)
                vec_s[7:8, :] += jnp.sum(low.astype(F32), axis=0, keepdims=True)
                vec_s[10:11, :] += jnp.sum(error * unit, axis=0, keepdims=True)
                vec_s[11:12, :] += jnp.sum(error, axis=0, keepdims=True)

    def go_back(source, target):
        waits = []
        for step in range(2):
            place = 2 * core + lax.rem(slot + step, 2)
            upper = lax.div(slot, 2)
            here = jnp.logical_and(upper == core, place == slot)
            waits.append(
                net.send_or_keep(
                    here,
                    source.at[step * piece : (step + 1) * piece],
                    target.at[lax.rem(slot, 2)],
                    (base + upper, place),
                )
            )
        return waits

    second[0].wait_recv()
    norm_two(core * half, True)
    g_column = Column(g_all)
    second[1].wait_recv()
    norm_two((1 - core) * half, False)
    def mixed_pass():
        for mask, made in enumerate(m_plane, 1):
            made.wait_recv()
            spot = m_all.at[mask * rows : (mask + 1) * rows, my_lanes]
            m_passes.append(net.send(spot, spot, peer))


    def slope_of(value, cdf):
        return cdf + value * (jnp.exp(-0.5 * value * value) * 0.3989422804014327)

    @pl.loop(0, chips)
    def _(mask):
        at = pl.ds(pl.multiple_of(mask * wide, wide), wide)
        value = pre_s[:, at]
        grad = through(g_all[0:rows, :], w_down[at, :])
        hid[:, at] = (grad * slope_of(value, normal_cdf(value))).astype(BF16)

    third = exchange(lambda at: through(hid[at, :], w_up[...]), part_c, second)

    def norm_one_back(start, own):
        @pl.loop(0, half // chunk)
        def _(step):
            at = pl.ds(pl.multiple_of(start + step * chunk, chunk), chunk)
            center, scale = layer_norm_stats(summed[at, :])
            error = grad_two[at, :] + (part[at, :] + part_c[at, :])
            grad = layer_norm_back(center, scale, vec[8:9, :], error)
            low = grad.astype(BF16)
            b_all[at, :] = low
            grad_one[at, :] = grad
            if own:
                vec_s[2:3, :] += jnp.sum(low.astype(F32), axis=0, keepdims=True)
                vec_s[8:9, :] += jnp.sum(error * (center * scale), axis=0, keepdims=True)
                vec_s[9:10, :] += jnp.sum(error, axis=0, keepdims=True)

    n_column.relay()
    x_pass = plane_pass(x_plane, x_all)

    third[0].wait_recv()
    norm_one_back(core * half, True)
    third[1].wait_recv()
    norm_one_back((1 - core) * half, False)
    n_column.hand_over(1)
    n_column.hand_over(3)

    class Line:
        def __init__(self, chunks, from_left, from_right):
            self.chunks, self.from_left, self.from_right = chunks, from_left, from_right
            self.up, self.down, self.first_up, self.first_down = [], [], [], []
            after = (me, lax.rem(slot + 1, depth))
            before = (me, lax.rem(slot + depth - 1, depth))
            for order in range(depth - 1):
                top, low = depth - 1 - order, order
                spot = from_left.at[order]
                self.up.append(net.copy(spot, spot, after))
                self.first_up.append(net.again(chunks.at[top], spot, after))
                net.open.append((self.up[-1], slot < top))
                spot = from_right.at[order]
                self.down.append(net.copy(spot, spot, before))
                self.first_down.append(net.again(chunks.at[low], spot, before))
                net.open.append((self.down[-1], slot > low))

        def first(self):
            for order in range(depth - 1):
                pl.when(slot == 0)(self.first_up[order].start)
                pl.when(slot == depth - 1)(self.first_down[order].start)

        def stage(self, time):
            for order in range(time):
                top, low = depth - 1 - order, order

                @pl.when(slot == time - order)
                def _(order=order, top=top):
                    self.up[order].wait_recv()
                    if time < depth - 1:
                        self.from_left[order] = (
                            self.from_left[order].astype(F32) + self.chunks[top].astype(F32)
                        ).astype(BF16)
                        self.up[order].start()

                @pl.when(depth - 1 - slot == time - order)
                def _(order=order, low=low):
                    self.down[order].wait_recv()
                    if time < depth - 1:
                        self.from_right[order] = (
                            self.from_right[order].astype(F32) + self.chunks[low].astype(F32)
                        ).astype(BF16)
                        self.down[order].start()

    grad_parts = range(1, chips)

    def attention_back(mask):
        start = mask * 3 * block
        queries = qkv[:, start : start + block]
        keys = qkv[:, start + block : start + 2 * block]
        values = qkv[:, start + 2 * block : start + 3 * block]
        turn = pl.ds(pl.multiple_of(lax.div(where[mask], 2) * block, block), block)
        grad_mixed = through(b_all[0:rows, :], wo[turn, :]).astype(BF16)
        grad_q = jnp.zeros((rows, block), F32)
        grad_k = grad_q
        grad_v = grad_q
        for head in range(block // HD):
            mine = lax.div(lane, HD) == head
            probs = head_probs(jnp.where(mine, queries, jnp.zeros_like(queries)), keys, live)
            grad_probs = through(jnp.where(mine, grad_mixed, jnp.zeros_like(grad_mixed)), values)
            dsum = jnp.sum(probs * grad_probs, axis=-1, keepdims=True)
            grad_scores = (probs * (grad_probs - dsum)).astype(BF16)
            grad_q = jnp.where(mine, dot(grad_scores, keys), grad_q)
            grad_k = jnp.where(mine, inner(grad_scores, queries), grad_k)
            grad_v = jnp.where(mine, inner(probs.astype(BF16), grad_mixed), grad_v)
        grad_q = grad_q.astype(BF16) * jnp.bfloat16(0.125)
        grad_k = grad_k.astype(BF16)
        grad_v = grad_v.astype(BF16)
        spot = pl.ds(pl.multiple_of(where[mask] * block, block), block)
        vec_s[0:1, spot] = jnp.sum(grad_q.astype(F32), axis=0, keepdims=True)
        vec_s[1:2, spot] = jnp.sum(grad_v.astype(F32), axis=0, keepdims=True)
        dqkv[:, start : start + block] = grad_q
        dqkv[:, start + block : start + 2 * block] = grad_k
        dqkv[:, start + 2 * block : start + 3 * block] = grad_v
        if mask:
            joint = j_send.at[mask - 1]
        else:
            joint = j_all.at[0:rows]
        joint[:, 0:block] = grad_q
        joint[:, block : 2 * block] = grad_k
        joint[:, 2 * block : 3 * block] = grad_v
        joint[:, 3 * block : 4 * block] = b_all[0:rows, spot]
        if mask:
            return net.send(
                joint, j_all.at[mask * rows : (mask + 1) * rows], (flip(me, 2 * mask), slot)
            )
        return None

    j_copies = [attention_back(mask) for mask in grad_parts]
    attention_back(0)
    mixed_pass()
    for made in third:
        made.wait_send()
    part[0:half, :] = through(dqkv[other_at, :], wqkv[...])
    tg_copy = net.copy(part.at[0:half], part_d, peer)
    tg_copy.start()
    part[half:rows, :] = grad_one[mine_at, :] + through(dqkv[mine_at, :], wqkv[...])
    tg_copy.wait_recv()
    tg_half[...] = (part[half:rows, :] + part_d[...]).astype(BF16)

    fine = wide // depth
    span = lines * depth
    features_at = pl.ds(pl.multiple_of((depth * core + slot) * fine, fine), fine)
    bias_mine = jnp.concatenate([vec[3 + number : 4 + number, features_at] for number in range(chips)], axis=1)

    def feed_rows(place):
        at = slice(place * rows, (place + 1) * rows)
        value = dot(n_all[at, :], up_mine[...]) + bias_mine
        cdf = normal_cdf(value)
        hid_all[at, :] = (value * cdf).astype(BF16)
        low = (through(g_all[at, :], down_mine[...]) * slope_of(value, cdf)).astype(BF16)
        gp_all[at, :] = low
        return jnp.sum(low.astype(F32), axis=0, keepdims=True)

    bias_sum = feed_rows(0)
    g_column.relay()
    for made in m_passes + x_pass + j_copies:
        made.wait_recv()
    for group in range(devices):
        at = slice(group * span, (group + 1) * span)
        begin = (group % 2) * chips * block + (group // 2) * block
        both = inner(x_all[:, at], j_all[:, 0 : 3 * block]).astype(BF16)
        across = inner(m_all[:, begin : begin + block], j_all[:, 3 * block : 4 * block]).astype(BF16)
        row = group * lines
        for number in range(depth):
            at = slice(number * lines, (number + 1) * lines)
            packed_two[number, row : row + lines, 0 : 3 * block] = both[at, :]
            packed_two[number, row : row + lines, 3 * block : 4 * block] = across[at, :]
    input_line = Line(packed_two, right_two, left_two)
    input_line.first()

    g_column.hand_over(1)
    g_column.hand_over(3)
    for place in (2, 1, 3):
        n_column.passes[place].wait_recv()
        g_column.passes[place].wait_recv()
        bias_sum = bias_sum + feed_rows(place)
    for number in range(chips):
        vec_s[3 + number : 4 + number, features_at] = bias_sum[:, number * fine : (number + 1) * fine]
    depth_rows = D // chips
    for number in range(chips):
        block_up = inner(n_all[:, number * depth_rows : (number + 1) * depth_rows], gp_all[...]).astype(BF16)
        packed[number, fine : 2 * fine, 0:wide] = block_up[0:fine, :]
        packed[number, fine : 2 * fine, wide : 2 * wide] = block_up[fine : 2 * fine, :]

    def scatter_plane(lines_at):
        return [
            net.send(
                packed.at[flip_traced(chip, mask, chips), lines_at],
                plane_got.at[mask - 1, lines_at],
                (flip(me, 2 * mask), slot),
            )
            for mask in range(1, chips)
        ]

    up_copies = scatter_plane(slice(fine, 2 * fine))
    packed[:, 0:fine, :] = inner(hid_all[...], g_all[...]).astype(BF16).reshape(chips, fine, D)
    down_copies = scatter_plane(slice(0, fine))

    tiles = vec.shape[0] * D // 128
    share = tiles // (devices * depth)
    vec_by[...] = jnp.zeros_like(vec_by)
    for tile in range(tiles):
        owner, lane_group = tile // share, tile % share
        row, col = tile // (D // 128), (tile % (D // 128)) * 128
        spot = (owner % depth) * devices + owner // depth
        vec_by[spot : spot + 1, lane_group * 128 : (lane_group + 1) * 128] = vec_s[
            row : row + 1, col : col + 128
        ]
    vec_copies = []
    for shift in range(1, depth):
        far = lax.rem(slot + shift, depth)
        spot = vec_by.at[pl.ds(pl.multiple_of(far * devices, devices), devices)]
        vec_copies.append(net.send(spot, vec_got.at[shift - 1], (me, far)))

    def finish(line, target, rows_at):
        target[...] = line.chunks[slot, rows_at, :].astype(F32)

        @pl.when(slot >= 1)
        def _():
            target[...] += line.from_left[depth - 1 - slot, rows_at, :].astype(F32)

        @pl.when(slot <= depth - 2)
        def _():
            target[...] += line.from_right[slot, rows_at, :].astype(F32)

    def plane_sum(copies, lines_at):
        for made in copies:
            made.wait_recv()
        value = packed[chip, lines_at, :].astype(F32)
        for number in range(chips - 1):
            value = value + plane_got[number, lines_at, :].astype(F32)
        return value

    def trade(source, target):
        return [
            net.send(source.at[flip(me, mask)], target.at[me], (flip(me, mask), slot))
            for mask in range(1, devices)
        ]

    for time in range(1, depth - 1):
        input_line.stage(time)
    low_sum = plane_sum(up_copies, slice(fine, 2 * fine)).astype(BF16)
    for upper in range(2):
        for number in range(depth):
            trade_in[upper * depth + number] = low_sum[
                number * lines : (number + 1) * lines, upper * wide : (upper + 1) * wide
            ]
    here = core * depth + slot
    in_copies = []
    for shift in range(1, 2 * depth):
        far = lax.rem(slot + shift % depth, depth)
        upper = core if shift < depth else 1 - core
        in_copies.append(net.send(trade_in.at[upper * depth + far], got_in.at[here], (base + upper, far)))
    out_waits = go_back(out_half, out_got)
    tg_waits = go_back(tg_half, tg_got)
    input_line.stage(depth - 1)
    tg_copy.wait_send()
    finish(input_line, sums, slice(0, rows))
    vec_sum = vec_by[pl.ds(pl.multiple_of(slot * devices, devices), devices), :]
    for number, made in enumerate(vec_copies):
        made.wait_recv()
        vec_sum = vec_sum + vec_got[number]
    first_row = lax.broadcasted_iota(jnp.int32, (16, 4 * block), 0) == 0
    for group in range(devices):
        trade_qkv[group, 0:lines, :] = sums[group * lines : (group + 1) * lines, :].astype(BF16)
        trade_qkv[group, lines : lines + 16, :] = jnp.where(
            first_row, vec_sum[group : group + 1, :], 0.0
        ).astype(BF16)
    qkv_copies = trade(trade_qkv, got_qkv)
    for made in in_copies:
        made.wait_recv()
    got_in[here] = trade_in[here]
    for group in range(2 * depth):
        for number in range(chips):
            start = number * 2 * wide + group * fine
            g_in[:, start : start + fine] = got_in[group, :, number * fine : (number + 1) * fine].astype(F32)
    g_fc2[...] = plane_sum(down_copies, slice(0, fine))
    for wait in out_waits + tg_waits:
        wait()
    out_ref[...] = out_got[...]
    tgrad_ref[...] = tg_got[...]
    for made in qkv_copies:
        made.wait_recv()
    got_qkv[me] = trade_qkv[me]
    vec_sum = jnp.zeros((16, 3 * block), F32)
    for group in range(devices):
        vec_sum = vec_sum + got_qkv[group, lines : lines + 16, 0 : 3 * block].astype(F32)
        got = got_qkv[group, 0:lines, :].astype(F32)
        for kind in range(3):
            g_qkv[:, kind * D + group * block : kind * D + (group + 1) * block] = got[
                :, kind * block : (kind + 1) * block
            ]
        g_out[:, group * block : (group + 1) * block] = got[:, 3 * block : 4 * block]
    g_vec[...] = vec_sum[0:8, :]
    net.close()


def adam_kernel(count, *refs):
    (
        g_qkv, g_out, g_in, g_fc2, g_vec, vec, out_in, tgrad_in, w_qkv, w_out, w_in, w_fc2, m_one, m_two,
        out_ref, tgrad_ref, rows_out, params_out, one_out, two_out,
        grads, params, one, two, b_qkv, b_out, b_in, b_fc2, vec_flat, in_sems, w_sems, out_sems,
    ) = refs
    index = lax.axis_index("dp") * lax.axis_size("ctx") + lax.axis_index("ctx")
    size = m_one.shape[1] // 128
    parts = in_sems.shape[1]
    step = grads.shape[0] // parts
    spans = [(number * step, min((number + 1) * step, size) - number * step) for number in range(parts)]
    loads = []
    for number, (start, length) in enumerate(spans):
        pair = []
        for kind, (source, target) in enumerate(((m_one, one), (m_two, two))):
            pair.append(
                pltpu.make_async_copy(
                    source.reshape(size, 128).at[start : start + length],
                    target.at[start : start + length],
                    in_sems.at[kind, number],
                )
            )
            pair[-1].start()
        loads.append(pair)
    weights = []
    for number, (source, target) in enumerate(
        ((w_qkv, b_qkv), (w_out, b_out), (w_in, b_in), (w_fc2, b_fc2))
    ):
        lines = target.shape[0]
        start = pl.multiple_of(index * lines, lines)
        weights.append(
            pltpu.make_async_copy(source.at[pl.ds(start, lines), :], target, w_sems.at[number])
        )
        weights[-1].start()
    out_ref[...] = out_in[...]
    tgrad_ref[...] = tgrad_in[...]

    def flatten(source, target, base):
        lines, groups = source.shape[0], source.shape[1] // 128
        for col in range(groups):
            value = source[:, col * 128 : (col + 1) * 128].astype(F32)
            for row in range(0, lines, 8):
                target[pl.ds(base + row * groups + col, 8, stride=groups), :] = value[row : row + 8, :]

    base = 0
    for grad in (g_qkv, g_out, g_in, g_fc2):
        flatten(grad, grads, base)
        base += grad.shape[0] * grad.shape[1] // 128
    share = g_vec.shape[1] // 128
    groups = vec.shape[1] // 128
    for col in range(groups):
        lanes = slice(col * 128, (col + 1) * 128)
        vec_flat[pl.ds(col, 8, stride=groups), :] = vec[0:8, lanes]
        for row in range(8, vec.shape[0]):
            vec_flat[row * groups + col : row * groups + col + 1, :] = vec[row : row + 1, lanes]
    place = lax.broadcasted_iota(jnp.int32, vec_flat.shape, 0)
    for number in range(share):
        grads[base + number : base + number + 1, :] = g_vec[0:1, number * 128 : (number + 1) * 128]
        params[base + number : base + number + 1, :] = jnp.sum(
            jnp.where(place == index * share + number, vec_flat[...], 0.0), axis=0, keepdims=True
        )
    base = 0
    for made, weight in zip(weights, (b_qkv, b_out, b_in, b_fc2)):
        made.wait()
        flatten(weight, params, base)
        base += weight.shape[0] * weight.shape[1] // 128
    fix_one = 1.0 / (1.0 - beta_one**step_count)
    fix_two = 1.0 / (1.0 - beta_two**step_count)
    copies = []
    for number, (start, length) in enumerate(spans):
        for made in loads[number]:
            made.wait()

        @pl.loop(0, step // 56)
        def _(chunk, start=start):
            at = pl.ds(pl.multiple_of(start + chunk * 56, 8), 56)
            grad, param = grads[at, :], params[at, :]
            new_one = beta_one * one[at, :] + (1.0 - beta_one) * grad
            new_two = beta_two * two[at, :] + (1.0 - beta_two) * grad * grad
            one[at, :] = new_one
            two[at, :] = new_two
            change = new_one * fix_one / (jnp.sqrt(new_two * fix_two) + adam_eps)
            params[at, :] = param - learn_rate * (change + decay_rate * param)

        for kind, (source, target) in enumerate(
            ((grads, rows_out), (params, params_out), (one, one_out), (two, two_out))
        ):
            copies.append(
                pltpu.make_async_copy(
                    source.at[start : start + length],
                    target.reshape(size, 128).at[start : start + length],
                    out_sems.at[kind, number],
                )
            )
            copies[-1].start()
    for made in copies:
        made.wait()


def slot_body(tokens, out_grad, lengths, w_qkv, w_out, w_in, w_fc2, vectors, moment_one, moment_two):
    slots, piece, width = tokens.shape
    devices, depth = lax.axis_size("dp"), lax.axis_size("ctx")
    chips = devices // 2
    count = devices * depth
    features = w_in.shape[1]
    half = 2 * piece
    rows = 2 * half
    block = D // devices
    wide = features // devices
    lines = D // count
    total = rows * chips
    low = lambda *shape: pltpu.VMEM(shape, BF16)
    wide_f32 = lambda *shape: pltpu.VMEM(shape, F32)
    anywhere = pl.BlockSpec(memory_space=pl.ANY)
    inside = pl.BlockSpec(memory_space=pltpu.VMEM)
    copies = 96
    out, tokens_grad, grad_qkv, grad_out_w, grad_in, grad_fc2, vector_grad = pl.pallas_call(
        partial(slot_kernel, devices, depth, features),
        out_shape=(
            jax.ShapeDtypeStruct(tokens.shape, BF16),
            jax.ShapeDtypeStruct(tokens.shape, BF16),
            jax.ShapeDtypeStruct((lines, 3 * D), F32),
            jax.ShapeDtypeStruct((lines, D), F32),
            jax.ShapeDtypeStruct((lines, features), F32),
            jax.ShapeDtypeStruct((features // count, D), F32),
            jax.ShapeDtypeStruct((8, 3 * block), F32),
        ),
        in_specs=[anywhere, anywhere, pl.BlockSpec(memory_space=pltpu.SMEM), inside] + [anywhere] * 4,
        out_specs=(inside,) * 7,
        scratch_shapes=[
            low(D, 3 * D // 2),
            low(D // 2, D),
            low(D, features // 2),
            low(features // 2, D),
            low(total, D),
            low(total, D),
            low(total, D),
            low(total, D),
            low(rows, D),
            low(total, 4 * block),
            low(chips - 1, rows, 4 * block),
            low(rows, D),
            pltpu.VMEM((slots, 128), jnp.int32),
            low(rows, 3 * D // 2),
            wide_f32(rows, D),
            wide_f32(rows, D),
            wide_f32(rows, D),
            wide_f32(rows, D),
            wide_f32(half, D),
            wide_f32(rows, D),
            wide_f32(rows, D),
            wide_f32(rows, D),
            wide_f32(rows, features // 2),
            low(rows, features // 2),
            low(total, wide),
            low(total, wide),
            low(chips, 2 * wide // depth, D),
            low(chips - 1, 2 * wide // depth, D),
            low(D, wide),
            low(wide, D),
            low(depth, devices * lines, 4 * block),
            low(depth - 1, devices * lines, 4 * block),
            low(depth - 1, devices * lines, 4 * block),
            low(devices, lines, wide),
            low(devices, lines, wide),
            low(devices, lines + 16, 4 * block),
            low(devices, lines + 16, 4 * block),
            wide_f32(16, D),
            wide_f32(devices * depth, 4 * block),
            wide_f32(depth - 1, devices, 4 * block),
            wide_f32(rows, 4 * block),
            low(rows, 3 * D // 2),
            low(half, D),
            low(*tokens.shape),
            low(half, D),
            low(*tokens.shape),
            pltpu.VMEM((slots, 128), jnp.int32),
            pltpu.SemaphoreType.DMA((6 * chips,)),
            pltpu.SemaphoreType.DMA((copies,)),
            pltpu.SemaphoreType.DMA((copies,)),
        ],
        compiler_params=pltpu.CompilerParams(
            collective_id=0, has_side_effects=True, vmem_limit_bytes=64 * 1024 * 1024 - 64 * 1024
        ),
        name="slot",
    )(tokens, out_grad, lengths, vectors, w_qkv, w_out, w_in, w_fc2)
    size = moment_one.shape[1] // 128
    padded = (size + 279) // 280 * 280
    flat = jax.ShapeDtypeStruct(moment_one.shape, F32)
    return pl.pallas_call(
        partial(adam_kernel, count),
        out_shape=(
            jax.ShapeDtypeStruct(tokens.shape, BF16),
            jax.ShapeDtypeStruct(tokens.shape, BF16),
            flat,
            flat,
            flat,
            flat,
        ),
        in_specs=[inside] * 8 + [anywhere] * 6,
        out_specs=(inside, inside) + (anywhere,) * 4,
        scratch_shapes=[wide_f32(padded, 128)] * 4
        + [
            low(lines, 3 * D),
            low(lines, D),
            low(lines, features),
            low(features // count, D),
            wide_f32(vectors.shape[0] * D // 128, 128),
            pltpu.SemaphoreType.DMA((2, 5)),
            pltpu.SemaphoreType.DMA((4,)),
            pltpu.SemaphoreType.DMA((4, 5)),
        ],
        compiler_params=pltpu.CompilerParams(vmem_limit_bytes=64 * 1024 * 1024 - 64 * 1024),
        name="adam",
    )(
        grad_qkv, grad_out_w, grad_in, grad_fc2, vector_grad, vectors, out, tokens_grad,
        w_qkv, w_out, w_in, w_fc2, moment_one, moment_two,
    )


def layer(tokens, *rest):
    slots, piece, width = tokens.shape
    devices, depth = lax.axis_size("dp"), lax.axis_size("ctx")
    fits = slots == 2 and depth == 2 * slots and devices == 2 * depth and FF == (devices // 2) * D
    if fits and (H * HD // devices) % 128 == 0 and (FF // devices) % 128 == 0:
        return slot_body(tokens, *rest)
    return body(tokens, *rest)


def solution(mesh):
    placed = (
        P("dp", "ctx", None),
        P("dp", "ctx", None),
        P("dp"),
        P(),
        P(),
        P(),
        P(),
        P(),
        P(("dp", "ctx"), None),
        P(("dp", "ctx"), None),
    )
    return jax.shard_map(
        layer,
        mesh=mesh,
        in_specs=placed,
        out_specs=(
            P("dp", "ctx", None),
            P("dp", "ctx", None),
            P(("dp", "ctx"), None),
            P(("dp", "ctx"), None),
            P(("dp", "ctx"), None),
            P(("dp", "ctx"), None),
        ),
        check_vma=False,
    )
```

```python
from functools import partial

import jax
import jax.numpy as jnp
from jax import lax
from jax.experimental import pallas as pl
from jax.experimental.pallas import tpu as pltpu
from jax.sharding import PartitionSpec as P

D = 1024
H = 16
HD = 64
FF = 4096


EPSILON = 1e-05
learn_rate = 0.01
beta_one = 0.9
beta_two = 0.999
adam_eps = 1e-08
decay_rate = 0.01
step_count = 10.0


def layer_norm(values, gain, shift):
    center = values - jnp.mean(values, axis=-1, keepdims=True)
    spread = jnp.mean(center * center, axis=-1, keepdims=True)
    return center * lax.rsqrt(spread + EPSILON) * gain + shift


def split_vectors(vectors):
    ratio = FF // D
    return (
        vectors[0],
        vectors[1],
        vectors[2],
        vectors[3 : 3 + ratio].reshape(FF),
        vectors[3 + ratio],
        vectors[4 + ratio],
        vectors[5 + ratio],
        vectors[6 + ratio],
        vectors[7 + ratio],
    )


def inner(left, right):
    return lax.dot_general(
        left, right, (((0,), (0,)), ((), ())), preferred_element_type=jnp.float32
    )


def through(left, weight):
    return lax.dot_general(
        left, weight, (((1,), (1,)), ((), ())), preferred_element_type=jnp.float32
    )


def run_slots(function, items):
    return lax.map(lambda item: function(*item), items)


def heads_block():
    return 4


def split_heads(matrix):
    count = matrix.shape[0]
    group = heads_block()
    return jnp.moveaxis(matrix.reshape(count, H // group, group, HD), 1, 0)


def join_heads(blocked):
    return jnp.moveaxis(blocked, 0, 1).reshape(blocked.shape[1], H * HD)


def split_stats(stats):
    group = heads_block()
    return stats.reshape(H // group, group, stats.shape[-1])


def shard_piece(left, right, number, shard_count):
    weight_rows = left.shape[1]
    columns = right.shape[1]
    per_shard = weight_rows * columns // shard_count
    block = inner(left, right).reshape(-1)
    return block.reshape(number, per_shard)


def project(flat_tokens, w_qkv, vectors):
    joined = jnp.dot(flat_tokens, w_qkv, preferred_element_type=jnp.float32)
    queries = ((joined[:, :D] + vectors[0]) * 0.125).astype(jnp.bfloat16)
    keys = joined[:, D : 2 * D].astype(jnp.bfloat16)
    values = (joined[:, 2 * D :] + vectors[1]).astype(jnp.bfloat16)
    return (queries, keys, values)


def attend_slot(queries, keys, values, live):
    rows = queries.shape[0]

    def attend_one_block(item):
        query_heads, key_heads, value_heads = item
        scores = jnp.einsum(
            "qhd,khd->hqk", query_heads, key_heads, preferred_element_type=jnp.float32
        )
        scores = jnp.where(live[None, None, :], scores, -1e30)
        maximum = jnp.max(scores, axis=-1, keepdims=True)
        expo = jnp.exp(scores - maximum)
        total = jnp.sum(expo, axis=-1, keepdims=True)
        probs_low = (expo / total).astype(jnp.bfloat16)
        mixed = jnp.einsum(
            "hqk,khd->qhd", probs_low, value_heads, preferred_element_type=jnp.float32
        )
        return (mixed, (maximum + jnp.log(total))[..., 0])

    mixed, log_total = lax.map(
        attend_one_block, (split_heads(queries), split_heads(keys), split_heads(values))
    )
    return (join_heads(mixed), log_total.reshape(H, rows))


def query_back(queries, keys, values, live, log_total, grad_mixed, with_keys):
    rows = queries.shape[0]

    def query_one_block(item):
        query_heads, key_heads, value_heads, grad_heads, block_log = item
        scores = jnp.einsum(
            "qhd,khd->hqk", query_heads, key_heads, preferred_element_type=jnp.float32
        )
        scores = jnp.where(live[None, None, :], scores, -1e30)
        probs = jnp.exp(scores - block_log[:, :, None])
        grad_probs = jnp.einsum(
            "qhd,khd->hqk", grad_heads, value_heads, preferred_element_type=jnp.float32
        )
        row_sums = jnp.sum(probs * grad_probs, axis=-1)
        grad_scores = (probs * (grad_probs - row_sums[:, :, None])).astype(jnp.bfloat16)
        grad_query = jnp.einsum(
            "hqk,khd->qhd", grad_scores, key_heads, preferred_element_type=jnp.float32
        )
        grad_key = jnp.einsum(
            "hqk,qhd->khd", grad_scores, query_heads, preferred_element_type=jnp.float32
        )
        grad_value = jnp.einsum(
            "hqk,qhd->khd",
            probs.astype(jnp.bfloat16),
            grad_heads,
            preferred_element_type=jnp.float32,
        )
        return (grad_query, row_sums, grad_key, grad_value)

    items = (
        split_heads(queries),
        split_heads(keys),
        split_heads(values),
        split_heads(grad_mixed),
        split_stats(log_total),
    )
    results = lax.map(query_one_block, items)
    grad_query, row_sums, grad_key, grad_value = results
    return (
        join_heads(grad_query),
        row_sums.reshape(H, rows),
        join_heads(grad_key),
        join_heads(grad_value),
    )


def tail(flat_tokens, mixed, w_out, w_in, w_fc2, vectors):
    bias_q, bias_v, bias_o, bias_in, bias_fc2, gain_one, shift_one, gain_two, shift_two = (
        split_vectors(vectors)
    )
    mixed_low = mixed.astype(jnp.bfloat16)
    summed_one = (
        flat_tokens.astype(jnp.float32)
        + jnp.dot(mixed_low, w_out, preferred_element_type=jnp.float32)
        + bias_o
    )
    normed = layer_norm(summed_one, gain_one, shift_one)
    normed_low = normed.astype(jnp.bfloat16)
    hidden_pre = jnp.dot(normed_low, w_in, preferred_element_type=jnp.float32) + bias_in
    hidden_low = jax.nn.gelu(hidden_pre, approximate=False).astype(jnp.bfloat16)
    summed_two = normed + jnp.dot(hidden_low, w_fc2, preferred_element_type=jnp.float32) + bias_fc2
    result = layer_norm(summed_two, gain_two, shift_two)
    return (mixed_low, summed_one, normed_low, hidden_pre, hidden_low, summed_two, result)


def body(tokens, out_grad, lengths, w_qkv, w_out, w_in, w_fc2, vectors, moment_one, moment_two):
    slots, piece, width = tokens.shape
    length = piece * lax.axis_size("ctx")
    local_pos = lax.axis_index("ctx") * piece + jnp.arange(piece, dtype=jnp.int32)
    own_live = local_pos[None, :] < lengths[:, None]
    valid = own_live.astype(jnp.float32)
    key_live = jnp.arange(length, dtype=jnp.int32)[None, :] < lengths[:, None]
    bias_q, bias_v, bias_o, bias_in, bias_fc2, gain_one, shift_one, gain_two, shift_two = (
        split_vectors(vectors)
    )
    flat_tokens = tokens.reshape(slots * piece, width)
    queries, keys, values = project(flat_tokens, w_qkv, vectors)
    keys_all, values_all = (
        lax.all_gather(keys.reshape(slots, piece, width), "ctx", axis=1, tiled=True),
        lax.all_gather(values.reshape(slots, piece, width), "ctx", axis=1, tiled=True),
    )
    mixed, log_total = run_slots(
        attend_slot, (queries.reshape(slots, piece, width), keys_all, values_all, key_live)
    )
    saved = tail(flat_tokens, mixed.reshape(slots * piece, width), w_out, w_in, w_fc2, vectors)
    out = (saved[6].reshape(slots, piece, width) * valid[..., None]).astype(jnp.bfloat16)
    again = lax.optimization_barrier(flat_tokens)
    queries, keys, values = project(again, w_qkv, vectors)
    keys_all, values_all = (
        lax.all_gather(keys.reshape(slots, piece, width), "ctx", axis=1, tiled=True),
        lax.all_gather(values.reshape(slots, piece, width), "ctx", axis=1, tiled=True),
    )
    mixed, log_total = run_slots(
        attend_slot, (queries.reshape(slots, piece, width), keys_all, values_all, key_live)
    )
    saved = tail(again, mixed.reshape(slots * piece, width), w_out, w_in, w_fc2, vectors)
    mixed_low, summed_one, normed_low, hidden_pre, hidden_low, summed_two, result = saved
    cotangent = (out_grad.astype(jnp.float32) * valid[..., None]).reshape(slots * piece, width)
    unused_two, norm_two_back = jax.vjp(layer_norm, summed_two, gain_two, shift_two)
    grad_two, grad_gain_two, grad_shift_two = norm_two_back(cotangent)
    grad_fc2_low = grad_two.astype(jnp.bfloat16)
    bias_fc2_grad = jnp.sum(grad_fc2_low.astype(jnp.float32), axis=0)
    grad_hidden = through(grad_fc2_low, w_fc2)
    unused_gelu, gelu_back = jax.vjp(partial(jax.nn.gelu, approximate=False), hidden_pre)
    grad_pre_low = gelu_back(grad_hidden)[0].astype(jnp.bfloat16)
    bias_in_grad = jnp.sum(grad_pre_low.astype(jnp.float32), axis=0)
    grad_normed = grad_two + through(grad_pre_low, w_in)
    unused_one, norm_one_back = jax.vjp(layer_norm, summed_one, gain_one, shift_one)
    grad_one, grad_gain_one, grad_shift_one = norm_one_back(grad_normed)
    grad_branch_low = grad_one.astype(jnp.bfloat16)
    bias_out_grad = jnp.sum(grad_branch_low.astype(jnp.float32), axis=0)
    grad_mixed_low = (
        through(grad_branch_low, w_out).astype(jnp.bfloat16).reshape(slots, piece, width)
    )
    queries_slots = queries.reshape(slots, piece, width)
    grad_query, row_sums, grad_key, grad_value = run_slots(
        partial(query_back, with_keys=True),
        (queries_slots, keys_all, values_all, key_live, log_total, grad_mixed_low),
    )
    grad_key, grad_value = (
        lax.psum_scatter(
            grad_key.astype(jnp.bfloat16), "ctx", scatter_dimension=1, tiled=True
        ).astype(jnp.float32),
        lax.psum_scatter(
            grad_value.astype(jnp.bfloat16), "ctx", scatter_dimension=1, tiled=True
        ).astype(jnp.float32),
    )
    rows = slots * piece
    grad_query_low = grad_query.reshape(rows, width).astype(jnp.bfloat16) * jnp.bfloat16(0.125)
    grad_key_low = grad_key.reshape(rows, width).astype(jnp.bfloat16)
    grad_value_low = grad_value.reshape(rows, width).astype(jnp.bfloat16)
    grad_joined = jnp.concatenate([grad_query_low, grad_key_low, grad_value_low], axis=1)
    bias_q_grad = jnp.sum(grad_query_low.astype(jnp.float32), axis=0)
    bias_v_grad = jnp.sum(grad_value_low.astype(jnp.float32), axis=0)
    tokens_grad = (
        (grad_one + through(grad_joined, w_qkv)).reshape(slots, piece, width).astype(jnp.bfloat16)
    )
    vector_grad = jnp.concatenate(
        [
            bias_q_grad[None],
            bias_v_grad[None],
            bias_out_grad[None],
            bias_in_grad.reshape(FF // D, D),
            bias_fc2_grad[None],
            grad_gain_one[None],
            grad_shift_one[None],
            grad_gain_two[None],
            grad_shift_two[None],
        ],
        axis=0,
    )
    count = lax.axis_size(("dp", "ctx"))
    vector_rows = vector_grad.reshape(count, -1)
    pairs = (
        (flat_tokens, grad_joined),
        (mixed_low, grad_branch_low),
        (normed_low, grad_pre_low),
        (hidden_low, grad_fc2_low),
    )
    blocks = [
        shard_piece(left, right, 1 * lax.axis_size(("dp", "ctx")), count) for left, right in pairs
    ]
    blocks.append(vector_rows)
    grad_rows = lax.psum_scatter(
        jnp.concatenate(blocks, axis=1), ("dp", "ctx"), scatter_dimension=0, tiled=True
    )
    index = lax.axis_index(("dp", "ctx"))
    params = jnp.concatenate(
        [
            lax.dynamic_slice_in_dim(weight.reshape(count, -1), index, 1, 0).astype(jnp.float32)
            for weight in (w_qkv, w_out, w_in, w_fc2, vectors)
        ],
        axis=1,
    )
    new_one = beta_one * moment_one + (1.0 - beta_one) * grad_rows
    new_two = beta_two * moment_two + (1.0 - beta_two) * grad_rows * grad_rows
    fix_one = 1.0 - beta_one**step_count
    fix_two = 1.0 - beta_two**step_count
    update = new_one / fix_one / (jnp.sqrt(new_two / fix_two) + adam_eps)
    new_params = params - learn_rate * (update + decay_rate * params)
    return (out, tokens_grad, grad_rows, new_params, new_one, new_two)


BF16 = jnp.bfloat16
F32 = jnp.float32


def layer_norm_stats(values):
    center = values - jnp.mean(values, axis=-1, keepdims=True)
    spread = jnp.mean(center * center, axis=-1, keepdims=True)
    return center, lax.rsqrt(spread + EPSILON)


def layer_norm_back(center, scale, gain, cotangent):
    scaled = cotangent * gain
    mean_scaled = jnp.mean(scaled, axis=-1, keepdims=True)
    mean_cross = jnp.mean(scaled * center, axis=-1, keepdims=True)
    return scale * (scaled - mean_scaled - center * (scale * scale) * mean_cross)


def normal_cdf(values):
    return 0.5 * (1.0 + lax.erf(values * 0.7071067811865476))


def dot(left, right):
    return jnp.dot(left, right, preferred_element_type=F32)


def positions(axis, shape, slot, piece):
    place = lax.broadcasted_iota(jnp.int32, shape, axis)
    block = lax.div(place, piece)
    half = lax.div(block, 2)
    step = lax.rem(block, 2)
    return (2 * half + lax.rem(slot + step, 2)) * piece + lax.rem(place, piece)


def head_probs(queries, keys, live):
    scores = through(queries, keys)
    scores = jnp.where(live, scores, -1e30)
    expo = jnp.exp(scores - jnp.max(scores, axis=-1, keepdims=True))
    return expo / jnp.sum(expo, axis=-1, keepdims=True)


MESH = pl.DeviceIdType.MESH


class Links:
    def __init__(self, sends, recvs):
        self.sends, self.recvs = sends, recvs
        self.used = 0
        self.open = []

    def copy(self, source, target, device):
        self.used += 1
        return self.again(source, target, device)

    def again(self, source, target, device):
        number = self.used - 1
        return pltpu.make_async_remote_copy(
            src_ref=source,
            dst_ref=target,
            send_sem=self.sends.at[number],
            recv_sem=self.recvs.at[number],
            device_id=device,
            device_id_type=MESH,
        )

    def forward(self, source, target, device, earlier):
        self.used += 1
        return pltpu.make_async_remote_copy(
            src_ref=source,
            dst_ref=target,
            send_sem=self.sends.at[self.used - 1],
            recv_sem=self.recvs.at[earlier],
            device_id=device,
            device_id_type=MESH,
        )

    def send(self, source, target, device):
        made = self.copy(source, target, device)
        made.start()
        self.open.append((made, None))
        return made

    def send_if(self, condition, source, target, device):
        made = self.copy(source, target, device)
        pl.when(condition)(made.start)
        self.open.append((made, condition))
        return made

    def send_or_keep(self, here, source, target, device):
        number = self.used
        made = self.copy(source, target, device)
        local = pltpu.make_async_copy(source, target, self.recvs.at[number])
        pl.when(here)(local.start)
        away = jnp.logical_not(here)
        pl.when(away)(made.start)
        self.open.append((made, away))

        def wait():
            pl.when(here)(local.wait)
            pl.when(away)(made.wait_recv)

        return wait

    def close(self):
        for made, condition in self.open:
            if condition is None:
                made.wait_send()
            else:
                pl.when(condition)(made.wait_send)


def flip(value, mask):
    result = value
    bit = 1
    while bit <= mask:
        if mask & bit:
            result = result + bit * (1 - 2 * lax.rem(lax.div(value, bit), 2))
        bit *= 2
    return result


def flip_traced(value, mask, size):
    result = value
    bit = 1
    while bit < size:
        set_bit = lax.rem(lax.div(mask, bit), 2)
        result = result + bit * set_bit * (1 - 2 * lax.rem(lax.div(value, bit), 2))
        bit *= 2
    return result


def at_rows(start, size):
    return pl.ds(pl.multiple_of(start, 64), size)


def slot_kernel(devices, depth, features, *refs):
    (
        tokens, out_grad, lengths, vec, w_qkv, w_out, w_in, w_fc2,
        out_ref, tgrad_ref, g_qkv, g_out, g_in, g_fc2, g_vec,
        wqkv, wo, w_up, w_down,
        x_all, n_all, g_all, m_all, b_all, j_all, j_send, g_rows, lens_peer,
        qkv, part, part_a, part_b, part_c, part_d, summed, grad_two, grad_one,
        pre_s, hid, hid_all, gp_all, packed, plane_got, up_mine, down_mine, packed_two, right_two, left_two,
        trade_in, got_in, trade_qkv, got_qkv, vec_s, vec_by, vec_got, sums, dqkv, out_half, out_got, tg_half, tg_got, lens,
        local_sems, sends, recvs,
    ) = refs
    chips = devices // 2
    me, slot = lax.axis_index("dp"), lax.axis_index("ctx")
    core, chip = lax.rem(me, 2), lax.div(me, 2)
    base = me - core
    peer = (base + 1 - core, slot)
    piece = tokens.shape[1]
    half = 2 * piece
    rows = 2 * half
    block = D // devices
    wide = features // devices
    lines = D // (devices * depth)
    net = Links(sends, recvs)
    mine_at = at_rows(core * half, half)
    other_at = at_rows((1 - core) * half, half)
    chunk = 32

    row_of = lax.broadcasted_iota(jnp.int32, lens.shape, 0)
    lens[...] = jnp.where(row_of == 0, lengths[0], lengths[1])
    vec_s[...] = jnp.zeros_like(vec_s)
    loads = []

    def load(source, target):
        made = pltpu.make_async_copy(source, target, local_sems.at[len(loads)])
        made.start()
        loads.append(made)

    where = [2 * flip(chip, mask) + core for mask in range(chips)]
    for mask in range(chips):
        for kind in range(3):
            start = pl.multiple_of(kind * D + where[mask] * block, block)
            load(
                w_qkv.at[:, pl.ds(start, block)],
                wqkv.at[:, (3 * mask + kind) * block : (3 * mask + kind + 1) * block],
            )
    n_qkv = len(loads)
    for number in range(chips):
        start = pl.multiple_of((2 * number + core) * block, block)
        load(w_out.at[pl.ds(start, block), :], wo.at[number * block : (number + 1) * block, :])
    n_out = len(loads)
    for mask in range(chips):
        start = pl.multiple_of(where[mask] * wide, wide)
        load(w_in.at[:, pl.ds(start, wide)], w_up.at[:, mask * wide : (mask + 1) * wide])
    n_up = len(loads)
    for mask in range(chips):
        start = pl.multiple_of(where[mask] * wide, wide)
        load(w_fc2.at[pl.ds(start, wide), :], w_down.at[mask * wide : (mask + 1) * wide, :])

    barrier = pltpu.get_barrier_semaphore()
    friends = [(flip(me, mask), slot) for mask in range(1, devices)]
    for shift in range(1, depth):
        far = lax.rem(slot + shift, depth)
        friends += [(me, far), (flip(me, 1), far)]
    for friend in friends:
        pl.semaphore_signal(barrier, inc=1, device_id=friend, device_id_type=MESH)
    pl.semaphore_wait(barrier, len(friends))

    def spread(source, target):
        waits = []
        for step in range(2):
            pick = lax.rem(slot + step, 2)
            upper = lax.div(slot, 2)
            place = 2 * core + pick
            here = jnp.logical_and(upper == core, place == slot)
            waits.append(
                net.send_or_keep(
                    here,
                    source.at[pick],
                    target.at[at_rows((2 * upper + step) * piece, piece)],
                    (base + upper, place),
                )
            )
        return waits

    def pass_on(waits, target):
        made = []
        for step, wait in enumerate(waits):
            wait()
            spot = target.at[at_rows((2 * core + step) * piece, piece)]
            made.append(net.send(spot, spot, peer))
        return made

    token_waits = spread(tokens, x_all)
    grad_waits = spread(out_grad, g_rows)
    lens_copy = net.send(lens, lens_peer, peer)
    token_passes = pass_on(token_waits, x_all)

    def plane_start(target):
        source = target.at[mine_at]
        return [
            net.send(
                source, target.at[at_rows(mask * rows + core * half, half)], (flip(me, 2 * mask), slot)
            )
            for mask in range(1, chips)
        ]

    def plane_pass(copies, target):
        made = []
        for mask, copy in enumerate(copies, 1):
            copy.wait_recv()
            spot = target.at[at_rows(mask * rows + core * half, half)]
            made.append(net.send(spot, spot, peer))
        return made

    class Column:
        def __init__(self, target):
            self.target = target
            self.parts, self.numbers = {}, {}
            for place in (2, 1, 3):
                far = lax.rem(slot + depth - place, depth)
                made = net.copy(target.at[mine_at], self.spot(place), (me, far))
                self.parts[place], self.numbers[place] = made, net.used - 1
                goes = {1: slot != 0, 2: slot >= 0, 3: slot != depth - 1}[place]
                net.open.append((made, goes))
                pl.when(goes)(made.start)
            self.passes = {}

        def spot(self, place):
            return self.target.at[at_rows(place * rows + core * half, half)]

        def relay(self):
            self.parts[2].wait_recv()
            up = net.forward(self.spot(2), self.spot(1), (me, depth - 1), self.numbers[1])
            down = net.forward(self.spot(2), self.spot(3), (me, 0), self.numbers[3])
            for made, here in ((up, slot == 2), (down, slot == 1)):
                pl.when(here)(made.start)
                net.open.append((made, here))
            self.passes[2] = net.send(self.spot(2), self.spot(2), peer)

        def hand_over(self, place):
            self.parts[place].wait_recv()
            self.passes[place] = net.send(self.spot(place), self.spot(place), peer)

    x_plane = plane_start(x_all)
    for made in loads[:n_qkv]:
        made.wait()
    lens_copy.wait_recv()
    for made in token_passes:
        made.wait_recv()
    owned = jnp.where(lax.div(slot, 2) == core, lens[...], lens_peer[...])
    length = jnp.where(lax.rem(slot, 2) == 0, owned[0:1, 0:1], owned[1:2, 0:1])
    live = positions(1, (1, rows), slot, piece) < length
    lane = lax.broadcasted_iota(jnp.int32, (1, block), 1)

    @pl.loop(0, chips)
    def _(mask):
        spot = 2 * flip_traced(chip, mask, chips) + core
        lanes = pl.ds(pl.multiple_of(spot * block, block), block)
        joined = dot(x_all[0:rows, :], wqkv[:, pl.ds(pl.multiple_of(mask * 3 * block, block), 3 * block)])
        queries = ((joined[:, 0:block] + vec[0:1, lanes]) * 0.125).astype(BF16)
        keys = joined[:, block : 2 * block].astype(BF16)
        values = (joined[:, 2 * block :] + vec[1:2, lanes]).astype(BF16)
        total = jnp.zeros((rows, block), F32)
        for head in range(block // HD):
            mine = lax.div(lane, HD) == head
            probs = head_probs(jnp.where(mine, queries, jnp.zeros_like(queries)), keys, live)
            total = jnp.where(mine, dot(probs.astype(BF16), values), total)
        start = pl.multiple_of(mask * 3 * block, block)
        qkv[:, pl.ds(start, block)] = queries
        qkv[:, pl.ds(pl.multiple_of(start + block, block), block)] = keys
        qkv[:, pl.ds(pl.multiple_of(start + 2 * block, block), block)] = values
        lanes = pl.ds(pl.multiple_of(core * chips * block + lax.div(spot, 2) * block, block), block)
        m_all[0:rows, lanes] = total.astype(BF16)

    for made in loads[n_qkv:n_out]:
        made.wait()

    def exchange(compute, target, before):
        made = []
        for number, at in enumerate((other_at, mine_at)):
            if before is not None:
                before[number].wait_send()
            part[at, :] = compute(at)
            made.append(net.copy(part.at[at], target.at[at], peer))
            made[-1].start()
        return made

    my_lanes = pl.ds(pl.multiple_of(core * chips * block, chips * block), chips * block)
    first = exchange(lambda at: dot(m_all[at, my_lanes], wo[...]), part_a, None)
    own_mixed = m_all.at[0:rows, my_lanes]
    m_passes = [net.send(own_mixed, own_mixed, peer)]
    m_plane = [
        net.send(own_mixed, m_all.at[mask * rows : (mask + 1) * rows, my_lanes], (flip(me, 2 * mask), slot))
        for mask in range(1, chips)
    ]
    grad_passes = pass_on(grad_waits, g_rows)

    def norm_one(start):
        @pl.loop(0, half // chunk)
        def _(step):
            at = pl.ds(pl.multiple_of(start + step * chunk, chunk), chunk)
            total = x_all[at, :].astype(F32) + (part[at, :] + part_a[at, :]) + vec[2:3, :]
            center, scale = layer_norm_stats(total)
            summed[at, :] = total
            n_all[at, :] = (center * scale * vec[8:9, :] + vec[9:10, :]).astype(BF16)

    first[0].wait_recv()
    norm_one(core * half)
    n_column = Column(n_all)
    first[1].wait_recv()
    norm_one((1 - core) * half)
    for made in loads[n_out:]:
        made.wait()

    for number in range(chips):
        fine_cols = wide // depth
        begin = flip_traced(chip, number, chips) * wide + slot * fine_cols
        at = pl.ds(pl.multiple_of(begin, fine_cols), fine_cols)
        up_mine[:, number * fine_cols : (number + 1) * fine_cols] = w_up[:, at]
        down_mine[number * fine_cols : (number + 1) * fine_cols, :] = w_down[at, :]

    def bias_of(mask):
        spot = flip_traced(chip, mask, chips)
        lanes = pl.ds(pl.multiple_of(core * wide, wide), wide)
        result = vec[3:4, lanes]
        for row in range(1, chips):
            result = jnp.where(spot == row, vec[3 + row : 4 + row, lanes], result)
        return result

    @pl.loop(0, chips)
    def _(mask):
        at = pl.ds(pl.multiple_of(mask * wide, wide), wide)
        value = dot(n_all[0:rows, :], w_up[:, at]) + bias_of(mask)
        pre_s[:, at] = value
        hid[:, at] = (value * normal_cdf(value)).astype(BF16)

    second = exchange(lambda at: dot(hid[at, :], w_down[...]), part_b, first)
    for made in grad_passes:
        made.wait_recv()

    def norm_two(start, own):
        @pl.loop(0, half // chunk)
        def _(step):
            begin = pl.multiple_of(start + step * chunk, chunk)
            at = pl.ds(begin, chunk)
            center, scale = layer_norm_stats(summed[at, :])
            normed = center * scale * vec[8:9, :] + vec[9:10, :]
            center, scale = layer_norm_stats(normed + (part[at, :] + part_b[at, :]) + vec[7:8, :])
            place = begin + lax.broadcasted_iota(jnp.int32, (chunk, 1), 0)
            piece_of = lax.div(place, piece)
            spot = 2 * lax.div(piece_of, 2) + lax.rem(slot + lax.rem(piece_of, 2), 2)
            valid = (spot * piece + lax.rem(place, piece) < length).astype(F32)
            unit = center * scale
            error = g_rows[at, :].astype(F32) * valid
            grad = layer_norm_back(center, scale, vec[10:11, :], error)
            grad_two[at, :] = grad
            low = grad.astype(BF16)
            g_all[at, :] = low
            if own:
                out_half[pl.ds(pl.multiple_of(step * chunk, chunk), chunk), :] = (
                    valid * (unit * vec[10:11, :] + vec[11:12, :])
                ).astype(BF16)
                vec_s[7:8, :] += jnp.sum(low.astype(F32), axis=0, keepdims=True)
                vec_s[10:11, :] += jnp.sum(error * unit, axis=0, keepdims=True)
                vec_s[11:12, :] += jnp.sum(error, axis=0, keepdims=True)

    def go_back(source, target):
        waits = []
        for step in range(2):
            place = 2 * core + lax.rem(slot + step, 2)
            upper = lax.div(slot, 2)
            here = jnp.logical_and(upper == core, place == slot)
            waits.append(
                net.send_or_keep(
                    here,
                    source.at[step * piece : (step + 1) * piece],
                    target.at[lax.rem(slot, 2)],
                    (base + upper, place),
                )
            )
        return waits

    second[0].wait_recv()
    norm_two(core * half, True)
    g_column = Column(g_all)
    second[1].wait_recv()
    norm_two((1 - core) * half, False)
    def mixed_pass():
        for mask, made in enumerate(m_plane, 1):
            made.wait_recv()
            spot = m_all.at[mask * rows : (mask + 1) * rows, my_lanes]
            m_passes.append(net.send(spot, spot, peer))


    def slope_of(value, cdf):
        return cdf + value * (jnp.exp(-0.5 * value * value) * 0.3989422804014327)

    @pl.loop(0, chips)
    def _(mask):
        at = pl.ds(pl.multiple_of(mask * wide, wide), wide)
        value = pre_s[:, at]
        grad = through(g_all[0:rows, :], w_down[at, :])
        hid[:, at] = (grad * slope_of(value, normal_cdf(value))).astype(BF16)

    third = exchange(lambda at: through(hid[at, :], w_up[...]), part_c, second)

    def norm_one_back(start, own):
        @pl.loop(0, half // chunk)
        def _(step):
            at = pl.ds(pl.multiple_of(start + step * chunk, chunk), chunk)
            center, scale = layer_norm_stats(summed[at, :])
            error = grad_two[at, :] + (part[at, :] + part_c[at, :])
            grad = layer_norm_back(center, scale, vec[8:9, :], error)
            low = grad.astype(BF16)
            b_all[at, :] = low
            grad_one[at, :] = grad
            if own:
                vec_s[2:3, :] += jnp.sum(low.astype(F32), axis=0, keepdims=True)
                vec_s[8:9, :] += jnp.sum(error * (center * scale), axis=0, keepdims=True)
                vec_s[9:10, :] += jnp.sum(error, axis=0, keepdims=True)

    x_pass = plane_pass(x_plane, x_all)

    third[0].wait_recv()
    norm_one_back(core * half, True)
    third[1].wait_recv()
    norm_one_back((1 - core) * half, False)
    class Line:
        def __init__(self, chunks, from_left, from_right):
            self.chunks, self.from_left, self.from_right = chunks, from_left, from_right
            self.up, self.down, self.first_up, self.first_down = [], [], [], []
            after = (me, lax.rem(slot + 1, depth))
            before = (me, lax.rem(slot + depth - 1, depth))
            for order in range(depth - 1):
                top, low = depth - 1 - order, order
                spot = from_left.at[order]
                self.up.append(net.copy(spot, spot, after))
                self.first_up.append(net.again(chunks.at[top], spot, after))
                net.open.append((self.up[-1], slot < top))
                spot = from_right.at[order]
                self.down.append(net.copy(spot, spot, before))
                self.first_down.append(net.again(chunks.at[low], spot, before))
                net.open.append((self.down[-1], slot > low))

        def first(self):
            for order in range(depth - 1):
                pl.when(slot == 0)(self.first_up[order].start)
                pl.when(slot == depth - 1)(self.first_down[order].start)

        def stage(self, time):
            for order in range(time):
                top, low = depth - 1 - order, order

                @pl.when(slot == time - order)
                def _(order=order, top=top):
                    self.up[order].wait_recv()
                    if time < depth - 1:
                        self.from_left[order] = (
                            self.from_left[order].astype(F32) + self.chunks[top].astype(F32)
                        ).astype(BF16)
                        self.up[order].start()

                @pl.when(depth - 1 - slot == time - order)
                def _(order=order, low=low):
                    self.down[order].wait_recv()
                    if time < depth - 1:
                        self.from_right[order] = (
                            self.from_right[order].astype(F32) + self.chunks[low].astype(F32)
                        ).astype(BF16)
                        self.down[order].start()

    grad_parts = range(1, chips)

    def attention_back(mask):
        start = mask * 3 * block
        queries = qkv[:, start : start + block]
        keys = qkv[:, start + block : start + 2 * block]
        values = qkv[:, start + 2 * block : start + 3 * block]
        turn = pl.ds(pl.multiple_of(lax.div(where[mask], 2) * block, block), block)
        grad_mixed = through(b_all[0:rows, :], wo[turn, :]).astype(BF16)
        grad_q = jnp.zeros((rows, block), F32)
        grad_k = grad_q
        grad_v = grad_q
        for head in range(block // HD):
            mine = lax.div(lane, HD) == head
            probs = head_probs(jnp.where(mine, queries, jnp.zeros_like(queries)), keys, live)
            grad_probs = through(jnp.where(mine, grad_mixed, jnp.zeros_like(grad_mixed)), values)
            dsum = jnp.sum(probs * grad_probs, axis=-1, keepdims=True)
            grad_scores = (probs * (grad_probs - dsum)).astype(BF16)
            grad_q = jnp.where(mine, dot(grad_scores, keys), grad_q)
            grad_k = jnp.where(mine, inner(grad_scores, queries), grad_k)
            grad_v = jnp.where(mine, inner(probs.astype(BF16), grad_mixed), grad_v)
        grad_q = grad_q.astype(BF16) * jnp.bfloat16(0.125)
        grad_k = grad_k.astype(BF16)
        grad_v = grad_v.astype(BF16)
        spot = pl.ds(pl.multiple_of(where[mask] * block, block), block)
        vec_s[0:1, spot] = jnp.sum(grad_q.astype(F32), axis=0, keepdims=True)
        vec_s[1:2, spot] = jnp.sum(grad_v.astype(F32), axis=0, keepdims=True)
        dqkv[:, start : start + block] = grad_q
        dqkv[:, start + block : start + 2 * block] = grad_k
        dqkv[:, start + 2 * block : start + 3 * block] = grad_v
        if mask:
            joint = j_send.at[mask - 1]
        else:
            joint = j_all.at[0:rows]
        joint[:, 0:block] = grad_q
        joint[:, block : 2 * block] = grad_k
        joint[:, 2 * block : 3 * block] = grad_v
        joint[:, 3 * block : 4 * block] = b_all[0:rows, spot]
        if mask:
            return net.send(
                joint, j_all.at[mask * rows : (mask + 1) * rows], (flip(me, 2 * mask), slot)
            )
        return None

    j_copies = [attention_back(mask) for mask in grad_parts]
    n_column.relay()
    attention_back(0)
    mixed_pass()
    n_column.hand_over(1)
    n_column.hand_over(3)
    for made in third:
        made.wait_send()
    part[0:half, :] = through(dqkv[other_at, :], wqkv[...])
    tg_copy = net.copy(part.at[0:half], part_d, peer)
    tg_copy.start()
    part[half:rows, :] = grad_one[mine_at, :] + through(dqkv[mine_at, :], wqkv[...])
    tg_copy.wait_recv()
    tg_half[...] = (part[half:rows, :] + part_d[...]).astype(BF16)

    fine = wide // depth
    span = lines * depth
    features_at = pl.ds(pl.multiple_of((depth * core + slot) * fine, fine), fine)
    bias_mine = jnp.concatenate([vec[3 + number : 4 + number, features_at] for number in range(chips)], axis=1)

    def feed_rows(place):
        at = slice(place * rows, (place + 1) * rows)
        value = dot(n_all[at, :], up_mine[...]) + bias_mine
        cdf = normal_cdf(value)
        hid_all[at, :] = (value * cdf).astype(BF16)
        low = (through(g_all[at, :], down_mine[...]) * slope_of(value, cdf)).astype(BF16)
        gp_all[at, :] = low
        return jnp.sum(low.astype(F32), axis=0, keepdims=True)

    bias_sum = feed_rows(0)
    g_column.relay()
    for made in m_passes + x_pass + j_copies:
        made.wait_recv()
    for group in range(devices):
        at = slice(group * span, (group + 1) * span)
        begin = (group % 2) * chips * block + (group // 2) * block
        both = inner(x_all[:, at], j_all[:, 0 : 3 * block]).astype(BF16)
        across = inner(m_all[:, begin : begin + block], j_all[:, 3 * block : 4 * block]).astype(BF16)
        row = group * lines
        for number in range(depth):
            at = slice(number * lines, (number + 1) * lines)
            packed_two[number, row : row + lines, 0 : 3 * block] = both[at, :]
            packed_two[number, row : row + lines, 3 * block : 4 * block] = across[at, :]
    input_line = Line(packed_two, right_two, left_two)
    input_line.first()
    out_waits = go_back(out_half, out_got)

    g_column.hand_over(1)
    g_column.hand_over(3)
    for place in (2, 1, 3):
        n_column.passes[place].wait_recv()
        g_column.passes[place].wait_recv()
        bias_sum = bias_sum + feed_rows(place)
    for number in range(chips):
        vec_s[3 + number : 4 + number, features_at] = bias_sum[:, number * fine : (number + 1) * fine]
    depth_rows = D // chips
    for number in range(chips):
        block_up = inner(n_all[:, number * depth_rows : (number + 1) * depth_rows], gp_all[...]).astype(BF16)
        packed[number, fine : 2 * fine, 0:wide] = block_up[0:fine, :]
        packed[number, fine : 2 * fine, wide : 2 * wide] = block_up[fine : 2 * fine, :]

    def scatter_plane(lines_at):
        return [
            net.send(
                packed.at[flip_traced(chip, mask, chips), lines_at],
                plane_got.at[mask - 1, lines_at],
                (flip(me, 2 * mask), slot),
            )
            for mask in range(1, chips)
        ]

    up_copies = scatter_plane(slice(fine, 2 * fine))
    packed[:, 0:fine, :] = inner(hid_all[...], g_all[...]).astype(BF16).reshape(chips, fine, D)
    down_copies = scatter_plane(slice(0, fine))

    tiles = vec.shape[0] * D // 128
    share = tiles // (devices * depth)
    vec_by[...] = jnp.zeros_like(vec_by)
    for tile in range(tiles):
        owner, lane_group = tile // share, tile % share
        row, col = tile // (D // 128), (tile % (D // 128)) * 128
        spot = (owner % depth) * devices + owner // depth
        vec_by[spot : spot + 1, lane_group * 128 : (lane_group + 1) * 128] = vec_s[
            row : row + 1, col : col + 128
        ]
    vec_copies = []
    for shift in range(1, depth):
        far = lax.rem(slot + shift, depth)
        spot = vec_by.at[pl.ds(pl.multiple_of(far * devices, devices), devices)]
        vec_copies.append(net.send(spot, vec_got.at[shift - 1], (me, far)))

    def finish(line, target, rows_at):
        target[...] = line.chunks[slot, rows_at, :].astype(F32)

        @pl.when(slot >= 1)
        def _():
            target[...] += line.from_left[depth - 1 - slot, rows_at, :].astype(F32)

        @pl.when(slot <= depth - 2)
        def _():
            target[...] += line.from_right[slot, rows_at, :].astype(F32)

    def plane_sum(copies, lines_at):
        for made in copies:
            made.wait_recv()
        value = packed[chip, lines_at, :].astype(F32)
        for number in range(chips - 1):
            value = value + plane_got[number, lines_at, :].astype(F32)
        return value

    def trade(source, target):
        return [
            net.send(source.at[flip(me, mask)], target.at[me], (flip(me, mask), slot))
            for mask in range(1, devices)
        ]

    tg_waits = go_back(tg_half, tg_got)
    for time in range(1, depth - 1):
        input_line.stage(time)
    low_sum = plane_sum(up_copies, slice(fine, 2 * fine)).astype(BF16)
    for upper in range(2):
        for number in range(depth):
            trade_in[upper * depth + number] = low_sum[
                number * lines : (number + 1) * lines, upper * wide : (upper + 1) * wide
            ]
    here = core * depth + slot
    in_copies = []
    for shift in range(1, 2 * depth):
        far = lax.rem(slot + shift % depth, depth)
        upper = core if shift < depth else 1 - core
        in_copies.append(net.send(trade_in.at[upper * depth + far], got_in.at[here], (base + upper, far)))
    input_line.stage(depth - 1)
    tg_copy.wait_send()
    finish(input_line, sums, slice(0, rows))
    vec_sum = vec_by[pl.ds(pl.multiple_of(slot * devices, devices), devices), :]
    for number, made in enumerate(vec_copies):
        made.wait_recv()
        vec_sum = vec_sum + vec_got[number]
    first_row = lax.broadcasted_iota(jnp.int32, (16, 4 * block), 0) == 0
    for group in range(devices):
        trade_qkv[group, 0:lines, :] = sums[group * lines : (group + 1) * lines, :].astype(BF16)
        trade_qkv[group, lines : lines + 16, :] = jnp.where(
            first_row, vec_sum[group : group + 1, :], 0.0
        ).astype(BF16)
    qkv_copies = trade(trade_qkv, got_qkv)
    for made in in_copies:
        made.wait_recv()
    got_in[here] = trade_in[here]
    for group in range(2 * depth):
        for number in range(chips):
            start = number * 2 * wide + group * fine
            g_in[:, start : start + fine] = got_in[group, :, number * fine : (number + 1) * fine].astype(F32)
    g_fc2[...] = plane_sum(down_copies, slice(0, fine))
    for wait in out_waits + tg_waits:
        wait()
    out_ref[...] = out_got[...]
    tgrad_ref[...] = tg_got[...]
    for made in qkv_copies:
        made.wait_recv()
    got_qkv[me] = trade_qkv[me]
    vec_sum = jnp.zeros((16, 3 * block), F32)
    for group in range(devices):
        vec_sum = vec_sum + got_qkv[group, lines : lines + 16, 0 : 3 * block].astype(F32)
        got = got_qkv[group, 0:lines, :].astype(F32)
        for kind in range(3):
            g_qkv[:, kind * D + group * block : kind * D + (group + 1) * block] = got[
                :, kind * block : (kind + 1) * block
            ]
        g_out[:, group * block : (group + 1) * block] = got[:, 3 * block : 4 * block]
    g_vec[...] = vec_sum[0:8, :]
    net.close()


def adam_kernel(count, *refs):
    (
        g_qkv, g_out, g_in, g_fc2, g_vec, vec, out_in, tgrad_in, w_qkv, w_out, w_in, w_fc2, m_one, m_two,
        out_ref, tgrad_ref, rows_out, params_out, one_out, two_out,
        grads, params, one, two, b_qkv, b_out, b_in, b_fc2, vec_flat, in_sems, w_sems, out_sems,
    ) = refs
    index = lax.axis_index("dp") * lax.axis_size("ctx") + lax.axis_index("ctx")
    size = m_one.shape[1] // 128
    parts = in_sems.shape[1]
    step = grads.shape[0] // parts
    spans = [(number * step, min((number + 1) * step, size) - number * step) for number in range(parts)]
    loads = []
    for number, (start, length) in enumerate(spans):
        pair = []
        for kind, (source, target) in enumerate(((m_one, one), (m_two, two))):
            pair.append(
                pltpu.make_async_copy(
                    source.reshape(size, 128).at[start : start + length],
                    target.at[start : start + length],
                    in_sems.at[kind, number],
                )
            )
            pair[-1].start()
        loads.append(pair)
    weights = []
    for number, (source, target) in enumerate(
        ((w_qkv, b_qkv), (w_out, b_out), (w_in, b_in), (w_fc2, b_fc2))
    ):
        lines = target.shape[0]
        start = pl.multiple_of(index * lines, lines)
        weights.append(
            pltpu.make_async_copy(source.at[pl.ds(start, lines), :], target, w_sems.at[number])
        )
        weights[-1].start()
    out_ref[...] = out_in[...]
    tgrad_ref[...] = tgrad_in[...]

    def flatten(source, target, base):
        lines, groups = source.shape[0], source.shape[1] // 128
        for col in range(groups):
            value = source[:, col * 128 : (col + 1) * 128].astype(F32)
            for row in range(0, lines, 8):
                target[pl.ds(base + row * groups + col, 8, stride=groups), :] = value[row : row + 8, :]

    base = 0
    for grad in (g_qkv, g_out, g_in, g_fc2):
        flatten(grad, grads, base)
        base += grad.shape[0] * grad.shape[1] // 128
    share = g_vec.shape[1] // 128
    groups = vec.shape[1] // 128
    for col in range(groups):
        lanes = slice(col * 128, (col + 1) * 128)
        vec_flat[pl.ds(col, 8, stride=groups), :] = vec[0:8, lanes]
        for row in range(8, vec.shape[0]):
            vec_flat[row * groups + col : row * groups + col + 1, :] = vec[row : row + 1, lanes]
    place = lax.broadcasted_iota(jnp.int32, vec_flat.shape, 0)
    for number in range(share):
        grads[base + number : base + number + 1, :] = g_vec[0:1, number * 128 : (number + 1) * 128]
        params[base + number : base + number + 1, :] = jnp.sum(
            jnp.where(place == index * share + number, vec_flat[...], 0.0), axis=0, keepdims=True
        )
    base = 0
    for made, weight in zip(weights, (b_qkv, b_out, b_in, b_fc2)):
        made.wait()
        flatten(weight, params, base)
        base += weight.shape[0] * weight.shape[1] // 128
    fix_one = 1.0 / (1.0 - beta_one**step_count)
    fix_two = 1.0 / (1.0 - beta_two**step_count)
    copies = []
    for number, (start, length) in enumerate(spans):
        for made in loads[number]:
            made.wait()

        @pl.loop(0, step // 56)
        def _(chunk, start=start):
            at = pl.ds(pl.multiple_of(start + chunk * 56, 8), 56)
            grad, param = grads[at, :], params[at, :]
            new_one = beta_one * one[at, :] + (1.0 - beta_one) * grad
            new_two = beta_two * two[at, :] + (1.0 - beta_two) * grad * grad
            one[at, :] = new_one
            two[at, :] = new_two
            change = new_one * fix_one / (jnp.sqrt(new_two * fix_two) + adam_eps)
            params[at, :] = param - learn_rate * (change + decay_rate * param)

        for kind, (source, target) in enumerate(
            ((grads, rows_out), (params, params_out), (one, one_out), (two, two_out))
        ):
            copies.append(
                pltpu.make_async_copy(
                    source.at[start : start + length],
                    target.reshape(size, 128).at[start : start + length],
                    out_sems.at[kind, number],
                )
            )
            copies[-1].start()
    for made in copies:
        made.wait()


def slot_body(tokens, out_grad, lengths, w_qkv, w_out, w_in, w_fc2, vectors, moment_one, moment_two):
    slots, piece, width = tokens.shape
    devices, depth = lax.axis_size("dp"), lax.axis_size("ctx")
    chips = devices // 2
    count = devices * depth
    features = w_in.shape[1]
    half = 2 * piece
    rows = 2 * half
    block = D // devices
    wide = features // devices
    lines = D // count
    total = rows * chips
    low = lambda *shape: pltpu.VMEM(shape, BF16)
    wide_f32 = lambda *shape: pltpu.VMEM(shape, F32)
    anywhere = pl.BlockSpec(memory_space=pl.ANY)
    inside = pl.BlockSpec(memory_space=pltpu.VMEM)
    copies = 96
    out, tokens_grad, grad_qkv, grad_out_w, grad_in, grad_fc2, vector_grad = pl.pallas_call(
        partial(slot_kernel, devices, depth, features),
        out_shape=(
            jax.ShapeDtypeStruct(tokens.shape, BF16),
            jax.ShapeDtypeStruct(tokens.shape, BF16),
            jax.ShapeDtypeStruct((lines, 3 * D), F32),
            jax.ShapeDtypeStruct((lines, D), F32),
            jax.ShapeDtypeStruct((lines, features), F32),
            jax.ShapeDtypeStruct((features // count, D), F32),
            jax.ShapeDtypeStruct((8, 3 * block), F32),
        ),
        in_specs=[anywhere, anywhere, pl.BlockSpec(memory_space=pltpu.SMEM), inside] + [anywhere] * 4,
        out_specs=(inside,) * 7,
        scratch_shapes=[
            low(D, 3 * D // 2),
            low(D // 2, D),
            low(D, features // 2),
            low(features // 2, D),
            low(total, D),
            low(total, D),
            low(total, D),
            low(total, D),
            low(rows, D),
            low(total, 4 * block),
            low(chips - 1, rows, 4 * block),
            low(rows, D),
            pltpu.VMEM((slots, 128), jnp.int32),
            low(rows, 3 * D // 2),
            wide_f32(rows, D),
            wide_f32(rows, D),
            wide_f32(rows, D),
            wide_f32(rows, D),
            wide_f32(half, D),
            wide_f32(rows, D),
            wide_f32(rows, D),
            wide_f32(rows, D),
            wide_f32(rows, features // 2),
            low(rows, features // 2),
            low(total, wide),
            low(total, wide),
            low(chips, 2 * wide // depth, D),
            low(chips - 1, 2 * wide // depth, D),
            low(D, wide),
            low(wide, D),
            low(depth, devices * lines, 4 * block),
            low(depth - 1, devices * lines, 4 * block),
            low(depth - 1, devices * lines, 4 * block),
            low(devices, lines, wide),
            low(devices, lines, wide),
            low(devices, lines + 16, 4 * block),
            low(devices, lines + 16, 4 * block),
            wide_f32(16, D),
            wide_f32(devices * depth, 4 * block),
            wide_f32(depth - 1, devices, 4 * block),
            wide_f32(rows, 4 * block),
            low(rows, 3 * D // 2),
            low(half, D),
            low(*tokens.shape),
            low(half, D),
            low(*tokens.shape),
            pltpu.VMEM((slots, 128), jnp.int32),
            pltpu.SemaphoreType.DMA((6 * chips,)),
            pltpu.SemaphoreType.DMA((copies,)),
            pltpu.SemaphoreType.DMA((copies,)),
        ],
        compiler_params=pltpu.CompilerParams(
            collective_id=0, has_side_effects=True, vmem_limit_bytes=64 * 1024 * 1024 - 64 * 1024
        ),
        name="slot",
    )(tokens, out_grad, lengths, vectors, w_qkv, w_out, w_in, w_fc2)
    size = moment_one.shape[1] // 128
    padded = (size + 279) // 280 * 280
    flat = jax.ShapeDtypeStruct(moment_one.shape, F32)
    return pl.pallas_call(
        partial(adam_kernel, count),
        out_shape=(
            jax.ShapeDtypeStruct(tokens.shape, BF16),
            jax.ShapeDtypeStruct(tokens.shape, BF16),
            flat,
            flat,
            flat,
            flat,
        ),
        in_specs=[inside] * 8 + [anywhere] * 6,
        out_specs=(inside, inside) + (anywhere,) * 4,
        scratch_shapes=[wide_f32(padded, 128)] * 4
        + [
            low(lines, 3 * D),
            low(lines, D),
            low(lines, features),
            low(features // count, D),
            wide_f32(vectors.shape[0] * D // 128, 128),
            pltpu.SemaphoreType.DMA((2, 5)),
            pltpu.SemaphoreType.DMA((4,)),
            pltpu.SemaphoreType.DMA((4, 5)),
        ],
        compiler_params=pltpu.CompilerParams(vmem_limit_bytes=64 * 1024 * 1024 - 64 * 1024),
        name="adam",
    )(
        grad_qkv, grad_out_w, grad_in, grad_fc2, vector_grad, vectors, out, tokens_grad,
        w_qkv, w_out, w_in, w_fc2, moment_one, moment_two,
    )


def layer(tokens, *rest):
    slots, piece, width = tokens.shape
    devices, depth = lax.axis_size("dp"), lax.axis_size("ctx")
    fits = slots == 2 and depth == 2 * slots and devices == 2 * depth and FF == (devices // 2) * D
    if fits and (H * HD // devices) % 128 == 0 and (FF // devices) % 128 == 0:
        return slot_body(tokens, *rest)
    return body(tokens, *rest)


def solution(mesh):
    placed = (
        P("dp", "ctx", None),
        P("dp", "ctx", None),
        P("dp"),
        P(),
        P(),
        P(),
        P(),
        P(),
        P(("dp", "ctx"), None),
        P(("dp", "ctx"), None),
    )
    return jax.shard_map(
        layer,
        mesh=mesh,
        in_specs=placed,
        out_specs=(
            P("dp", "ctx", None),
            P("dp", "ctx", None),
            P(("dp", "ctx"), None),
            P(("dp", "ctx"), None),
            P(("dp", "ctx"), None),
            P(("dp", "ctx"), None),
        ),
        check_vma=False,
    )
```

```python
from functools import partial

import jax
import jax.numpy as jnp
from jax import lax
from jax.experimental import pallas as pl
from jax.experimental.pallas import tpu as pltpu
from jax.sharding import PartitionSpec as P

D = 1024
H = 16
HD = 64
FF = 4096


EPSILON = 1e-05
learn_rate = 0.01
beta_one = 0.9
beta_two = 0.999
adam_eps = 1e-08
decay_rate = 0.01
step_count = 10.0


def layer_norm(values, gain, shift):
    center = values - jnp.mean(values, axis=-1, keepdims=True)
    spread = jnp.mean(center * center, axis=-1, keepdims=True)
    return center * lax.rsqrt(spread + EPSILON) * gain + shift


def split_vectors(vectors):
    ratio = FF // D
    return (
        vectors[0],
        vectors[1],
        vectors[2],
        vectors[3 : 3 + ratio].reshape(FF),
        vectors[3 + ratio],
        vectors[4 + ratio],
        vectors[5 + ratio],
        vectors[6 + ratio],
        vectors[7 + ratio],
    )


def inner(left, right):
    return lax.dot_general(
        left, right, (((0,), (0,)), ((), ())), preferred_element_type=jnp.float32
    )


def through(left, weight):
    return lax.dot_general(
        left, weight, (((1,), (1,)), ((), ())), preferred_element_type=jnp.float32
    )


def run_slots(function, items):
    return lax.map(lambda item: function(*item), items)


def heads_block():
    return 4


def split_heads(matrix):
    count = matrix.shape[0]
    group = heads_block()
    return jnp.moveaxis(matrix.reshape(count, H // group, group, HD), 1, 0)


def join_heads(blocked):
    return jnp.moveaxis(blocked, 0, 1).reshape(blocked.shape[1], H * HD)


def split_stats(stats):
    group = heads_block()
    return stats.reshape(H // group, group, stats.shape[-1])


def shard_piece(left, right, number, shard_count):
    weight_rows = left.shape[1]
    columns = right.shape[1]
    per_shard = weight_rows * columns // shard_count
    block = inner(left, right).reshape(-1)
    return block.reshape(number, per_shard)


def project(flat_tokens, w_qkv, vectors):
    joined = jnp.dot(flat_tokens, w_qkv, preferred_element_type=jnp.float32)
    queries = ((joined[:, :D] + vectors[0]) * 0.125).astype(jnp.bfloat16)
    keys = joined[:, D : 2 * D].astype(jnp.bfloat16)
    values = (joined[:, 2 * D :] + vectors[1]).astype(jnp.bfloat16)
    return (queries, keys, values)


def attend_slot(queries, keys, values, live):
    rows = queries.shape[0]

    def attend_one_block(item):
        query_heads, key_heads, value_heads = item
        scores = jnp.einsum(
            "qhd,khd->hqk", query_heads, key_heads, preferred_element_type=jnp.float32
        )
        scores = jnp.where(live[None, None, :], scores, -1e30)
        maximum = jnp.max(scores, axis=-1, keepdims=True)
        expo = jnp.exp(scores - maximum)
        total = jnp.sum(expo, axis=-1, keepdims=True)
        probs_low = (expo / total).astype(jnp.bfloat16)
        mixed = jnp.einsum(
            "hqk,khd->qhd", probs_low, value_heads, preferred_element_type=jnp.float32
        )
        return (mixed, (maximum + jnp.log(total))[..., 0])

    mixed, log_total = lax.map(
        attend_one_block, (split_heads(queries), split_heads(keys), split_heads(values))
    )
    return (join_heads(mixed), log_total.reshape(H, rows))


def query_back(queries, keys, values, live, log_total, grad_mixed, with_keys):
    rows = queries.shape[0]

    def query_one_block(item):
        query_heads, key_heads, value_heads, grad_heads, block_log = item
        scores = jnp.einsum(
            "qhd,khd->hqk", query_heads, key_heads, preferred_element_type=jnp.float32
        )
        scores = jnp.where(live[None, None, :], scores, -1e30)
        probs = jnp.exp(scores - block_log[:, :, None])
        grad_probs = jnp.einsum(
            "qhd,khd->hqk", grad_heads, value_heads, preferred_element_type=jnp.float32
        )
        row_sums = jnp.sum(probs * grad_probs, axis=-1)
        grad_scores = (probs * (grad_probs - row_sums[:, :, None])).astype(jnp.bfloat16)
        grad_query = jnp.einsum(
            "hqk,khd->qhd", grad_scores, key_heads, preferred_element_type=jnp.float32
        )
        grad_key = jnp.einsum(
            "hqk,qhd->khd", grad_scores, query_heads, preferred_element_type=jnp.float32
        )
        grad_value = jnp.einsum(
            "hqk,qhd->khd",
            probs.astype(jnp.bfloat16),
            grad_heads,
            preferred_element_type=jnp.float32,
        )
        return (grad_query, row_sums, grad_key, grad_value)

    items = (
        split_heads(queries),
        split_heads(keys),
        split_heads(values),
        split_heads(grad_mixed),
        split_stats(log_total),
    )
    results = lax.map(query_one_block, items)
    grad_query, row_sums, grad_key, grad_value = results
    return (
        join_heads(grad_query),
        row_sums.reshape(H, rows),
        join_heads(grad_key),
        join_heads(grad_value),
    )


def tail(flat_tokens, mixed, w_out, w_in, w_fc2, vectors):
    bias_q, bias_v, bias_o, bias_in, bias_fc2, gain_one, shift_one, gain_two, shift_two = (
        split_vectors(vectors)
    )
    mixed_low = mixed.astype(jnp.bfloat16)
    summed_one = (
        flat_tokens.astype(jnp.float32)
        + jnp.dot(mixed_low, w_out, preferred_element_type=jnp.float32)
        + bias_o
    )
    normed = layer_norm(summed_one, gain_one, shift_one)
    normed_low = normed.astype(jnp.bfloat16)
    hidden_pre = jnp.dot(normed_low, w_in, preferred_element_type=jnp.float32) + bias_in
    hidden_low = jax.nn.gelu(hidden_pre, approximate=False).astype(jnp.bfloat16)
    summed_two = normed + jnp.dot(hidden_low, w_fc2, preferred_element_type=jnp.float32) + bias_fc2
    result = layer_norm(summed_two, gain_two, shift_two)
    return (mixed_low, summed_one, normed_low, hidden_pre, hidden_low, summed_two, result)


def body(tokens, out_grad, lengths, w_qkv, w_out, w_in, w_fc2, vectors, moment_one, moment_two):
    slots, piece, width = tokens.shape
    length = piece * lax.axis_size("ctx")
    local_pos = lax.axis_index("ctx") * piece + jnp.arange(piece, dtype=jnp.int32)
    own_live = local_pos[None, :] < lengths[:, None]
    valid = own_live.astype(jnp.float32)
    key_live = jnp.arange(length, dtype=jnp.int32)[None, :] < lengths[:, None]
    bias_q, bias_v, bias_o, bias_in, bias_fc2, gain_one, shift_one, gain_two, shift_two = (
        split_vectors(vectors)
    )
    flat_tokens = tokens.reshape(slots * piece, width)
    queries, keys, values = project(flat_tokens, w_qkv, vectors)
    keys_all, values_all = (
        lax.all_gather(keys.reshape(slots, piece, width), "ctx", axis=1, tiled=True),
        lax.all_gather(values.reshape(slots, piece, width), "ctx", axis=1, tiled=True),
    )
    mixed, log_total = run_slots(
        attend_slot, (queries.reshape(slots, piece, width), keys_all, values_all, key_live)
    )
    saved = tail(flat_tokens, mixed.reshape(slots * piece, width), w_out, w_in, w_fc2, vectors)
    out = (saved[6].reshape(slots, piece, width) * valid[..., None]).astype(jnp.bfloat16)
    again = lax.optimization_barrier(flat_tokens)
    queries, keys, values = project(again, w_qkv, vectors)
    keys_all, values_all = (
        lax.all_gather(keys.reshape(slots, piece, width), "ctx", axis=1, tiled=True),
        lax.all_gather(values.reshape(slots, piece, width), "ctx", axis=1, tiled=True),
    )
    mixed, log_total = run_slots(
        attend_slot, (queries.reshape(slots, piece, width), keys_all, values_all, key_live)
    )
    saved = tail(again, mixed.reshape(slots * piece, width), w_out, w_in, w_fc2, vectors)
    mixed_low, summed_one, normed_low, hidden_pre, hidden_low, summed_two, result = saved
    cotangent = (out_grad.astype(jnp.float32) * valid[..., None]).reshape(slots * piece, width)
    unused_two, norm_two_back = jax.vjp(layer_norm, summed_two, gain_two, shift_two)
    grad_two, grad_gain_two, grad_shift_two = norm_two_back(cotangent)
    grad_fc2_low = grad_two.astype(jnp.bfloat16)
    bias_fc2_grad = jnp.sum(grad_fc2_low.astype(jnp.float32), axis=0)
    grad_hidden = through(grad_fc2_low, w_fc2)
    unused_gelu, gelu_back = jax.vjp(partial(jax.nn.gelu, approximate=False), hidden_pre)
    grad_pre_low = gelu_back(grad_hidden)[0].astype(jnp.bfloat16)
    bias_in_grad = jnp.sum(grad_pre_low.astype(jnp.float32), axis=0)
    grad_normed = grad_two + through(grad_pre_low, w_in)
    unused_one, norm_one_back = jax.vjp(layer_norm, summed_one, gain_one, shift_one)
    grad_one, grad_gain_one, grad_shift_one = norm_one_back(grad_normed)
    grad_branch_low = grad_one.astype(jnp.bfloat16)
    bias_out_grad = jnp.sum(grad_branch_low.astype(jnp.float32), axis=0)
    grad_mixed_low = (
        through(grad_branch_low, w_out).astype(jnp.bfloat16).reshape(slots, piece, width)
    )
    queries_slots = queries.reshape(slots, piece, width)
    grad_query, row_sums, grad_key, grad_value = run_slots(
        partial(query_back, with_keys=True),
        (queries_slots, keys_all, values_all, key_live, log_total, grad_mixed_low),
    )
    grad_key, grad_value = (
        lax.psum_scatter(
            grad_key.astype(jnp.bfloat16), "ctx", scatter_dimension=1, tiled=True
        ).astype(jnp.float32),
        lax.psum_scatter(
            grad_value.astype(jnp.bfloat16), "ctx", scatter_dimension=1, tiled=True
        ).astype(jnp.float32),
    )
    rows = slots * piece
    grad_query_low = grad_query.reshape(rows, width).astype(jnp.bfloat16) * jnp.bfloat16(0.125)
    grad_key_low = grad_key.reshape(rows, width).astype(jnp.bfloat16)
    grad_value_low = grad_value.reshape(rows, width).astype(jnp.bfloat16)
    grad_joined = jnp.concatenate([grad_query_low, grad_key_low, grad_value_low], axis=1)
    bias_q_grad = jnp.sum(grad_query_low.astype(jnp.float32), axis=0)
    bias_v_grad = jnp.sum(grad_value_low.astype(jnp.float32), axis=0)
    tokens_grad = (
        (grad_one + through(grad_joined, w_qkv)).reshape(slots, piece, width).astype(jnp.bfloat16)
    )
    vector_grad = jnp.concatenate(
        [
            bias_q_grad[None],
            bias_v_grad[None],
            bias_out_grad[None],
            bias_in_grad.reshape(FF // D, D),
            bias_fc2_grad[None],
            grad_gain_one[None],
            grad_shift_one[None],
            grad_gain_two[None],
            grad_shift_two[None],
        ],
        axis=0,
    )
    count = lax.axis_size(("dp", "ctx"))
    vector_rows = vector_grad.reshape(count, -1)
    pairs = (
        (flat_tokens, grad_joined),
        (mixed_low, grad_branch_low),
        (normed_low, grad_pre_low),
        (hidden_low, grad_fc2_low),
    )
    blocks = [
        shard_piece(left, right, 1 * lax.axis_size(("dp", "ctx")), count) for left, right in pairs
    ]
    blocks.append(vector_rows)
    grad_rows = lax.psum_scatter(
        jnp.concatenate(blocks, axis=1), ("dp", "ctx"), scatter_dimension=0, tiled=True
    )
    index = lax.axis_index(("dp", "ctx"))
    params = jnp.concatenate(
        [
            lax.dynamic_slice_in_dim(weight.reshape(count, -1), index, 1, 0).astype(jnp.float32)
            for weight in (w_qkv, w_out, w_in, w_fc2, vectors)
        ],
        axis=1,
    )
    new_one = beta_one * moment_one + (1.0 - beta_one) * grad_rows
    new_two = beta_two * moment_two + (1.0 - beta_two) * grad_rows * grad_rows
    fix_one = 1.0 - beta_one**step_count
    fix_two = 1.0 - beta_two**step_count
    update = new_one / fix_one / (jnp.sqrt(new_two / fix_two) + adam_eps)
    new_params = params - learn_rate * (update + decay_rate * params)
    return (out, tokens_grad, grad_rows, new_params, new_one, new_two)


BF16 = jnp.bfloat16
F32 = jnp.float32


def layer_norm_stats(values):
    center = values - jnp.mean(values, axis=-1, keepdims=True)
    spread = jnp.mean(center * center, axis=-1, keepdims=True)
    return center, lax.rsqrt(spread + EPSILON)


def layer_norm_back(center, scale, gain, cotangent):
    scaled = cotangent * gain
    mean_scaled = jnp.mean(scaled, axis=-1, keepdims=True)
    mean_cross = jnp.mean(scaled * center, axis=-1, keepdims=True)
    return scale * (scaled - mean_scaled - center * (scale * scale) * mean_cross)


def normal_cdf(values):
    return 0.5 * (1.0 + lax.erf(values * 0.7071067811865476))


def dot(left, right):
    return jnp.dot(left, right, preferred_element_type=F32)


def positions(axis, shape, slot, piece):
    place = lax.broadcasted_iota(jnp.int32, shape, axis)
    block = lax.div(place, piece)
    half = lax.div(block, 2)
    step = lax.rem(block, 2)
    return (2 * half + lax.rem(slot + step, 2)) * piece + lax.rem(place, piece)


def head_probs(queries, keys, live):
    scores = through(queries, keys)
    scores = jnp.where(live, scores, -1e30)
    expo = jnp.exp(scores - jnp.max(scores, axis=-1, keepdims=True))
    return expo / jnp.sum(expo, axis=-1, keepdims=True)


MESH = pl.DeviceIdType.MESH


class Links:
    def __init__(self, sends, recvs):
        self.sends, self.recvs = sends, recvs
        self.used = 0
        self.open = []

    def copy(self, source, target, device):
        self.used += 1
        return self.again(source, target, device)

    def again(self, source, target, device):
        number = self.used - 1
        return pltpu.make_async_remote_copy(
            src_ref=source,
            dst_ref=target,
            send_sem=self.sends.at[number],
            recv_sem=self.recvs.at[number],
            device_id=device,
            device_id_type=MESH,
        )

    def forward(self, source, target, device, earlier):
        self.used += 1
        return pltpu.make_async_remote_copy(
            src_ref=source,
            dst_ref=target,
            send_sem=self.sends.at[self.used - 1],
            recv_sem=self.recvs.at[earlier],
            device_id=device,
            device_id_type=MESH,
        )

    def send(self, source, target, device):
        made = self.copy(source, target, device)
        made.start()
        self.open.append((made, None))
        return made

    def send_if(self, condition, source, target, device):
        made = self.copy(source, target, device)
        pl.when(condition)(made.start)
        self.open.append((made, condition))
        return made

    def send_or_keep(self, here, source, target, device):
        number = self.used
        made = self.copy(source, target, device)
        local = pltpu.make_async_copy(source, target, self.recvs.at[number])
        pl.when(here)(local.start)
        away = jnp.logical_not(here)
        pl.when(away)(made.start)
        self.open.append((made, away))

        def wait():
            pl.when(here)(local.wait)
            pl.when(away)(made.wait_recv)

        return wait

    def close(self):
        for made, condition in self.open:
            if condition is None:
                made.wait_send()
            else:
                pl.when(condition)(made.wait_send)


def flip(value, mask):
    result = value
    bit = 1
    while bit <= mask:
        if mask & bit:
            result = result + bit * (1 - 2 * lax.rem(lax.div(value, bit), 2))
        bit *= 2
    return result


def flip_traced(value, mask, size):
    result = value
    bit = 1
    while bit < size:
        set_bit = lax.rem(lax.div(mask, bit), 2)
        result = result + bit * set_bit * (1 - 2 * lax.rem(lax.div(value, bit), 2))
        bit *= 2
    return result


def at_rows(start, size):
    return pl.ds(pl.multiple_of(start, 64), size)


def slot_kernel(devices, depth, features, *refs):
    (
        tokens, out_grad, lengths, vec, w_qkv, w_out, w_in, w_fc2,
        out_ref, tgrad_ref, g_qkv, g_out, g_in, g_fc2, g_vec,
        wqkv, wo, w_up, w_down,
        x_all, n_all, g_all, m_all, b_all, j_all, j_send, g_rows, lens_peer,
        qkv, part, part_low, part_a, part_b, part_c, part_d, summed, grad_two, grad_one,
        pre_s, hid, hid_all, gp_all, packed, plane_got, up_mine, down_mine, packed_two, right_two, left_two,
        trade_in, got_in, trade_qkv, got_qkv, vec_s, vec_by, vec_got, sums, dqkv, out_half, out_got, tg_half, tg_got, lens,
        local_sems, sends, recvs,
    ) = refs
    chips = devices // 2
    me, slot = lax.axis_index("dp"), lax.axis_index("ctx")
    core, chip = lax.rem(me, 2), lax.div(me, 2)
    base = me - core
    peer = (base + 1 - core, slot)
    piece = tokens.shape[1]
    half = 2 * piece
    rows = 2 * half
    block = D // devices
    wide = features // devices
    lines = D // (devices * depth)
    net = Links(sends, recvs)
    mine_at = at_rows(core * half, half)
    other_at = at_rows((1 - core) * half, half)
    chunk = 32

    row_of = lax.broadcasted_iota(jnp.int32, lens.shape, 0)
    lens[...] = jnp.where(row_of == 0, lengths[0], lengths[1])
    vec_s[...] = jnp.zeros_like(vec_s)
    loads = []

    def load(source, target):
        made = pltpu.make_async_copy(source, target, local_sems.at[len(loads)])
        made.start()
        loads.append(made)

    where = [2 * flip(chip, mask) + core for mask in range(chips)]
    for mask in range(chips):
        for kind in range(3):
            start = pl.multiple_of(kind * D + where[mask] * block, block)
            load(
                w_qkv.at[:, pl.ds(start, block)],
                wqkv.at[:, (3 * mask + kind) * block : (3 * mask + kind + 1) * block],
            )
    n_qkv = len(loads)
    for number in range(chips):
        start = pl.multiple_of((2 * number + core) * block, block)
        load(w_out.at[pl.ds(start, block), :], wo.at[number * block : (number + 1) * block, :])
    n_out = len(loads)
    for mask in range(chips):
        start = pl.multiple_of(where[mask] * wide, wide)
        load(w_in.at[:, pl.ds(start, wide)], w_up.at[:, mask * wide : (mask + 1) * wide])
    n_up = len(loads)
    for mask in range(chips):
        start = pl.multiple_of(where[mask] * wide, wide)
        load(w_fc2.at[pl.ds(start, wide), :], w_down.at[mask * wide : (mask + 1) * wide, :])

    barrier = pltpu.get_barrier_semaphore()
    friends = [(flip(me, mask), slot) for mask in range(1, devices)]
    for shift in range(1, depth):
        far = lax.rem(slot + shift, depth)
        friends += [(me, far), (flip(me, 1), far)]
    for friend in friends:
        pl.semaphore_signal(barrier, inc=1, device_id=friend, device_id_type=MESH)
    pl.semaphore_wait(barrier, len(friends))

    def spread(source, target):
        waits = []
        for step in range(2):
            pick = lax.rem(slot + step, 2)
            upper = lax.div(slot, 2)
            place = 2 * core + pick
            here = jnp.logical_and(upper == core, place == slot)
            waits.append(
                net.send_or_keep(
                    here,
                    source.at[pick],
                    target.at[at_rows((2 * upper + step) * piece, piece)],
                    (base + upper, place),
                )
            )
        return waits

    def pass_on(waits, target):
        made = []
        for step, wait in enumerate(waits):
            wait()
            spot = target.at[at_rows((2 * core + step) * piece, piece)]
            made.append(net.send(spot, spot, peer))
        return made

    token_waits = spread(tokens, x_all)
    grad_waits = spread(out_grad, g_rows)
    lens_copy = net.send(lens, lens_peer, peer)
    token_passes = pass_on(token_waits, x_all)

    def plane_start(target):
        source = target.at[mine_at]
        return [
            net.send(
                source, target.at[at_rows(mask * rows + core * half, half)], (flip(me, 2 * mask), slot)
            )
            for mask in range(1, chips)
        ]

    def plane_pass(copies, target):
        made = []
        for mask, copy in enumerate(copies, 1):
            copy.wait_recv()
            spot = target.at[at_rows(mask * rows + core * half, half)]
            made.append(net.send(spot, spot, peer))
        return made

    class Column:
        def __init__(self, target):
            self.target = target
            self.parts, self.numbers = {}, {}
            for place in (2, 1, 3):
                far = lax.rem(slot + depth - place, depth)
                made = net.copy(target.at[mine_at], self.spot(place), (me, far))
                self.parts[place], self.numbers[place] = made, net.used - 1
                goes = {1: slot != 0, 2: slot >= 0, 3: slot != depth - 1}[place]
                net.open.append((made, goes))
                pl.when(goes)(made.start)
            self.passes = {}

        def spot(self, place):
            return self.target.at[at_rows(place * rows + core * half, half)]

        def relay(self):
            self.parts[2].wait_recv()
            up = net.forward(self.spot(2), self.spot(1), (me, depth - 1), self.numbers[1])
            down = net.forward(self.spot(2), self.spot(3), (me, 0), self.numbers[3])
            for made, here in ((up, slot == 2), (down, slot == 1)):
                pl.when(here)(made.start)
                net.open.append((made, here))
            self.passes[2] = net.send(self.spot(2), self.spot(2), peer)

        def hand_over(self, place):
            self.parts[place].wait_recv()
            self.passes[place] = net.send(self.spot(place), self.spot(place), peer)

    x_plane = plane_start(x_all)
    for made in loads[:n_qkv]:
        made.wait()
    lens_copy.wait_recv()
    for made in token_passes:
        made.wait_recv()
    owned = jnp.where(lax.div(slot, 2) == core, lens[...], lens_peer[...])
    length = jnp.where(lax.rem(slot, 2) == 0, owned[0:1, 0:1], owned[1:2, 0:1])
    live = positions(1, (1, rows), slot, piece) < length
    lane = lax.broadcasted_iota(jnp.int32, (1, block), 1)

    @pl.loop(0, chips)
    def _(mask):
        spot = 2 * flip_traced(chip, mask, chips) + core
        lanes = pl.ds(pl.multiple_of(spot * block, block), block)
        joined = dot(x_all[0:rows, :], wqkv[:, pl.ds(pl.multiple_of(mask * 3 * block, block), 3 * block)])
        queries = ((joined[:, 0:block] + vec[0:1, lanes]) * 0.125).astype(BF16)
        keys = joined[:, block : 2 * block].astype(BF16)
        values = (joined[:, 2 * block :] + vec[1:2, lanes]).astype(BF16)
        total = jnp.zeros((rows, block), F32)
        for head in range(block // HD):
            mine = lax.div(lane, HD) == head
            probs = head_probs(jnp.where(mine, queries, jnp.zeros_like(queries)), keys, live)
            total = jnp.where(mine, dot(probs.astype(BF16), values), total)
        start = pl.multiple_of(mask * 3 * block, block)
        qkv[:, pl.ds(start, block)] = queries
        qkv[:, pl.ds(pl.multiple_of(start + block, block), block)] = keys
        qkv[:, pl.ds(pl.multiple_of(start + 2 * block, block), block)] = values
        lanes = pl.ds(pl.multiple_of(core * chips * block + lax.div(spot, 2) * block, block), block)
        m_all[0:rows, lanes] = total.astype(BF16)

    for made in loads[n_qkv:n_out]:
        made.wait()

    def exchange(compute, target, before):
        made = []
        for number, at in enumerate((other_at, mine_at)):
            if before is not None:
                before[number].wait_send()
            value = compute(at)
            part[at, :] = value
            part_low[at, :] = value.astype(BF16)
            made.append(net.copy(part_low.at[at], target.at[at], peer))
            made[-1].start()
        return made

    my_lanes = pl.ds(pl.multiple_of(core * chips * block, chips * block), chips * block)
    first = exchange(lambda at: dot(m_all[at, my_lanes], wo[...]), part_a, None)
    own_mixed = m_all.at[0:rows, my_lanes]
    m_passes = [net.send(own_mixed, own_mixed, peer)]
    m_plane = [
        net.send(own_mixed, m_all.at[mask * rows : (mask + 1) * rows, my_lanes], (flip(me, 2 * mask), slot))
        for mask in range(1, chips)
    ]
    grad_passes = pass_on(grad_waits, g_rows)

    def norm_one(start):
        @pl.loop(0, half // chunk)
        def _(step):
            at = pl.ds(pl.multiple_of(start + step * chunk, chunk), chunk)
            total = x_all[at, :].astype(F32) + (part[at, :] + part_a[at, :].astype(F32)) + vec[2:3, :]
            center, scale = layer_norm_stats(total)
            summed[at, :] = total
            n_all[at, :] = (center * scale * vec[8:9, :] + vec[9:10, :]).astype(BF16)

    first[0].wait_recv()
    norm_one(core * half)
    n_column = Column(n_all)
    first[1].wait_recv()
    norm_one((1 - core) * half)
    for made in loads[n_out:]:
        made.wait()

    for number in range(chips):
        fine_cols = wide // depth
        begin = flip_traced(chip, number, chips) * wide + slot * fine_cols
        at = pl.ds(pl.multiple_of(begin, fine_cols), fine_cols)
        up_mine[:, number * fine_cols : (number + 1) * fine_cols] = w_up[:, at]
        down_mine[number * fine_cols : (number + 1) * fine_cols, :] = w_down[at, :]

    def bias_of(mask):
        spot = flip_traced(chip, mask, chips)
        lanes = pl.ds(pl.multiple_of(core * wide, wide), wide)
        result = vec[3:4, lanes]
        for row in range(1, chips):
            result = jnp.where(spot == row, vec[3 + row : 4 + row, lanes], result)
        return result

    @pl.loop(0, chips)
    def _(mask):
        at = pl.ds(pl.multiple_of(mask * wide, wide), wide)
        value = dot(n_all[0:rows, :], w_up[:, at]) + bias_of(mask)
        pre_s[:, at] = value
        hid[:, at] = (value * normal_cdf(value)).astype(BF16)

    second = exchange(lambda at: dot(hid[at, :], w_down[...]), part_b, first)
    for made in grad_passes:
        made.wait_recv()

    def norm_two(start, own):
        @pl.loop(0, half // chunk)
        def _(step):
            begin = pl.multiple_of(start + step * chunk, chunk)
            at = pl.ds(begin, chunk)
            center, scale = layer_norm_stats(summed[at, :])
            normed = center * scale * vec[8:9, :] + vec[9:10, :]
            center, scale = layer_norm_stats(normed + (part[at, :] + part_b[at, :].astype(F32)) + vec[7:8, :])
            place = begin + lax.broadcasted_iota(jnp.int32, (chunk, 1), 0)
            piece_of = lax.div(place, piece)
            spot = 2 * lax.div(piece_of, 2) + lax.rem(slot + lax.rem(piece_of, 2), 2)
            valid = (spot * piece + lax.rem(place, piece) < length).astype(F32)
            unit = center * scale
            error = g_rows[at, :].astype(F32) * valid
            grad = layer_norm_back(center, scale, vec[10:11, :], error)
            grad_two[at, :] = grad
            low = grad.astype(BF16)
            g_all[at, :] = low
            if own:
                out_half[pl.ds(pl.multiple_of(step * chunk, chunk), chunk), :] = (
                    valid * (unit * vec[10:11, :] + vec[11:12, :])
                ).astype(BF16)
                vec_s[7:8, :] += jnp.sum(low.astype(F32), axis=0, keepdims=True)
                vec_s[10:11, :] += jnp.sum(error * unit, axis=0, keepdims=True)
                vec_s[11:12, :] += jnp.sum(error, axis=0, keepdims=True)

    def go_back(source, target):
        waits = []
        for step in range(2):
            place = 2 * core + lax.rem(slot + step, 2)
            upper = lax.div(slot, 2)
            here = jnp.logical_and(upper == core, place == slot)
            waits.append(
                net.send_or_keep(
                    here,
                    source.at[step * piece : (step + 1) * piece],
                    target.at[lax.rem(slot, 2)],
                    (base + upper, place),
                )
            )
        return waits

    second[0].wait_recv()
    norm_two(core * half, True)
    g_column = Column(g_all)
    second[1].wait_recv()
    norm_two((1 - core) * half, False)
    out_waits = go_back(out_half, out_got)

    def mixed_pass():
        for mask, made in enumerate(m_plane, 1):
            made.wait_recv()
            spot = m_all.at[mask * rows : (mask + 1) * rows, my_lanes]
            m_passes.append(net.send(spot, spot, peer))

    def slope_of(value, cdf):
        return cdf + value * (jnp.exp(-0.5 * value * value) * 0.3989422804014327)

    @pl.loop(0, chips)
    def _(mask):
        at = pl.ds(pl.multiple_of(mask * wide, wide), wide)
        value = pre_s[:, at]
        grad = through(g_all[0:rows, :], w_down[at, :])
        hid[:, at] = (grad * slope_of(value, normal_cdf(value))).astype(BF16)

    third = exchange(lambda at: through(hid[at, :], w_up[...]), part_c, second)

    def norm_one_back(start, own):
        @pl.loop(0, half // chunk)
        def _(step):
            at = pl.ds(pl.multiple_of(start + step * chunk, chunk), chunk)
            center, scale = layer_norm_stats(summed[at, :])
            error = grad_two[at, :] + (part[at, :] + part_c[at, :].astype(F32))
            grad = layer_norm_back(center, scale, vec[8:9, :], error)
            low = grad.astype(BF16)
            b_all[at, :] = low
            grad_one[at, :] = grad
            if own:
                vec_s[2:3, :] += jnp.sum(low.astype(F32), axis=0, keepdims=True)
                vec_s[8:9, :] += jnp.sum(error * (center * scale), axis=0, keepdims=True)
                vec_s[9:10, :] += jnp.sum(error, axis=0, keepdims=True)

    x_pass = plane_pass(x_plane, x_all)

    third[0].wait_recv()
    norm_one_back(core * half, True)
    third[1].wait_recv()
    norm_one_back((1 - core) * half, False)
    class Line:
        def __init__(self, chunks, from_left, from_right):
            self.chunks, self.from_left, self.from_right = chunks, from_left, from_right
            self.up, self.down, self.first_up, self.first_down = [], [], [], []
            after = (me, lax.rem(slot + 1, depth))
            before = (me, lax.rem(slot + depth - 1, depth))
            for order in range(depth - 1):
                top, low = depth - 1 - order, order
                spot = from_left.at[order]
                self.up.append(net.copy(spot, spot, after))
                self.first_up.append(net.again(chunks.at[top], spot, after))
                net.open.append((self.up[-1], slot < top))
                spot = from_right.at[order]
                self.down.append(net.copy(spot, spot, before))
                self.first_down.append(net.again(chunks.at[low], spot, before))
                net.open.append((self.down[-1], slot > low))

        def first(self):
            for order in range(depth - 1):
                pl.when(slot == 0)(self.first_up[order].start)
                pl.when(slot == depth - 1)(self.first_down[order].start)

        def stage(self, time):
            for order in range(time):
                top, low = depth - 1 - order, order

                @pl.when(slot == time - order)
                def _(order=order, top=top):
                    self.up[order].wait_recv()
                    if time < depth - 1:
                        self.from_left[order] = (
                            self.from_left[order].astype(F32) + self.chunks[top].astype(F32)
                        ).astype(BF16)
                        self.up[order].start()

                @pl.when(depth - 1 - slot == time - order)
                def _(order=order, low=low):
                    self.down[order].wait_recv()
                    if time < depth - 1:
                        self.from_right[order] = (
                            self.from_right[order].astype(F32) + self.chunks[low].astype(F32)
                        ).astype(BF16)
                        self.down[order].start()

    grad_parts = range(1, chips)

    def attention_back(mask):
        start = mask * 3 * block
        queries = qkv[:, start : start + block]
        keys = qkv[:, start + block : start + 2 * block]
        values = qkv[:, start + 2 * block : start + 3 * block]
        turn = pl.ds(pl.multiple_of(lax.div(where[mask], 2) * block, block), block)
        grad_mixed = through(b_all[0:rows, :], wo[turn, :]).astype(BF16)
        grad_q = jnp.zeros((rows, block), F32)
        grad_k = grad_q
        grad_v = grad_q
        for head in range(block // HD):
            mine = lax.div(lane, HD) == head
            probs = head_probs(jnp.where(mine, queries, jnp.zeros_like(queries)), keys, live)
            grad_probs = through(jnp.where(mine, grad_mixed, jnp.zeros_like(grad_mixed)), values)
            dsum = jnp.sum(probs * grad_probs, axis=-1, keepdims=True)
            grad_scores = (probs * (grad_probs - dsum)).astype(BF16)
            grad_q = jnp.where(mine, dot(grad_scores, keys), grad_q)
            grad_k = jnp.where(mine, inner(grad_scores, queries), grad_k)
            grad_v = jnp.where(mine, inner(probs.astype(BF16), grad_mixed), grad_v)
        grad_q = grad_q.astype(BF16) * jnp.bfloat16(0.125)
        grad_k = grad_k.astype(BF16)
        grad_v = grad_v.astype(BF16)
        spot = pl.ds(pl.multiple_of(where[mask] * block, block), block)
        vec_s[0:1, spot] = jnp.sum(grad_q.astype(F32), axis=0, keepdims=True)
        vec_s[1:2, spot] = jnp.sum(grad_v.astype(F32), axis=0, keepdims=True)
        dqkv[:, start : start + block] = grad_q
        dqkv[:, start + block : start + 2 * block] = grad_k
        dqkv[:, start + 2 * block : start + 3 * block] = grad_v
        if mask:
            joint = j_send.at[mask - 1]
        else:
            joint = j_all.at[0:rows]
        joint[:, 0:block] = grad_q
        joint[:, block : 2 * block] = grad_k
        joint[:, 2 * block : 3 * block] = grad_v
        joint[:, 3 * block : 4 * block] = b_all[0:rows, spot]
        if mask:
            return net.send(
                joint, j_all.at[mask * rows : (mask + 1) * rows], (flip(me, 2 * mask), slot)
            )
        return None

    n_column.relay()
    j_copies = [attention_back(mask) for mask in grad_parts]
    attention_back(0)
    mixed_pass()
    n_column.hand_over(1)
    n_column.hand_over(3)
    for made in third:
        made.wait_send()
    part[0:half, :] = through(dqkv[other_at, :], wqkv[...])
    tg_copy = net.copy(part.at[0:half], part_d, peer)
    tg_copy.start()
    part[half:rows, :] = grad_one[mine_at, :] + through(dqkv[mine_at, :], wqkv[...])
    tg_copy.wait_recv()
    tg_half[...] = (part[half:rows, :] + part_d[...]).astype(BF16)

    fine = wide // depth
    span = lines * depth
    features_at = pl.ds(pl.multiple_of((depth * core + slot) * fine, fine), fine)
    bias_mine = jnp.concatenate([vec[3 + number : 4 + number, features_at] for number in range(chips)], axis=1)

    def feed_rows(place):
        at = slice(place * rows, (place + 1) * rows)
        value = dot(n_all[at, :], up_mine[...]) + bias_mine
        cdf = normal_cdf(value)
        hid_all[at, :] = (value * cdf).astype(BF16)
        low = (through(g_all[at, :], down_mine[...]) * slope_of(value, cdf)).astype(BF16)
        gp_all[at, :] = low
        return jnp.sum(low.astype(F32), axis=0, keepdims=True)

    bias_sum = feed_rows(0)
    g_column.relay()
    for made in m_passes + x_pass + j_copies:
        made.wait_recv()
    for group in range(devices):
        at = slice(group * span, (group + 1) * span)
        begin = (group % 2) * chips * block + (group // 2) * block
        both = inner(x_all[:, at], j_all[:, 0 : 3 * block]).astype(BF16)
        across = inner(m_all[:, begin : begin + block], j_all[:, 3 * block : 4 * block]).astype(BF16)
        row = group * lines
        for number in range(depth):
            at = slice(number * lines, (number + 1) * lines)
            packed_two[number, row : row + lines, 0 : 3 * block] = both[at, :]
            packed_two[number, row : row + lines, 3 * block : 4 * block] = across[at, :]
    input_line = Line(packed_two, right_two, left_two)
    input_line.first()

    g_column.hand_over(1)
    g_column.hand_over(3)
    for place in (2, 1, 3):
        n_column.passes[place].wait_recv()
        g_column.passes[place].wait_recv()
        bias_sum = bias_sum + feed_rows(place)
    for number in range(chips):
        vec_s[3 + number : 4 + number, features_at] = bias_sum[:, number * fine : (number + 1) * fine]
    depth_rows = D // chips
    for number in range(chips):
        block_up = inner(n_all[:, number * depth_rows : (number + 1) * depth_rows], gp_all[...]).astype(BF16)
        packed[number, fine : 2 * fine, 0:wide] = block_up[0:fine, :]
        packed[number, fine : 2 * fine, wide : 2 * wide] = block_up[fine : 2 * fine, :]

    def scatter_plane(lines_at):
        return [
            net.send(
                packed.at[flip_traced(chip, mask, chips), lines_at],
                plane_got.at[mask - 1, lines_at],
                (flip(me, 2 * mask), slot),
            )
            for mask in range(1, chips)
        ]

    up_copies = scatter_plane(slice(fine, 2 * fine))
    packed[:, 0:fine, :] = inner(hid_all[...], g_all[...]).astype(BF16).reshape(chips, fine, D)
    down_copies = scatter_plane(slice(0, fine))

    tiles = vec.shape[0] * D // 128
    share = tiles // (devices * depth)
    vec_by[...] = jnp.zeros_like(vec_by)
    for tile in range(tiles):
        owner, lane_group = tile // share, tile % share
        row, col = tile // (D // 128), (tile % (D // 128)) * 128
        spot = (owner % depth) * devices + owner // depth
        vec_by[spot : spot + 1, lane_group * 128 : (lane_group + 1) * 128] = vec_s[
            row : row + 1, col : col + 128
        ]
    vec_copies = []
    for shift in range(1, depth):
        far = lax.rem(slot + shift, depth)
        spot = vec_by.at[pl.ds(pl.multiple_of(far * devices, devices), devices)]
        vec_copies.append(net.send(spot, vec_got.at[shift - 1], (me, far)))

    def finish(line, target, rows_at):
        target[...] = line.chunks[slot, rows_at, :].astype(F32)

        @pl.when(slot >= 1)
        def _():
            target[...] += line.from_left[depth - 1 - slot, rows_at, :].astype(F32)

        @pl.when(slot <= depth - 2)
        def _():
            target[...] += line.from_right[slot, rows_at, :].astype(F32)

    def plane_sum(copies, lines_at):
        for made in copies:
            made.wait_recv()
        value = packed[chip, lines_at, :].astype(F32)
        for number in range(chips - 1):
            value = value + plane_got[number, lines_at, :].astype(F32)
        return value

    def trade(source, target):
        return [
            net.send(source.at[flip(me, mask)], target.at[me], (flip(me, mask), slot))
            for mask in range(1, devices)
        ]

    tg_waits = go_back(tg_half, tg_got)
    for time in range(1, depth - 1):
        input_line.stage(time)
    low_sum = plane_sum(up_copies, slice(fine, 2 * fine)).astype(BF16)
    for upper in range(2):
        for number in range(depth):
            trade_in[upper * depth + number] = low_sum[
                number * lines : (number + 1) * lines, upper * wide : (upper + 1) * wide
            ]
    here = core * depth + slot
    in_copies = []
    for shift in range(1, 2 * depth):
        far = lax.rem(slot + shift % depth, depth)
        upper = core if shift < depth else 1 - core
        in_copies.append(net.send(trade_in.at[upper * depth + far], got_in.at[here], (base + upper, far)))
    input_line.stage(depth - 1)
    tg_copy.wait_send()
    finish(input_line, sums, slice(0, rows))
    vec_sum = vec_by[pl.ds(pl.multiple_of(slot * devices, devices), devices), :]
    for number, made in enumerate(vec_copies):
        made.wait_recv()
        vec_sum = vec_sum + vec_got[number]
    first_row = lax.broadcasted_iota(jnp.int32, (16, 4 * block), 0) == 0
    for group in range(devices):
        trade_qkv[group, 0:lines, :] = sums[group * lines : (group + 1) * lines, :].astype(BF16)
        trade_qkv[group, lines : lines + 16, :] = jnp.where(
            first_row, vec_sum[group : group + 1, :], 0.0
        ).astype(BF16)
    qkv_copies = trade(trade_qkv, got_qkv)
    for made in in_copies:
        made.wait_recv()
    got_in[here] = trade_in[here]
    for group in range(2 * depth):
        for number in range(chips):
            start = number * 2 * wide + group * fine
            g_in[:, start : start + fine] = got_in[group, :, number * fine : (number + 1) * fine].astype(F32)
    g_fc2[...] = plane_sum(down_copies, slice(0, fine))
    for wait in out_waits + tg_waits:
        wait()
    out_ref[...] = out_got[...]
    tgrad_ref[...] = tg_got[...]
    for made in qkv_copies:
        made.wait_recv()
    got_qkv[me] = trade_qkv[me]
    vec_sum = jnp.zeros((16, 3 * block), F32)
    for group in range(devices):
        vec_sum = vec_sum + got_qkv[group, lines : lines + 16, 0 : 3 * block].astype(F32)
        got = got_qkv[group, 0:lines, :].astype(F32)
        for kind in range(3):
            g_qkv[:, kind * D + group * block : kind * D + (group + 1) * block] = got[
                :, kind * block : (kind + 1) * block
            ]
        g_out[:, group * block : (group + 1) * block] = got[:, 3 * block : 4 * block]
    g_vec[...] = vec_sum[0:8, :]
    net.close()


def adam_kernel(count, *refs):
    (
        g_qkv, g_out, g_in, g_fc2, g_vec, vec, out_in, tgrad_in, w_qkv, w_out, w_in, w_fc2, m_one, m_two,
        out_ref, tgrad_ref, rows_out, params_out, one_out, two_out,
        grads, params, one, two, b_qkv, b_out, b_in, b_fc2, vec_flat, in_sems, w_sems, out_sems,
    ) = refs
    index = lax.axis_index("dp") * lax.axis_size("ctx") + lax.axis_index("ctx")
    size = m_one.shape[1] // 128
    parts = in_sems.shape[1]
    step = grads.shape[0] // parts
    spans = [(number * step, min((number + 1) * step, size) - number * step) for number in range(parts)]
    loads = []
    for number, (start, length) in enumerate(spans):
        pair = []
        for kind, (source, target) in enumerate(((m_one, one), (m_two, two))):
            pair.append(
                pltpu.make_async_copy(
                    source.reshape(size, 128).at[start : start + length],
                    target.at[start : start + length],
                    in_sems.at[kind, number],
                )
            )
            pair[-1].start()
        loads.append(pair)
    weights = []
    for number, (source, target) in enumerate(
        ((w_qkv, b_qkv), (w_out, b_out), (w_in, b_in), (w_fc2, b_fc2))
    ):
        lines = target.shape[0]
        start = pl.multiple_of(index * lines, lines)
        weights.append(
            pltpu.make_async_copy(source.at[pl.ds(start, lines), :], target, w_sems.at[number])
        )
        weights[-1].start()
    out_ref[...] = out_in[...]
    tgrad_ref[...] = tgrad_in[...]

    def flatten(source, target, base):
        lines, groups = source.shape[0], source.shape[1] // 128
        for col in range(groups):
            value = source[:, col * 128 : (col + 1) * 128].astype(F32)
            for row in range(0, lines, 8):
                target[pl.ds(base + row * groups + col, 8, stride=groups), :] = value[row : row + 8, :]

    base = 0
    for grad in (g_qkv, g_out, g_in, g_fc2):
        flatten(grad, grads, base)
        base += grad.shape[0] * grad.shape[1] // 128
    share = g_vec.shape[1] // 128
    groups = vec.shape[1] // 128
    for col in range(groups):
        lanes = slice(col * 128, (col + 1) * 128)
        vec_flat[pl.ds(col, 8, stride=groups), :] = vec[0:8, lanes]
        for row in range(8, vec.shape[0]):
            vec_flat[row * groups + col : row * groups + col + 1, :] = vec[row : row + 1, lanes]
    place = lax.broadcasted_iota(jnp.int32, vec_flat.shape, 0)
    for number in range(share):
        grads[base + number : base + number + 1, :] = g_vec[0:1, number * 128 : (number + 1) * 128]
        params[base + number : base + number + 1, :] = jnp.sum(
            jnp.where(place == index * share + number, vec_flat[...], 0.0), axis=0, keepdims=True
        )
    base = 0
    for made, weight in zip(weights, (b_qkv, b_out, b_in, b_fc2)):
        made.wait()
        flatten(weight, params, base)
        base += weight.shape[0] * weight.shape[1] // 128
    fix_one = 1.0 / (1.0 - beta_one**step_count)
    fix_two = 1.0 / (1.0 - beta_two**step_count)
    copies = []
    for number, (start, length) in enumerate(spans):
        for made in loads[number]:
            made.wait()

        @pl.loop(0, step // 56)
        def _(chunk, start=start):
            at = pl.ds(pl.multiple_of(start + chunk * 56, 8), 56)
            grad, param = grads[at, :], params[at, :]
            new_one = beta_one * one[at, :] + (1.0 - beta_one) * grad
            new_two = beta_two * two[at, :] + (1.0 - beta_two) * grad * grad
            one[at, :] = new_one
            two[at, :] = new_two
            change = new_one * fix_one / (jnp.sqrt(new_two * fix_two) + adam_eps)
            params[at, :] = param - learn_rate * (change + decay_rate * param)

        for kind, (source, target) in enumerate(
            ((grads, rows_out), (params, params_out), (one, one_out), (two, two_out))
        ):
            copies.append(
                pltpu.make_async_copy(
                    source.at[start : start + length],
                    target.reshape(size, 128).at[start : start + length],
                    out_sems.at[kind, number],
                )
            )
            copies[-1].start()
    for made in copies:
        made.wait()


def slot_body(tokens, out_grad, lengths, w_qkv, w_out, w_in, w_fc2, vectors, moment_one, moment_two):
    slots, piece, width = tokens.shape
    devices, depth = lax.axis_size("dp"), lax.axis_size("ctx")
    chips = devices // 2
    count = devices * depth
    features = w_in.shape[1]
    half = 2 * piece
    rows = 2 * half
    block = D // devices
    wide = features // devices
    lines = D // count
    total = rows * chips
    low = lambda *shape: pltpu.VMEM(shape, BF16)
    wide_f32 = lambda *shape: pltpu.VMEM(shape, F32)
    anywhere = pl.BlockSpec(memory_space=pl.ANY)
    inside = pl.BlockSpec(memory_space=pltpu.VMEM)
    copies = 96
    out, tokens_grad, grad_qkv, grad_out_w, grad_in, grad_fc2, vector_grad = pl.pallas_call(
        partial(slot_kernel, devices, depth, features),
        out_shape=(
            jax.ShapeDtypeStruct(tokens.shape, BF16),
            jax.ShapeDtypeStruct(tokens.shape, BF16),
            jax.ShapeDtypeStruct((lines, 3 * D), F32),
            jax.ShapeDtypeStruct((lines, D), F32),
            jax.ShapeDtypeStruct((lines, features), F32),
            jax.ShapeDtypeStruct((features // count, D), F32),
            jax.ShapeDtypeStruct((8, 3 * block), F32),
        ),
        in_specs=[anywhere, anywhere, pl.BlockSpec(memory_space=pltpu.SMEM), inside] + [anywhere] * 4,
        out_specs=(inside,) * 7,
        scratch_shapes=[
            low(D, 3 * D // 2),
            low(D // 2, D),
            low(D, features // 2),
            low(features // 2, D),
            low(total, D),
            low(total, D),
            low(total, D),
            low(total, D),
            low(rows, D),
            low(total, 4 * block),
            low(chips - 1, rows, 4 * block),
            low(rows, D),
            pltpu.VMEM((slots, 128), jnp.int32),
            low(rows, 3 * D // 2),
            wide_f32(rows, D),
            low(rows, D),
            low(rows, D),
            low(rows, D),
            low(rows, D),
            wide_f32(half, D),
            wide_f32(rows, D),
            wide_f32(rows, D),
            wide_f32(rows, D),
            wide_f32(rows, features // 2),
            low(rows, features // 2),
            low(total, wide),
            low(total, wide),
            low(chips, 2 * wide // depth, D),
            low(chips - 1, 2 * wide // depth, D),
            low(D, wide),
            low(wide, D),
            low(depth, devices * lines, 4 * block),
            low(depth - 1, devices * lines, 4 * block),
            low(depth - 1, devices * lines, 4 * block),
            low(devices, lines, wide),
            low(devices, lines, wide),
            low(devices, lines + 16, 4 * block),
            low(devices, lines + 16, 4 * block),
            wide_f32(16, D),
            wide_f32(devices * depth, 4 * block),
            wide_f32(depth - 1, devices, 4 * block),
            wide_f32(rows, 4 * block),
            low(rows, 3 * D // 2),
            low(half, D),
            low(*tokens.shape),
            low(half, D),
            low(*tokens.shape),
            pltpu.VMEM((slots, 128), jnp.int32),
            pltpu.SemaphoreType.DMA((6 * chips,)),
            pltpu.SemaphoreType.DMA((copies,)),
            pltpu.SemaphoreType.DMA((copies,)),
        ],
        compiler_params=pltpu.CompilerParams(
            collective_id=0, has_side_effects=True, vmem_limit_bytes=64 * 1024 * 1024 - 64 * 1024
        ),
        name="slot",
    )(tokens, out_grad, lengths, vectors, w_qkv, w_out, w_in, w_fc2)
    size = moment_one.shape[1] // 128
    padded = (size + 279) // 280 * 280
    flat = jax.ShapeDtypeStruct(moment_one.shape, F32)
    return pl.pallas_call(
        partial(adam_kernel, count),
        out_shape=(
            jax.ShapeDtypeStruct(tokens.shape, BF16),
            jax.ShapeDtypeStruct(tokens.shape, BF16),
            flat,
            flat,
            flat,
            flat,
        ),
        in_specs=[inside] * 8 + [anywhere] * 6,
        out_specs=(inside, inside) + (anywhere,) * 4,
        scratch_shapes=[wide_f32(padded, 128)] * 4
        + [
            low(lines, 3 * D),
            low(lines, D),
            low(lines, features),
            low(features // count, D),
            wide_f32(vectors.shape[0] * D // 128, 128),
            pltpu.SemaphoreType.DMA((2, 5)),
            pltpu.SemaphoreType.DMA((4,)),
            pltpu.SemaphoreType.DMA((4, 5)),
        ],
        compiler_params=pltpu.CompilerParams(vmem_limit_bytes=64 * 1024 * 1024 - 64 * 1024),
        name="adam",
    )(
        grad_qkv, grad_out_w, grad_in, grad_fc2, vector_grad, vectors, out, tokens_grad,
        w_qkv, w_out, w_in, w_fc2, moment_one, moment_two,
    )


def layer(tokens, *rest):
    slots, piece, width = tokens.shape
    devices, depth = lax.axis_size("dp"), lax.axis_size("ctx")
    fits = slots == 2 and depth == 2 * slots and devices == 2 * depth and FF == (devices // 2) * D
    if fits and (H * HD // devices) % 128 == 0 and (FF // devices) % 128 == 0:
        return slot_body(tokens, *rest)
    return body(tokens, *rest)


def solution(mesh):
    placed = (
        P("dp", "ctx", None),
        P("dp", "ctx", None),
        P("dp"),
        P(),
        P(),
        P(),
        P(),
        P(),
        P(("dp", "ctx"), None),
        P(("dp", "ctx"), None),
    )
    return jax.shard_map(
        layer,
        mesh=mesh,
        in_specs=placed,
        out_specs=(
            P("dp", "ctx", None),
            P("dp", "ctx", None),
            P(("dp", "ctx"), None),
            P(("dp", "ctx"), None),
            P(("dp", "ctx"), None),
            P(("dp", "ctx"), None),
        ),
        check_vma=False,
    )
```

```python
from functools import partial

import jax
import jax.numpy as jnp
from jax import lax
from jax.experimental import pallas as pl
from jax.experimental.pallas import tpu as pltpu
from jax.sharding import PartitionSpec as P

D = 1024
H = 16
HD = 64
FF = 4096


EPSILON = 1e-05
learn_rate = 0.01
beta_one = 0.9
beta_two = 0.999
adam_eps = 1e-08
decay_rate = 0.01
step_count = 10.0


def layer_norm(values, gain, shift):
    center = values - jnp.mean(values, axis=-1, keepdims=True)
    spread = jnp.mean(center * center, axis=-1, keepdims=True)
    return center * lax.rsqrt(spread + EPSILON) * gain + shift


def split_vectors(vectors):
    ratio = FF // D
    return (
        vectors[0],
        vectors[1],
        vectors[2],
        vectors[3 : 3 + ratio].reshape(FF),
        vectors[3 + ratio],
        vectors[4 + ratio],
        vectors[5 + ratio],
        vectors[6 + ratio],
        vectors[7 + ratio],
    )


def inner(left, right):
    return lax.dot_general(
        left, right, (((0,), (0,)), ((), ())), preferred_element_type=jnp.float32
    )


def through(left, weight):
    return lax.dot_general(
        left, weight, (((1,), (1,)), ((), ())), preferred_element_type=jnp.float32
    )


def run_slots(function, items):
    return lax.map(lambda item: function(*item), items)


def heads_block():
    return 4


def split_heads(matrix):
    count = matrix.shape[0]
    group = heads_block()
    return jnp.moveaxis(matrix.reshape(count, H // group, group, HD), 1, 0)


def join_heads(blocked):
    return jnp.moveaxis(blocked, 0, 1).reshape(blocked.shape[1], H * HD)


def split_stats(stats):
    group = heads_block()
    return stats.reshape(H // group, group, stats.shape[-1])


def shard_piece(left, right, number, shard_count):
    weight_rows = left.shape[1]
    columns = right.shape[1]
    per_shard = weight_rows * columns // shard_count
    block = inner(left, right).reshape(-1)
    return block.reshape(number, per_shard)


def project(flat_tokens, w_qkv, vectors):
    joined = jnp.dot(flat_tokens, w_qkv, preferred_element_type=jnp.float32)
    queries = ((joined[:, :D] + vectors[0]) * 0.125).astype(jnp.bfloat16)
    keys = joined[:, D : 2 * D].astype(jnp.bfloat16)
    values = (joined[:, 2 * D :] + vectors[1]).astype(jnp.bfloat16)
    return (queries, keys, values)


def attend_slot(queries, keys, values, live):
    rows = queries.shape[0]

    def attend_one_block(item):
        query_heads, key_heads, value_heads = item
        scores = jnp.einsum(
            "qhd,khd->hqk", query_heads, key_heads, preferred_element_type=jnp.float32
        )
        scores = jnp.where(live[None, None, :], scores, -1e30)
        maximum = jnp.max(scores, axis=-1, keepdims=True)
        expo = jnp.exp(scores - maximum)
        total = jnp.sum(expo, axis=-1, keepdims=True)
        probs_low = (expo / total).astype(jnp.bfloat16)
        mixed = jnp.einsum(
            "hqk,khd->qhd", probs_low, value_heads, preferred_element_type=jnp.float32
        )
        return (mixed, (maximum + jnp.log(total))[..., 0])

    mixed, log_total = lax.map(
        attend_one_block, (split_heads(queries), split_heads(keys), split_heads(values))
    )
    return (join_heads(mixed), log_total.reshape(H, rows))


def query_back(queries, keys, values, live, log_total, grad_mixed, with_keys):
    rows = queries.shape[0]

    def query_one_block(item):
        query_heads, key_heads, value_heads, grad_heads, block_log = item
        scores = jnp.einsum(
            "qhd,khd->hqk", query_heads, key_heads, preferred_element_type=jnp.float32
        )
        scores = jnp.where(live[None, None, :], scores, -1e30)
        probs = jnp.exp(scores - block_log[:, :, None])
        grad_probs = jnp.einsum(
            "qhd,khd->hqk", grad_heads, value_heads, preferred_element_type=jnp.float32
        )
        row_sums = jnp.sum(probs * grad_probs, axis=-1)
        grad_scores = (probs * (grad_probs - row_sums[:, :, None])).astype(jnp.bfloat16)
        grad_query = jnp.einsum(
            "hqk,khd->qhd", grad_scores, key_heads, preferred_element_type=jnp.float32
        )
        grad_key = jnp.einsum(
            "hqk,qhd->khd", grad_scores, query_heads, preferred_element_type=jnp.float32
        )
        grad_value = jnp.einsum(
            "hqk,qhd->khd",
            probs.astype(jnp.bfloat16),
            grad_heads,
            preferred_element_type=jnp.float32,
        )
        return (grad_query, row_sums, grad_key, grad_value)

    items = (
        split_heads(queries),
        split_heads(keys),
        split_heads(values),
        split_heads(grad_mixed),
        split_stats(log_total),
    )
    results = lax.map(query_one_block, items)
    grad_query, row_sums, grad_key, grad_value = results
    return (
        join_heads(grad_query),
        row_sums.reshape(H, rows),
        join_heads(grad_key),
        join_heads(grad_value),
    )


def tail(flat_tokens, mixed, w_out, w_in, w_fc2, vectors):
    bias_q, bias_v, bias_o, bias_in, bias_fc2, gain_one, shift_one, gain_two, shift_two = (
        split_vectors(vectors)
    )
    mixed_low = mixed.astype(jnp.bfloat16)
    summed_one = (
        flat_tokens.astype(jnp.float32)
        + jnp.dot(mixed_low, w_out, preferred_element_type=jnp.float32)
        + bias_o
    )
    normed = layer_norm(summed_one, gain_one, shift_one)
    normed_low = normed.astype(jnp.bfloat16)
    hidden_pre = jnp.dot(normed_low, w_in, preferred_element_type=jnp.float32) + bias_in
    hidden_low = jax.nn.gelu(hidden_pre, approximate=False).astype(jnp.bfloat16)
    summed_two = normed + jnp.dot(hidden_low, w_fc2, preferred_element_type=jnp.float32) + bias_fc2
    result = layer_norm(summed_two, gain_two, shift_two)
    return (mixed_low, summed_one, normed_low, hidden_pre, hidden_low, summed_two, result)


def body(tokens, out_grad, lengths, w_qkv, w_out, w_in, w_fc2, vectors, moment_one, moment_two):
    slots, piece, width = tokens.shape
    length = piece * lax.axis_size("ctx")
    local_pos = lax.axis_index("ctx") * piece + jnp.arange(piece, dtype=jnp.int32)
    own_live = local_pos[None, :] < lengths[:, None]
    valid = own_live.astype(jnp.float32)
    key_live = jnp.arange(length, dtype=jnp.int32)[None, :] < lengths[:, None]
    bias_q, bias_v, bias_o, bias_in, bias_fc2, gain_one, shift_one, gain_two, shift_two = (
        split_vectors(vectors)
    )
    flat_tokens = tokens.reshape(slots * piece, width)
    queries, keys, values = project(flat_tokens, w_qkv, vectors)
    keys_all, values_all = (
        lax.all_gather(keys.reshape(slots, piece, width), "ctx", axis=1, tiled=True),
        lax.all_gather(values.reshape(slots, piece, width), "ctx", axis=1, tiled=True),
    )
    mixed, log_total = run_slots(
        attend_slot, (queries.reshape(slots, piece, width), keys_all, values_all, key_live)
    )
    saved = tail(flat_tokens, mixed.reshape(slots * piece, width), w_out, w_in, w_fc2, vectors)
    out = (saved[6].reshape(slots, piece, width) * valid[..., None]).astype(jnp.bfloat16)
    again = lax.optimization_barrier(flat_tokens)
    queries, keys, values = project(again, w_qkv, vectors)
    keys_all, values_all = (
        lax.all_gather(keys.reshape(slots, piece, width), "ctx", axis=1, tiled=True),
        lax.all_gather(values.reshape(slots, piece, width), "ctx", axis=1, tiled=True),
    )
    mixed, log_total = run_slots(
        attend_slot, (queries.reshape(slots, piece, width), keys_all, values_all, key_live)
    )
    saved = tail(again, mixed.reshape(slots * piece, width), w_out, w_in, w_fc2, vectors)
    mixed_low, summed_one, normed_low, hidden_pre, hidden_low, summed_two, result = saved
    cotangent = (out_grad.astype(jnp.float32) * valid[..., None]).reshape(slots * piece, width)
    unused_two, norm_two_back = jax.vjp(layer_norm, summed_two, gain_two, shift_two)
    grad_two, grad_gain_two, grad_shift_two = norm_two_back(cotangent)
    grad_fc2_low = grad_two.astype(jnp.bfloat16)
    bias_fc2_grad = jnp.sum(grad_fc2_low.astype(jnp.float32), axis=0)
    grad_hidden = through(grad_fc2_low, w_fc2)
    unused_gelu, gelu_back = jax.vjp(partial(jax.nn.gelu, approximate=False), hidden_pre)
    grad_pre_low = gelu_back(grad_hidden)[0].astype(jnp.bfloat16)
    bias_in_grad = jnp.sum(grad_pre_low.astype(jnp.float32), axis=0)
    grad_normed = grad_two + through(grad_pre_low, w_in)
    unused_one, norm_one_back = jax.vjp(layer_norm, summed_one, gain_one, shift_one)
    grad_one, grad_gain_one, grad_shift_one = norm_one_back(grad_normed)
    grad_branch_low = grad_one.astype(jnp.bfloat16)
    bias_out_grad = jnp.sum(grad_branch_low.astype(jnp.float32), axis=0)
    grad_mixed_low = (
        through(grad_branch_low, w_out).astype(jnp.bfloat16).reshape(slots, piece, width)
    )
    queries_slots = queries.reshape(slots, piece, width)
    grad_query, row_sums, grad_key, grad_value = run_slots(
        partial(query_back, with_keys=True),
        (queries_slots, keys_all, values_all, key_live, log_total, grad_mixed_low),
    )
    grad_key, grad_value = (
        lax.psum_scatter(
            grad_key.astype(jnp.bfloat16), "ctx", scatter_dimension=1, tiled=True
        ).astype(jnp.float32),
        lax.psum_scatter(
            grad_value.astype(jnp.bfloat16), "ctx", scatter_dimension=1, tiled=True
        ).astype(jnp.float32),
    )
    rows = slots * piece
    grad_query_low = grad_query.reshape(rows, width).astype(jnp.bfloat16) * jnp.bfloat16(0.125)
    grad_key_low = grad_key.reshape(rows, width).astype(jnp.bfloat16)
    grad_value_low = grad_value.reshape(rows, width).astype(jnp.bfloat16)
    grad_joined = jnp.concatenate([grad_query_low, grad_key_low, grad_value_low], axis=1)
    bias_q_grad = jnp.sum(grad_query_low.astype(jnp.float32), axis=0)
    bias_v_grad = jnp.sum(grad_value_low.astype(jnp.float32), axis=0)
    tokens_grad = (
        (grad_one + through(grad_joined, w_qkv)).reshape(slots, piece, width).astype(jnp.bfloat16)
    )
    vector_grad = jnp.concatenate(
        [
            bias_q_grad[None],
            bias_v_grad[None],
            bias_out_grad[None],
            bias_in_grad.reshape(FF // D, D),
            bias_fc2_grad[None],
            grad_gain_one[None],
            grad_shift_one[None],
            grad_gain_two[None],
            grad_shift_two[None],
        ],
        axis=0,
    )
    count = lax.axis_size(("dp", "ctx"))
    vector_rows = vector_grad.reshape(count, -1)
    pairs = (
        (flat_tokens, grad_joined),
        (mixed_low, grad_branch_low),
        (normed_low, grad_pre_low),
        (hidden_low, grad_fc2_low),
    )
    blocks = [
        shard_piece(left, right, 1 * lax.axis_size(("dp", "ctx")), count) for left, right in pairs
    ]
    blocks.append(vector_rows)
    grad_rows = lax.psum_scatter(
        jnp.concatenate(blocks, axis=1), ("dp", "ctx"), scatter_dimension=0, tiled=True
    )
    index = lax.axis_index(("dp", "ctx"))
    params = jnp.concatenate(
        [
            lax.dynamic_slice_in_dim(weight.reshape(count, -1), index, 1, 0).astype(jnp.float32)
            for weight in (w_qkv, w_out, w_in, w_fc2, vectors)
        ],
        axis=1,
    )
    new_one = beta_one * moment_one + (1.0 - beta_one) * grad_rows
    new_two = beta_two * moment_two + (1.0 - beta_two) * grad_rows * grad_rows
    fix_one = 1.0 - beta_one**step_count
    fix_two = 1.0 - beta_two**step_count
    update = new_one / fix_one / (jnp.sqrt(new_two / fix_two) + adam_eps)
    new_params = params - learn_rate * (update + decay_rate * params)
    return (out, tokens_grad, grad_rows, new_params, new_one, new_two)


BF16 = jnp.bfloat16
F32 = jnp.float32


def layer_norm_stats(values):
    center = values - jnp.mean(values, axis=-1, keepdims=True)
    spread = jnp.mean(center * center, axis=-1, keepdims=True)
    return center, lax.rsqrt(spread + EPSILON)


def layer_norm_back(center, scale, gain, cotangent):
    scaled = cotangent * gain
    mean_scaled = jnp.mean(scaled, axis=-1, keepdims=True)
    mean_cross = jnp.mean(scaled * center, axis=-1, keepdims=True)
    return scale * (scaled - mean_scaled - center * (scale * scale) * mean_cross)


def normal_cdf(values):
    return 0.5 * (1.0 + lax.erf(values * 0.7071067811865476))


def dot(left, right):
    return jnp.dot(left, right, preferred_element_type=F32)


def positions(axis, shape, slot, piece):
    place = lax.broadcasted_iota(jnp.int32, shape, axis)
    block = lax.div(place, piece)
    half = lax.div(block, 2)
    step = lax.rem(block, 2)
    return (2 * half + lax.rem(slot + step, 2)) * piece + lax.rem(place, piece)


def head_probs(queries, keys, live):
    scores = through(queries, keys)
    scores = jnp.where(live, scores, -1e30)
    expo = jnp.exp(scores - jnp.max(scores, axis=-1, keepdims=True))
    return expo / jnp.sum(expo, axis=-1, keepdims=True)


MESH = pl.DeviceIdType.MESH


class Links:
    def __init__(self, sends, recvs):
        self.sends, self.recvs = sends, recvs
        self.used = 0
        self.open = []

    def copy(self, source, target, device):
        self.used += 1
        return self.again(source, target, device)

    def again(self, source, target, device):
        number = self.used - 1
        return pltpu.make_async_remote_copy(
            src_ref=source,
            dst_ref=target,
            send_sem=self.sends.at[number],
            recv_sem=self.recvs.at[number],
            device_id=device,
            device_id_type=MESH,
        )

    def forward(self, source, target, device, earlier):
        self.used += 1
        return pltpu.make_async_remote_copy(
            src_ref=source,
            dst_ref=target,
            send_sem=self.sends.at[self.used - 1],
            recv_sem=self.recvs.at[earlier],
            device_id=device,
            device_id_type=MESH,
        )

    def send(self, source, target, device):
        made = self.copy(source, target, device)
        made.start()
        self.open.append((made, None))
        return made

    def send_if(self, condition, source, target, device):
        made = self.copy(source, target, device)
        pl.when(condition)(made.start)
        self.open.append((made, condition))
        return made

    def send_or_keep(self, here, source, target, device):
        number = self.used
        made = self.copy(source, target, device)
        local = pltpu.make_async_copy(source, target, self.recvs.at[number])
        pl.when(here)(local.start)
        away = jnp.logical_not(here)
        pl.when(away)(made.start)
        self.open.append((made, away))

        def wait():
            pl.when(here)(local.wait)
            pl.when(away)(made.wait_recv)

        return wait

    def close(self):
        for made, condition in self.open:
            if condition is None:
                made.wait_send()
            else:
                pl.when(condition)(made.wait_send)


def flip(value, mask):
    result = value
    bit = 1
    while bit <= mask:
        if mask & bit:
            result = result + bit * (1 - 2 * lax.rem(lax.div(value, bit), 2))
        bit *= 2
    return result


def flip_traced(value, mask, size):
    result = value
    bit = 1
    while bit < size:
        set_bit = lax.rem(lax.div(mask, bit), 2)
        result = result + bit * set_bit * (1 - 2 * lax.rem(lax.div(value, bit), 2))
        bit *= 2
    return result


def at_rows(start, size):
    return pl.ds(pl.multiple_of(start, 64), size)


def slot_kernel(devices, depth, features, *refs):
    (
        tokens, out_grad, lengths, vec, w_qkv, w_out, w_in, w_fc2,
        out_ref, tgrad_ref, g_qkv, g_out, g_in, g_fc2, g_vec,
        wqkv, wo, w_up, w_down,
        x_all, n_all, g_all, m_all, b_all, j_all, j_send, g_rows, lens_peer,
        qkv, part, part_low, part_a, part_b, part_c, part_d, summed, grad_two, grad_one,
        pre_s, hid, hid_all, gp_all, packed, plane_got, up_mine, down_mine, packed_two, right_two, left_two,
        trade_in, got_in, trade_qkv, got_qkv, vec_s, vec_by, vec_got, sums, dqkv, out_half, out_got, tg_half, tg_got, lens,
        local_sems, sends, recvs,
    ) = refs
    chips = devices // 2
    me, slot = lax.axis_index("dp"), lax.axis_index("ctx")
    core, chip = lax.rem(me, 2), lax.div(me, 2)
    base = me - core
    peer = (base + 1 - core, slot)
    piece = tokens.shape[1]
    half = 2 * piece
    rows = 2 * half
    block = D // devices
    wide = features // devices
    lines = D // (devices * depth)
    net = Links(sends, recvs)
    mine_at = at_rows(core * half, half)
    other_at = at_rows((1 - core) * half, half)
    chunk = 32

    row_of = lax.broadcasted_iota(jnp.int32, lens.shape, 0)
    lens[...] = jnp.where(row_of == 0, lengths[0], lengths[1])
    vec_s[...] = jnp.zeros_like(vec_s)
    loads = []

    def load(source, target):
        made = pltpu.make_async_copy(source, target, local_sems.at[len(loads)])
        made.start()
        loads.append(made)

    where = [2 * flip(chip, mask) + core for mask in range(chips)]
    for mask in range(chips):
        for kind in range(3):
            start = pl.multiple_of(kind * D + where[mask] * block, block)
            load(
                w_qkv.at[:, pl.ds(start, block)],
                wqkv.at[:, (3 * mask + kind) * block : (3 * mask + kind + 1) * block],
            )
    n_qkv = len(loads)
    for number in range(chips):
        start = pl.multiple_of((2 * number + core) * block, block)
        load(w_out.at[pl.ds(start, block), :], wo.at[number * block : (number + 1) * block, :])
    n_out = len(loads)
    for mask in range(chips):
        start = pl.multiple_of(where[mask] * wide, wide)
        load(w_in.at[:, pl.ds(start, wide)], w_up.at[:, mask * wide : (mask + 1) * wide])
    n_up = len(loads)
    for mask in range(chips):
        start = pl.multiple_of(where[mask] * wide, wide)
        load(w_fc2.at[pl.ds(start, wide), :], w_down.at[mask * wide : (mask + 1) * wide, :])

    barrier = pltpu.get_barrier_semaphore()
    friends = [(flip(me, mask), slot) for mask in range(1, devices)]
    for shift in range(1, depth):
        far = lax.rem(slot + shift, depth)
        friends += [(me, far), (flip(me, 1), far)]
    for friend in friends:
        pl.semaphore_signal(barrier, inc=1, device_id=friend, device_id_type=MESH)
    pl.semaphore_wait(barrier, len(friends))

    def spread(source, target):
        waits = []
        for step in range(2):
            pick = lax.rem(slot + step, 2)
            upper = lax.div(slot, 2)
            place = 2 * core + pick
            here = jnp.logical_and(upper == core, place == slot)
            waits.append(
                net.send_or_keep(
                    here,
                    source.at[pick],
                    target.at[at_rows((2 * upper + step) * piece, piece)],
                    (base + upper, place),
                )
            )
        return waits

    def pass_on(waits, target):
        made = []
        for step, wait in enumerate(waits):
            wait()
            spot = target.at[at_rows((2 * core + step) * piece, piece)]
            made.append(net.send(spot, spot, peer))
        return made

    token_waits = spread(tokens, x_all)
    grad_waits = spread(out_grad, g_rows)
    lens_copy = net.send(lens, lens_peer, peer)
    token_passes = pass_on(token_waits, x_all)

    def plane_start(target):
        source = target.at[mine_at]
        return [
            net.send(
                source, target.at[at_rows(mask * rows + core * half, half)], (flip(me, 2 * mask), slot)
            )
            for mask in range(1, chips)
        ]

    def plane_pass(copies, target):
        made = []
        for mask, copy in enumerate(copies, 1):
            copy.wait_recv()
            spot = target.at[at_rows(mask * rows + core * half, half)]
            made.append(net.send(spot, spot, peer))
        return made

    class Column:
        def __init__(self, target):
            self.target = target
            self.parts, self.numbers = {}, {}
            for place in (2, 1, 3):
                far = lax.rem(slot + depth - place, depth)
                made = net.copy(target.at[mine_at], self.spot(place), (me, far))
                self.parts[place], self.numbers[place] = made, net.used - 1
                goes = {1: slot != 0, 2: slot >= 0, 3: slot != depth - 1}[place]
                net.open.append((made, goes))
                pl.when(goes)(made.start)
            self.passes = {}

        def spot(self, place):
            return self.target.at[at_rows(place * rows + core * half, half)]

        def relay(self):
            self.parts[2].wait_recv()
            up = net.forward(self.spot(2), self.spot(1), (me, depth - 1), self.numbers[1])
            down = net.forward(self.spot(2), self.spot(3), (me, 0), self.numbers[3])
            for made, here in ((up, slot == 2), (down, slot == 1)):
                pl.when(here)(made.start)
                net.open.append((made, here))
            self.passes[2] = net.send(self.spot(2), self.spot(2), peer)

        def hand_over(self, place):
            self.parts[place].wait_recv()
            self.passes[place] = net.send(self.spot(place), self.spot(place), peer)

    x_plane = plane_start(x_all)
    for made in loads[:n_qkv]:
        made.wait()
    lens_copy.wait_recv()
    for made in token_passes:
        made.wait_recv()
    owned = jnp.where(lax.div(slot, 2) == core, lens[...], lens_peer[...])
    length = jnp.where(lax.rem(slot, 2) == 0, owned[0:1, 0:1], owned[1:2, 0:1])
    live = positions(1, (1, rows), slot, piece) < length
    lane = lax.broadcasted_iota(jnp.int32, (1, block), 1)

    @pl.loop(0, chips)
    def _(mask):
        spot = 2 * flip_traced(chip, mask, chips) + core
        lanes = pl.ds(pl.multiple_of(spot * block, block), block)
        joined = dot(x_all[0:rows, :], wqkv[:, pl.ds(pl.multiple_of(mask * 3 * block, block), 3 * block)])
        queries = ((joined[:, 0:block] + vec[0:1, lanes]) * 0.125).astype(BF16)
        keys = joined[:, block : 2 * block].astype(BF16)
        values = (joined[:, 2 * block :] + vec[1:2, lanes]).astype(BF16)
        total = jnp.zeros((rows, block), F32)
        for head in range(block // HD):
            mine = lax.div(lane, HD) == head
            probs = head_probs(jnp.where(mine, queries, jnp.zeros_like(queries)), keys, live)
            total = jnp.where(mine, dot(probs.astype(BF16), values), total)
        start = pl.multiple_of(mask * 3 * block, block)
        qkv[:, pl.ds(start, block)] = queries
        qkv[:, pl.ds(pl.multiple_of(start + block, block), block)] = keys
        qkv[:, pl.ds(pl.multiple_of(start + 2 * block, block), block)] = values
        lanes = pl.ds(pl.multiple_of(core * chips * block + lax.div(spot, 2) * block, block), block)
        m_all[0:rows, lanes] = total.astype(BF16)

    for made in loads[n_qkv:n_out]:
        made.wait()

    def exchange(compute, target, before):
        made = []
        for number, at in enumerate((other_at, mine_at)):
            if before is not None:
                before[number].wait_send()
            value = compute(at)
            part[at, :] = value
            part_low[at, :] = value.astype(BF16)
            made.append(net.copy(part_low.at[at], target.at[at], peer))
            made[-1].start()
        return made

    my_lanes = pl.ds(pl.multiple_of(core * chips * block, chips * block), chips * block)
    first = exchange(lambda at: dot(m_all[at, my_lanes], wo[...]), part_a, None)
    own_mixed = m_all.at[0:rows, my_lanes]
    m_passes = [net.send(own_mixed, own_mixed, peer)]
    m_plane = [
        net.send(own_mixed, m_all.at[mask * rows : (mask + 1) * rows, my_lanes], (flip(me, 2 * mask), slot))
        for mask in range(1, chips)
    ]
    grad_passes = pass_on(grad_waits, g_rows)

    def norm_one(start):
        @pl.loop(0, half // chunk)
        def _(step):
            at = pl.ds(pl.multiple_of(start + step * chunk, chunk), chunk)
            total = x_all[at, :].astype(F32) + (part[at, :] + part_a[at, :].astype(F32)) + vec[2:3, :]
            center, scale = layer_norm_stats(total)
            summed[at, :] = total
            n_all[at, :] = (center * scale * vec[8:9, :] + vec[9:10, :]).astype(BF16)

    first[0].wait_recv()
    norm_one(core * half)
    n_column = Column(n_all)
    first[1].wait_recv()
    norm_one((1 - core) * half)
    for made in loads[n_out:]:
        made.wait()

    for number in range(chips):
        fine_cols = wide // depth
        begin = flip_traced(chip, number, chips) * wide + slot * fine_cols
        at = pl.ds(pl.multiple_of(begin, fine_cols), fine_cols)
        up_mine[:, number * fine_cols : (number + 1) * fine_cols] = w_up[:, at]
        down_mine[number * fine_cols : (number + 1) * fine_cols, :] = w_down[at, :]

    def bias_of(mask):
        spot = flip_traced(chip, mask, chips)
        lanes = pl.ds(pl.multiple_of(core * wide, wide), wide)
        result = vec[3:4, lanes]
        for row in range(1, chips):
            result = jnp.where(spot == row, vec[3 + row : 4 + row, lanes], result)
        return result

    @pl.loop(0, chips)
    def _(mask):
        at = pl.ds(pl.multiple_of(mask * wide, wide), wide)
        value = dot(n_all[0:rows, :], w_up[:, at]) + bias_of(mask)
        pre_s[:, at] = value
        hid[:, at] = (value * normal_cdf(value)).astype(BF16)

    second = exchange(lambda at: dot(hid[at, :], w_down[...]), part_b, first)
    for made in grad_passes:
        made.wait_recv()

    def norm_two(start, own):
        @pl.loop(0, half // chunk)
        def _(step):
            begin = pl.multiple_of(start + step * chunk, chunk)
            at = pl.ds(begin, chunk)
            center, scale = layer_norm_stats(summed[at, :])
            normed = center * scale * vec[8:9, :] + vec[9:10, :]
            center, scale = layer_norm_stats(normed + (part[at, :] + part_b[at, :].astype(F32)) + vec[7:8, :])
            place = begin + lax.broadcasted_iota(jnp.int32, (chunk, 1), 0)
            piece_of = lax.div(place, piece)
            spot = 2 * lax.div(piece_of, 2) + lax.rem(slot + lax.rem(piece_of, 2), 2)
            valid = (spot * piece + lax.rem(place, piece) < length).astype(F32)
            unit = center * scale
            error = g_rows[at, :].astype(F32) * valid
            grad = layer_norm_back(center, scale, vec[10:11, :], error)
            grad_two[at, :] = grad
            low = grad.astype(BF16)
            g_all[at, :] = low
            if own:
                out_half[pl.ds(pl.multiple_of(step * chunk, chunk), chunk), :] = (
                    valid * (unit * vec[10:11, :] + vec[11:12, :])
                ).astype(BF16)
                vec_s[7:8, :] += jnp.sum(low.astype(F32), axis=0, keepdims=True)
                vec_s[10:11, :] += jnp.sum(error * unit, axis=0, keepdims=True)
                vec_s[11:12, :] += jnp.sum(error, axis=0, keepdims=True)

    def go_back(source, target):
        waits = []
        for step in range(2):
            place = 2 * core + lax.rem(slot + step, 2)
            upper = lax.div(slot, 2)
            here = jnp.logical_and(upper == core, place == slot)
            waits.append(
                net.send_or_keep(
                    here,
                    source.at[step * piece : (step + 1) * piece],
                    target.at[lax.rem(slot, 2)],
                    (base + upper, place),
                )
            )
        return waits

    second[0].wait_recv()
    norm_two(core * half, True)
    g_column = Column(g_all)
    second[1].wait_recv()
    norm_two((1 - core) * half, False)
    out_waits = go_back(out_half, out_got)

    def mixed_pass():
        for mask, made in enumerate(m_plane, 1):
            made.wait_recv()
            spot = m_all.at[mask * rows : (mask + 1) * rows, my_lanes]
            m_passes.append(net.send(spot, spot, peer))

    def slope_of(value, cdf):
        return cdf + value * (jnp.exp(-0.5 * value * value) * 0.3989422804014327)

    @pl.loop(0, chips)
    def _(mask):
        at = pl.ds(pl.multiple_of(mask * wide, wide), wide)
        value = pre_s[:, at]
        grad = through(g_all[0:rows, :], w_down[at, :])
        hid[:, at] = (grad * slope_of(value, normal_cdf(value))).astype(BF16)

    third = exchange(lambda at: through(hid[at, :], w_up[...]), part_c, second)

    def norm_one_back(start, own):
        @pl.loop(0, half // chunk)
        def _(step):
            at = pl.ds(pl.multiple_of(start + step * chunk, chunk), chunk)
            center, scale = layer_norm_stats(summed[at, :])
            error = grad_two[at, :] + (part[at, :] + part_c[at, :].astype(F32))
            grad = layer_norm_back(center, scale, vec[8:9, :], error)
            low = grad.astype(BF16)
            b_all[at, :] = low
            grad_one[at, :] = grad
            if own:
                vec_s[2:3, :] += jnp.sum(low.astype(F32), axis=0, keepdims=True)
                vec_s[8:9, :] += jnp.sum(error * (center * scale), axis=0, keepdims=True)
                vec_s[9:10, :] += jnp.sum(error, axis=0, keepdims=True)

    x_pass = plane_pass(x_plane, x_all)

    third[0].wait_recv()
    norm_one_back(core * half, True)
    third[1].wait_recv()
    norm_one_back((1 - core) * half, False)
    class Line:
        def __init__(self, chunks, from_left, from_right):
            self.chunks, self.from_left, self.from_right = chunks, from_left, from_right
            self.up, self.down, self.first_up, self.first_down = [], [], [], []
            after = (me, lax.rem(slot + 1, depth))
            before = (me, lax.rem(slot + depth - 1, depth))
            for order in range(depth - 1):
                top, low = depth - 1 - order, order
                spot = from_left.at[order]
                self.up.append(net.copy(spot, spot, after))
                self.first_up.append(net.again(chunks.at[top], spot, after))
                net.open.append((self.up[-1], slot < top))
                spot = from_right.at[order]
                self.down.append(net.copy(spot, spot, before))
                self.first_down.append(net.again(chunks.at[low], spot, before))
                net.open.append((self.down[-1], slot > low))

        def first(self):
            for order in range(depth - 1):
                pl.when(slot == 0)(self.first_up[order].start)
                pl.when(slot == depth - 1)(self.first_down[order].start)

        def stage(self, time):
            for order in range(time):
                top, low = depth - 1 - order, order

                @pl.when(slot == time - order)
                def _(order=order, top=top):
                    self.up[order].wait_recv()
                    if time < depth - 1:
                        self.from_left[order] = (
                            self.from_left[order].astype(F32) + self.chunks[top].astype(F32)
                        ).astype(BF16)
                        self.up[order].start()

                @pl.when(depth - 1 - slot == time - order)
                def _(order=order, low=low):
                    self.down[order].wait_recv()
                    if time < depth - 1:
                        self.from_right[order] = (
                            self.from_right[order].astype(F32) + self.chunks[low].astype(F32)
                        ).astype(BF16)
                        self.down[order].start()

    grad_parts = range(1, chips)

    def attention_back(mask):
        start = mask * 3 * block
        queries = qkv[:, start : start + block]
        keys = qkv[:, start + block : start + 2 * block]
        values = qkv[:, start + 2 * block : start + 3 * block]
        turn = pl.ds(pl.multiple_of(lax.div(where[mask], 2) * block, block), block)
        grad_mixed = through(b_all[0:rows, :], wo[turn, :]).astype(BF16)
        grad_q = jnp.zeros((rows, block), F32)
        grad_k = grad_q
        grad_v = grad_q
        for head in range(block // HD):
            mine = lax.div(lane, HD) == head
            probs = head_probs(jnp.where(mine, queries, jnp.zeros_like(queries)), keys, live)
            grad_probs = through(jnp.where(mine, grad_mixed, jnp.zeros_like(grad_mixed)), values)
            dsum = jnp.sum(probs * grad_probs, axis=-1, keepdims=True)
            grad_scores = (probs * (grad_probs - dsum)).astype(BF16)
            grad_q = jnp.where(mine, dot(grad_scores, keys), grad_q)
            grad_k = jnp.where(mine, inner(grad_scores, queries), grad_k)
            grad_v = jnp.where(mine, inner(probs.astype(BF16), grad_mixed), grad_v)
        grad_q = grad_q.astype(BF16) * jnp.bfloat16(0.125)
        grad_k = grad_k.astype(BF16)
        grad_v = grad_v.astype(BF16)
        spot = pl.ds(pl.multiple_of(where[mask] * block, block), block)
        vec_s[0:1, spot] = jnp.sum(grad_q.astype(F32), axis=0, keepdims=True)
        vec_s[1:2, spot] = jnp.sum(grad_v.astype(F32), axis=0, keepdims=True)
        dqkv[:, start : start + block] = grad_q
        dqkv[:, start + block : start + 2 * block] = grad_k
        dqkv[:, start + 2 * block : start + 3 * block] = grad_v
        if mask:
            joint = j_send.at[mask - 1]
        else:
            joint = j_all.at[0:rows]
        joint[:, 0:block] = grad_q
        joint[:, block : 2 * block] = grad_k
        joint[:, 2 * block : 3 * block] = grad_v
        joint[:, 3 * block : 4 * block] = b_all[0:rows, spot]
        if mask:
            return net.send(
                joint, j_all.at[mask * rows : (mask + 1) * rows], (flip(me, 2 * mask), slot)
            )
        return None

    n_column.relay()
    j_copies = [attention_back(mask) for mask in grad_parts]
    attention_back(0)
    mixed_pass()
    n_column.hand_over(1)
    n_column.hand_over(3)
    for made in third:
        made.wait_send()
    part[0:half, :] = through(dqkv[other_at, :], wqkv[...])
    tg_copy = net.copy(part.at[0:half], part_d, peer)
    tg_copy.start()
    part[half:rows, :] = grad_one[mine_at, :] + through(dqkv[mine_at, :], wqkv[...])
    tg_copy.wait_recv()
    tg_half[...] = (part[half:rows, :] + part_d[...]).astype(BF16)

    fine = wide // depth
    span = lines * depth
    features_at = pl.ds(pl.multiple_of((depth * core + slot) * fine, fine), fine)
    bias_mine = jnp.concatenate([vec[3 + number : 4 + number, features_at] for number in range(chips)], axis=1)

    def feed_rows(place):
        at = slice(place * rows, (place + 1) * rows)
        value = dot(n_all[at, :], up_mine[...]) + bias_mine
        cdf = normal_cdf(value)
        hid_all[at, :] = (value * cdf).astype(BF16)
        low = (through(g_all[at, :], down_mine[...]) * slope_of(value, cdf)).astype(BF16)
        gp_all[at, :] = low
        return jnp.sum(low.astype(F32), axis=0, keepdims=True)

    bias_sum = feed_rows(0)
    g_column.relay()
    for made in m_passes + x_pass + j_copies:
        made.wait_recv()
    for group in range(devices):
        at = slice(group * span, (group + 1) * span)
        begin = (group % 2) * chips * block + (group // 2) * block
        both = inner(x_all[:, at], j_all[:, 0 : 3 * block]).astype(BF16)
        across = inner(m_all[:, begin : begin + block], j_all[:, 3 * block : 4 * block]).astype(BF16)
        row = group * lines
        for number in range(depth):
            at = slice(number * lines, (number + 1) * lines)
            packed_two[number, row : row + lines, 0 : 3 * block] = both[at, :]
            packed_two[number, row : row + lines, 3 * block : 4 * block] = across[at, :]
    input_line = Line(packed_two, right_two, left_two)
    input_line.first()

    g_column.hand_over(1)
    g_column.hand_over(3)
    for place in (2, 1, 3):
        n_column.passes[place].wait_recv()
        g_column.passes[place].wait_recv()
        bias_sum = bias_sum + feed_rows(place)
    for number in range(chips):
        vec_s[3 + number : 4 + number, features_at] = bias_sum[:, number * fine : (number + 1) * fine]
    depth_rows = D // chips
    for number in range(chips):
        block_up = inner(n_all[:, number * depth_rows : (number + 1) * depth_rows], gp_all[...]).astype(BF16)
        packed[number, fine : 2 * fine, 0:wide] = block_up[0:fine, :]
        packed[number, fine : 2 * fine, wide : 2 * wide] = block_up[fine : 2 * fine, :]

    def scatter_plane(lines_at):
        return [
            net.send(
                packed.at[flip_traced(chip, mask, chips), lines_at],
                plane_got.at[mask - 1, lines_at],
                (flip(me, 2 * mask), slot),
            )
            for mask in range(1, chips)
        ]

    up_copies = scatter_plane(slice(fine, 2 * fine))
    packed[:, 0:fine, :] = inner(hid_all[...], g_all[...]).astype(BF16).reshape(chips, fine, D)
    down_copies = scatter_plane(slice(0, fine))

    tiles = vec.shape[0] * D // 128
    share = tiles // (devices * depth)
    vec_by[...] = jnp.zeros_like(vec_by)
    for tile in range(tiles):
        owner, lane_group = tile // share, tile % share
        row, col = tile // (D // 128), (tile % (D // 128)) * 128
        spot = (owner % depth) * devices + owner // depth
        vec_by[spot : spot + 1, lane_group * 128 : (lane_group + 1) * 128] = vec_s[
            row : row + 1, col : col + 128
        ]
    vec_copies = []
    for shift in range(1, depth):
        far = lax.rem(slot + shift, depth)
        spot = vec_by.at[pl.ds(pl.multiple_of(far * devices, devices), devices)]
        vec_copies.append(net.send(spot, vec_got.at[shift - 1], (me, far)))

    def finish(line, target, rows_at):
        target[...] = line.chunks[slot, rows_at, :].astype(F32)

        @pl.when(slot >= 1)
        def _():
            target[...] += line.from_left[depth - 1 - slot, rows_at, :].astype(F32)

        @pl.when(slot <= depth - 2)
        def _():
            target[...] += line.from_right[slot, rows_at, :].astype(F32)

    def plane_sum(copies, lines_at):
        for made in copies:
            made.wait_recv()
        value = packed[chip, lines_at, :].astype(F32)
        for number in range(chips - 1):
            value = value + plane_got[number, lines_at, :].astype(F32)
        return value

    def trade(source, target):
        return [
            net.send(source.at[flip(me, mask)], target.at[me], (flip(me, mask), slot))
            for mask in range(1, devices)
        ]

    tg_waits = go_back(tg_half, tg_got)
    for time in range(1, depth - 1):
        input_line.stage(time)
    low_sum = plane_sum(up_copies, slice(fine, 2 * fine)).astype(BF16)
    for upper in range(2):
        for number in range(depth):
            trade_in[upper * depth + number] = low_sum[
                number * lines : (number + 1) * lines, upper * wide : (upper + 1) * wide
            ]
    here = core * depth + slot
    in_copies = []
    for shift in range(1, 2 * depth):
        far = lax.rem(slot + shift % depth, depth)
        upper = core if shift < depth else 1 - core
        in_copies.append(net.send(trade_in.at[upper * depth + far], got_in.at[here], (base + upper, far)))
    input_line.stage(depth - 1)
    tg_copy.wait_send()
    finish(input_line, sums, slice(0, rows))
    vec_sum = vec_by[pl.ds(pl.multiple_of(slot * devices, devices), devices), :]
    for number, made in enumerate(vec_copies):
        made.wait_recv()
        vec_sum = vec_sum + vec_got[number]
    first_row = lax.broadcasted_iota(jnp.int32, (16, 4 * block), 0) == 0
    for group in range(devices):
        trade_qkv[group, 0:lines, :] = sums[group * lines : (group + 1) * lines, :].astype(BF16)
        trade_qkv[group, lines : lines + 16, :] = jnp.where(
            first_row, vec_sum[group : group + 1, :], 0.0
        ).astype(BF16)
    qkv_copies = trade(trade_qkv, got_qkv)
    for made in in_copies:
        made.wait_recv()
    got_in[here] = trade_in[here]
    for group in range(2 * depth):
        for number in range(chips):
            start = number * 2 * wide + group * fine
            g_in[:, start : start + fine] = got_in[group, :, number * fine : (number + 1) * fine].astype(F32)
    g_fc2[...] = plane_sum(down_copies, slice(0, fine))
    for wait in out_waits + tg_waits:
        wait()
    out_ref[...] = out_got[...]
    tgrad_ref[...] = tg_got[...]
    for made in qkv_copies:
        made.wait_recv()
    got_qkv[me] = trade_qkv[me]
    vec_sum = jnp.zeros((16, 3 * block), F32)
    for group in range(devices):
        vec_sum = vec_sum + got_qkv[group, lines : lines + 16, 0 : 3 * block].astype(F32)
        got = got_qkv[group, 0:lines, :].astype(F32)
        for kind in range(3):
            g_qkv[:, kind * D + group * block : kind * D + (group + 1) * block] = got[
                :, kind * block : (kind + 1) * block
            ]
        g_out[:, group * block : (group + 1) * block] = got[:, 3 * block : 4 * block]
    g_vec[...] = vec_sum[0:8, :]
    net.close()


def adam_kernel(count, *refs):
    (
        g_qkv, g_out, g_in, g_fc2, g_vec, vec, out_in, tgrad_in, w_qkv, w_out, w_in, w_fc2, m_one, m_two,
        out_ref, tgrad_ref, rows_out, params_out, one_out, two_out,
        grads, params, one, two, d_qkv, d_out, d_in, d_fc2, b_qkv, b_out, b_in, b_fc2, out_by, tgrad_by, vec_flat,
        in_sems, g_sems, w_sems, out_sems, pass_sems,
    ) = refs
    index = lax.axis_index("dp") * lax.axis_size("ctx") + lax.axis_index("ctx")
    size = m_one.shape[1] // 128
    kinds = (
        (g_qkv, d_qkv, w_qkv, b_qkv),
        (g_out, d_out, w_out, b_out),
        (g_in, d_in, w_in, b_in),
        (g_fc2, d_fc2, w_fc2, b_fc2),
    )
    lengths = [kind[1].shape[0] * kind[1].shape[1] // 128 for kind in kinds]
    starts = [sum(lengths[:number]) for number in range(len(kinds))]
    tail = sum(lengths)
    order = (3, 2, 0, 1, 4)
    spans = [(start, length) for start, length in zip(starts, lengths)] + [(tail, size - tail)]

    def load(source, target, sem):
        made = pltpu.make_async_copy(source, target, sem)
        made.start()
        return made

    blocks, loads = {}, {}
    for number in order:
        start, length = spans[number]
        if number < len(kinds):
            grad, grad_by, weight, weight_by = kinds[number]
            lines = weight_by.shape[0]
            mine = pl.ds(pl.multiple_of(index * lines, lines), lines)
            blocks[number] = [
                load(grad, grad_by, g_sems.at[number]),
                load(weight.at[mine, :], weight_by, w_sems.at[number]),
            ]
        loads[number] = [
            load(
                source.reshape(size, 128).at[start : start + length],
                target.at[start : start + length],
                in_sems.at[kind, number],
            )
            for kind, (source, target) in enumerate(((m_one, one), (m_two, two)))
        ]
    passes = [load(out_in, out_by, pass_sems.at[0]), load(tgrad_in, tgrad_by, pass_sems.at[1])]

    def flatten(source, target, base):
        lines, groups = source.shape[0], source.shape[1] // 128
        for col in range(groups):
            value = source[:, col * 128 : (col + 1) * 128].astype(F32)
            for row in range(0, lines, 8):
                target[pl.ds(base + row * groups + col, 8, stride=groups), :] = value[row : row + 8, :]

    def vector_rows():
        share = g_vec.shape[1] // 128
        groups = vec.shape[1] // 128
        for col in range(groups):
            lanes = slice(col * 128, (col + 1) * 128)
            vec_flat[pl.ds(col, 8, stride=groups), :] = vec[0:8, lanes]
            for row in range(8, vec.shape[0]):
                vec_flat[row * groups + col : row * groups + col + 1, :] = vec[row : row + 1, lanes]
        place = lax.broadcasted_iota(jnp.int32, vec_flat.shape, 0)
        for number in range(share):
            spot = slice(tail + number, tail + number + 1)
            grads[spot, :] = g_vec[0:1, number * 128 : (number + 1) * 128]
            params[spot, :] = jnp.sum(
                jnp.where(place == index * share + number, vec_flat[...], 0.0), axis=0, keepdims=True
            )

    fix_one = 1.0 / (1.0 - beta_one**step_count)
    fix_two = 1.0 / (1.0 - beta_two**step_count)

    def update(at):
        grad, param = grads[at, :], params[at, :]
        new_one = beta_one * one[at, :] + (1.0 - beta_one) * grad
        new_two = beta_two * two[at, :] + (1.0 - beta_two) * grad * grad
        one[at, :] = new_one
        two[at, :] = new_two
        change = new_one * fix_one / (jnp.sqrt(new_two * fix_two) + adam_eps)
        params[at, :] = param - learn_rate * (change + decay_rate * param)

    vector_rows()
    copies = []
    for number in order:
        start, length = spans[number]
        if number < len(kinds):
            grad, grad_by, weight, weight_by = kinds[number]
            for made in blocks[number]:
                made.wait()
            flatten(grad_by, grads, start)
            flatten(weight_by, params, start)
        for made in loads[number]:
            made.wait()
        if number < len(kinds):

            @pl.loop(0, length // 64)
            def _(chunk, start=start):
                update(pl.ds(pl.multiple_of(start + chunk * 64, 64), 64))

        else:
            update(slice(start, start + 8))
        for kind, (source, target) in enumerate(
            ((grads, rows_out), (params, params_out), (one, one_out), (two, two_out))
        ):
            copies.append(
                load(
                    source.at[start : start + length],
                    target.reshape(size, 128).at[start : start + length],
                    out_sems.at[kind, number],
                )
            )
        if number == order[0]:
            for made, source, target, sem in zip(
                passes, (out_by, tgrad_by), (out_ref, tgrad_ref), (pass_sems.at[2], pass_sems.at[3])
            ):
                made.wait()
                copies.append(load(source, target, sem))
    for made in copies:
        made.wait()


def slot_body(tokens, out_grad, lengths, w_qkv, w_out, w_in, w_fc2, vectors, moment_one, moment_two):
    slots, piece, width = tokens.shape
    devices, depth = lax.axis_size("dp"), lax.axis_size("ctx")
    chips = devices // 2
    count = devices * depth
    features = w_in.shape[1]
    half = 2 * piece
    rows = 2 * half
    block = D // devices
    wide = features // devices
    lines = D // count
    total = rows * chips
    low = lambda *shape: pltpu.VMEM(shape, BF16)
    wide_f32 = lambda *shape: pltpu.VMEM(shape, F32)
    anywhere = pl.BlockSpec(memory_space=pl.ANY)
    inside = pl.BlockSpec(memory_space=pltpu.VMEM)
    copies = 96
    out, tokens_grad, grad_qkv, grad_out_w, grad_in, grad_fc2, vector_grad = pl.pallas_call(
        partial(slot_kernel, devices, depth, features),
        out_shape=(
            jax.ShapeDtypeStruct(tokens.shape, BF16),
            jax.ShapeDtypeStruct(tokens.shape, BF16),
            jax.ShapeDtypeStruct((lines, 3 * D), F32),
            jax.ShapeDtypeStruct((lines, D), F32),
            jax.ShapeDtypeStruct((lines, features), F32),
            jax.ShapeDtypeStruct((features // count, D), F32),
            jax.ShapeDtypeStruct((8, 3 * block), F32),
        ),
        in_specs=[anywhere, anywhere, pl.BlockSpec(memory_space=pltpu.SMEM), inside] + [anywhere] * 4,
        out_specs=(inside,) * 7,
        scratch_shapes=[
            low(D, 3 * D // 2),
            low(D // 2, D),
            low(D, features // 2),
            low(features // 2, D),
            low(total, D),
            low(total, D),
            low(total, D),
            low(total, D),
            low(rows, D),
            low(total, 4 * block),
            low(chips - 1, rows, 4 * block),
            low(rows, D),
            pltpu.VMEM((slots, 128), jnp.int32),
            low(rows, 3 * D // 2),
            wide_f32(rows, D),
            low(rows, D),
            low(rows, D),
            low(rows, D),
            low(rows, D),
            wide_f32(half, D),
            wide_f32(rows, D),
            wide_f32(rows, D),
            wide_f32(rows, D),
            wide_f32(rows, features // 2),
            low(rows, features // 2),
            low(total, wide),
            low(total, wide),
            low(chips, 2 * wide // depth, D),
            low(chips - 1, 2 * wide // depth, D),
            low(D, wide),
            low(wide, D),
            low(depth, devices * lines, 4 * block),
            low(depth - 1, devices * lines, 4 * block),
            low(depth - 1, devices * lines, 4 * block),
            low(devices, lines, wide),
            low(devices, lines, wide),
            low(devices, lines + 16, 4 * block),
            low(devices, lines + 16, 4 * block),
            wide_f32(16, D),
            wide_f32(devices * depth, 4 * block),
            wide_f32(depth - 1, devices, 4 * block),
            wide_f32(rows, 4 * block),
            low(rows, 3 * D // 2),
            low(half, D),
            low(*tokens.shape),
            low(half, D),
            low(*tokens.shape),
            pltpu.VMEM((slots, 128), jnp.int32),
            pltpu.SemaphoreType.DMA((6 * chips,)),
            pltpu.SemaphoreType.DMA((copies,)),
            pltpu.SemaphoreType.DMA((copies,)),
        ],
        compiler_params=pltpu.CompilerParams(
            collective_id=0, has_side_effects=True, vmem_limit_bytes=64 * 1024 * 1024 - 64 * 1024
        ),
        name="slot",
    )(tokens, out_grad, lengths, vectors, w_qkv, w_out, w_in, w_fc2)
    size = moment_one.shape[1] // 128
    padded = (size + 7) // 8 * 8
    flat = jax.ShapeDtypeStruct(moment_one.shape, F32)
    return pl.pallas_call(
        partial(adam_kernel, count),
        out_shape=(
            jax.ShapeDtypeStruct(tokens.shape, BF16),
            jax.ShapeDtypeStruct(tokens.shape, BF16),
            flat,
            flat,
            flat,
            flat,
        ),
        in_specs=[anywhere] * 4 + [inside] * 2 + [anywhere] * 8,
        out_specs=(anywhere,) * 6,
        scratch_shapes=[wide_f32(padded, 128)] * 4
        + [
            wide_f32(lines, 3 * D),
            wide_f32(lines, D),
            wide_f32(lines, features),
            wide_f32(features // count, D),
            low(lines, 3 * D),
            low(lines, D),
            low(lines, features),
            low(features // count, D),
            low(*tokens.shape),
            low(*tokens.shape),
            wide_f32(vectors.shape[0] * D // 128, 128),
            pltpu.SemaphoreType.DMA((2, 5)),
            pltpu.SemaphoreType.DMA((4,)),
            pltpu.SemaphoreType.DMA((4,)),
            pltpu.SemaphoreType.DMA((4, 5)),
            pltpu.SemaphoreType.DMA((4,)),
        ],
        compiler_params=pltpu.CompilerParams(vmem_limit_bytes=64 * 1024 * 1024 - 64 * 1024),
        name="adam",
    )(
        grad_qkv, grad_out_w, grad_in, grad_fc2, vector_grad, vectors, out, tokens_grad,
        w_qkv, w_out, w_in, w_fc2, moment_one, moment_two,
    )


def layer(tokens, *rest):
    slots, piece, width = tokens.shape
    devices, depth = lax.axis_size("dp"), lax.axis_size("ctx")
    fits = slots == 2 and depth == 2 * slots and devices == 2 * depth and FF == (devices // 2) * D
    if fits and (H * HD // devices) % 128 == 0 and (FF // devices) % 128 == 0:
        return slot_body(tokens, *rest)
    return body(tokens, *rest)


def solution(mesh):
    placed = (
        P("dp", "ctx", None),
        P("dp", "ctx", None),
        P("dp"),
        P(),
        P(),
        P(),
        P(),
        P(),
        P(("dp", "ctx"), None),
        P(("dp", "ctx"), None),
    )
    return jax.shard_map(
        layer,
        mesh=mesh,
        in_specs=placed,
        out_specs=(
            P("dp", "ctx", None),
            P("dp", "ctx", None),
            P(("dp", "ctx"), None),
            P(("dp", "ctx"), None),
            P(("dp", "ctx"), None),
            P(("dp", "ctx"), None),
        ),
        check_vma=False,
    )
```

```python
from functools import partial

import jax
import jax.numpy as jnp
from jax import lax
from jax.experimental import pallas as pl
from jax.experimental.pallas import tpu as pltpu
from jax.sharding import PartitionSpec as P

D = 1024
H = 16
HD = 64
FF = 4096


EPSILON = 1e-05
learn_rate = 0.01
beta_one = 0.9
beta_two = 0.999
adam_eps = 1e-08
decay_rate = 0.01
step_count = 10.0


def layer_norm(values, gain, shift):
    center = values - jnp.mean(values, axis=-1, keepdims=True)
    spread = jnp.mean(center * center, axis=-1, keepdims=True)
    return center * lax.rsqrt(spread + EPSILON) * gain + shift


def split_vectors(vectors):
    ratio = FF // D
    return (
        vectors[0],
        vectors[1],
        vectors[2],
        vectors[3 : 3 + ratio].reshape(FF),
        vectors[3 + ratio],
        vectors[4 + ratio],
        vectors[5 + ratio],
        vectors[6 + ratio],
        vectors[7 + ratio],
    )


def inner(left, right):
    return lax.dot_general(
        left, right, (((0,), (0,)), ((), ())), preferred_element_type=jnp.float32
    )


def through(left, weight):
    return lax.dot_general(
        left, weight, (((1,), (1,)), ((), ())), preferred_element_type=jnp.float32
    )


def run_slots(function, items):
    return lax.map(lambda item: function(*item), items)


def heads_block():
    return 4


def split_heads(matrix):
    count = matrix.shape[0]
    group = heads_block()
    return jnp.moveaxis(matrix.reshape(count, H // group, group, HD), 1, 0)


def join_heads(blocked):
    return jnp.moveaxis(blocked, 0, 1).reshape(blocked.shape[1], H * HD)


def split_stats(stats):
    group = heads_block()
    return stats.reshape(H // group, group, stats.shape[-1])


def shard_piece(left, right, number, shard_count):
    weight_rows = left.shape[1]
    columns = right.shape[1]
    per_shard = weight_rows * columns // shard_count
    block = inner(left, right).reshape(-1)
    return block.reshape(number, per_shard)


def project(flat_tokens, w_qkv, vectors):
    joined = jnp.dot(flat_tokens, w_qkv, preferred_element_type=jnp.float32)
    queries = ((joined[:, :D] + vectors[0]) * 0.125).astype(jnp.bfloat16)
    keys = joined[:, D : 2 * D].astype(jnp.bfloat16)
    values = (joined[:, 2 * D :] + vectors[1]).astype(jnp.bfloat16)
    return (queries, keys, values)


def attend_slot(queries, keys, values, live):
    rows = queries.shape[0]

    def attend_one_block(item):
        query_heads, key_heads, value_heads = item
        scores = jnp.einsum(
            "qhd,khd->hqk", query_heads, key_heads, preferred_element_type=jnp.float32
        )
        scores = jnp.where(live[None, None, :], scores, -1e30)
        maximum = jnp.max(scores, axis=-1, keepdims=True)
        expo = jnp.exp(scores - maximum)
        total = jnp.sum(expo, axis=-1, keepdims=True)
        probs_low = (expo / total).astype(jnp.bfloat16)
        mixed = jnp.einsum(
            "hqk,khd->qhd", probs_low, value_heads, preferred_element_type=jnp.float32
        )
        return (mixed, (maximum + jnp.log(total))[..., 0])

    mixed, log_total = lax.map(
        attend_one_block, (split_heads(queries), split_heads(keys), split_heads(values))
    )
    return (join_heads(mixed), log_total.reshape(H, rows))


def query_back(queries, keys, values, live, log_total, grad_mixed, with_keys):
    rows = queries.shape[0]

    def query_one_block(item):
        query_heads, key_heads, value_heads, grad_heads, block_log = item
        scores = jnp.einsum(
            "qhd,khd->hqk", query_heads, key_heads, preferred_element_type=jnp.float32
        )
        scores = jnp.where(live[None, None, :], scores, -1e30)
        probs = jnp.exp(scores - block_log[:, :, None])
        grad_probs = jnp.einsum(
            "qhd,khd->hqk", grad_heads, value_heads, preferred_element_type=jnp.float32
        )
        row_sums = jnp.sum(probs * grad_probs, axis=-1)
        grad_scores = (probs * (grad_probs - row_sums[:, :, None])).astype(jnp.bfloat16)
        grad_query = jnp.einsum(
            "hqk,khd->qhd", grad_scores, key_heads, preferred_element_type=jnp.float32
        )
        grad_key = jnp.einsum(
            "hqk,qhd->khd", grad_scores, query_heads, preferred_element_type=jnp.float32
        )
        grad_value = jnp.einsum(
            "hqk,qhd->khd",
            probs.astype(jnp.bfloat16),
            grad_heads,
            preferred_element_type=jnp.float32,
        )
        return (grad_query, row_sums, grad_key, grad_value)

    items = (
        split_heads(queries),
        split_heads(keys),
        split_heads(values),
        split_heads(grad_mixed),
        split_stats(log_total),
    )
    results = lax.map(query_one_block, items)
    grad_query, row_sums, grad_key, grad_value = results
    return (
        join_heads(grad_query),
        row_sums.reshape(H, rows),
        join_heads(grad_key),
        join_heads(grad_value),
    )


def tail(flat_tokens, mixed, w_out, w_in, w_fc2, vectors):
    bias_q, bias_v, bias_o, bias_in, bias_fc2, gain_one, shift_one, gain_two, shift_two = (
        split_vectors(vectors)
    )
    mixed_low = mixed.astype(jnp.bfloat16)
    summed_one = (
        flat_tokens.astype(jnp.float32)
        + jnp.dot(mixed_low, w_out, preferred_element_type=jnp.float32)
        + bias_o
    )
    normed = layer_norm(summed_one, gain_one, shift_one)
    normed_low = normed.astype(jnp.bfloat16)
    hidden_pre = jnp.dot(normed_low, w_in, preferred_element_type=jnp.float32) + bias_in
    hidden_low = jax.nn.gelu(hidden_pre, approximate=False).astype(jnp.bfloat16)
    summed_two = normed + jnp.dot(hidden_low, w_fc2, preferred_element_type=jnp.float32) + bias_fc2
    result = layer_norm(summed_two, gain_two, shift_two)
    return (mixed_low, summed_one, normed_low, hidden_pre, hidden_low, summed_two, result)


def body(tokens, out_grad, lengths, w_qkv, w_out, w_in, w_fc2, vectors, moment_one, moment_two):
    slots, piece, width = tokens.shape
    length = piece * lax.axis_size("ctx")
    local_pos = lax.axis_index("ctx") * piece + jnp.arange(piece, dtype=jnp.int32)
    own_live = local_pos[None, :] < lengths[:, None]
    valid = own_live.astype(jnp.float32)
    key_live = jnp.arange(length, dtype=jnp.int32)[None, :] < lengths[:, None]
    bias_q, bias_v, bias_o, bias_in, bias_fc2, gain_one, shift_one, gain_two, shift_two = (
        split_vectors(vectors)
    )
    flat_tokens = tokens.reshape(slots * piece, width)
    queries, keys, values = project(flat_tokens, w_qkv, vectors)
    keys_all, values_all = (
        lax.all_gather(keys.reshape(slots, piece, width), "ctx", axis=1, tiled=True),
        lax.all_gather(values.reshape(slots, piece, width), "ctx", axis=1, tiled=True),
    )
    mixed, log_total = run_slots(
        attend_slot, (queries.reshape(slots, piece, width), keys_all, values_all, key_live)
    )
    saved = tail(flat_tokens, mixed.reshape(slots * piece, width), w_out, w_in, w_fc2, vectors)
    out = (saved[6].reshape(slots, piece, width) * valid[..., None]).astype(jnp.bfloat16)
    again = lax.optimization_barrier(flat_tokens)
    queries, keys, values = project(again, w_qkv, vectors)
    keys_all, values_all = (
        lax.all_gather(keys.reshape(slots, piece, width), "ctx", axis=1, tiled=True),
        lax.all_gather(values.reshape(slots, piece, width), "ctx", axis=1, tiled=True),
    )
    mixed, log_total = run_slots(
        attend_slot, (queries.reshape(slots, piece, width), keys_all, values_all, key_live)
    )
    saved = tail(again, mixed.reshape(slots * piece, width), w_out, w_in, w_fc2, vectors)
    mixed_low, summed_one, normed_low, hidden_pre, hidden_low, summed_two, result = saved
    cotangent = (out_grad.astype(jnp.float32) * valid[..., None]).reshape(slots * piece, width)
    unused_two, norm_two_back = jax.vjp(layer_norm, summed_two, gain_two, shift_two)
    grad_two, grad_gain_two, grad_shift_two = norm_two_back(cotangent)
    grad_fc2_low = grad_two.astype(jnp.bfloat16)
    bias_fc2_grad = jnp.sum(grad_fc2_low.astype(jnp.float32), axis=0)
    grad_hidden = through(grad_fc2_low, w_fc2)
    unused_gelu, gelu_back = jax.vjp(partial(jax.nn.gelu, approximate=False), hidden_pre)
    grad_pre_low = gelu_back(grad_hidden)[0].astype(jnp.bfloat16)
    bias_in_grad = jnp.sum(grad_pre_low.astype(jnp.float32), axis=0)
    grad_normed = grad_two + through(grad_pre_low, w_in)
    unused_one, norm_one_back = jax.vjp(layer_norm, summed_one, gain_one, shift_one)
    grad_one, grad_gain_one, grad_shift_one = norm_one_back(grad_normed)
    grad_branch_low = grad_one.astype(jnp.bfloat16)
    bias_out_grad = jnp.sum(grad_branch_low.astype(jnp.float32), axis=0)
    grad_mixed_low = (
        through(grad_branch_low, w_out).astype(jnp.bfloat16).reshape(slots, piece, width)
    )
    queries_slots = queries.reshape(slots, piece, width)
    grad_query, row_sums, grad_key, grad_value = run_slots(
        partial(query_back, with_keys=True),
        (queries_slots, keys_all, values_all, key_live, log_total, grad_mixed_low),
    )
    grad_key, grad_value = (
        lax.psum_scatter(
            grad_key.astype(jnp.bfloat16), "ctx", scatter_dimension=1, tiled=True
        ).astype(jnp.float32),
        lax.psum_scatter(
            grad_value.astype(jnp.bfloat16), "ctx", scatter_dimension=1, tiled=True
        ).astype(jnp.float32),
    )
    rows = slots * piece
    grad_query_low = grad_query.reshape(rows, width).astype(jnp.bfloat16) * jnp.bfloat16(0.125)
    grad_key_low = grad_key.reshape(rows, width).astype(jnp.bfloat16)
    grad_value_low = grad_value.reshape(rows, width).astype(jnp.bfloat16)
    grad_joined = jnp.concatenate([grad_query_low, grad_key_low, grad_value_low], axis=1)
    bias_q_grad = jnp.sum(grad_query_low.astype(jnp.float32), axis=0)
    bias_v_grad = jnp.sum(grad_value_low.astype(jnp.float32), axis=0)
    tokens_grad = (
        (grad_one + through(grad_joined, w_qkv)).reshape(slots, piece, width).astype(jnp.bfloat16)
    )
    vector_grad = jnp.concatenate(
        [
            bias_q_grad[None],
            bias_v_grad[None],
            bias_out_grad[None],
            bias_in_grad.reshape(FF // D, D),
            bias_fc2_grad[None],
            grad_gain_one[None],
            grad_shift_one[None],
            grad_gain_two[None],
            grad_shift_two[None],
        ],
        axis=0,
    )
    count = lax.axis_size(("dp", "ctx"))
    vector_rows = vector_grad.reshape(count, -1)
    pairs = (
        (flat_tokens, grad_joined),
        (mixed_low, grad_branch_low),
        (normed_low, grad_pre_low),
        (hidden_low, grad_fc2_low),
    )
    blocks = [
        shard_piece(left, right, 1 * lax.axis_size(("dp", "ctx")), count) for left, right in pairs
    ]
    blocks.append(vector_rows)
    grad_rows = lax.psum_scatter(
        jnp.concatenate(blocks, axis=1), ("dp", "ctx"), scatter_dimension=0, tiled=True
    )
    index = lax.axis_index(("dp", "ctx"))
    params = jnp.concatenate(
        [
            lax.dynamic_slice_in_dim(weight.reshape(count, -1), index, 1, 0).astype(jnp.float32)
            for weight in (w_qkv, w_out, w_in, w_fc2, vectors)
        ],
        axis=1,
    )
    new_one = beta_one * moment_one + (1.0 - beta_one) * grad_rows
    new_two = beta_two * moment_two + (1.0 - beta_two) * grad_rows * grad_rows
    fix_one = 1.0 - beta_one**step_count
    fix_two = 1.0 - beta_two**step_count
    update = new_one / fix_one / (jnp.sqrt(new_two / fix_two) + adam_eps)
    new_params = params - learn_rate * (update + decay_rate * params)
    return (out, tokens_grad, grad_rows, new_params, new_one, new_two)


BF16 = jnp.bfloat16
F32 = jnp.float32


def layer_norm_stats(values):
    center = values - jnp.mean(values, axis=-1, keepdims=True)
    spread = jnp.mean(center * center, axis=-1, keepdims=True)
    return center, lax.rsqrt(spread + EPSILON)


def layer_norm_back(center, scale, gain, cotangent):
    scaled = cotangent * gain
    mean_scaled = jnp.mean(scaled, axis=-1, keepdims=True)
    mean_cross = jnp.mean(scaled * center, axis=-1, keepdims=True)
    return scale * (scaled - mean_scaled - center * (scale * scale) * mean_cross)


def normal_cdf(values):
    return 0.5 * (1.0 + lax.erf(values * 0.7071067811865476))


def dot(left, right):
    return jnp.dot(left, right, preferred_element_type=F32)


def positions(axis, shape, slot, piece):
    place = lax.broadcasted_iota(jnp.int32, shape, axis)
    block = lax.div(place, piece)
    half = lax.div(block, 2)
    step = lax.rem(block, 2)
    return (2 * half + lax.rem(slot + step, 2)) * piece + lax.rem(place, piece)


def head_probs(queries, keys, live):
    scores = through(queries, keys)
    scores = jnp.where(live, scores, -1e30)
    expo = jnp.exp(scores - jnp.max(scores, axis=-1, keepdims=True))
    return expo / jnp.sum(expo, axis=-1, keepdims=True)


MESH = pl.DeviceIdType.MESH


class Links:
    def __init__(self, sends, recvs):
        self.sends, self.recvs = sends, recvs
        self.used = 0
        self.open = []

    def copy(self, source, target, device):
        self.used += 1
        return self.again(source, target, device)

    def again(self, source, target, device):
        number = self.used - 1
        return pltpu.make_async_remote_copy(
            src_ref=source,
            dst_ref=target,
            send_sem=self.sends.at[number],
            recv_sem=self.recvs.at[number],
            device_id=device,
            device_id_type=MESH,
        )

    def forward(self, source, target, device, earlier):
        self.used += 1
        return pltpu.make_async_remote_copy(
            src_ref=source,
            dst_ref=target,
            send_sem=self.sends.at[self.used - 1],
            recv_sem=self.recvs.at[earlier],
            device_id=device,
            device_id_type=MESH,
        )

    def send(self, source, target, device):
        made = self.copy(source, target, device)
        made.start()
        self.open.append((made, None))
        return made

    def send_if(self, condition, source, target, device):
        made = self.copy(source, target, device)
        pl.when(condition)(made.start)
        self.open.append((made, condition))
        return made

    def send_or_keep(self, here, source, target, device):
        number = self.used
        made = self.copy(source, target, device)
        local = pltpu.make_async_copy(source, target, self.recvs.at[number])
        pl.when(here)(local.start)
        away = jnp.logical_not(here)
        pl.when(away)(made.start)
        self.open.append((made, away))

        def wait():
            pl.when(here)(local.wait)
            pl.when(away)(made.wait_recv)

        return wait

    def close(self):
        for made, condition in self.open:
            if condition is None:
                made.wait_send()
            else:
                pl.when(condition)(made.wait_send)


def flip(value, mask):
    result = value
    bit = 1
    while bit <= mask:
        if mask & bit:
            result = result + bit * (1 - 2 * lax.rem(lax.div(value, bit), 2))
        bit *= 2
    return result


def flip_traced(value, mask, size):
    result = value
    bit = 1
    while bit < size:
        set_bit = lax.rem(lax.div(mask, bit), 2)
        result = result + bit * set_bit * (1 - 2 * lax.rem(lax.div(value, bit), 2))
        bit *= 2
    return result


def at_rows(start, size):
    return pl.ds(pl.multiple_of(start, 64), size)


def slot_kernel(devices, depth, features, *refs):
    (
        tokens, out_grad, lengths, vec, w_qkv, w_out, w_in, w_fc2,
        out_ref, tgrad_ref, g_qkv, g_out, g_in, g_fc2, g_vec,
        wqkv, wo, w_up, w_down,
        x_all, n_all, g_all, m_all, b_all, j_all, j_send, g_rows, lens_peer,
        qkv, part, part_low, part_a, part_b, part_c, part_d, summed, grad_two, grad_one,
        pre_s, hid, hid_all, gp_all, packed, plane_got, up_mine, down_mine, packed_two, right_two, left_two,
        trade_in, got_in, trade_qkv, got_qkv, vec_s, vec_by, vec_got, sums, dqkv, out_half, out_got, tg_half, tg_got, lens,
        local_sems, sends, recvs,
    ) = refs
    chips = devices // 2
    me, slot = lax.axis_index("dp"), lax.axis_index("ctx")
    core, chip = lax.rem(me, 2), lax.div(me, 2)
    base = me - core
    peer = (base + 1 - core, slot)
    piece = tokens.shape[1]
    half = 2 * piece
    rows = 2 * half
    block = D // devices
    wide = features // devices
    lines = D // (devices * depth)
    net = Links(sends, recvs)
    mine_at = at_rows(core * half, half)
    other_at = at_rows((1 - core) * half, half)
    chunk = 32

    row_of = lax.broadcasted_iota(jnp.int32, lens.shape, 0)
    lens[...] = jnp.where(row_of == 0, lengths[0], lengths[1])
    vec_s[...] = jnp.zeros_like(vec_s)
    loads = []

    def load(source, target):
        made = pltpu.make_async_copy(source, target, local_sems.at[len(loads)])
        made.start()
        loads.append(made)

    where = [2 * flip(chip, mask) + core for mask in range(chips)]
    for mask in range(chips):
        for kind in range(3):
            start = pl.multiple_of(kind * D + where[mask] * block, block)
            load(
                w_qkv.at[:, pl.ds(start, block)],
                wqkv.at[:, (3 * mask + kind) * block : (3 * mask + kind + 1) * block],
            )
    n_qkv = len(loads)
    for number in range(chips):
        start = pl.multiple_of((2 * number + core) * block, block)
        load(w_out.at[pl.ds(start, block), :], wo.at[number * block : (number + 1) * block, :])
    n_out = len(loads)
    for mask in range(chips):
        start = pl.multiple_of(where[mask] * wide, wide)
        load(w_in.at[:, pl.ds(start, wide)], w_up.at[:, mask * wide : (mask + 1) * wide])
    n_up = len(loads)
    for mask in range(chips):
        start = pl.multiple_of(where[mask] * wide, wide)
        load(w_fc2.at[pl.ds(start, wide), :], w_down.at[mask * wide : (mask + 1) * wide, :])

    barrier = pltpu.get_barrier_semaphore()
    friends = [(flip(me, mask), slot) for mask in range(1, devices)]
    for shift in range(1, depth):
        far = lax.rem(slot + shift, depth)
        friends += [(me, far), (flip(me, 1), far)]
    for friend in friends:
        pl.semaphore_signal(barrier, inc=1, device_id=friend, device_id_type=MESH)
    pl.semaphore_wait(barrier, len(friends))

    def spread(source, target):
        waits = []
        for step in range(2):
            pick = lax.rem(slot + step, 2)
            upper = lax.div(slot, 2)
            place = 2 * core + pick
            here = jnp.logical_and(upper == core, place == slot)
            waits.append(
                net.send_or_keep(
                    here,
                    source.at[pick],
                    target.at[at_rows((2 * upper + step) * piece, piece)],
                    (base + upper, place),
                )
            )
        return waits

    def pass_on(waits, target):
        made = []
        for step, wait in enumerate(waits):
            wait()
            spot = target.at[at_rows((2 * core + step) * piece, piece)]
            made.append(net.send(spot, spot, peer))
        return made

    token_waits = spread(tokens, x_all)
    grad_waits = spread(out_grad, g_rows)
    lens_copy = net.send(lens, lens_peer, peer)
    token_passes = pass_on(token_waits, x_all)

    def plane_start(target):
        source = target.at[mine_at]
        return [
            net.send(
                source, target.at[at_rows(mask * rows + core * half, half)], (flip(me, 2 * mask), slot)
            )
            for mask in range(1, chips)
        ]

    def plane_pass(copies, target):
        made = []
        for mask, copy in enumerate(copies, 1):
            copy.wait_recv()
            spot = target.at[at_rows(mask * rows + core * half, half)]
            made.append(net.send(spot, spot, peer))
        return made

    class Column:
        def __init__(self, target):
            self.target = target
            self.parts, self.numbers = {}, {}
            for place in (2, 1, 3):
                far = lax.rem(slot + depth - place, depth)
                made = net.copy(target.at[mine_at], self.spot(place), (me, far))
                self.parts[place], self.numbers[place] = made, net.used - 1
                goes = {1: slot != 0, 2: slot >= 0, 3: slot != depth - 1}[place]
                net.open.append((made, goes))
                pl.when(goes)(made.start)
            self.passes = {}

        def spot(self, place):
            return self.target.at[at_rows(place * rows + core * half, half)]

        def relay(self):
            self.parts[2].wait_recv()
            up = net.forward(self.spot(2), self.spot(1), (me, depth - 1), self.numbers[1])
            down = net.forward(self.spot(2), self.spot(3), (me, 0), self.numbers[3])
            for made, here in ((up, slot == 2), (down, slot == 1)):
                pl.when(here)(made.start)
                net.open.append((made, here))
            self.passes[2] = net.send(self.spot(2), self.spot(2), peer)

        def hand_over(self, place):
            self.parts[place].wait_recv()
            self.passes[place] = net.send(self.spot(place), self.spot(place), peer)

    x_plane = plane_start(x_all)
    for made in loads[:n_qkv]:
        made.wait()
    lens_copy.wait_recv()
    for made in token_passes:
        made.wait_recv()
    owned = jnp.where(lax.div(slot, 2) == core, lens[...], lens_peer[...])
    length = jnp.where(lax.rem(slot, 2) == 0, owned[0:1, 0:1], owned[1:2, 0:1])
    live = positions(1, (1, rows), slot, piece) < length
    lane = lax.broadcasted_iota(jnp.int32, (1, block), 1)

    @pl.loop(0, chips)
    def _(mask):
        spot = 2 * flip_traced(chip, mask, chips) + core
        lanes = pl.ds(pl.multiple_of(spot * block, block), block)
        joined = dot(x_all[0:rows, :], wqkv[:, pl.ds(pl.multiple_of(mask * 3 * block, block), 3 * block)])
        queries = ((joined[:, 0:block] + vec[0:1, lanes]) * 0.125).astype(BF16)
        keys = joined[:, block : 2 * block].astype(BF16)
        values = (joined[:, 2 * block :] + vec[1:2, lanes]).astype(BF16)
        total = jnp.zeros((rows, block), F32)
        for head in range(block // HD):
            mine = lax.div(lane, HD) == head
            probs = head_probs(jnp.where(mine, queries, jnp.zeros_like(queries)), keys, live)
            total = jnp.where(mine, dot(probs.astype(BF16), values), total)
        start = pl.multiple_of(mask * 3 * block, block)
        qkv[:, pl.ds(start, block)] = queries
        qkv[:, pl.ds(pl.multiple_of(start + block, block), block)] = keys
        qkv[:, pl.ds(pl.multiple_of(start + 2 * block, block), block)] = values
        lanes = pl.ds(pl.multiple_of(core * chips * block + lax.div(spot, 2) * block, block), block)
        m_all[0:rows, lanes] = total.astype(BF16)

    for made in loads[n_qkv:n_out]:
        made.wait()

    def exchange(compute, target, before):
        made = []
        for number, at in enumerate((other_at, mine_at)):
            if before is not None:
                before[number].wait_send()
            value = compute(at)
            part[at, :] = value
            part_low[at, :] = value.astype(BF16)
            made.append(net.copy(part_low.at[at], target.at[at], peer))
            made[-1].start()
        return made

    my_lanes = pl.ds(pl.multiple_of(core * chips * block, chips * block), chips * block)
    first = exchange(lambda at: dot(m_all[at, my_lanes], wo[...]), part_a, None)
    own_mixed = m_all.at[0:rows, my_lanes]
    m_passes = [net.send(own_mixed, own_mixed, peer)]
    m_plane = [
        net.send(own_mixed, m_all.at[mask * rows : (mask + 1) * rows, my_lanes], (flip(me, 2 * mask), slot))
        for mask in range(1, chips)
    ]
    grad_passes = pass_on(grad_waits, g_rows)

    def norm_one(start):
        @pl.loop(0, half // chunk)
        def _(step):
            at = pl.ds(pl.multiple_of(start + step * chunk, chunk), chunk)
            total = x_all[at, :].astype(F32) + (part[at, :] + part_a[at, :].astype(F32)) + vec[2:3, :]
            center, scale = layer_norm_stats(total)
            summed[at, :] = total
            n_all[at, :] = (center * scale * vec[8:9, :] + vec[9:10, :]).astype(BF16)

    first[0].wait_recv()
    norm_one(core * half)
    n_column = Column(n_all)
    first[1].wait_recv()
    norm_one((1 - core) * half)
    for made in loads[n_out:]:
        made.wait()

    for number in range(chips):
        fine_cols = wide // depth
        begin = flip_traced(chip, number, chips) * wide + slot * fine_cols
        at = pl.ds(pl.multiple_of(begin, fine_cols), fine_cols)
        up_mine[:, number * fine_cols : (number + 1) * fine_cols] = w_up[:, at]
        down_mine[number * fine_cols : (number + 1) * fine_cols, :] = w_down[at, :]

    def bias_of(mask):
        spot = flip_traced(chip, mask, chips)
        lanes = pl.ds(pl.multiple_of(core * wide, wide), wide)
        result = vec[3:4, lanes]
        for row in range(1, chips):
            result = jnp.where(spot == row, vec[3 + row : 4 + row, lanes], result)
        return result

    @pl.loop(0, chips)
    def _(mask):
        at = pl.ds(pl.multiple_of(mask * wide, wide), wide)
        value = dot(n_all[0:rows, :], w_up[:, at]) + bias_of(mask)
        pre_s[:, at] = value
        hid[:, at] = (value * normal_cdf(value)).astype(BF16)

    second = exchange(lambda at: dot(hid[at, :], w_down[...]), part_b, first)
    for made in grad_passes:
        made.wait_recv()

    def norm_two(start, own):
        @pl.loop(0, half // chunk)
        def _(step):
            begin = pl.multiple_of(start + step * chunk, chunk)
            at = pl.ds(begin, chunk)
            center, scale = layer_norm_stats(summed[at, :])
            normed = center * scale * vec[8:9, :] + vec[9:10, :]
            center, scale = layer_norm_stats(normed + (part[at, :] + part_b[at, :].astype(F32)) + vec[7:8, :])
            place = begin + lax.broadcasted_iota(jnp.int32, (chunk, 1), 0)
            piece_of = lax.div(place, piece)
            spot = 2 * lax.div(piece_of, 2) + lax.rem(slot + lax.rem(piece_of, 2), 2)
            valid = (spot * piece + lax.rem(place, piece) < length).astype(F32)
            unit = center * scale
            error = g_rows[at, :].astype(F32) * valid
            grad = layer_norm_back(center, scale, vec[10:11, :], error)
            grad_two[at, :] = grad
            low = grad.astype(BF16)
            g_all[at, :] = low
            if own:
                out_half[pl.ds(pl.multiple_of(step * chunk, chunk), chunk), :] = (
                    valid * (unit * vec[10:11, :] + vec[11:12, :])
                ).astype(BF16)
                vec_s[7:8, :] += jnp.sum(low.astype(F32), axis=0, keepdims=True)
                vec_s[10:11, :] += jnp.sum(error * unit, axis=0, keepdims=True)
                vec_s[11:12, :] += jnp.sum(error, axis=0, keepdims=True)

    def go_back(source, target):
        waits = []
        for step in range(2):
            place = 2 * core + lax.rem(slot + step, 2)
            upper = lax.div(slot, 2)
            here = jnp.logical_and(upper == core, place == slot)
            waits.append(
                net.send_or_keep(
                    here,
                    source.at[step * piece : (step + 1) * piece],
                    target.at[lax.rem(slot, 2)],
                    (base + upper, place),
                )
            )
        return waits

    second[0].wait_recv()
    norm_two(core * half, True)
    g_column = Column(g_all)
    second[1].wait_recv()
    norm_two((1 - core) * half, False)
    out_waits = go_back(out_half, out_got)

    def mixed_pass():
        for mask, made in enumerate(m_plane, 1):
            made.wait_recv()
            spot = m_all.at[mask * rows : (mask + 1) * rows, my_lanes]
            m_passes.append(net.send(spot, spot, peer))

    def slope_of(value, cdf):
        return cdf + value * (jnp.exp(-0.5 * value * value) * 0.3989422804014327)

    @pl.loop(0, chips)
    def _(mask):
        at = pl.ds(pl.multiple_of(mask * wide, wide), wide)
        value = pre_s[:, at]
        grad = through(g_all[0:rows, :], w_down[at, :])
        hid[:, at] = (grad * slope_of(value, normal_cdf(value))).astype(BF16)

    third = exchange(lambda at: through(hid[at, :], w_up[...]), part_c, second)

    def norm_one_back(start, own):
        @pl.loop(0, half // chunk)
        def _(step):
            at = pl.ds(pl.multiple_of(start + step * chunk, chunk), chunk)
            center, scale = layer_norm_stats(summed[at, :])
            error = grad_two[at, :] + (part[at, :] + part_c[at, :].astype(F32))
            grad = layer_norm_back(center, scale, vec[8:9, :], error)
            low = grad.astype(BF16)
            b_all[at, :] = low
            grad_one[at, :] = grad
            if own:
                vec_s[2:3, :] += jnp.sum(low.astype(F32), axis=0, keepdims=True)
                vec_s[8:9, :] += jnp.sum(error * (center * scale), axis=0, keepdims=True)
                vec_s[9:10, :] += jnp.sum(error, axis=0, keepdims=True)

    x_pass = plane_pass(x_plane, x_all)

    third[0].wait_recv()
    norm_one_back(core * half, True)
    third[1].wait_recv()
    norm_one_back((1 - core) * half, False)
    class Line:
        def __init__(self, chunks, from_left, from_right):
            self.chunks, self.from_left, self.from_right = chunks, from_left, from_right
            self.up, self.down, self.first_up, self.first_down = [], [], [], []
            after = (me, lax.rem(slot + 1, depth))
            before = (me, lax.rem(slot + depth - 1, depth))
            for order in range(depth - 1):
                top, low = depth - 1 - order, order
                spot = from_left.at[order]
                self.up.append(net.copy(spot, spot, after))
                self.first_up.append(net.again(chunks.at[top], spot, after))
                net.open.append((self.up[-1], slot < top))
                spot = from_right.at[order]
                self.down.append(net.copy(spot, spot, before))
                self.first_down.append(net.again(chunks.at[low], spot, before))
                net.open.append((self.down[-1], slot > low))

        def first(self):
            for order in range(depth - 1):
                pl.when(slot == 0)(self.first_up[order].start)
                pl.when(slot == depth - 1)(self.first_down[order].start)

        def stage(self, time):
            for order in range(time):
                top, low = depth - 1 - order, order

                @pl.when(slot == time - order)
                def _(order=order, top=top):
                    self.up[order].wait_recv()
                    if time < depth - 1:
                        self.from_left[order] = (
                            self.from_left[order].astype(F32) + self.chunks[top].astype(F32)
                        ).astype(BF16)
                        self.up[order].start()

                @pl.when(depth - 1 - slot == time - order)
                def _(order=order, low=low):
                    self.down[order].wait_recv()
                    if time < depth - 1:
                        self.from_right[order] = (
                            self.from_right[order].astype(F32) + self.chunks[low].astype(F32)
                        ).astype(BF16)
                        self.down[order].start()

    grad_parts = range(1, chips)

    def attention_back(mask):
        start = mask * 3 * block
        queries = qkv[:, start : start + block]
        keys = qkv[:, start + block : start + 2 * block]
        values = qkv[:, start + 2 * block : start + 3 * block]
        turn = pl.ds(pl.multiple_of(lax.div(where[mask], 2) * block, block), block)
        grad_mixed = through(b_all[0:rows, :], wo[turn, :]).astype(BF16)
        grad_q = jnp.zeros((rows, block), F32)
        grad_k = grad_q
        grad_v = grad_q
        for head in range(block // HD):
            mine = lax.div(lane, HD) == head
            probs = head_probs(jnp.where(mine, queries, jnp.zeros_like(queries)), keys, live)
            grad_probs = through(jnp.where(mine, grad_mixed, jnp.zeros_like(grad_mixed)), values)
            dsum = jnp.sum(probs * grad_probs, axis=-1, keepdims=True)
            grad_scores = (probs * (grad_probs - dsum)).astype(BF16)
            grad_q = jnp.where(mine, dot(grad_scores, keys), grad_q)
            grad_k = jnp.where(mine, inner(grad_scores, queries), grad_k)
            grad_v = jnp.where(mine, inner(probs.astype(BF16), grad_mixed), grad_v)
        grad_q = grad_q.astype(BF16) * jnp.bfloat16(0.125)
        grad_k = grad_k.astype(BF16)
        grad_v = grad_v.astype(BF16)
        spot = pl.ds(pl.multiple_of(where[mask] * block, block), block)
        vec_s[0:1, spot] = jnp.sum(grad_q.astype(F32), axis=0, keepdims=True)
        vec_s[1:2, spot] = jnp.sum(grad_v.astype(F32), axis=0, keepdims=True)
        dqkv[:, start : start + block] = grad_q
        dqkv[:, start + block : start + 2 * block] = grad_k
        dqkv[:, start + 2 * block : start + 3 * block] = grad_v
        if mask:
            joint = j_send.at[mask - 1]
        else:
            joint = j_all.at[0:rows]
        joint[:, 0:block] = grad_q
        joint[:, block : 2 * block] = grad_k
        joint[:, 2 * block : 3 * block] = grad_v
        joint[:, 3 * block : 4 * block] = b_all[0:rows, spot]
        if mask:
            return net.send(
                joint, j_all.at[mask * rows : (mask + 1) * rows], (flip(me, 2 * mask), slot)
            )
        return None

    n_column.relay()
    j_copies = [attention_back(mask) for mask in grad_parts]
    attention_back(0)
    mixed_pass()
    n_column.hand_over(1)
    n_column.hand_over(3)
    for made in third:
        made.wait_send()
    part[0:half, :] = through(dqkv[other_at, :], wqkv[...])
    tg_copy = net.copy(part.at[0:half], part_d, peer)
    tg_copy.start()
    part[half:rows, :] = grad_one[mine_at, :] + through(dqkv[mine_at, :], wqkv[...])
    tg_copy.wait_recv()
    tg_half[...] = (part[half:rows, :] + part_d[...]).astype(BF16)

    fine = wide // depth
    span = lines * depth
    features_at = pl.ds(pl.multiple_of((depth * core + slot) * fine, fine), fine)
    bias_mine = jnp.concatenate([vec[3 + number : 4 + number, features_at] for number in range(chips)], axis=1)

    def feed_rows(place):
        at = slice(place * rows, (place + 1) * rows)
        value = dot(n_all[at, :], up_mine[...]) + bias_mine
        cdf = normal_cdf(value)
        hid_all[at, :] = (value * cdf).astype(BF16)
        low = (through(g_all[at, :], down_mine[...]) * slope_of(value, cdf)).astype(BF16)
        gp_all[at, :] = low
        return jnp.sum(low.astype(F32), axis=0, keepdims=True)

    bias_sum = feed_rows(0)
    g_column.relay()
    tg_waits = go_back(tg_half, tg_got)
    for column in (n_column, g_column):
        column.passes[2].wait_recv()
    bias_sum = bias_sum + feed_rows(2)
    for made in m_passes + x_pass + j_copies:
        made.wait_recv()
    for group in range(devices):
        at = slice(group * span, (group + 1) * span)
        begin = (group % 2) * chips * block + (group // 2) * block
        both = inner(x_all[:, at], j_all[:, 0 : 3 * block]).astype(BF16)
        across = inner(m_all[:, begin : begin + block], j_all[:, 3 * block : 4 * block]).astype(BF16)
        row = group * lines
        for number in range(depth):
            at = slice(number * lines, (number + 1) * lines)
            packed_two[number, row : row + lines, 0 : 3 * block] = both[at, :]
            packed_two[number, row : row + lines, 3 * block : 4 * block] = across[at, :]
    input_line = Line(packed_two, right_two, left_two)
    input_line.first()

    g_column.hand_over(1)
    g_column.hand_over(3)
    for place in (1, 3):
        n_column.passes[place].wait_recv()
        g_column.passes[place].wait_recv()
        bias_sum = bias_sum + feed_rows(place)
    for number in range(chips):
        vec_s[3 + number : 4 + number, features_at] = bias_sum[:, number * fine : (number + 1) * fine]
    depth_rows = D // chips
    for number in range(chips):
        block_up = inner(n_all[:, number * depth_rows : (number + 1) * depth_rows], gp_all[...]).astype(BF16)
        packed[number, fine : 2 * fine, 0:wide] = block_up[0:fine, :]
        packed[number, fine : 2 * fine, wide : 2 * wide] = block_up[fine : 2 * fine, :]

    def scatter_plane(lines_at):
        return [
            net.send(
                packed.at[flip_traced(chip, mask, chips), lines_at],
                plane_got.at[mask - 1, lines_at],
                (flip(me, 2 * mask), slot),
            )
            for mask in range(1, chips)
        ]

    up_copies = scatter_plane(slice(fine, 2 * fine))
    packed[:, 0:fine, :] = inner(hid_all[...], g_all[...]).astype(BF16).reshape(chips, fine, D)
    down_copies = scatter_plane(slice(0, fine))

    tiles = vec.shape[0] * D // 128
    share = tiles // (devices * depth)
    vec_by[...] = jnp.zeros_like(vec_by)
    for tile in range(tiles):
        owner, lane_group = tile // share, tile % share
        row, col = tile // (D // 128), (tile % (D // 128)) * 128
        spot = (owner % depth) * devices + owner // depth
        vec_by[spot : spot + 1, lane_group * 128 : (lane_group + 1) * 128] = vec_s[
            row : row + 1, col : col + 128
        ]
    vec_copies = []
    for shift in range(1, depth):
        far = lax.rem(slot + shift, depth)
        spot = vec_by.at[pl.ds(pl.multiple_of(far * devices, devices), devices)]
        vec_copies.append(net.send(spot, vec_got.at[shift - 1], (me, far)))

    def finish(line, target, rows_at):
        target[...] = line.chunks[slot, rows_at, :].astype(F32)

        @pl.when(slot >= 1)
        def _():
            target[...] += line.from_left[depth - 1 - slot, rows_at, :].astype(F32)

        @pl.when(slot <= depth - 2)
        def _():
            target[...] += line.from_right[slot, rows_at, :].astype(F32)

    def plane_sum(copies, lines_at):
        for made in copies:
            made.wait_recv()
        value = packed[chip, lines_at, :].astype(F32)
        for number in range(chips - 1):
            value = value + plane_got[number, lines_at, :].astype(F32)
        return value

    def trade(source, target):
        return [
            net.send(source.at[flip(me, mask)], target.at[me], (flip(me, mask), slot))
            for mask in range(1, devices)
        ]

    for time in range(1, depth - 1):
        input_line.stage(time)
    low_sum = plane_sum(up_copies, slice(fine, 2 * fine)).astype(BF16)
    for upper in range(2):
        for number in range(depth):
            trade_in[upper * depth + number] = low_sum[
                number * lines : (number + 1) * lines, upper * wide : (upper + 1) * wide
            ]
    here = core * depth + slot
    in_copies = []
    for shift in range(1, 2 * depth):
        far = lax.rem(slot + shift % depth, depth)
        upper = core if shift < depth else 1 - core
        in_copies.append(net.send(trade_in.at[upper * depth + far], got_in.at[here], (base + upper, far)))
    input_line.stage(depth - 1)
    tg_copy.wait_send()
    finish(input_line, sums, slice(0, rows))
    vec_sum = vec_by[pl.ds(pl.multiple_of(slot * devices, devices), devices), :]
    for number, made in enumerate(vec_copies):
        made.wait_recv()
        vec_sum = vec_sum + vec_got[number]
    first_row = lax.broadcasted_iota(jnp.int32, (16, 4 * block), 0) == 0
    for group in range(devices):
        trade_qkv[group, 0:lines, :] = sums[group * lines : (group + 1) * lines, :].astype(BF16)
        trade_qkv[group, lines : lines + 16, :] = jnp.where(
            first_row, vec_sum[group : group + 1, :], 0.0
        ).astype(BF16)
    qkv_copies = trade(trade_qkv, got_qkv)
    for made in in_copies:
        made.wait_recv()
    got_in[here] = trade_in[here]
    for group in range(2 * depth):
        for number in range(chips):
            start = number * 2 * wide + group * fine
            g_in[:, start : start + fine] = got_in[group, :, number * fine : (number + 1) * fine].astype(F32)
    g_fc2[...] = plane_sum(down_copies, slice(0, fine))
    for wait in out_waits + tg_waits:
        wait()
    out_ref[...] = out_got[...]
    tgrad_ref[...] = tg_got[...]
    for made in qkv_copies:
        made.wait_recv()
    got_qkv[me] = trade_qkv[me]
    vec_sum = jnp.zeros((16, 3 * block), F32)
    for group in range(devices):
        vec_sum = vec_sum + got_qkv[group, lines : lines + 16, 0 : 3 * block].astype(F32)
        got = got_qkv[group, 0:lines, :].astype(F32)
        for kind in range(3):
            g_qkv[:, kind * D + group * block : kind * D + (group + 1) * block] = got[
                :, kind * block : (kind + 1) * block
            ]
        g_out[:, group * block : (group + 1) * block] = got[:, 3 * block : 4 * block]
    g_vec[...] = vec_sum[0:8, :]
    net.close()


def adam_kernel(count, *refs):
    (
        g_qkv, g_out, g_in, g_fc2, g_vec, vec, out_in, tgrad_in, w_qkv, w_out, w_in, w_fc2, m_one, m_two,
        out_ref, tgrad_ref, rows_out, params_out, one_out, two_out,
        grads, params, one, two, d_qkv, d_out, d_in, d_fc2, b_qkv, b_out, b_in, b_fc2, out_by, tgrad_by, vec_flat,
        in_sems, g_sems, w_sems, out_sems, pass_sems,
    ) = refs
    index = lax.axis_index("dp") * lax.axis_size("ctx") + lax.axis_index("ctx")
    size = m_one.shape[1] // 128
    kinds = (
        (g_qkv, d_qkv, w_qkv, b_qkv),
        (g_out, d_out, w_out, b_out),
        (g_in, d_in, w_in, b_in),
        (g_fc2, d_fc2, w_fc2, b_fc2),
    )
    lengths = [kind[1].shape[0] * kind[1].shape[1] // 128 for kind in kinds]
    starts = [sum(lengths[:number]) for number in range(len(kinds))]
    tail = sum(lengths)
    order = (3, 2, 0, 1, 4)
    spans = [(start, length) for start, length in zip(starts, lengths)] + [(tail, size - tail)]

    def load(source, target, sem):
        made = pltpu.make_async_copy(source, target, sem)
        made.start()
        return made

    blocks, loads = {}, {}
    for number in order:
        start, length = spans[number]
        if number < len(kinds):
            grad, grad_by, weight, weight_by = kinds[number]
            lines = weight_by.shape[0]
            mine = pl.ds(pl.multiple_of(index * lines, lines), lines)
            blocks[number] = [
                load(grad, grad_by, g_sems.at[number]),
                load(weight.at[mine, :], weight_by, w_sems.at[number]),
            ]
        loads[number] = [
            load(
                source.reshape(size, 128).at[start : start + length],
                target.at[start : start + length],
                in_sems.at[kind, number],
            )
            for kind, (source, target) in enumerate(((m_one, one), (m_two, two)))
        ]
    passes = [load(out_in, out_by, pass_sems.at[0]), load(tgrad_in, tgrad_by, pass_sems.at[1])]

    def flatten(source, target, base):
        lines, groups = source.shape[0], source.shape[1] // 128
        for col in range(groups):
            value = source[:, col * 128 : (col + 1) * 128].astype(F32)
            for row in range(0, lines, 8):
                target[pl.ds(base + row * groups + col, 8, stride=groups), :] = value[row : row + 8, :]

    def vector_rows():
        share = g_vec.shape[1] // 128
        groups = vec.shape[1] // 128
        for col in range(groups):
            lanes = slice(col * 128, (col + 1) * 128)
            vec_flat[pl.ds(col, 8, stride=groups), :] = vec[0:8, lanes]
            for row in range(8, vec.shape[0]):
                vec_flat[row * groups + col : row * groups + col + 1, :] = vec[row : row + 1, lanes]
        place = lax.broadcasted_iota(jnp.int32, vec_flat.shape, 0)
        for number in range(share):
            spot = slice(tail + number, tail + number + 1)
            grads[spot, :] = g_vec[0:1, number * 128 : (number + 1) * 128]
            params[spot, :] = jnp.sum(
                jnp.where(place == index * share + number, vec_flat[...], 0.0), axis=0, keepdims=True
            )

    fix_one = 1.0 / (1.0 - beta_one**step_count)
    fix_two = 1.0 / (1.0 - beta_two**step_count)

    def update(at):
        grad, param = grads[at, :], params[at, :]
        new_one = beta_one * one[at, :] + (1.0 - beta_one) * grad
        new_two = beta_two * two[at, :] + (1.0 - beta_two) * grad * grad
        one[at, :] = new_one
        two[at, :] = new_two
        change = new_one * fix_one / (jnp.sqrt(new_two * fix_two) + adam_eps)
        params[at, :] = param - learn_rate * (change + decay_rate * param)

    vector_rows()
    copies = []
    for number in order:
        start, length = spans[number]
        if number < len(kinds):
            grad, grad_by, weight, weight_by = kinds[number]
            for made in blocks[number]:
                made.wait()
            flatten(grad_by, grads, start)
            flatten(weight_by, params, start)
        for made in loads[number]:
            made.wait()
        if number < len(kinds):

            @pl.loop(0, length // 64)
            def _(chunk, start=start):
                update(pl.ds(pl.multiple_of(start + chunk * 64, 64), 64))

        else:
            update(slice(start, start + 8))
        for kind, (source, target) in enumerate(
            ((grads, rows_out), (params, params_out), (one, one_out), (two, two_out))
        ):
            copies.append(
                load(
                    source.at[start : start + length],
                    target.reshape(size, 128).at[start : start + length],
                    out_sems.at[kind, number],
                )
            )
        if number == order[0]:
            for made, source, target, sem in zip(
                passes, (out_by, tgrad_by), (out_ref, tgrad_ref), (pass_sems.at[2], pass_sems.at[3])
            ):
                made.wait()
                copies.append(load(source, target, sem))
    for made in copies:
        made.wait()


def slot_body(tokens, out_grad, lengths, w_qkv, w_out, w_in, w_fc2, vectors, moment_one, moment_two):
    slots, piece, width = tokens.shape
    devices, depth = lax.axis_size("dp"), lax.axis_size("ctx")
    chips = devices // 2
    count = devices * depth
    features = w_in.shape[1]
    half = 2 * piece
    rows = 2 * half
    block = D // devices
    wide = features // devices
    lines = D // count
    total = rows * chips
    low = lambda *shape: pltpu.VMEM(shape, BF16)
    wide_f32 = lambda *shape: pltpu.VMEM(shape, F32)
    anywhere = pl.BlockSpec(memory_space=pl.ANY)
    inside = pl.BlockSpec(memory_space=pltpu.VMEM)
    copies = 96
    out, tokens_grad, grad_qkv, grad_out_w, grad_in, grad_fc2, vector_grad = pl.pallas_call(
        partial(slot_kernel, devices, depth, features),
        out_shape=(
            jax.ShapeDtypeStruct(tokens.shape, BF16),
            jax.ShapeDtypeStruct(tokens.shape, BF16),
            jax.ShapeDtypeStruct((lines, 3 * D), F32),
            jax.ShapeDtypeStruct((lines, D), F32),
            jax.ShapeDtypeStruct((lines, features), F32),
            jax.ShapeDtypeStruct((features // count, D), F32),
            jax.ShapeDtypeStruct((8, 3 * block), F32),
        ),
        in_specs=[anywhere, anywhere, pl.BlockSpec(memory_space=pltpu.SMEM), inside] + [anywhere] * 4,
        out_specs=(inside,) * 7,
        scratch_shapes=[
            low(D, 3 * D // 2),
            low(D // 2, D),
            low(D, features // 2),
            low(features // 2, D),
            low(total, D),
            low(total, D),
            low(total, D),
            low(total, D),
            low(rows, D),
            low(total, 4 * block),
            low(chips - 1, rows, 4 * block),
            low(rows, D),
            pltpu.VMEM((slots, 128), jnp.int32),
            low(rows, 3 * D // 2),
            wide_f32(rows, D),
            low(rows, D),
            low(rows, D),
            low(rows, D),
            low(rows, D),
            wide_f32(half, D),
            wide_f32(rows, D),
            wide_f32(rows, D),
            wide_f32(rows, D),
            wide_f32(rows, features // 2),
            low(rows, features // 2),
            low(total, wide),
            low(total, wide),
            low(chips, 2 * wide // depth, D),
            low(chips - 1, 2 * wide // depth, D),
            low(D, wide),
            low(wide, D),
            low(depth, devices * lines, 4 * block),
            low(depth - 1, devices * lines, 4 * block),
            low(depth - 1, devices * lines, 4 * block),
            low(devices, lines, wide),
            low(devices, lines, wide),
            low(devices, lines + 16, 4 * block),
            low(devices, lines + 16, 4 * block),
            wide_f32(16, D),
            wide_f32(devices * depth, 4 * block),
            wide_f32(depth - 1, devices, 4 * block),
            wide_f32(rows, 4 * block),
            low(rows, 3 * D // 2),
            low(half, D),
            low(*tokens.shape),
            low(half, D),
            low(*tokens.shape),
            pltpu.VMEM((slots, 128), jnp.int32),
            pltpu.SemaphoreType.DMA((6 * chips,)),
            pltpu.SemaphoreType.DMA((copies,)),
            pltpu.SemaphoreType.DMA((copies,)),
        ],
        compiler_params=pltpu.CompilerParams(
            collective_id=0, has_side_effects=True, vmem_limit_bytes=64 * 1024 * 1024 - 64 * 1024
        ),
        name="slot",
    )(tokens, out_grad, lengths, vectors, w_qkv, w_out, w_in, w_fc2)
    size = moment_one.shape[1] // 128
    padded = (size + 7) // 8 * 8
    flat = jax.ShapeDtypeStruct(moment_one.shape, F32)
    return pl.pallas_call(
        partial(adam_kernel, count),
        out_shape=(
            jax.ShapeDtypeStruct(tokens.shape, BF16),
            jax.ShapeDtypeStruct(tokens.shape, BF16),
            flat,
            flat,
            flat,
            flat,
        ),
        in_specs=[anywhere] * 4 + [inside] * 2 + [anywhere] * 8,
        out_specs=(anywhere,) * 6,
        scratch_shapes=[wide_f32(padded, 128)] * 4
        + [
            wide_f32(lines, 3 * D),
            wide_f32(lines, D),
            wide_f32(lines, features),
            wide_f32(features // count, D),
            low(lines, 3 * D),
            low(lines, D),
            low(lines, features),
            low(features // count, D),
            low(*tokens.shape),
            low(*tokens.shape),
            wide_f32(vectors.shape[0] * D // 128, 128),
            pltpu.SemaphoreType.DMA((2, 5)),
            pltpu.SemaphoreType.DMA((4,)),
            pltpu.SemaphoreType.DMA((4,)),
            pltpu.SemaphoreType.DMA((4, 5)),
            pltpu.SemaphoreType.DMA((4,)),
        ],
        compiler_params=pltpu.CompilerParams(vmem_limit_bytes=64 * 1024 * 1024 - 64 * 1024),
        name="adam",
    )(
        grad_qkv, grad_out_w, grad_in, grad_fc2, vector_grad, vectors, out, tokens_grad,
        w_qkv, w_out, w_in, w_fc2, moment_one, moment_two,
    )


def layer(tokens, *rest):
    slots, piece, width = tokens.shape
    devices, depth = lax.axis_size("dp"), lax.axis_size("ctx")
    fits = slots == 2 and depth == 2 * slots and devices == 2 * depth and FF == (devices // 2) * D
    if fits and (H * HD // devices) % 128 == 0 and (FF // devices) % 128 == 0:
        return slot_body(tokens, *rest)
    return body(tokens, *rest)


def solution(mesh):
    placed = (
        P("dp", "ctx", None),
        P("dp", "ctx", None),
        P("dp"),
        P(),
        P(),
        P(),
        P(),
        P(),
        P(("dp", "ctx"), None),
        P(("dp", "ctx"), None),
    )
    return jax.shard_map(
        layer,
        mesh=mesh,
        in_specs=placed,
        out_specs=(
            P("dp", "ctx", None),
            P("dp", "ctx", None),
            P(("dp", "ctx"), None),
            P(("dp", "ctx"), None),
            P(("dp", "ctx"), None),
            P(("dp", "ctx"), None),
        ),
        check_vma=False,
    )
```

```python
from functools import partial

import jax
import jax.numpy as jnp
from jax import lax
from jax.experimental import pallas as pl
from jax.experimental.pallas import tpu as pltpu
from jax.sharding import PartitionSpec as P

D = 1024
H = 16
HD = 64
FF = 4096


EPSILON = 1e-05
learn_rate = 0.01
beta_one = 0.9
beta_two = 0.999
adam_eps = 1e-08
decay_rate = 0.01
step_count = 10.0


def layer_norm(values, gain, shift):
    center = values - jnp.mean(values, axis=-1, keepdims=True)
    spread = jnp.mean(center * center, axis=-1, keepdims=True)
    return center * lax.rsqrt(spread + EPSILON) * gain + shift


def split_vectors(vectors):
    ratio = FF // D
    return (
        vectors[0],
        vectors[1],
        vectors[2],
        vectors[3 : 3 + ratio].reshape(FF),
        vectors[3 + ratio],
        vectors[4 + ratio],
        vectors[5 + ratio],
        vectors[6 + ratio],
        vectors[7 + ratio],
    )


def inner(left, right):
    return lax.dot_general(
        left, right, (((0,), (0,)), ((), ())), preferred_element_type=jnp.float32
    )


def through(left, weight):
    return lax.dot_general(
        left, weight, (((1,), (1,)), ((), ())), preferred_element_type=jnp.float32
    )


def run_slots(function, items):
    return lax.map(lambda item: function(*item), items)


def heads_block():
    return 4


def split_heads(matrix):
    count = matrix.shape[0]
    group = heads_block()
    return jnp.moveaxis(matrix.reshape(count, H // group, group, HD), 1, 0)


def join_heads(blocked):
    return jnp.moveaxis(blocked, 0, 1).reshape(blocked.shape[1], H * HD)


def split_stats(stats):
    group = heads_block()
    return stats.reshape(H // group, group, stats.shape[-1])


def shard_piece(left, right, number, shard_count):
    weight_rows = left.shape[1]
    columns = right.shape[1]
    per_shard = weight_rows * columns // shard_count
    block = inner(left, right).reshape(-1)
    return block.reshape(number, per_shard)


def project(flat_tokens, w_qkv, vectors):
    joined = jnp.dot(flat_tokens, w_qkv, preferred_element_type=jnp.float32)
    queries = ((joined[:, :D] + vectors[0]) * 0.125).astype(jnp.bfloat16)
    keys = joined[:, D : 2 * D].astype(jnp.bfloat16)
    values = (joined[:, 2 * D :] + vectors[1]).astype(jnp.bfloat16)
    return (queries, keys, values)


def attend_slot(queries, keys, values, live):
    rows = queries.shape[0]

    def attend_one_block(item):
        query_heads, key_heads, value_heads = item
        scores = jnp.einsum(
            "qhd,khd->hqk", query_heads, key_heads, preferred_element_type=jnp.float32
        )
        scores = jnp.where(live[None, None, :], scores, -1e30)
        maximum = jnp.max(scores, axis=-1, keepdims=True)
        expo = jnp.exp(scores - maximum)
        total = jnp.sum(expo, axis=-1, keepdims=True)
        probs_low = (expo / total).astype(jnp.bfloat16)
        mixed = jnp.einsum(
            "hqk,khd->qhd", probs_low, value_heads, preferred_element_type=jnp.float32
        )
        return (mixed, (maximum + jnp.log(total))[..., 0])

    mixed, log_total = lax.map(
        attend_one_block, (split_heads(queries), split_heads(keys), split_heads(values))
    )
    return (join_heads(mixed), log_total.reshape(H, rows))


def query_back(queries, keys, values, live, log_total, grad_mixed, with_keys):
    rows = queries.shape[0]

    def query_one_block(item):
        query_heads, key_heads, value_heads, grad_heads, block_log = item
        scores = jnp.einsum(
            "qhd,khd->hqk", query_heads, key_heads, preferred_element_type=jnp.float32
        )
        scores = jnp.where(live[None, None, :], scores, -1e30)
        probs = jnp.exp(scores - block_log[:, :, None])
        grad_probs = jnp.einsum(
            "qhd,khd->hqk", grad_heads, value_heads, preferred_element_type=jnp.float32
        )
        row_sums = jnp.sum(probs * grad_probs, axis=-1)
        grad_scores = (probs * (grad_probs - row_sums[:, :, None])).astype(jnp.bfloat16)
        grad_query = jnp.einsum(
            "hqk,khd->qhd", grad_scores, key_heads, preferred_element_type=jnp.float32
        )
        grad_key = jnp.einsum(
            "hqk,qhd->khd", grad_scores, query_heads, preferred_element_type=jnp.float32
        )
        grad_value = jnp.einsum(
            "hqk,qhd->khd",
            probs.astype(jnp.bfloat16),
            grad_heads,
            preferred_element_type=jnp.float32,
        )
        return (grad_query, row_sums, grad_key, grad_value)

    items = (
        split_heads(queries),
        split_heads(keys),
        split_heads(values),
        split_heads(grad_mixed),
        split_stats(log_total),
    )
    results = lax.map(query_one_block, items)
    grad_query, row_sums, grad_key, grad_value = results
    return (
        join_heads(grad_query),
        row_sums.reshape(H, rows),
        join_heads(grad_key),
        join_heads(grad_value),
    )


def tail(flat_tokens, mixed, w_out, w_in, w_fc2, vectors):
    bias_q, bias_v, bias_o, bias_in, bias_fc2, gain_one, shift_one, gain_two, shift_two = (
        split_vectors(vectors)
    )
    mixed_low = mixed.astype(jnp.bfloat16)
    summed_one = (
        flat_tokens.astype(jnp.float32)
        + jnp.dot(mixed_low, w_out, preferred_element_type=jnp.float32)
        + bias_o
    )
    normed = layer_norm(summed_one, gain_one, shift_one)
    normed_low = normed.astype(jnp.bfloat16)
    hidden_pre = jnp.dot(normed_low, w_in, preferred_element_type=jnp.float32) + bias_in
    hidden_low = jax.nn.gelu(hidden_pre, approximate=False).astype(jnp.bfloat16)
    summed_two = normed + jnp.dot(hidden_low, w_fc2, preferred_element_type=jnp.float32) + bias_fc2
    result = layer_norm(summed_two, gain_two, shift_two)
    return (mixed_low, summed_one, normed_low, hidden_pre, hidden_low, summed_two, result)


def body(tokens, out_grad, lengths, w_qkv, w_out, w_in, w_fc2, vectors, moment_one, moment_two):
    slots, piece, width = tokens.shape
    length = piece * lax.axis_size("ctx")
    local_pos = lax.axis_index("ctx") * piece + jnp.arange(piece, dtype=jnp.int32)
    own_live = local_pos[None, :] < lengths[:, None]
    valid = own_live.astype(jnp.float32)
    key_live = jnp.arange(length, dtype=jnp.int32)[None, :] < lengths[:, None]
    bias_q, bias_v, bias_o, bias_in, bias_fc2, gain_one, shift_one, gain_two, shift_two = (
        split_vectors(vectors)
    )
    flat_tokens = tokens.reshape(slots * piece, width)
    queries, keys, values = project(flat_tokens, w_qkv, vectors)
    keys_all, values_all = (
        lax.all_gather(keys.reshape(slots, piece, width), "ctx", axis=1, tiled=True),
        lax.all_gather(values.reshape(slots, piece, width), "ctx", axis=1, tiled=True),
    )
    mixed, log_total = run_slots(
        attend_slot, (queries.reshape(slots, piece, width), keys_all, values_all, key_live)
    )
    saved = tail(flat_tokens, mixed.reshape(slots * piece, width), w_out, w_in, w_fc2, vectors)
    out = (saved[6].reshape(slots, piece, width) * valid[..., None]).astype(jnp.bfloat16)
    again = lax.optimization_barrier(flat_tokens)
    queries, keys, values = project(again, w_qkv, vectors)
    keys_all, values_all = (
        lax.all_gather(keys.reshape(slots, piece, width), "ctx", axis=1, tiled=True),
        lax.all_gather(values.reshape(slots, piece, width), "ctx", axis=1, tiled=True),
    )
    mixed, log_total = run_slots(
        attend_slot, (queries.reshape(slots, piece, width), keys_all, values_all, key_live)
    )
    saved = tail(again, mixed.reshape(slots * piece, width), w_out, w_in, w_fc2, vectors)
    mixed_low, summed_one, normed_low, hidden_pre, hidden_low, summed_two, result = saved
    cotangent = (out_grad.astype(jnp.float32) * valid[..., None]).reshape(slots * piece, width)
    unused_two, norm_two_back = jax.vjp(layer_norm, summed_two, gain_two, shift_two)
    grad_two, grad_gain_two, grad_shift_two = norm_two_back(cotangent)
    grad_fc2_low = grad_two.astype(jnp.bfloat16)
    bias_fc2_grad = jnp.sum(grad_fc2_low.astype(jnp.float32), axis=0)
    grad_hidden = through(grad_fc2_low, w_fc2)
    unused_gelu, gelu_back = jax.vjp(partial(jax.nn.gelu, approximate=False), hidden_pre)
    grad_pre_low = gelu_back(grad_hidden)[0].astype(jnp.bfloat16)
    bias_in_grad = jnp.sum(grad_pre_low.astype(jnp.float32), axis=0)
    grad_normed = grad_two + through(grad_pre_low, w_in)
    unused_one, norm_one_back = jax.vjp(layer_norm, summed_one, gain_one, shift_one)
    grad_one, grad_gain_one, grad_shift_one = norm_one_back(grad_normed)
    grad_branch_low = grad_one.astype(jnp.bfloat16)
    bias_out_grad = jnp.sum(grad_branch_low.astype(jnp.float32), axis=0)
    grad_mixed_low = (
        through(grad_branch_low, w_out).astype(jnp.bfloat16).reshape(slots, piece, width)
    )
    queries_slots = queries.reshape(slots, piece, width)
    grad_query, row_sums, grad_key, grad_value = run_slots(
        partial(query_back, with_keys=True),
        (queries_slots, keys_all, values_all, key_live, log_total, grad_mixed_low),
    )
    grad_key, grad_value = (
        lax.psum_scatter(
            grad_key.astype(jnp.bfloat16), "ctx", scatter_dimension=1, tiled=True
        ).astype(jnp.float32),
        lax.psum_scatter(
            grad_value.astype(jnp.bfloat16), "ctx", scatter_dimension=1, tiled=True
        ).astype(jnp.float32),
    )
    rows = slots * piece
    grad_query_low = grad_query.reshape(rows, width).astype(jnp.bfloat16) * jnp.bfloat16(0.125)
    grad_key_low = grad_key.reshape(rows, width).astype(jnp.bfloat16)
    grad_value_low = grad_value.reshape(rows, width).astype(jnp.bfloat16)
    grad_joined = jnp.concatenate([grad_query_low, grad_key_low, grad_value_low], axis=1)
    bias_q_grad = jnp.sum(grad_query_low.astype(jnp.float32), axis=0)
    bias_v_grad = jnp.sum(grad_value_low.astype(jnp.float32), axis=0)
    tokens_grad = (
        (grad_one + through(grad_joined, w_qkv)).reshape(slots, piece, width).astype(jnp.bfloat16)
    )
    vector_grad = jnp.concatenate(
        [
            bias_q_grad[None],
            bias_v_grad[None],
            bias_out_grad[None],
            bias_in_grad.reshape(FF // D, D),
            bias_fc2_grad[None],
            grad_gain_one[None],
            grad_shift_one[None],
            grad_gain_two[None],
            grad_shift_two[None],
        ],
        axis=0,
    )
    count = lax.axis_size(("dp", "ctx"))
    vector_rows = vector_grad.reshape(count, -1)
    pairs = (
        (flat_tokens, grad_joined),
        (mixed_low, grad_branch_low),
        (normed_low, grad_pre_low),
        (hidden_low, grad_fc2_low),
    )
    blocks = [
        shard_piece(left, right, 1 * lax.axis_size(("dp", "ctx")), count) for left, right in pairs
    ]
    blocks.append(vector_rows)
    grad_rows = lax.psum_scatter(
        jnp.concatenate(blocks, axis=1), ("dp", "ctx"), scatter_dimension=0, tiled=True
    )
    index = lax.axis_index(("dp", "ctx"))
    params = jnp.concatenate(
        [
            lax.dynamic_slice_in_dim(weight.reshape(count, -1), index, 1, 0).astype(jnp.float32)
            for weight in (w_qkv, w_out, w_in, w_fc2, vectors)
        ],
        axis=1,
    )
    new_one = beta_one * moment_one + (1.0 - beta_one) * grad_rows
    new_two = beta_two * moment_two + (1.0 - beta_two) * grad_rows * grad_rows
    fix_one = 1.0 - beta_one**step_count
    fix_two = 1.0 - beta_two**step_count
    update = new_one / fix_one / (jnp.sqrt(new_two / fix_two) + adam_eps)
    new_params = params - learn_rate * (update + decay_rate * params)
    return (out, tokens_grad, grad_rows, new_params, new_one, new_two)


BF16 = jnp.bfloat16
F32 = jnp.float32


def layer_norm_stats(values):
    center = values - jnp.mean(values, axis=-1, keepdims=True)
    spread = jnp.mean(center * center, axis=-1, keepdims=True)
    return center, lax.rsqrt(spread + EPSILON)


def layer_norm_back(center, scale, gain, cotangent):
    scaled = cotangent * gain
    mean_scaled = jnp.mean(scaled, axis=-1, keepdims=True)
    mean_cross = jnp.mean(scaled * center, axis=-1, keepdims=True)
    return scale * (scaled - mean_scaled - center * (scale * scale) * mean_cross)


def normal_cdf(values):
    return 0.5 * (1.0 + lax.erf(values * 0.7071067811865476))


def dot(left, right):
    return jnp.dot(left, right, preferred_element_type=F32)


def positions(axis, shape, slot, piece):
    place = lax.broadcasted_iota(jnp.int32, shape, axis)
    block = lax.div(place, piece)
    half = lax.div(block, 2)
    step = lax.rem(block, 2)
    return (2 * half + lax.rem(slot + step, 2)) * piece + lax.rem(place, piece)


def head_probs(queries, keys, live):
    scores = through(queries, keys)
    scores = jnp.where(live, scores, -1e30)
    expo = jnp.exp(scores - jnp.max(scores, axis=-1, keepdims=True))
    return expo / jnp.sum(expo, axis=-1, keepdims=True)


MESH = pl.DeviceIdType.MESH


class Links:
    def __init__(self, sends, recvs):
        self.sends, self.recvs = sends, recvs
        self.used = 0
        self.open = []

    def copy(self, source, target, device):
        self.used += 1
        return self.again(source, target, device)

    def again(self, source, target, device):
        number = self.used - 1
        return pltpu.make_async_remote_copy(
            src_ref=source,
            dst_ref=target,
            send_sem=self.sends.at[number],
            recv_sem=self.recvs.at[number],
            device_id=device,
            device_id_type=MESH,
        )

    def forward(self, source, target, device, earlier):
        self.used += 1
        return pltpu.make_async_remote_copy(
            src_ref=source,
            dst_ref=target,
            send_sem=self.sends.at[self.used - 1],
            recv_sem=self.recvs.at[earlier],
            device_id=device,
            device_id_type=MESH,
        )

    def send(self, source, target, device):
        made = self.copy(source, target, device)
        made.start()
        self.open.append((made, None))
        return made

    def send_if(self, condition, source, target, device):
        made = self.copy(source, target, device)
        pl.when(condition)(made.start)
        self.open.append((made, condition))
        return made

    def send_or_keep(self, here, source, target, device):
        number = self.used
        made = self.copy(source, target, device)
        local = pltpu.make_async_copy(source, target, self.recvs.at[number])
        pl.when(here)(local.start)
        away = jnp.logical_not(here)
        pl.when(away)(made.start)
        self.open.append((made, away))

        def wait():
            pl.when(here)(local.wait)
            pl.when(away)(made.wait_recv)

        return wait

    def close(self):
        for made, condition in self.open:
            if condition is None:
                made.wait_send()
            else:
                pl.when(condition)(made.wait_send)


def flip(value, mask):
    result = value
    bit = 1
    while bit <= mask:
        if mask & bit:
            result = result + bit * (1 - 2 * lax.rem(lax.div(value, bit), 2))
        bit *= 2
    return result


def flip_traced(value, mask, size):
    result = value
    bit = 1
    while bit < size:
        set_bit = lax.rem(lax.div(mask, bit), 2)
        result = result + bit * set_bit * (1 - 2 * lax.rem(lax.div(value, bit), 2))
        bit *= 2
    return result


def at_rows(start, size):
    return pl.ds(pl.multiple_of(start, 64), size)


def slot_kernel(devices, depth, features, *refs):
    (
        tokens, out_grad, lengths, vec, w_qkv, w_out, w_in, w_fc2,
        out_ref, tgrad_ref, g_qkv, g_out, g_in, g_fc2, g_vec,
        wqkv, wo, w_up, w_down,
        x_all, n_all, g_all, m_all, b_all, j_all, j_send, g_rows, lens_peer,
        qkv, part, part_low, part_a, part_b, part_c, part_d, summed, grad_two, grad_one,
        pre_s, hid, hid_all, gp_all, packed, plane_got, up_mine, down_mine, packed_two, right_two, left_two,
        trade_in, got_in, trade_qkv, got_qkv, vec_s, vec_by, vec_got, sums, dqkv, out_half, out_got, tg_half, tg_got, lens,
        local_sems, sends, recvs,
    ) = refs
    chips = devices // 2
    me, slot = lax.axis_index("dp"), lax.axis_index("ctx")
    core, chip = lax.rem(me, 2), lax.div(me, 2)
    base = me - core
    peer = (base + 1 - core, slot)
    piece = tokens.shape[1]
    half = 2 * piece
    rows = 2 * half
    block = D // devices
    wide = features // devices
    lines = D // (devices * depth)
    net = Links(sends, recvs)
    mine_at = at_rows(core * half, half)
    other_at = at_rows((1 - core) * half, half)
    chunk = 32

    row_of = lax.broadcasted_iota(jnp.int32, lens.shape, 0)
    lens[...] = jnp.where(row_of == 0, lengths[0], lengths[1])
    vec_s[...] = jnp.zeros_like(vec_s)
    loads = []

    def load(source, target):
        made = pltpu.make_async_copy(source, target, local_sems.at[len(loads)])
        made.start()
        loads.append(made)

    where = [2 * flip(chip, mask) + core for mask in range(chips)]
    for mask in range(chips):
        for kind in range(3):
            start = pl.multiple_of(kind * D + where[mask] * block, block)
            load(
                w_qkv.at[:, pl.ds(start, block)],
                wqkv.at[:, (3 * mask + kind) * block : (3 * mask + kind + 1) * block],
            )
    n_qkv = len(loads)
    for number in range(chips):
        start = pl.multiple_of((2 * number + core) * block, block)
        load(w_out.at[pl.ds(start, block), :], wo.at[number * block : (number + 1) * block, :])
    n_out = len(loads)
    for mask in range(chips):
        start = pl.multiple_of(where[mask] * wide, wide)
        load(w_in.at[:, pl.ds(start, wide)], w_up.at[:, mask * wide : (mask + 1) * wide])
    n_up = len(loads)
    for mask in range(chips):
        start = pl.multiple_of(where[mask] * wide, wide)
        load(w_fc2.at[pl.ds(start, wide), :], w_down.at[mask * wide : (mask + 1) * wide, :])

    barrier = pltpu.get_barrier_semaphore()
    friends = [(flip(me, mask), slot) for mask in range(1, devices)]
    for shift in range(1, depth):
        far = lax.rem(slot + shift, depth)
        friends += [(me, far), (flip(me, 1), far)]
    for friend in friends:
        pl.semaphore_signal(barrier, inc=1, device_id=friend, device_id_type=MESH)
    pl.semaphore_wait(barrier, len(friends))

    def spread(source, target):
        waits = []
        for step in range(2):
            pick = lax.rem(slot + step, 2)
            upper = lax.div(slot, 2)
            place = 2 * core + pick
            here = jnp.logical_and(upper == core, place == slot)
            waits.append(
                net.send_or_keep(
                    here,
                    source.at[pick],
                    target.at[at_rows((2 * upper + step) * piece, piece)],
                    (base + upper, place),
                )
            )
        return waits

    def pass_on(waits, target):
        made = []
        for step, wait in enumerate(waits):
            wait()
            spot = target.at[at_rows((2 * core + step) * piece, piece)]
            made.append(net.send(spot, spot, peer))
        return made

    token_waits = spread(tokens, x_all)
    grad_waits = spread(out_grad, g_rows)
    lens_copy = net.send(lens, lens_peer, peer)
    token_passes = pass_on(token_waits, x_all)

    def plane_start(target):
        source = target.at[mine_at]
        return [
            net.send(
                source, target.at[at_rows(mask * rows + core * half, half)], (flip(me, 2 * mask), slot)
            )
            for mask in range(1, chips)
        ]

    def plane_pass(copies, target):
        made = []
        for mask, copy in enumerate(copies, 1):
            copy.wait_recv()
            spot = target.at[at_rows(mask * rows + core * half, half)]
            made.append(net.send(spot, spot, peer))
        return made

    class Column:
        def __init__(self, target):
            self.target = target
            self.parts, self.numbers = {}, {}
            for place in (2, 1, 3):
                far = lax.rem(slot + depth - place, depth)
                made = net.copy(target.at[mine_at], self.spot(place), (me, far))
                self.parts[place], self.numbers[place] = made, net.used - 1
                goes = {1: slot != 0, 2: slot >= 0, 3: slot != depth - 1}[place]
                net.open.append((made, goes))
                pl.when(goes)(made.start)
            self.passes = {}

        def spot(self, place):
            return self.target.at[at_rows(place * rows + core * half, half)]

        def relay(self):
            self.parts[2].wait_recv()
            up = net.forward(self.spot(2), self.spot(1), (me, depth - 1), self.numbers[1])
            down = net.forward(self.spot(2), self.spot(3), (me, 0), self.numbers[3])
            for made, here in ((up, slot == 2), (down, slot == 1)):
                pl.when(here)(made.start)
                net.open.append((made, here))
            self.passes[2] = net.send(self.spot(2), self.spot(2), peer)

        def hand_over(self, place):
            self.parts[place].wait_recv()
            self.passes[place] = net.send(self.spot(place), self.spot(place), peer)

    x_plane = plane_start(x_all)
    for made in loads[:n_qkv]:
        made.wait()
    lens_copy.wait_recv()
    for made in token_passes:
        made.wait_recv()
    owned = jnp.where(lax.div(slot, 2) == core, lens[...], lens_peer[...])
    length = jnp.where(lax.rem(slot, 2) == 0, owned[0:1, 0:1], owned[1:2, 0:1])
    live = positions(1, (1, rows), slot, piece) < length
    lane = lax.broadcasted_iota(jnp.int32, (1, block), 1)

    @pl.loop(0, chips)
    def _(mask):
        spot = 2 * flip_traced(chip, mask, chips) + core
        lanes = pl.ds(pl.multiple_of(spot * block, block), block)
        joined = dot(x_all[0:rows, :], wqkv[:, pl.ds(pl.multiple_of(mask * 3 * block, block), 3 * block)])
        queries = ((joined[:, 0:block] + vec[0:1, lanes]) * 0.125).astype(BF16)
        keys = joined[:, block : 2 * block].astype(BF16)
        values = (joined[:, 2 * block :] + vec[1:2, lanes]).astype(BF16)
        total = jnp.zeros((rows, block), F32)
        for head in range(block // HD):
            mine = lax.div(lane, HD) == head
            probs = head_probs(jnp.where(mine, queries, jnp.zeros_like(queries)), keys, live)
            total = jnp.where(mine, dot(probs.astype(BF16), values), total)
        start = pl.multiple_of(mask * 3 * block, block)
        qkv[:, pl.ds(start, block)] = queries
        qkv[:, pl.ds(pl.multiple_of(start + block, block), block)] = keys
        qkv[:, pl.ds(pl.multiple_of(start + 2 * block, block), block)] = values
        lanes = pl.ds(pl.multiple_of(core * chips * block + lax.div(spot, 2) * block, block), block)
        m_all[0:rows, lanes] = total.astype(BF16)

    for made in loads[n_qkv:n_out]:
        made.wait()

    def exchange(compute, target, before):
        made = []
        for number, at in enumerate((other_at, mine_at)):
            if before is not None:
                before[number].wait_send()
            value = compute(at)
            part[at, :] = value
            part_low[at, :] = value.astype(BF16)
            made.append(net.copy(part_low.at[at], target.at[at], peer))
            made[-1].start()
        return made

    my_lanes = pl.ds(pl.multiple_of(core * chips * block, chips * block), chips * block)
    first = exchange(lambda at: dot(m_all[at, my_lanes], wo[...]), part_a, None)
    own_mixed = m_all.at[0:rows, my_lanes]
    m_passes = [net.send(own_mixed, own_mixed, peer)]
    m_plane = [
        net.send(own_mixed, m_all.at[mask * rows : (mask + 1) * rows, my_lanes], (flip(me, 2 * mask), slot))
        for mask in range(1, chips)
    ]
    grad_passes = pass_on(grad_waits, g_rows)

    def norm_one(start):
        @pl.loop(0, half // chunk)
        def _(step):
            at = pl.ds(pl.multiple_of(start + step * chunk, chunk), chunk)
            total = x_all[at, :].astype(F32) + (part[at, :] + part_a[at, :].astype(F32)) + vec[2:3, :]
            center, scale = layer_norm_stats(total)
            summed[at, :] = total
            n_all[at, :] = (center * scale * vec[8:9, :] + vec[9:10, :]).astype(BF16)

    first[0].wait_recv()
    norm_one(core * half)
    n_column = Column(n_all)
    first[1].wait_recv()
    norm_one((1 - core) * half)
    for made in loads[n_out:]:
        made.wait()

    for number in range(chips):
        fine_cols = wide // depth
        begin = flip_traced(chip, number, chips) * wide + slot * fine_cols
        at = pl.ds(pl.multiple_of(begin, fine_cols), fine_cols)
        up_mine[:, number * fine_cols : (number + 1) * fine_cols] = w_up[:, at]
        down_mine[number * fine_cols : (number + 1) * fine_cols, :] = w_down[at, :]

    def bias_of(mask):
        spot = flip_traced(chip, mask, chips)
        lanes = pl.ds(pl.multiple_of(core * wide, wide), wide)
        result = vec[3:4, lanes]
        for row in range(1, chips):
            result = jnp.where(spot == row, vec[3 + row : 4 + row, lanes], result)
        return result

    @pl.loop(0, chips)
    def _(mask):
        at = pl.ds(pl.multiple_of(mask * wide, wide), wide)
        value = dot(n_all[0:rows, :], w_up[:, at]) + bias_of(mask)
        pre_s[:, at] = value
        hid[:, at] = (value * normal_cdf(value)).astype(BF16)

    second = exchange(lambda at: dot(hid[at, :], w_down[...]), part_b, first)
    for made in grad_passes:
        made.wait_recv()

    def norm_two(start, own):
        @pl.loop(0, half // chunk)
        def _(step):
            begin = pl.multiple_of(start + step * chunk, chunk)
            at = pl.ds(begin, chunk)
            center, scale = layer_norm_stats(summed[at, :])
            normed = center * scale * vec[8:9, :] + vec[9:10, :]
            center, scale = layer_norm_stats(normed + (part[at, :] + part_b[at, :].astype(F32)) + vec[7:8, :])
            place = begin + lax.broadcasted_iota(jnp.int32, (chunk, 1), 0)
            piece_of = lax.div(place, piece)
            spot = 2 * lax.div(piece_of, 2) + lax.rem(slot + lax.rem(piece_of, 2), 2)
            valid = (spot * piece + lax.rem(place, piece) < length).astype(F32)
            unit = center * scale
            error = g_rows[at, :].astype(F32) * valid
            grad = layer_norm_back(center, scale, vec[10:11, :], error)
            grad_two[at, :] = grad
            low = grad.astype(BF16)
            g_all[at, :] = low
            if own:
                out_half[pl.ds(pl.multiple_of(step * chunk, chunk), chunk), :] = (
                    valid * (unit * vec[10:11, :] + vec[11:12, :])
                ).astype(BF16)
                vec_s[7:8, :] += jnp.sum(low.astype(F32), axis=0, keepdims=True)
                vec_s[10:11, :] += jnp.sum(error * unit, axis=0, keepdims=True)
                vec_s[11:12, :] += jnp.sum(error, axis=0, keepdims=True)

    def go_back(source, target):
        waits = []
        for step in range(2):
            place = 2 * core + lax.rem(slot + step, 2)
            upper = lax.div(slot, 2)
            here = jnp.logical_and(upper == core, place == slot)
            waits.append(
                net.send_or_keep(
                    here,
                    source.at[step * piece : (step + 1) * piece],
                    target.at[lax.rem(slot, 2)],
                    (base + upper, place),
                )
            )
        return waits

    second[0].wait_recv()
    norm_two(core * half, True)
    g_column = Column(g_all)
    second[1].wait_recv()
    norm_two((1 - core) * half, False)
    out_waits = go_back(out_half, out_got)

    def mixed_pass():
        for mask, made in enumerate(m_plane, 1):
            made.wait_recv()
            spot = m_all.at[mask * rows : (mask + 1) * rows, my_lanes]
            m_passes.append(net.send(spot, spot, peer))

    def slope_of(value, cdf):
        return cdf + value * (jnp.exp(-0.5 * value * value) * 0.3989422804014327)

    @pl.loop(0, chips)
    def _(mask):
        at = pl.ds(pl.multiple_of(mask * wide, wide), wide)
        value = pre_s[:, at]
        grad = through(g_all[0:rows, :], w_down[at, :])
        hid[:, at] = (grad * slope_of(value, normal_cdf(value))).astype(BF16)

    third = exchange(lambda at: through(hid[at, :], w_up[...]), part_c, second)

    def norm_one_back(start, own):
        @pl.loop(0, half // chunk)
        def _(step):
            at = pl.ds(pl.multiple_of(start + step * chunk, chunk), chunk)
            center, scale = layer_norm_stats(summed[at, :])
            error = grad_two[at, :] + (part[at, :] + part_c[at, :].astype(F32))
            grad = layer_norm_back(center, scale, vec[8:9, :], error)
            low = grad.astype(BF16)
            b_all[at, :] = low
            grad_one[at, :] = grad
            if own:
                vec_s[2:3, :] += jnp.sum(low.astype(F32), axis=0, keepdims=True)
                vec_s[8:9, :] += jnp.sum(error * (center * scale), axis=0, keepdims=True)
                vec_s[9:10, :] += jnp.sum(error, axis=0, keepdims=True)

    x_pass = plane_pass(x_plane, x_all)

    third[0].wait_recv()
    norm_one_back(core * half, True)
    third[1].wait_recv()
    norm_one_back((1 - core) * half, False)
    class Line:
        def __init__(self, chunks, from_left, from_right):
            self.chunks, self.from_left, self.from_right = chunks, from_left, from_right
            self.up, self.down, self.first_up, self.first_down = [], [], [], []
            after = (me, lax.rem(slot + 1, depth))
            before = (me, lax.rem(slot + depth - 1, depth))
            for order in range(depth - 1):
                top, low = depth - 1 - order, order
                spot = from_left.at[order]
                self.up.append(net.copy(spot, spot, after))
                self.first_up.append(net.again(chunks.at[top], spot, after))
                net.open.append((self.up[-1], slot < top))
                spot = from_right.at[order]
                self.down.append(net.copy(spot, spot, before))
                self.first_down.append(net.again(chunks.at[low], spot, before))
                net.open.append((self.down[-1], slot > low))

        def first(self):
            for order in range(depth - 1):
                pl.when(slot == 0)(self.first_up[order].start)
                pl.when(slot == depth - 1)(self.first_down[order].start)

        def stage(self, time):
            for order in range(time):
                top, low = depth - 1 - order, order

                @pl.when(slot == time - order)
                def _(order=order, top=top):
                    self.up[order].wait_recv()
                    if time < depth - 1:
                        self.from_left[order] = (
                            self.from_left[order].astype(F32) + self.chunks[top].astype(F32)
                        ).astype(BF16)
                        self.up[order].start()

                @pl.when(depth - 1 - slot == time - order)
                def _(order=order, low=low):
                    self.down[order].wait_recv()
                    if time < depth - 1:
                        self.from_right[order] = (
                            self.from_right[order].astype(F32) + self.chunks[low].astype(F32)
                        ).astype(BF16)
                        self.down[order].start()

    grad_parts = range(1, chips)

    def attention_back(mask):
        start = mask * 3 * block
        queries = qkv[:, start : start + block]
        keys = qkv[:, start + block : start + 2 * block]
        values = qkv[:, start + 2 * block : start + 3 * block]
        turn = pl.ds(pl.multiple_of(lax.div(where[mask], 2) * block, block), block)
        grad_mixed = through(b_all[0:rows, :], wo[turn, :]).astype(BF16)
        grad_q = jnp.zeros((rows, block), F32)
        grad_k = grad_q
        grad_v = grad_q
        for head in range(block // HD):
            mine = lax.div(lane, HD) == head
            probs = head_probs(jnp.where(mine, queries, jnp.zeros_like(queries)), keys, live)
            grad_probs = through(jnp.where(mine, grad_mixed, jnp.zeros_like(grad_mixed)), values)
            dsum = jnp.sum(probs * grad_probs, axis=-1, keepdims=True)
            grad_scores = (probs * (grad_probs - dsum)).astype(BF16)
            grad_q = jnp.where(mine, dot(grad_scores, keys), grad_q)
            grad_k = jnp.where(mine, inner(grad_scores, queries), grad_k)
            grad_v = jnp.where(mine, inner(probs.astype(BF16), grad_mixed), grad_v)
        grad_q = grad_q.astype(BF16) * jnp.bfloat16(0.125)
        grad_k = grad_k.astype(BF16)
        grad_v = grad_v.astype(BF16)
        spot = pl.ds(pl.multiple_of(where[mask] * block, block), block)
        vec_s[0:1, spot] = jnp.sum(grad_q.astype(F32), axis=0, keepdims=True)
        vec_s[1:2, spot] = jnp.sum(grad_v.astype(F32), axis=0, keepdims=True)
        dqkv[:, start : start + block] = grad_q
        dqkv[:, start + block : start + 2 * block] = grad_k
        dqkv[:, start + 2 * block : start + 3 * block] = grad_v
        if mask:
            joint = j_send.at[mask - 1]
        else:
            joint = j_all.at[0:rows]
        joint[:, 0:block] = grad_q
        joint[:, block : 2 * block] = grad_k
        joint[:, 2 * block : 3 * block] = grad_v
        joint[:, 3 * block : 4 * block] = b_all[0:rows, spot]
        if mask:
            return net.send(
                joint, j_all.at[mask * rows : (mask + 1) * rows], (flip(me, 2 * mask), slot)
            )
        return None

    n_column.relay()
    j_copies = [attention_back(mask) for mask in grad_parts]
    attention_back(0)
    mixed_pass()
    n_column.hand_over(1)
    n_column.hand_over(3)
    for made in third:
        made.wait_send()
    part[0:half, :] = through(dqkv[other_at, :], wqkv[...])
    tg_copy = net.copy(part.at[0:half], part_d, peer)
    tg_copy.start()
    part[half:rows, :] = grad_one[mine_at, :] + through(dqkv[mine_at, :], wqkv[...])
    tg_copy.wait_recv()
    tg_half[...] = (part[half:rows, :] + part_d[...]).astype(BF16)

    fine = wide // depth
    span = lines * depth
    features_at = pl.ds(pl.multiple_of((depth * core + slot) * fine, fine), fine)
    bias_mine = jnp.concatenate([vec[3 + number : 4 + number, features_at] for number in range(chips)], axis=1)

    def feed_rows(place):
        at = slice(place * rows, (place + 1) * rows)
        value = dot(n_all[at, :], up_mine[...]) + bias_mine
        cdf = normal_cdf(value)
        hid_all[at, :] = (value * cdf).astype(BF16)
        low = (through(g_all[at, :], down_mine[...]) * slope_of(value, cdf)).astype(BF16)
        gp_all[at, :] = low
        return jnp.sum(low.astype(F32), axis=0, keepdims=True)

    bias_sum = feed_rows(0)
    g_column.relay()
    for column in (n_column, g_column):
        column.passes[2].wait_recv()
    bias_sum = bias_sum + feed_rows(2)
    for made in m_passes + x_pass + j_copies:
        made.wait_recv()
    for group in range(devices):
        at = slice(group * span, (group + 1) * span)
        begin = (group % 2) * chips * block + (group // 2) * block
        both = inner(x_all[:, at], j_all[:, 0 : 3 * block]).astype(BF16)
        across = inner(m_all[:, begin : begin + block], j_all[:, 3 * block : 4 * block]).astype(BF16)
        row = group * lines
        for number in range(depth):
            at = slice(number * lines, (number + 1) * lines)
            packed_two[number, row : row + lines, 0 : 3 * block] = both[at, :]
            packed_two[number, row : row + lines, 3 * block : 4 * block] = across[at, :]
    input_line = Line(packed_two, right_two, left_two)
    input_line.first()

    g_column.hand_over(1)
    g_column.hand_over(3)
    for place in (1, 3):
        n_column.passes[place].wait_recv()
        g_column.passes[place].wait_recv()
        bias_sum = bias_sum + feed_rows(place)
    for number in range(chips):
        vec_s[3 + number : 4 + number, features_at] = bias_sum[:, number * fine : (number + 1) * fine]
    depth_rows = D // chips
    for number in range(chips):
        block_up = inner(n_all[:, number * depth_rows : (number + 1) * depth_rows], gp_all[...]).astype(BF16)
        packed[number, fine : 2 * fine, 0:wide] = block_up[0:fine, :]
        packed[number, fine : 2 * fine, wide : 2 * wide] = block_up[fine : 2 * fine, :]

    def scatter_plane(lines_at):
        return [
            net.send(
                packed.at[flip_traced(chip, mask, chips), lines_at],
                plane_got.at[mask - 1, lines_at],
                (flip(me, 2 * mask), slot),
            )
            for mask in range(1, chips)
        ]

    up_copies = scatter_plane(slice(fine, 2 * fine))
    packed[:, 0:fine, :] = inner(hid_all[...], g_all[...]).astype(BF16).reshape(chips, fine, D)
    down_copies = scatter_plane(slice(0, fine))

    tiles = vec.shape[0] * D // 128
    share = tiles // (devices * depth)
    vec_by[...] = jnp.zeros_like(vec_by)
    for tile in range(tiles):
        owner, lane_group = tile // share, tile % share
        row, col = tile // (D // 128), (tile % (D // 128)) * 128
        spot = (owner % depth) * devices + owner // depth
        vec_by[spot : spot + 1, lane_group * 128 : (lane_group + 1) * 128] = vec_s[
            row : row + 1, col : col + 128
        ]
    vec_copies = []
    for shift in range(1, depth):
        far = lax.rem(slot + shift, depth)
        spot = vec_by.at[pl.ds(pl.multiple_of(far * devices, devices), devices)]
        vec_copies.append(net.send(spot, vec_got.at[shift - 1], (me, far)))

    def finish(line, target, rows_at):
        target[...] = line.chunks[slot, rows_at, :].astype(F32)

        @pl.when(slot >= 1)
        def _():
            target[...] += line.from_left[depth - 1 - slot, rows_at, :].astype(F32)

        @pl.when(slot <= depth - 2)
        def _():
            target[...] += line.from_right[slot, rows_at, :].astype(F32)

    def plane_sum(copies, lines_at):
        for made in copies:
            made.wait_recv()
        value = packed[chip, lines_at, :].astype(F32)
        for number in range(chips - 1):
            value = value + plane_got[number, lines_at, :].astype(F32)
        return value

    def trade(source, target):
        return [
            net.send(source.at[flip(me, mask)], target.at[me], (flip(me, mask), slot))
            for mask in range(1, devices)
        ]

    tg_waits = go_back(tg_half, tg_got)
    for time in range(1, depth - 1):
        input_line.stage(time)
    low_sum = plane_sum(up_copies, slice(fine, 2 * fine)).astype(BF16)
    for upper in range(2):
        for number in range(depth):
            trade_in[upper * depth + number] = low_sum[
                number * lines : (number + 1) * lines, upper * wide : (upper + 1) * wide
            ]
    here = core * depth + slot
    in_copies = []
    for shift in range(1, 2 * depth):
        far = lax.rem(slot + shift % depth, depth)
        upper = core if shift < depth else 1 - core
        in_copies.append(net.send(trade_in.at[upper * depth + far], got_in.at[here], (base + upper, far)))
    input_line.stage(depth - 1)
    tg_copy.wait_send()
    finish(input_line, sums, slice(0, rows))
    vec_sum = vec_by[pl.ds(pl.multiple_of(slot * devices, devices), devices), :]
    for number, made in enumerate(vec_copies):
        made.wait_recv()
        vec_sum = vec_sum + vec_got[number]
    first_row = lax.broadcasted_iota(jnp.int32, (16, 4 * block), 0) == 0
    for group in range(devices):
        trade_qkv[group, 0:lines, :] = sums[group * lines : (group + 1) * lines, :].astype(BF16)
        trade_qkv[group, lines : lines + 16, :] = jnp.where(
            first_row, vec_sum[group : group + 1, :], 0.0
        ).astype(BF16)
    qkv_copies = trade(trade_qkv, got_qkv)
    for made in in_copies:
        made.wait_recv()
    got_in[here] = trade_in[here]
    for group in range(2 * depth):
        for number in range(chips):
            start = number * 2 * wide + group * fine
            g_in[:, start : start + fine] = got_in[group, :, number * fine : (number + 1) * fine].astype(F32)
    g_fc2[...] = plane_sum(down_copies, slice(0, fine))
    for wait in out_waits + tg_waits:
        wait()
    out_ref[...] = out_got[...]
    tgrad_ref[...] = tg_got[...]
    for made in qkv_copies:
        made.wait_recv()
    got_qkv[me] = trade_qkv[me]
    vec_sum = jnp.zeros((16, 3 * block), F32)
    for group in range(devices):
        vec_sum = vec_sum + got_qkv[group, lines : lines + 16, 0 : 3 * block].astype(F32)
        got = got_qkv[group, 0:lines, :].astype(F32)
        for kind in range(3):
            g_qkv[:, kind * D + group * block : kind * D + (group + 1) * block] = got[
                :, kind * block : (kind + 1) * block
            ]
        g_out[:, group * block : (group + 1) * block] = got[:, 3 * block : 4 * block]
    g_vec[...] = vec_sum[0:8, :]
    net.close()


def adam_kernel(count, *refs):
    (
        g_qkv, g_out, g_in, g_fc2, g_vec, vec, out_in, tgrad_in, w_qkv, w_out, w_in, w_fc2, m_one, m_two,
        out_ref, tgrad_ref, rows_out, params_out, one_out, two_out,
        grads, params, one, two, d_qkv, d_out, d_in, d_fc2, b_qkv, b_out, b_in, b_fc2, out_by, tgrad_by, vec_flat,
        in_sems, g_sems, w_sems, out_sems, pass_sems,
    ) = refs
    index = lax.axis_index("dp") * lax.axis_size("ctx") + lax.axis_index("ctx")
    size = m_one.shape[1] // 128
    kinds = (
        (g_qkv, d_qkv, w_qkv, b_qkv),
        (g_out, d_out, w_out, b_out),
        (g_in, d_in, w_in, b_in),
        (g_fc2, d_fc2, w_fc2, b_fc2),
    )
    lengths = [kind[1].shape[0] * kind[1].shape[1] // 128 for kind in kinds]
    starts = [sum(lengths[:number]) for number in range(len(kinds))]
    tail = sum(lengths)
    order = (3, 2, 0, 1, 4)
    spans = [(start, length) for start, length in zip(starts, lengths)] + [(tail, size - tail)]

    def load(source, target, sem):
        made = pltpu.make_async_copy(source, target, sem)
        made.start()
        return made

    blocks, loads = {}, {}
    for number in order:
        start, length = spans[number]
        if number < len(kinds):
            grad, grad_by, weight, weight_by = kinds[number]
            lines = weight_by.shape[0]
            mine = pl.ds(pl.multiple_of(index * lines, lines), lines)
            blocks[number] = [
                load(grad, grad_by, g_sems.at[number]),
                load(weight.at[mine, :], weight_by, w_sems.at[number]),
            ]
        loads[number] = [
            load(
                source.reshape(size, 128).at[start : start + length],
                target.at[start : start + length],
                in_sems.at[kind, number],
            )
            for kind, (source, target) in enumerate(((m_one, one), (m_two, two)))
        ]
    passes = [load(out_in, out_by, pass_sems.at[0]), load(tgrad_in, tgrad_by, pass_sems.at[1])]

    def flatten(source, target, base):
        lines, groups = source.shape[0], source.shape[1] // 128
        for col in range(groups):
            value = source[:, col * 128 : (col + 1) * 128].astype(F32)
            for row in range(0, lines, 8):
                target[pl.ds(base + row * groups + col, 8, stride=groups), :] = value[row : row + 8, :]

    def vector_rows():
        share = g_vec.shape[1] // 128
        groups = vec.shape[1] // 128
        for col in range(groups):
            lanes = slice(col * 128, (col + 1) * 128)
            vec_flat[pl.ds(col, 8, stride=groups), :] = vec[0:8, lanes]
            for row in range(8, vec.shape[0]):
                vec_flat[row * groups + col : row * groups + col + 1, :] = vec[row : row + 1, lanes]
        place = lax.broadcasted_iota(jnp.int32, vec_flat.shape, 0)
        for number in range(share):
            spot = slice(tail + number, tail + number + 1)
            grads[spot, :] = g_vec[0:1, number * 128 : (number + 1) * 128]
            params[spot, :] = jnp.sum(
                jnp.where(place == index * share + number, vec_flat[...], 0.0), axis=0, keepdims=True
            )

    fix_one = 1.0 / (1.0 - beta_one**step_count)
    fix_two = 1.0 / (1.0 - beta_two**step_count)

    def update(at):
        grad, param = grads[at, :], params[at, :]
        new_one = beta_one * one[at, :] + (1.0 - beta_one) * grad
        new_two = beta_two * two[at, :] + (1.0 - beta_two) * grad * grad
        one[at, :] = new_one
        two[at, :] = new_two
        change = new_one * fix_one / (jnp.sqrt(new_two * fix_two) + adam_eps)
        params[at, :] = param - learn_rate * (change + decay_rate * param)

    vector_rows()
    copies = []
    for number in order:
        start, length = spans[number]
        if number < len(kinds):
            grad, grad_by, weight, weight_by = kinds[number]
            for made in blocks[number]:
                made.wait()
            flatten(grad_by, grads, start)
            flatten(weight_by, params, start)
        for made in loads[number]:
            made.wait()
        if number < len(kinds):

            @pl.loop(0, length // 64)
            def _(chunk, start=start):
                update(pl.ds(pl.multiple_of(start + chunk * 64, 64), 64))

        else:
            update(slice(start, start + 8))
        for kind, (source, target) in enumerate(
            ((grads, rows_out), (params, params_out), (one, one_out), (two, two_out))
        ):
            copies.append(
                load(
                    source.at[start : start + length],
                    target.reshape(size, 128).at[start : start + length],
                    out_sems.at[kind, number],
                )
            )
        if number == order[0]:
            for made, source, target, sem in zip(
                passes, (out_by, tgrad_by), (out_ref, tgrad_ref), (pass_sems.at[2], pass_sems.at[3])
            ):
                made.wait()
                copies.append(load(source, target, sem))
    for made in copies:
        made.wait()


def slot_body(tokens, out_grad, lengths, w_qkv, w_out, w_in, w_fc2, vectors, moment_one, moment_two):
    slots, piece, width = tokens.shape
    devices, depth = lax.axis_size("dp"), lax.axis_size("ctx")
    chips = devices // 2
    count = devices * depth
    features = w_in.shape[1]
    half = 2 * piece
    rows = 2 * half
    block = D // devices
    wide = features // devices
    lines = D // count
    total = rows * chips
    low = lambda *shape: pltpu.VMEM(shape, BF16)
    wide_f32 = lambda *shape: pltpu.VMEM(shape, F32)
    anywhere = pl.BlockSpec(memory_space=pl.ANY)
    inside = pl.BlockSpec(memory_space=pltpu.VMEM)
    copies = 96
    out, tokens_grad, grad_qkv, grad_out_w, grad_in, grad_fc2, vector_grad = pl.pallas_call(
        partial(slot_kernel, devices, depth, features),
        out_shape=(
            jax.ShapeDtypeStruct(tokens.shape, BF16),
            jax.ShapeDtypeStruct(tokens.shape, BF16),
            jax.ShapeDtypeStruct((lines, 3 * D), F32),
            jax.ShapeDtypeStruct((lines, D), F32),
            jax.ShapeDtypeStruct((lines, features), F32),
            jax.ShapeDtypeStruct((features // count, D), F32),
            jax.ShapeDtypeStruct((8, 3 * block), F32),
        ),
        in_specs=[anywhere, anywhere, pl.BlockSpec(memory_space=pltpu.SMEM), inside] + [anywhere] * 4,
        out_specs=(inside,) * 7,
        scratch_shapes=[
            low(D, 3 * D // 2),
            low(D // 2, D),
            low(D, features // 2),
            low(features // 2, D),
            low(total, D),
            low(total, D),
            low(total, D),
            low(total, D),
            low(rows, D),
            low(total, 4 * block),
            low(chips - 1, rows, 4 * block),
            low(rows, D),
            pltpu.VMEM((slots, 128), jnp.int32),
            low(rows, 3 * D // 2),
            wide_f32(rows, D),
            low(rows, D),
            low(rows, D),
            low(rows, D),
            low(rows, D),
            wide_f32(half, D),
            wide_f32(rows, D),
            wide_f32(rows, D),
            wide_f32(rows, D),
            wide_f32(rows, features // 2),
            low(rows, features // 2),
            low(total, wide),
            low(total, wide),
            low(chips, 2 * wide // depth, D),
            low(chips - 1, 2 * wide // depth, D),
            low(D, wide),
            low(wide, D),
            low(depth, devices * lines, 4 * block),
            low(depth - 1, devices * lines, 4 * block),
            low(depth - 1, devices * lines, 4 * block),
            low(devices, lines, wide),
            low(devices, lines, wide),
            low(devices, lines + 16, 4 * block),
            low(devices, lines + 16, 4 * block),
            wide_f32(16, D),
            wide_f32(devices * depth, 4 * block),
            wide_f32(depth - 1, devices, 4 * block),
            wide_f32(rows, 4 * block),
            low(rows, 3 * D // 2),
            low(half, D),
            low(*tokens.shape),
            low(half, D),
            low(*tokens.shape),
            pltpu.VMEM((slots, 128), jnp.int32),
            pltpu.SemaphoreType.DMA((6 * chips,)),
            pltpu.SemaphoreType.DMA((copies,)),
            pltpu.SemaphoreType.DMA((copies,)),
        ],
        compiler_params=pltpu.CompilerParams(
            collective_id=0, has_side_effects=True, vmem_limit_bytes=64 * 1024 * 1024 - 64 * 1024
        ),
        name="slot",
    )(tokens, out_grad, lengths, vectors, w_qkv, w_out, w_in, w_fc2)
    size = moment_one.shape[1] // 128
    padded = (size + 7) // 8 * 8
    flat = jax.ShapeDtypeStruct(moment_one.shape, F32)
    return pl.pallas_call(
        partial(adam_kernel, count),
        out_shape=(
            jax.ShapeDtypeStruct(tokens.shape, BF16),
            jax.ShapeDtypeStruct(tokens.shape, BF16),
            flat,
            flat,
            flat,
            flat,
        ),
        in_specs=[anywhere] * 4 + [inside] * 2 + [anywhere] * 8,
        out_specs=(anywhere,) * 6,
        scratch_shapes=[wide_f32(padded, 128)] * 4
        + [
            wide_f32(lines, 3 * D),
            wide_f32(lines, D),
            wide_f32(lines, features),
            wide_f32(features // count, D),
            low(lines, 3 * D),
            low(lines, D),
            low(lines, features),
            low(features // count, D),
            low(*tokens.shape),
            low(*tokens.shape),
            wide_f32(vectors.shape[0] * D // 128, 128),
            pltpu.SemaphoreType.DMA((2, 5)),
            pltpu.SemaphoreType.DMA((4,)),
            pltpu.SemaphoreType.DMA((4,)),
            pltpu.SemaphoreType.DMA((4, 5)),
            pltpu.SemaphoreType.DMA((4,)),
        ],
        compiler_params=pltpu.CompilerParams(vmem_limit_bytes=64 * 1024 * 1024 - 64 * 1024),
        name="adam",
    )(
        grad_qkv, grad_out_w, grad_in, grad_fc2, vector_grad, vectors, out, tokens_grad,
        w_qkv, w_out, w_in, w_fc2, moment_one, moment_two,
    )


def layer(tokens, *rest):
    slots, piece, width = tokens.shape
    devices, depth = lax.axis_size("dp"), lax.axis_size("ctx")
    fits = slots == 2 and depth == 2 * slots and devices == 2 * depth and FF == (devices // 2) * D
    if fits and (H * HD // devices) % 128 == 0 and (FF // devices) % 128 == 0:
        return slot_body(tokens, *rest)
    return body(tokens, *rest)


def solution(mesh):
    placed = (
        P("dp", "ctx", None),
        P("dp", "ctx", None),
        P("dp"),
        P(),
        P(),
        P(),
        P(),
        P(),
        P(("dp", "ctx"), None),
        P(("dp", "ctx"), None),
    )
    return jax.shard_map(
        layer,
        mesh=mesh,
        in_specs=placed,
        out_specs=(
            P("dp", "ctx", None),
            P("dp", "ctx", None),
            P(("dp", "ctx"), None),
            P(("dp", "ctx"), None),
            P(("dp", "ctx"), None),
            P(("dp", "ctx"), None),
        ),
        check_vma=False,
    )
```

```python
from functools import partial

import jax
import jax.numpy as jnp
from jax import lax
from jax.experimental import pallas as pl
from jax.experimental.pallas import tpu as pltpu
from jax.sharding import PartitionSpec as P

D = 1024
H = 16
HD = 64
FF = 4096


EPSILON = 1e-05
learn_rate = 0.01
beta_one = 0.9
beta_two = 0.999
adam_eps = 1e-08
decay_rate = 0.01
step_count = 10.0


def layer_norm(values, gain, shift):
    center = values - jnp.mean(values, axis=-1, keepdims=True)
    spread = jnp.mean(center * center, axis=-1, keepdims=True)
    return center * lax.rsqrt(spread + EPSILON) * gain + shift


def split_vectors(vectors):
    ratio = FF // D
    return (
        vectors[0],
        vectors[1],
        vectors[2],
        vectors[3 : 3 + ratio].reshape(FF),
        vectors[3 + ratio],
        vectors[4 + ratio],
        vectors[5 + ratio],
        vectors[6 + ratio],
        vectors[7 + ratio],
    )


def inner(left, right):
    return lax.dot_general(
        left, right, (((0,), (0,)), ((), ())), preferred_element_type=jnp.float32
    )


def through(left, weight):
    return lax.dot_general(
        left, weight, (((1,), (1,)), ((), ())), preferred_element_type=jnp.float32
    )


def run_slots(function, items):
    return lax.map(lambda item: function(*item), items)


def heads_block():
    return 4


def split_heads(matrix):
    count = matrix.shape[0]
    group = heads_block()
    return jnp.moveaxis(matrix.reshape(count, H // group, group, HD), 1, 0)


def join_heads(blocked):
    return jnp.moveaxis(blocked, 0, 1).reshape(blocked.shape[1], H * HD)


def split_stats(stats):
    group = heads_block()
    return stats.reshape(H // group, group, stats.shape[-1])


def shard_piece(left, right, number, shard_count):
    weight_rows = left.shape[1]
    columns = right.shape[1]
    per_shard = weight_rows * columns // shard_count
    block = inner(left, right).reshape(-1)
    return block.reshape(number, per_shard)


def project(flat_tokens, w_qkv, vectors):
    joined = jnp.dot(flat_tokens, w_qkv, preferred_element_type=jnp.float32)
    queries = ((joined[:, :D] + vectors[0]) * 0.125).astype(jnp.bfloat16)
    keys = joined[:, D : 2 * D].astype(jnp.bfloat16)
    values = (joined[:, 2 * D :] + vectors[1]).astype(jnp.bfloat16)
    return (queries, keys, values)


def attend_slot(queries, keys, values, live):
    rows = queries.shape[0]

    def attend_one_block(item):
        query_heads, key_heads, value_heads = item
        scores = jnp.einsum(
            "qhd,khd->hqk", query_heads, key_heads, preferred_element_type=jnp.float32
        )
        scores = jnp.where(live[None, None, :], scores, -1e30)
        maximum = jnp.max(scores, axis=-1, keepdims=True)
        expo = jnp.exp(scores - maximum)
        total = jnp.sum(expo, axis=-1, keepdims=True)
        probs_low = (expo / total).astype(jnp.bfloat16)
        mixed = jnp.einsum(
            "hqk,khd->qhd", probs_low, value_heads, preferred_element_type=jnp.float32
        )
        return (mixed, (maximum + jnp.log(total))[..., 0])

    mixed, log_total = lax.map(
        attend_one_block, (split_heads(queries), split_heads(keys), split_heads(values))
    )
    return (join_heads(mixed), log_total.reshape(H, rows))


def query_back(queries, keys, values, live, log_total, grad_mixed, with_keys):
    rows = queries.shape[0]

    def query_one_block(item):
        query_heads, key_heads, value_heads, grad_heads, block_log = item
        scores = jnp.einsum(
            "qhd,khd->hqk", query_heads, key_heads, preferred_element_type=jnp.float32
        )
        scores = jnp.where(live[None, None, :], scores, -1e30)
        probs = jnp.exp(scores - block_log[:, :, None])
        grad_probs = jnp.einsum(
            "qhd,khd->hqk", grad_heads, value_heads, preferred_element_type=jnp.float32
        )
        row_sums = jnp.sum(probs * grad_probs, axis=-1)
        grad_scores = (probs * (grad_probs - row_sums[:, :, None])).astype(jnp.bfloat16)
        grad_query = jnp.einsum(
            "hqk,khd->qhd", grad_scores, key_heads, preferred_element_type=jnp.float32
        )
        grad_key = jnp.einsum(
            "hqk,qhd->khd", grad_scores, query_heads, preferred_element_type=jnp.float32
        )
        grad_value = jnp.einsum(
            "hqk,qhd->khd",
            probs.astype(jnp.bfloat16),
            grad_heads,
            preferred_element_type=jnp.float32,
        )
        return (grad_query, row_sums, grad_key, grad_value)

    items = (
        split_heads(queries),
        split_heads(keys),
        split_heads(values),
        split_heads(grad_mixed),
        split_stats(log_total),
    )
    results = lax.map(query_one_block, items)
    grad_query, row_sums, grad_key, grad_value = results
    return (
        join_heads(grad_query),
        row_sums.reshape(H, rows),
        join_heads(grad_key),
        join_heads(grad_value),
    )


def tail(flat_tokens, mixed, w_out, w_in, w_fc2, vectors):
    bias_q, bias_v, bias_o, bias_in, bias_fc2, gain_one, shift_one, gain_two, shift_two = (
        split_vectors(vectors)
    )
    mixed_low = mixed.astype(jnp.bfloat16)
    summed_one = (
        flat_tokens.astype(jnp.float32)
        + jnp.dot(mixed_low, w_out, preferred_element_type=jnp.float32)
        + bias_o
    )
    normed = layer_norm(summed_one, gain_one, shift_one)
    normed_low = normed.astype(jnp.bfloat16)
    hidden_pre = jnp.dot(normed_low, w_in, preferred_element_type=jnp.float32) + bias_in
    hidden_low = jax.nn.gelu(hidden_pre, approximate=False).astype(jnp.bfloat16)
    summed_two = normed + jnp.dot(hidden_low, w_fc2, preferred_element_type=jnp.float32) + bias_fc2
    result = layer_norm(summed_two, gain_two, shift_two)
    return (mixed_low, summed_one, normed_low, hidden_pre, hidden_low, summed_two, result)


def body(tokens, out_grad, lengths, w_qkv, w_out, w_in, w_fc2, vectors, moment_one, moment_two):
    slots, piece, width = tokens.shape
    length = piece * lax.axis_size("ctx")
    local_pos = lax.axis_index("ctx") * piece + jnp.arange(piece, dtype=jnp.int32)
    own_live = local_pos[None, :] < lengths[:, None]
    valid = own_live.astype(jnp.float32)
    key_live = jnp.arange(length, dtype=jnp.int32)[None, :] < lengths[:, None]
    bias_q, bias_v, bias_o, bias_in, bias_fc2, gain_one, shift_one, gain_two, shift_two = (
        split_vectors(vectors)
    )
    flat_tokens = tokens.reshape(slots * piece, width)
    queries, keys, values = project(flat_tokens, w_qkv, vectors)
    keys_all, values_all = (
        lax.all_gather(keys.reshape(slots, piece, width), "ctx", axis=1, tiled=True),
        lax.all_gather(values.reshape(slots, piece, width), "ctx", axis=1, tiled=True),
    )
    mixed, log_total = run_slots(
        attend_slot, (queries.reshape(slots, piece, width), keys_all, values_all, key_live)
    )
    saved = tail(flat_tokens, mixed.reshape(slots * piece, width), w_out, w_in, w_fc2, vectors)
    out = (saved[6].reshape(slots, piece, width) * valid[..., None]).astype(jnp.bfloat16)
    again = lax.optimization_barrier(flat_tokens)
    queries, keys, values = project(again, w_qkv, vectors)
    keys_all, values_all = (
        lax.all_gather(keys.reshape(slots, piece, width), "ctx", axis=1, tiled=True),
        lax.all_gather(values.reshape(slots, piece, width), "ctx", axis=1, tiled=True),
    )
    mixed, log_total = run_slots(
        attend_slot, (queries.reshape(slots, piece, width), keys_all, values_all, key_live)
    )
    saved = tail(again, mixed.reshape(slots * piece, width), w_out, w_in, w_fc2, vectors)
    mixed_low, summed_one, normed_low, hidden_pre, hidden_low, summed_two, result = saved
    cotangent = (out_grad.astype(jnp.float32) * valid[..., None]).reshape(slots * piece, width)
    unused_two, norm_two_back = jax.vjp(layer_norm, summed_two, gain_two, shift_two)
    grad_two, grad_gain_two, grad_shift_two = norm_two_back(cotangent)
    grad_fc2_low = grad_two.astype(jnp.bfloat16)
    bias_fc2_grad = jnp.sum(grad_fc2_low.astype(jnp.float32), axis=0)
    grad_hidden = through(grad_fc2_low, w_fc2)
    unused_gelu, gelu_back = jax.vjp(partial(jax.nn.gelu, approximate=False), hidden_pre)
    grad_pre_low = gelu_back(grad_hidden)[0].astype(jnp.bfloat16)
    bias_in_grad = jnp.sum(grad_pre_low.astype(jnp.float32), axis=0)
    grad_normed = grad_two + through(grad_pre_low, w_in)
    unused_one, norm_one_back = jax.vjp(layer_norm, summed_one, gain_one, shift_one)
    grad_one, grad_gain_one, grad_shift_one = norm_one_back(grad_normed)
    grad_branch_low = grad_one.astype(jnp.bfloat16)
    bias_out_grad = jnp.sum(grad_branch_low.astype(jnp.float32), axis=0)
    grad_mixed_low = (
        through(grad_branch_low, w_out).astype(jnp.bfloat16).reshape(slots, piece, width)
    )
    queries_slots = queries.reshape(slots, piece, width)
    grad_query, row_sums, grad_key, grad_value = run_slots(
        partial(query_back, with_keys=True),
        (queries_slots, keys_all, values_all, key_live, log_total, grad_mixed_low),
    )
    grad_key, grad_value = (
        lax.psum_scatter(
            grad_key.astype(jnp.bfloat16), "ctx", scatter_dimension=1, tiled=True
        ).astype(jnp.float32),
        lax.psum_scatter(
            grad_value.astype(jnp.bfloat16), "ctx", scatter_dimension=1, tiled=True
        ).astype(jnp.float32),
    )
    rows = slots * piece
    grad_query_low = grad_query.reshape(rows, width).astype(jnp.bfloat16) * jnp.bfloat16(0.125)
    grad_key_low = grad_key.reshape(rows, width).astype(jnp.bfloat16)
    grad_value_low = grad_value.reshape(rows, width).astype(jnp.bfloat16)
    grad_joined = jnp.concatenate([grad_query_low, grad_key_low, grad_value_low], axis=1)
    bias_q_grad = jnp.sum(grad_query_low.astype(jnp.float32), axis=0)
    bias_v_grad = jnp.sum(grad_value_low.astype(jnp.float32), axis=0)
    tokens_grad = (
        (grad_one + through(grad_joined, w_qkv)).reshape(slots, piece, width).astype(jnp.bfloat16)
    )
    vector_grad = jnp.concatenate(
        [
            bias_q_grad[None],
            bias_v_grad[None],
            bias_out_grad[None],
            bias_in_grad.reshape(FF // D, D),
            bias_fc2_grad[None],
            grad_gain_one[None],
            grad_shift_one[None],
            grad_gain_two[None],
            grad_shift_two[None],
        ],
        axis=0,
    )
    count = lax.axis_size(("dp", "ctx"))
    vector_rows = vector_grad.reshape(count, -1)
    pairs = (
        (flat_tokens, grad_joined),
        (mixed_low, grad_branch_low),
        (normed_low, grad_pre_low),
        (hidden_low, grad_fc2_low),
    )
    blocks = [
        shard_piece(left, right, 1 * lax.axis_size(("dp", "ctx")), count) for left, right in pairs
    ]
    blocks.append(vector_rows)
    grad_rows = lax.psum_scatter(
        jnp.concatenate(blocks, axis=1), ("dp", "ctx"), scatter_dimension=0, tiled=True
    )
    index = lax.axis_index(("dp", "ctx"))
    params = jnp.concatenate(
        [
            lax.dynamic_slice_in_dim(weight.reshape(count, -1), index, 1, 0).astype(jnp.float32)
            for weight in (w_qkv, w_out, w_in, w_fc2, vectors)
        ],
        axis=1,
    )
    new_one = beta_one * moment_one + (1.0 - beta_one) * grad_rows
    new_two = beta_two * moment_two + (1.0 - beta_two) * grad_rows * grad_rows
    fix_one = 1.0 - beta_one**step_count
    fix_two = 1.0 - beta_two**step_count
    update = new_one / fix_one / (jnp.sqrt(new_two / fix_two) + adam_eps)
    new_params = params - learn_rate * (update + decay_rate * params)
    return (out, tokens_grad, grad_rows, new_params, new_one, new_two)


BF16 = jnp.bfloat16
F32 = jnp.float32


def layer_norm_stats(values):
    center = values - jnp.mean(values, axis=-1, keepdims=True)
    spread = jnp.mean(center * center, axis=-1, keepdims=True)
    return center, lax.rsqrt(spread + EPSILON)


def layer_norm_back(center, scale, gain, cotangent):
    scaled = cotangent * gain
    mean_scaled = jnp.mean(scaled, axis=-1, keepdims=True)
    mean_cross = jnp.mean(scaled * center, axis=-1, keepdims=True)
    return scale * (scaled - mean_scaled - center * (scale * scale) * mean_cross)


def normal_cdf(values):
    return 0.5 * (1.0 + lax.erf(values * 0.7071067811865476))


def dot(left, right):
    return jnp.dot(left, right, preferred_element_type=F32)


def positions(axis, shape, slot, piece):
    place = lax.broadcasted_iota(jnp.int32, shape, axis)
    block = lax.div(place, piece)
    half = lax.div(block, 2)
    step = lax.rem(block, 2)
    return (2 * half + lax.rem(slot + step, 2)) * piece + lax.rem(place, piece)


def head_probs(queries, keys, live):
    scores = through(queries, keys)
    scores = jnp.where(live, scores, -1e30)
    expo = jnp.exp(scores - jnp.max(scores, axis=-1, keepdims=True))
    return expo / jnp.sum(expo, axis=-1, keepdims=True)


MESH = pl.DeviceIdType.MESH


class Links:
    def __init__(self, sends, recvs):
        self.sends, self.recvs = sends, recvs
        self.used = 0
        self.open = []

    def copy(self, source, target, device):
        self.used += 1
        return self.again(source, target, device)

    def again(self, source, target, device):
        number = self.used - 1
        return pltpu.make_async_remote_copy(
            src_ref=source,
            dst_ref=target,
            send_sem=self.sends.at[number],
            recv_sem=self.recvs.at[number],
            device_id=device,
            device_id_type=MESH,
        )

    def forward(self, source, target, device, earlier):
        self.used += 1
        return pltpu.make_async_remote_copy(
            src_ref=source,
            dst_ref=target,
            send_sem=self.sends.at[self.used - 1],
            recv_sem=self.recvs.at[earlier],
            device_id=device,
            device_id_type=MESH,
        )

    def send(self, source, target, device):
        made = self.copy(source, target, device)
        made.start()
        self.open.append((made, None))
        return made

    def send_if(self, condition, source, target, device):
        made = self.copy(source, target, device)
        pl.when(condition)(made.start)
        self.open.append((made, condition))
        return made

    def send_or_keep(self, here, source, target, device):
        number = self.used
        made = self.copy(source, target, device)
        local = pltpu.make_async_copy(source, target, self.recvs.at[number])
        pl.when(here)(local.start)
        away = jnp.logical_not(here)
        pl.when(away)(made.start)
        self.open.append((made, away))

        def wait():
            pl.when(here)(local.wait)
            pl.when(away)(made.wait_recv)

        return wait

    def close(self):
        for made, condition in self.open:
            if condition is None:
                made.wait_send()
            else:
                pl.when(condition)(made.wait_send)


def flip(value, mask):
    result = value
    bit = 1
    while bit <= mask:
        if mask & bit:
            result = result + bit * (1 - 2 * lax.rem(lax.div(value, bit), 2))
        bit *= 2
    return result


def flip_traced(value, mask, size):
    result = value
    bit = 1
    while bit < size:
        set_bit = lax.rem(lax.div(mask, bit), 2)
        result = result + bit * set_bit * (1 - 2 * lax.rem(lax.div(value, bit), 2))
        bit *= 2
    return result


def at_rows(start, size):
    return pl.ds(pl.multiple_of(start, 64), size)


def slot_kernel(devices, depth, features, *refs):
    (
        tokens, out_grad, lengths, vec, w_qkv, w_out, w_in, w_fc2,
        out_ref, tgrad_ref, g_qkv, g_out, g_in, g_fc2, g_vec,
        wqkv, wo, w_up, w_down,
        x_all, n_all, g_all, m_all, b_all, j_all, j_send, g_rows, lens_peer,
        qkv, part, part_low, part_a, part_b, part_c, part_d, summed, grad_two, grad_one,
        pre_s, hid, hid_all, gp_all, packed, plane_got, up_mine, down_mine, packed_two, right_two, left_two,
        trade_in, got_in, trade_qkv, got_qkv, vec_s, vec_by, vec_got, sums, dqkv, out_half, out_got, tg_half, tg_got, lens,
        local_sems, sends, recvs,
    ) = refs
    chips = devices // 2
    me, slot = lax.axis_index("dp"), lax.axis_index("ctx")
    core, chip = lax.rem(me, 2), lax.div(me, 2)
    base = me - core
    peer = (base + 1 - core, slot)
    piece = tokens.shape[1]
    half = 2 * piece
    rows = 2 * half
    block = D // devices
    wide = features // devices
    lines = D // (devices * depth)
    net = Links(sends, recvs)
    mine_at = at_rows(core * half, half)
    other_at = at_rows((1 - core) * half, half)
    chunk = 32

    row_of = lax.broadcasted_iota(jnp.int32, lens.shape, 0)
    lens[...] = jnp.where(row_of == 0, lengths[0], lengths[1])
    vec_s[...] = jnp.zeros_like(vec_s)
    loads = []

    def load(source, target):
        made = pltpu.make_async_copy(source, target, local_sems.at[len(loads)])
        made.start()
        loads.append(made)

    where = [2 * flip(chip, mask) + core for mask in range(chips)]
    for mask in range(chips):
        for kind in range(3):
            start = pl.multiple_of(kind * D + where[mask] * block, block)
            load(
                w_qkv.at[:, pl.ds(start, block)],
                wqkv.at[:, (3 * mask + kind) * block : (3 * mask + kind + 1) * block],
            )
    n_qkv = len(loads)
    for number in range(chips):
        start = pl.multiple_of((2 * number + core) * block, block)
        load(w_out.at[pl.ds(start, block), :], wo.at[number * block : (number + 1) * block, :])
    n_out = len(loads)
    for mask in range(chips):
        start = pl.multiple_of(where[mask] * wide, wide)
        load(w_in.at[:, pl.ds(start, wide)], w_up.at[:, mask * wide : (mask + 1) * wide])
    n_up = len(loads)
    for mask in range(chips):
        start = pl.multiple_of(where[mask] * wide, wide)
        load(w_fc2.at[pl.ds(start, wide), :], w_down.at[mask * wide : (mask + 1) * wide, :])

    barrier = pltpu.get_barrier_semaphore()
    friends = [(flip(me, mask), slot) for mask in range(1, devices)]
    for shift in range(1, depth):
        far = lax.rem(slot + shift, depth)
        friends += [(me, far), (flip(me, 1), far)]
    for friend in friends:
        pl.semaphore_signal(barrier, inc=1, device_id=friend, device_id_type=MESH)
    pl.semaphore_wait(barrier, len(friends))

    def spread(source, target):
        waits = []
        for step in range(2):
            pick = lax.rem(slot + step, 2)
            upper = lax.div(slot, 2)
            place = 2 * core + pick
            here = jnp.logical_and(upper == core, place == slot)
            waits.append(
                net.send_or_keep(
                    here,
                    source.at[pick],
                    target.at[at_rows((2 * upper + step) * piece, piece)],
                    (base + upper, place),
                )
            )
        return waits

    def pass_on(waits, target):
        made = []
        for step, wait in enumerate(waits):
            wait()
            spot = target.at[at_rows((2 * core + step) * piece, piece)]
            made.append(net.send(spot, spot, peer))
        return made

    token_waits = spread(tokens, x_all)
    grad_waits = spread(out_grad, g_rows)
    lens_copy = net.send(lens, lens_peer, peer)
    token_passes = pass_on(token_waits, x_all)

    def plane_start(target):
        source = target.at[mine_at]
        return [
            net.send(
                source, target.at[at_rows(mask * rows + core * half, half)], (flip(me, 2 * mask), slot)
            )
            for mask in range(1, chips)
        ]

    def plane_pass(copies, target):
        made = []
        for mask, copy in enumerate(copies, 1):
            copy.wait_recv()
            spot = target.at[at_rows(mask * rows + core * half, half)]
            made.append(net.send(spot, spot, peer))
        return made

    class Column:
        def __init__(self, target):
            self.target = target
            self.parts, self.numbers = {}, {}
            for place in (2, 1, 3):
                far = lax.rem(slot + depth - place, depth)
                made = net.copy(target.at[mine_at], self.spot(place), (me, far))
                self.parts[place], self.numbers[place] = made, net.used - 1
                goes = {1: slot != 0, 2: slot >= 0, 3: slot != depth - 1}[place]
                net.open.append((made, goes))
                pl.when(goes)(made.start)
            self.passes = {}

        def spot(self, place):
            return self.target.at[at_rows(place * rows + core * half, half)]

        def relay(self):
            self.inner = jnp.logical_or(slot == 1, slot == 2)
            self.passes[2] = net.copy(self.spot(2), self.spot(2), peer)
            net.open.append((self.passes[2], None))
            pl.when(self.inner)(self.parts[2].wait_recv)
            up = net.forward(self.spot(2), self.spot(1), (me, depth - 1), self.numbers[1])
            down = net.forward(self.spot(2), self.spot(3), (me, 0), self.numbers[3])
            for made, here in ((up, slot == 2), (down, slot == 1)):
                pl.when(here)(made.start)
                net.open.append((made, here))
            pl.when(self.inner)(self.passes[2].start)

        def late(self):
            @pl.when(jnp.logical_not(self.inner))
            def _():
                self.parts[2].wait_recv()
                self.passes[2].start()

        def hand_over(self, place):
            self.parts[place].wait_recv()
            self.passes[place] = net.send(self.spot(place), self.spot(place), peer)

    x_plane = plane_start(x_all)
    for made in loads[:n_qkv]:
        made.wait()
    lens_copy.wait_recv()
    for made in token_passes:
        made.wait_recv()
    owned = jnp.where(lax.div(slot, 2) == core, lens[...], lens_peer[...])
    length = jnp.where(lax.rem(slot, 2) == 0, owned[0:1, 0:1], owned[1:2, 0:1])
    live = positions(1, (1, rows), slot, piece) < length
    lane = lax.broadcasted_iota(jnp.int32, (1, block), 1)

    @pl.loop(0, chips)
    def _(mask):
        spot = 2 * flip_traced(chip, mask, chips) + core
        lanes = pl.ds(pl.multiple_of(spot * block, block), block)
        joined = dot(x_all[0:rows, :], wqkv[:, pl.ds(pl.multiple_of(mask * 3 * block, block), 3 * block)])
        queries = ((joined[:, 0:block] + vec[0:1, lanes]) * 0.125).astype(BF16)
        keys = joined[:, block : 2 * block].astype(BF16)
        values = (joined[:, 2 * block :] + vec[1:2, lanes]).astype(BF16)
        total = jnp.zeros((rows, block), F32)
        for head in range(block // HD):
            mine = lax.div(lane, HD) == head
            probs = head_probs(jnp.where(mine, queries, jnp.zeros_like(queries)), keys, live)
            total = jnp.where(mine, dot(probs.astype(BF16), values), total)
        start = pl.multiple_of(mask * 3 * block, block)
        qkv[:, pl.ds(start, block)] = queries
        qkv[:, pl.ds(pl.multiple_of(start + block, block), block)] = keys
        qkv[:, pl.ds(pl.multiple_of(start + 2 * block, block), block)] = values
        lanes = pl.ds(pl.multiple_of(core * chips * block + lax.div(spot, 2) * block, block), block)
        m_all[0:rows, lanes] = total.astype(BF16)

    for made in loads[n_qkv:n_out]:
        made.wait()

    def exchange(compute, target, before):
        made = []
        for number, at in enumerate((other_at, mine_at)):
            if before is not None:
                before[number].wait_send()
            value = compute(at)
            part[at, :] = value
            part_low[at, :] = value.astype(BF16)
            made.append(net.copy(part_low.at[at], target.at[at], peer))
            made[-1].start()
        return made

    my_lanes = pl.ds(pl.multiple_of(core * chips * block, chips * block), chips * block)
    first = exchange(lambda at: dot(m_all[at, my_lanes], wo[...]), part_a, None)
    own_mixed = m_all.at[0:rows, my_lanes]
    m_passes = [net.send(own_mixed, own_mixed, peer)]
    m_plane = [
        net.send(own_mixed, m_all.at[mask * rows : (mask + 1) * rows, my_lanes], (flip(me, 2 * mask), slot))
        for mask in range(1, chips)
    ]
    grad_passes = pass_on(grad_waits, g_rows)

    def norm_one(start):
        @pl.loop(0, half // chunk)
        def _(step):
            at = pl.ds(pl.multiple_of(start + step * chunk, chunk), chunk)
            total = x_all[at, :].astype(F32) + (part[at, :] + part_a[at, :].astype(F32)) + vec[2:3, :]
            center, scale = layer_norm_stats(total)
            summed[at, :] = total
            n_all[at, :] = (center * scale * vec[8:9, :] + vec[9:10, :]).astype(BF16)

    first[0].wait_recv()
    norm_one(core * half)
    n_column = Column(n_all)
    first[1].wait_recv()
    norm_one((1 - core) * half)
    for made in loads[n_out:]:
        made.wait()

    for number in range(chips):
        fine_cols = wide // depth
        begin = flip_traced(chip, number, chips) * wide + slot * fine_cols
        at = pl.ds(pl.multiple_of(begin, fine_cols), fine_cols)
        up_mine[:, number * fine_cols : (number + 1) * fine_cols] = w_up[:, at]
        down_mine[number * fine_cols : (number + 1) * fine_cols, :] = w_down[at, :]

    def bias_of(mask):
        spot = flip_traced(chip, mask, chips)
        lanes = pl.ds(pl.multiple_of(core * wide, wide), wide)
        result = vec[3:4, lanes]
        for row in range(1, chips):
            result = jnp.where(spot == row, vec[3 + row : 4 + row, lanes], result)
        return result

    @pl.loop(0, chips)
    def _(mask):
        at = pl.ds(pl.multiple_of(mask * wide, wide), wide)
        value = dot(n_all[0:rows, :], w_up[:, at]) + bias_of(mask)
        pre_s[:, at] = value
        hid[:, at] = (value * normal_cdf(value)).astype(BF16)

    second = exchange(lambda at: dot(hid[at, :], w_down[...]), part_b, first)
    for made in grad_passes:
        made.wait_recv()

    def norm_two(start, own):
        @pl.loop(0, half // chunk)
        def _(step):
            begin = pl.multiple_of(start + step * chunk, chunk)
            at = pl.ds(begin, chunk)
            center, scale = layer_norm_stats(summed[at, :])
            normed = center * scale * vec[8:9, :] + vec[9:10, :]
            center, scale = layer_norm_stats(normed + (part[at, :] + part_b[at, :].astype(F32)) + vec[7:8, :])
            place = begin + lax.broadcasted_iota(jnp.int32, (chunk, 1), 0)
            piece_of = lax.div(place, piece)
            spot = 2 * lax.div(piece_of, 2) + lax.rem(slot + lax.rem(piece_of, 2), 2)
            valid = (spot * piece + lax.rem(place, piece) < length).astype(F32)
            unit = center * scale
            error = g_rows[at, :].astype(F32) * valid
            grad = layer_norm_back(center, scale, vec[10:11, :], error)
            grad_two[at, :] = grad
            low = grad.astype(BF16)
            g_all[at, :] = low
            if own:
                out_half[pl.ds(pl.multiple_of(step * chunk, chunk), chunk), :] = (
                    valid * (unit * vec[10:11, :] + vec[11:12, :])
                ).astype(BF16)
                vec_s[7:8, :] += jnp.sum(low.astype(F32), axis=0, keepdims=True)
                vec_s[10:11, :] += jnp.sum(error * unit, axis=0, keepdims=True)
                vec_s[11:12, :] += jnp.sum(error, axis=0, keepdims=True)

    def go_back(source, target):
        waits = []
        for step in range(2):
            place = 2 * core + lax.rem(slot + step, 2)
            upper = lax.div(slot, 2)
            here = jnp.logical_and(upper == core, place == slot)
            waits.append(
                net.send_or_keep(
                    here,
                    source.at[step * piece : (step + 1) * piece],
                    target.at[lax.rem(slot, 2)],
                    (base + upper, place),
                )
            )
        return waits

    second[0].wait_recv()
    norm_two(core * half, True)
    g_column = Column(g_all)
    second[1].wait_recv()
    norm_two((1 - core) * half, False)
    out_waits = go_back(out_half, out_got)

    def mixed_pass():
        for mask, made in enumerate(m_plane, 1):
            made.wait_recv()
            spot = m_all.at[mask * rows : (mask + 1) * rows, my_lanes]
            m_passes.append(net.send(spot, spot, peer))

    def slope_of(value, cdf):
        return cdf + value * (jnp.exp(-0.5 * value * value) * 0.3989422804014327)

    @pl.loop(0, chips)
    def _(mask):
        at = pl.ds(pl.multiple_of(mask * wide, wide), wide)
        value = pre_s[:, at]
        grad = through(g_all[0:rows, :], w_down[at, :])
        hid[:, at] = (grad * slope_of(value, normal_cdf(value))).astype(BF16)

    third = exchange(lambda at: through(hid[at, :], w_up[...]), part_c, second)

    def norm_one_back(start, own):
        @pl.loop(0, half // chunk)
        def _(step):
            at = pl.ds(pl.multiple_of(start + step * chunk, chunk), chunk)
            center, scale = layer_norm_stats(summed[at, :])
            error = grad_two[at, :] + (part[at, :] + part_c[at, :].astype(F32))
            grad = layer_norm_back(center, scale, vec[8:9, :], error)
            low = grad.astype(BF16)
            b_all[at, :] = low
            grad_one[at, :] = grad
            if own:
                vec_s[2:3, :] += jnp.sum(low.astype(F32), axis=0, keepdims=True)
                vec_s[8:9, :] += jnp.sum(error * (center * scale), axis=0, keepdims=True)
                vec_s[9:10, :] += jnp.sum(error, axis=0, keepdims=True)

    x_pass = plane_pass(x_plane, x_all)

    third[0].wait_recv()
    norm_one_back(core * half, True)
    third[1].wait_recv()
    norm_one_back((1 - core) * half, False)
    class Line:
        def __init__(self, chunks, from_left, from_right):
            self.chunks, self.from_left, self.from_right = chunks, from_left, from_right
            self.up, self.down, self.first_up, self.first_down = [], [], [], []
            after = (me, lax.rem(slot + 1, depth))
            before = (me, lax.rem(slot + depth - 1, depth))
            for order in range(depth - 1):
                top, low = depth - 1 - order, order
                spot = from_left.at[order]
                self.up.append(net.copy(spot, spot, after))
                self.first_up.append(net.again(chunks.at[top], spot, after))
                net.open.append((self.up[-1], slot < top))
                spot = from_right.at[order]
                self.down.append(net.copy(spot, spot, before))
                self.first_down.append(net.again(chunks.at[low], spot, before))
                net.open.append((self.down[-1], slot > low))

        def first(self):
            for order in range(depth - 1):
                pl.when(slot == 0)(self.first_up[order].start)
                pl.when(slot == depth - 1)(self.first_down[order].start)

        def stage(self, time):
            for order in range(time):
                top, low = depth - 1 - order, order

                @pl.when(slot == time - order)
                def _(order=order, top=top):
                    self.up[order].wait_recv()
                    if time < depth - 1:
                        self.from_left[order] = (
                            self.from_left[order].astype(F32) + self.chunks[top].astype(F32)
                        ).astype(BF16)
                        self.up[order].start()

                @pl.when(depth - 1 - slot == time - order)
                def _(order=order, low=low):
                    self.down[order].wait_recv()
                    if time < depth - 1:
                        self.from_right[order] = (
                            self.from_right[order].astype(F32) + self.chunks[low].astype(F32)
                        ).astype(BF16)
                        self.down[order].start()

    grad_parts = range(1, chips)

    def attention_back(mask):
        start = mask * 3 * block
        queries = qkv[:, start : start + block]
        keys = qkv[:, start + block : start + 2 * block]
        values = qkv[:, start + 2 * block : start + 3 * block]
        turn = pl.ds(pl.multiple_of(lax.div(where[mask], 2) * block, block), block)
        grad_mixed = through(b_all[0:rows, :], wo[turn, :]).astype(BF16)
        grad_q = jnp.zeros((rows, block), F32)
        grad_k = grad_q
        grad_v = grad_q
        for head in range(block // HD):
            mine = lax.div(lane, HD) == head
            probs = head_probs(jnp.where(mine, queries, jnp.zeros_like(queries)), keys, live)
            grad_probs = through(jnp.where(mine, grad_mixed, jnp.zeros_like(grad_mixed)), values)
            dsum = jnp.sum(probs * grad_probs, axis=-1, keepdims=True)
            grad_scores = (probs * (grad_probs - dsum)).astype(BF16)
            grad_q = jnp.where(mine, dot(grad_scores, keys), grad_q)
            grad_k = jnp.where(mine, inner(grad_scores, queries), grad_k)
            grad_v = jnp.where(mine, inner(probs.astype(BF16), grad_mixed), grad_v)
        grad_q = grad_q.astype(BF16) * jnp.bfloat16(0.125)
        grad_k = grad_k.astype(BF16)
        grad_v = grad_v.astype(BF16)
        spot = pl.ds(pl.multiple_of(where[mask] * block, block), block)
        vec_s[0:1, spot] = jnp.sum(grad_q.astype(F32), axis=0, keepdims=True)
        vec_s[1:2, spot] = jnp.sum(grad_v.astype(F32), axis=0, keepdims=True)
        dqkv[:, start : start + block] = grad_q
        dqkv[:, start + block : start + 2 * block] = grad_k
        dqkv[:, start + 2 * block : start + 3 * block] = grad_v
        if mask:
            joint = j_send.at[mask - 1]
        else:
            joint = j_all.at[0:rows]
        joint[:, 0:block] = grad_q
        joint[:, block : 2 * block] = grad_k
        joint[:, 2 * block : 3 * block] = grad_v
        joint[:, 3 * block : 4 * block] = b_all[0:rows, spot]
        if mask:
            return net.send(
                joint, j_all.at[mask * rows : (mask + 1) * rows], (flip(me, 2 * mask), slot)
            )
        return None

    n_column.relay()
    j_copies = [attention_back(mask) for mask in grad_parts]
    attention_back(0)
    mixed_pass()
    n_column.late()
    n_column.hand_over(1)
    n_column.hand_over(3)
    for made in third:
        made.wait_send()
    part[0:half, :] = through(dqkv[other_at, :], wqkv[...])
    tg_copy = net.copy(part.at[0:half], part_d, peer)
    tg_copy.start()
    part[half:rows, :] = grad_one[mine_at, :] + through(dqkv[mine_at, :], wqkv[...])
    tg_copy.wait_recv()
    tg_half[...] = (part[half:rows, :] + part_d[...]).astype(BF16)

    fine = wide // depth
    span = lines * depth
    features_at = pl.ds(pl.multiple_of((depth * core + slot) * fine, fine), fine)
    bias_mine = jnp.concatenate([vec[3 + number : 4 + number, features_at] for number in range(chips)], axis=1)

    def feed_rows(place):
        at = slice(place * rows, (place + 1) * rows)
        value = dot(n_all[at, :], up_mine[...]) + bias_mine
        cdf = normal_cdf(value)
        hid_all[at, :] = (value * cdf).astype(BF16)
        low = (through(g_all[at, :], down_mine[...]) * slope_of(value, cdf)).astype(BF16)
        gp_all[at, :] = low
        return jnp.sum(low.astype(F32), axis=0, keepdims=True)

    bias_sum = feed_rows(0)
    g_column.relay()
    for made in m_passes + x_pass + j_copies:
        made.wait_recv()
    for group in range(devices):
        at = slice(group * span, (group + 1) * span)
        begin = (group % 2) * chips * block + (group // 2) * block
        both = inner(x_all[:, at], j_all[:, 0 : 3 * block]).astype(BF16)
        across = inner(m_all[:, begin : begin + block], j_all[:, 3 * block : 4 * block]).astype(BF16)
        row = group * lines
        for number in range(depth):
            at = slice(number * lines, (number + 1) * lines)
            packed_two[number, row : row + lines, 0 : 3 * block] = both[at, :]
            packed_two[number, row : row + lines, 3 * block : 4 * block] = across[at, :]
    input_line = Line(packed_two, right_two, left_two)
    input_line.first()

    g_column.late()
    g_column.hand_over(1)
    g_column.hand_over(3)
    for place in (2, 1, 3):
        n_column.passes[place].wait_recv()
        g_column.passes[place].wait_recv()
        bias_sum = bias_sum + feed_rows(place)
    for number in range(chips):
        vec_s[3 + number : 4 + number, features_at] = bias_sum[:, number * fine : (number + 1) * fine]
    depth_rows = D // chips
    for number in range(chips):
        block_up = inner(n_all[:, number * depth_rows : (number + 1) * depth_rows], gp_all[...]).astype(BF16)
        packed[number, fine : 2 * fine, 0:wide] = block_up[0:fine, :]
        packed[number, fine : 2 * fine, wide : 2 * wide] = block_up[fine : 2 * fine, :]

    def scatter_plane(lines_at):
        return [
            net.send(
                packed.at[flip_traced(chip, mask, chips), lines_at],
                plane_got.at[mask - 1, lines_at],
                (flip(me, 2 * mask), slot),
            )
            for mask in range(1, chips)
        ]

    up_copies = scatter_plane(slice(fine, 2 * fine))
    packed[:, 0:fine, :] = inner(hid_all[...], g_all[...]).astype(BF16).reshape(chips, fine, D)
    down_copies = scatter_plane(slice(0, fine))

    tiles = vec.shape[0] * D // 128
    share = tiles // (devices * depth)
    vec_by[...] = jnp.zeros_like(vec_by)
    for tile in range(tiles):
        owner, lane_group = tile // share, tile % share
        row, col = tile // (D // 128), (tile % (D // 128)) * 128
        spot = (owner % depth) * devices + owner // depth
        vec_by[spot : spot + 1, lane_group * 128 : (lane_group + 1) * 128] = vec_s[
            row : row + 1, col : col + 128
        ]
    vec_copies = []
    for shift in range(1, depth):
        far = lax.rem(slot + shift, depth)
        spot = vec_by.at[pl.ds(pl.multiple_of(far * devices, devices), devices)]
        vec_copies.append(net.send(spot, vec_got.at[shift - 1], (me, far)))

    def finish(line, target, rows_at):
        target[...] = line.chunks[slot, rows_at, :].astype(F32)

        @pl.when(slot >= 1)
        def _():
            target[...] += line.from_left[depth - 1 - slot, rows_at, :].astype(F32)

        @pl.when(slot <= depth - 2)
        def _():
            target[...] += line.from_right[slot, rows_at, :].astype(F32)

    def plane_sum(copies, lines_at):
        for made in copies:
            made.wait_recv()
        value = packed[chip, lines_at, :].astype(F32)
        for number in range(chips - 1):
            value = value + plane_got[number, lines_at, :].astype(F32)
        return value

    def trade(source, target):
        return [
            net.send(source.at[flip(me, mask)], target.at[me], (flip(me, mask), slot))
            for mask in range(1, devices)
        ]

    tg_waits = go_back(tg_half, tg_got)
    for time in range(1, depth - 1):
        input_line.stage(time)
    low_sum = plane_sum(up_copies, slice(fine, 2 * fine)).astype(BF16)
    for upper in range(2):
        for number in range(depth):
            trade_in[upper * depth + number] = low_sum[
                number * lines : (number + 1) * lines, upper * wide : (upper + 1) * wide
            ]
    here = core * depth + slot
    in_copies = []
    for shift in range(1, 2 * depth):
        far = lax.rem(slot + shift % depth, depth)
        upper = core if shift < depth else 1 - core
        in_copies.append(net.send(trade_in.at[upper * depth + far], got_in.at[here], (base + upper, far)))
    input_line.stage(depth - 1)
    tg_copy.wait_send()
    finish(input_line, sums, slice(0, rows))
    vec_sum = vec_by[pl.ds(pl.multiple_of(slot * devices, devices), devices), :]
    for number, made in enumerate(vec_copies):
        made.wait_recv()
        vec_sum = vec_sum + vec_got[number]
    first_row = lax.broadcasted_iota(jnp.int32, (16, 4 * block), 0) == 0
    for group in range(devices):
        trade_qkv[group, 0:lines, :] = sums[group * lines : (group + 1) * lines, :].astype(BF16)
        trade_qkv[group, lines : lines + 16, :] = jnp.where(
            first_row, vec_sum[group : group + 1, :], 0.0
        ).astype(BF16)
    qkv_copies = trade(trade_qkv, got_qkv)
    for made in in_copies:
        made.wait_recv()
    got_in[here] = trade_in[here]
    for group in range(2 * depth):
        for number in range(chips):
            start = number * 2 * wide + group * fine
            g_in[:, start : start + fine] = got_in[group, :, number * fine : (number + 1) * fine].astype(F32)
    g_fc2[...] = plane_sum(down_copies, slice(0, fine))
    for wait in out_waits + tg_waits:
        wait()
    out_ref[...] = out_got[...]
    tgrad_ref[...] = tg_got[...]
    for made in qkv_copies:
        made.wait_recv()
    got_qkv[me] = trade_qkv[me]
    vec_sum = jnp.zeros((16, 3 * block), F32)
    for group in range(devices):
        vec_sum = vec_sum + got_qkv[group, lines : lines + 16, 0 : 3 * block].astype(F32)
        got = got_qkv[group, 0:lines, :].astype(F32)
        for kind in range(3):
            g_qkv[:, kind * D + group * block : kind * D + (group + 1) * block] = got[
                :, kind * block : (kind + 1) * block
            ]
        g_out[:, group * block : (group + 1) * block] = got[:, 3 * block : 4 * block]
    g_vec[...] = vec_sum[0:8, :]
    net.close()


def adam_kernel(count, *refs):
    (
        g_qkv, g_out, g_in, g_fc2, g_vec, vec, out_in, tgrad_in, w_qkv, w_out, w_in, w_fc2, m_one, m_two,
        out_ref, tgrad_ref, rows_out, params_out, one_out, two_out,
        grads, params, one, two, d_qkv, d_out, d_in, d_fc2, b_qkv, b_out, b_in, b_fc2, out_by, tgrad_by, vec_flat,
        in_sems, g_sems, w_sems, out_sems, pass_sems,
    ) = refs
    index = lax.axis_index("dp") * lax.axis_size("ctx") + lax.axis_index("ctx")
    size = m_one.shape[1] // 128
    kinds = (
        (g_qkv, d_qkv, w_qkv, b_qkv),
        (g_out, d_out, w_out, b_out),
        (g_in, d_in, w_in, b_in),
        (g_fc2, d_fc2, w_fc2, b_fc2),
    )
    lengths = [kind[1].shape[0] * kind[1].shape[1] // 128 for kind in kinds]
    starts = [sum(lengths[:number]) for number in range(len(kinds))]
    tail = sum(lengths)
    order = (3, 2, 0, 1, 4)
    spans = [(start, length) for start, length in zip(starts, lengths)] + [(tail, size - tail)]

    def load(source, target, sem):
        made = pltpu.make_async_copy(source, target, sem)
        made.start()
        return made

    blocks, loads = {}, {}
    for number in order:
        start, length = spans[number]
        if number < len(kinds):
            grad, grad_by, weight, weight_by = kinds[number]
            lines = weight_by.shape[0]
            mine = pl.ds(pl.multiple_of(index * lines, lines), lines)
            blocks[number] = [
                load(grad, grad_by, g_sems.at[number]),
                load(weight.at[mine, :], weight_by, w_sems.at[number]),
            ]
        loads[number] = [
            load(
                source.reshape(size, 128).at[start : start + length],
                target.at[start : start + length],
                in_sems.at[kind, number],
            )
            for kind, (source, target) in enumerate(((m_one, one), (m_two, two)))
        ]
    passes = [load(out_in, out_by, pass_sems.at[0]), load(tgrad_in, tgrad_by, pass_sems.at[1])]

    def flatten(source, target, base):
        lines, groups = source.shape[0], source.shape[1] // 128
        for col in range(groups):
            value = source[:, col * 128 : (col + 1) * 128].astype(F32)
            for row in range(0, lines, 8):
                target[pl.ds(base + row * groups + col, 8, stride=groups), :] = value[row : row + 8, :]

    def vector_rows():
        share = g_vec.shape[1] // 128
        groups = vec.shape[1] // 128
        for col in range(groups):
            lanes = slice(col * 128, (col + 1) * 128)
            vec_flat[pl.ds(col, 8, stride=groups), :] = vec[0:8, lanes]
            for row in range(8, vec.shape[0]):
                vec_flat[row * groups + col : row * groups + col + 1, :] = vec[row : row + 1, lanes]
        place = lax.broadcasted_iota(jnp.int32, vec_flat.shape, 0)
        for number in range(share):
            spot = slice(tail + number, tail + number + 1)
            grads[spot, :] = g_vec[0:1, number * 128 : (number + 1) * 128]
            params[spot, :] = jnp.sum(
                jnp.where(place == index * share + number, vec_flat[...], 0.0), axis=0, keepdims=True
            )

    fix_one = 1.0 / (1.0 - beta_one**step_count)
    fix_two = 1.0 / (1.0 - beta_two**step_count)

    def update(at):
        grad, param = grads[at, :], params[at, :]
        new_one = beta_one * one[at, :] + (1.0 - beta_one) * grad
        new_two = beta_two * two[at, :] + (1.0 - beta_two) * grad * grad
        one[at, :] = new_one
        two[at, :] = new_two
        change = new_one * fix_one / (jnp.sqrt(new_two * fix_two) + adam_eps)
        params[at, :] = param - learn_rate * (change + decay_rate * param)

    vector_rows()
    copies = []
    for number in order:
        start, length = spans[number]
        if number < len(kinds):
            grad, grad_by, weight, weight_by = kinds[number]
            for made in blocks[number]:
                made.wait()
            flatten(grad_by, grads, start)
            flatten(weight_by, params, start)
        for made in loads[number]:
            made.wait()
        if number < len(kinds):

            @pl.loop(0, length // 64)
            def _(chunk, start=start):
                update(pl.ds(pl.multiple_of(start + chunk * 64, 64), 64))

        else:
            update(slice(start, start + 8))
        for kind, (source, target) in enumerate(
            ((grads, rows_out), (params, params_out), (one, one_out), (two, two_out))
        ):
            copies.append(
                load(
                    source.at[start : start + length],
                    target.reshape(size, 128).at[start : start + length],
                    out_sems.at[kind, number],
                )
            )
        if number == order[0]:
            for made, source, target, sem in zip(
                passes, (out_by, tgrad_by), (out_ref, tgrad_ref), (pass_sems.at[2], pass_sems.at[3])
            ):
                made.wait()
                copies.append(load(source, target, sem))
    for made in copies:
        made.wait()


def slot_body(tokens, out_grad, lengths, w_qkv, w_out, w_in, w_fc2, vectors, moment_one, moment_two):
    slots, piece, width = tokens.shape
    devices, depth = lax.axis_size("dp"), lax.axis_size("ctx")
    chips = devices // 2
    count = devices * depth
    features = w_in.shape[1]
    half = 2 * piece
    rows = 2 * half
    block = D // devices
    wide = features // devices
    lines = D // count
    total = rows * chips
    low = lambda *shape: pltpu.VMEM(shape, BF16)
    wide_f32 = lambda *shape: pltpu.VMEM(shape, F32)
    anywhere = pl.BlockSpec(memory_space=pl.ANY)
    inside = pl.BlockSpec(memory_space=pltpu.VMEM)
    copies = 96
    out, tokens_grad, grad_qkv, grad_out_w, grad_in, grad_fc2, vector_grad = pl.pallas_call(
        partial(slot_kernel, devices, depth, features),
        out_shape=(
            jax.ShapeDtypeStruct(tokens.shape, BF16),
            jax.ShapeDtypeStruct(tokens.shape, BF16),
            jax.ShapeDtypeStruct((lines, 3 * D), F32),
            jax.ShapeDtypeStruct((lines, D), F32),
            jax.ShapeDtypeStruct((lines, features), F32),
            jax.ShapeDtypeStruct((features // count, D), F32),
            jax.ShapeDtypeStruct((8, 3 * block), F32),
        ),
        in_specs=[anywhere, anywhere, pl.BlockSpec(memory_space=pltpu.SMEM), inside] + [anywhere] * 4,
        out_specs=(inside,) * 7,
        scratch_shapes=[
            low(D, 3 * D // 2),
            low(D // 2, D),
            low(D, features // 2),
            low(features // 2, D),
            low(total, D),
            low(total, D),
            low(total, D),
            low(total, D),
            low(rows, D),
            low(total, 4 * block),
            low(chips - 1, rows, 4 * block),
            low(rows, D),
            pltpu.VMEM((slots, 128), jnp.int32),
            low(rows, 3 * D // 2),
            wide_f32(rows, D),
            low(rows, D),
            low(rows, D),
            low(rows, D),
            low(rows, D),
            wide_f32(half, D),
            wide_f32(rows, D),
            wide_f32(rows, D),
            wide_f32(rows, D),
            wide_f32(rows, features // 2),
            low(rows, features // 2),
            low(total, wide),
            low(total, wide),
            low(chips, 2 * wide // depth, D),
            low(chips - 1, 2 * wide // depth, D),
            low(D, wide),
            low(wide, D),
            low(depth, devices * lines, 4 * block),
            low(depth - 1, devices * lines, 4 * block),
            low(depth - 1, devices * lines, 4 * block),
            low(devices, lines, wide),
            low(devices, lines, wide),
            low(devices, lines + 16, 4 * block),
            low(devices, lines + 16, 4 * block),
            wide_f32(16, D),
            wide_f32(devices * depth, 4 * block),
            wide_f32(depth - 1, devices, 4 * block),
            wide_f32(rows, 4 * block),
            low(rows, 3 * D // 2),
            low(half, D),
            low(*tokens.shape),
            low(half, D),
            low(*tokens.shape),
            pltpu.VMEM((slots, 128), jnp.int32),
            pltpu.SemaphoreType.DMA((6 * chips,)),
            pltpu.SemaphoreType.DMA((copies,)),
            pltpu.SemaphoreType.DMA((copies,)),
        ],
        compiler_params=pltpu.CompilerParams(
            collective_id=0, has_side_effects=True, vmem_limit_bytes=64 * 1024 * 1024 - 64 * 1024
        ),
        name="slot",
    )(tokens, out_grad, lengths, vectors, w_qkv, w_out, w_in, w_fc2)
    size = moment_one.shape[1] // 128
    padded = (size + 7) // 8 * 8
    flat = jax.ShapeDtypeStruct(moment_one.shape, F32)
    return pl.pallas_call(
        partial(adam_kernel, count),
        out_shape=(
            jax.ShapeDtypeStruct(tokens.shape, BF16),
            jax.ShapeDtypeStruct(tokens.shape, BF16),
            flat,
            flat,
            flat,
            flat,
        ),
        in_specs=[anywhere] * 4 + [inside] * 2 + [anywhere] * 8,
        out_specs=(anywhere,) * 6,
        scratch_shapes=[wide_f32(padded, 128)] * 4
        + [
            wide_f32(lines, 3 * D),
            wide_f32(lines, D),
            wide_f32(lines, features),
            wide_f32(features // count, D),
            low(lines, 3 * D),
            low(lines, D),
            low(lines, features),
            low(features // count, D),
            low(*tokens.shape),
            low(*tokens.shape),
            wide_f32(vectors.shape[0] * D // 128, 128),
            pltpu.SemaphoreType.DMA((2, 5)),
            pltpu.SemaphoreType.DMA((4,)),
            pltpu.SemaphoreType.DMA((4,)),
            pltpu.SemaphoreType.DMA((4, 5)),
            pltpu.SemaphoreType.DMA((4,)),
        ],
        compiler_params=pltpu.CompilerParams(vmem_limit_bytes=64 * 1024 * 1024 - 64 * 1024),
        name="adam",
    )(
        grad_qkv, grad_out_w, grad_in, grad_fc2, vector_grad, vectors, out, tokens_grad,
        w_qkv, w_out, w_in, w_fc2, moment_one, moment_two,
    )


def layer(tokens, *rest):
    slots, piece, width = tokens.shape
    devices, depth = lax.axis_size("dp"), lax.axis_size("ctx")
    fits = slots == 2 and depth == 2 * slots and devices == 2 * depth and FF == (devices // 2) * D
    if fits and (H * HD // devices) % 128 == 0 and (FF // devices) % 128 == 0:
        return slot_body(tokens, *rest)
    return body(tokens, *rest)


def solution(mesh):
    placed = (
        P("dp", "ctx", None),
        P("dp", "ctx", None),
        P("dp"),
        P(),
        P(),
        P(),
        P(),
        P(),
        P(("dp", "ctx"), None),
        P(("dp", "ctx"), None),
    )
    return jax.shard_map(
        layer,
        mesh=mesh,
        in_specs=placed,
        out_specs=(
            P("dp", "ctx", None),
            P("dp", "ctx", None),
            P(("dp", "ctx"), None),
            P(("dp", "ctx"), None),
            P(("dp", "ctx"), None),
            P(("dp", "ctx"), None),
        ),
        check_vma=False,
    )
```
